32 devices in a mesh: ctx: 8 (over z, core), fsdp: 4 (over y, x).
Axes of the slice: x: 2, y: 2, z: 4, core: 2. Of those that a mesh axis runs over, the one named last changes fastest.
Arguments:
- tokens: bfloat16 [4, 1024, 2048], P('fsdp', 'ctx'), may hold values from -6 to 6
- cotangent: bfloat16 [4, 1024, 2048], P('fsdp', 'ctx'), may hold values from -6 to 6
- doc_ids: int32 [4, 1024], P('fsdp'), may hold values from 0 to 3, never falling along the last dimension, each value on 1 to 512 neighbouring positions
- block_order: int32 [16], replicated, may hold values from 0 to 15, each once
- front_weight: bfloat16 [2048, 14336], P(None, 'fsdp'), may hold values from -0.125 to 0.125
- back_weight: bfloat16 [10240, 2048], P(None, 'fsdp'), may hold values from -2 to 2
- front_master: float32 [2048, 14336], P('ctx', 'fsdp'), may hold values from -0.125 to 0.125
- back_master: float32 [10240, 2048], P('ctx', 'fsdp'), may hold values from -0.0625 to 0.0625
- front_first: float32 [2048, 14336], P('ctx', 'fsdp'), may hold values from -64 to 64
- back_first: float32 [10240, 2048], P('ctx', 'fsdp'), may hold values from -64 to 64
- front_second: float32 [2048, 14336], P('ctx', 'fsdp'), may hold values from 100 to 10000
- back_second: float32 [10240, 2048], P('ctx', 'fsdp'), may hold values from 2.048 to 204.8
- vectors: float32 [20480], replicated, may hold values from -2 to 2
- vector_first: float32 [20480], replicated, may hold values from -64 to 64
- vector_second: float32 [20480], replicated, may hold values from 100 to 10000
- learn_rates: float32 [3], replicated, may hold values from 0.02 to 0.2
- adam_step: int32 [1], replicated, may hold values from 1 to 8
Outputs:
- layer_out: bfloat16 [4, 1024, 2048], P('fsdp', 'ctx')
- tokens_grad: bfloat16 [4, 1024, 2048], P('fsdp', 'ctx')
- front_grad: float32 [2048, 14336], P('ctx', 'fsdp')
- back_grad: float32 [10240, 2048], P('ctx', 'fsdp')
- vector_grad: float32 [20480], replicated
- front_new: float32 [2048, 14336], P('ctx', 'fsdp')
- back_new: float32 [10240, 2048], P('ctx', 'fsdp')
- vectors_new: float32 [20480], replicated
- front_first_new: float32 [2048, 14336], P('ctx', 'fsdp')
- back_first_new: float32 [10240, 2048], P('ctx', 'fsdp')
- vector_first_new: float32 [20480], replicated
- front_second_new: float32 [2048, 14336], P('ctx', 'fsdp')
- back_second_new: float32 [10240, 2048], P('ctx', 'fsdp')
- vector_second_new: float32 [20480], replicated
- front_next: bfloat16 [2048, 14336], P(None, 'fsdp')
- back_next: bfloat16 [10240, 2048], P(None, 'fsdp')
The draws below stay inside these ranges and needn't reach their ends.
Inputs may be any that keep to these rules, and one draw needn't show every extreme that they name: `doc_ids`: within a sequence document numbers never fall; a document has 1 to 512 tokens, and one has exactly 512. `block_order`: A permutation of the block numbers.
All inputs are finite; a program needn't handle non-finite values.
Results may differ from the reference program's by a relative error of at most 0.02.
Values may be sent and summed in bfloat16 or wider, within the bound.
A program may use at most 512 MiB of HBM per device.

```python
import math
import jax
import jax.numpy as jnp
import numpy as np
from jax import lax

D = 2048
HEADS = 32
FF = 8192
ROT = 32
HEAD_DIM = 64
SEQ = 1024
SEQS = 4
BLOCKS = 16
IN_COLS = 14336
BACK_ROWS = 10240
VEC = 20480
DOCS = 4
DOC_MOST = 512


def draw_back_weight(key, part):
    normal_draw = jnp.clip(jax.random.normal(key, (BACK_ROWS, D), jnp.float32), -4.0, 4.0)
    row_number = jnp.arange(BACK_ROWS)[:, None]
    spread = jnp.where(row_number < D, 3.0 / math.sqrt(D), 1.0 / math.sqrt(FF))
    return (normal_draw * spread).astype(jnp.bfloat16)


def draw_vectors(key, part):
    normal_draw = jnp.clip(jax.random.normal(key, (VEC,), jnp.float32), -4.0, 4.0)
    position = jnp.arange(VEC)
    gain_zone = (position >= IN_COLS + D) & (position < IN_COLS + 2 * D)
    return jnp.where(gain_zone, 1.0 + 0.1 * normal_draw, 0.3 * normal_draw).astype(jnp.float32)


def shard_levels(own_key, extent, split, smallest, high):
    level, own = 1.0, jax.random.fold_in(own_key, 6)
    for dim, shards_of in split:
        draws = jnp.exp(jax.random.uniform(jax.random.fold_in(own, dim), (shards_of,), jnp.float32, smallest / len(split), high / len(split)))
        level = level * jnp.repeat(draws, extent[dim] // shards_of).reshape([-1 if axis == dim else 1 for axis in range(len(extent))])
    return level


def profile(count, total, reach, skew):
    weights = [(1 << 20) // math.isqrt(standing ** skew) + 1 for standing in range(2, count + 1)]
    surplus, counts = total - reach - (count - 1), [1] * (count - 1)
    while surplus > 0:
        free = [i for i in range(count - 1) if counts[i] < reach]
        pool, left = sum([weights[i] for i in free]), surplus
        for i in free:
            addition = min(reach - counts[i], max(1, left * weights[i] // pool), surplus)
            counts[i] = counts[i] + addition
            surplus = surplus - addition
    return np.array([reach] + counts)


def ragged(own_key, number_of, total, reach, skew):
    if number_of == 2:
        one = jax.random.randint(own_key, (), max(1, total - reach), min(reach, total - 1) + 1)
        return jnp.stack([one, total - one])
    sizes = jnp.asarray(profile(number_of, total, reach, skew), jnp.int32)
    twos = (number_of - 1) // 2
    donor, receiver = sizes[1:1 + 2 * twos:2], sizes[2:2 + 2 * twos:2]
    slack = jnp.minimum(donor - 1, reach - receiver)
    shifted = jax.random.randint(jax.random.fold_in(own_key, 1), (twos,), 0, 1 << 20) % (slack + 1)
    sizes = sizes.at[1:1 + 2 * twos:2].set(donor - shifted).at[2:2 + 2 * twos:2].set(receiver + shifted)
    return sizes[jax.random.permutation(jax.random.fold_in(own_key, 2), number_of)]


def bell_draw(key, dims, scale, bound, cuts=(), kind=jnp.bfloat16):
    entries = jax.random.normal(key, dims, jnp.float32) * scale
    if len(cuts) > 0:
        entries = shard_levels(key, dims, cuts, -0.22, 0.18) * entries
    return jnp.clip(entries, min=-bound, max=bound).astype(kind)


def setup_inputs(seed: int = 0) -> dict:
    keys = jax.random.split(jax.random.key(seed), 18)
    return {
        "tokens": bell_draw(keys[0], (SEQS, SEQ, D), 1.0, 6.0, ((0, 4), (1, 8))),
        "cotangent": bell_draw(keys[1], (SEQS, SEQ, D), 1.0, 6.0, ((0, 4), (1, 8))),
        "doc_ids": jax.vmap(lambda own: jnp.searchsorted(jnp.cumsum(ragged(own, DOCS, SEQ, DOC_MOST, 2)), jnp.arange(SEQ), side="right"))(jax.random.split(keys[2], SEQS)).reshape((SEQS, SEQ)).astype(jnp.int32),
        "block_order": jax.random.permutation(keys[3], BLOCKS).astype(jnp.int32),
        "front_weight": bell_draw(keys[4], (D, IN_COLS), D ** -0.5, 0.125, ((1, 4),)),
        "back_weight": draw_back_weight(jax.random.fold_in(keys[17], 71), 0),
        "front_master": bell_draw(keys[6], (D, IN_COLS), D ** -0.5, 0.125, ((0, 8), (1, 4)), jnp.float32),
        "back_master": bell_draw(keys[7], (BACK_ROWS, D), BACK_ROWS ** -0.5, 0.0625, ((0, 8), (1, 4)), jnp.float32),
        "front_first": bell_draw(keys[8], (D, IN_COLS), 10.0, 64.0, ((0, 8), (1, 4)), jnp.float32),
        "back_first": bell_draw(keys[9], (BACK_ROWS, D), 10.0, 64.0, ((0, 8), (1, 4)), jnp.float32),
        "front_second": jnp.clip(jnp.exp(math.log(10000.0) - 4.6051702 * jax.random.uniform(keys[10], (D, IN_COLS), jnp.float32) ** shard_levels(keys[10], (D, IN_COLS), ((0, 8), (1, 4)), -0.2, 0.2)), 100.0, 10000.0),
        "back_second": jnp.clip(jnp.exp(math.log(204.8) - 4.6051702 * jax.random.uniform(keys[11], (BACK_ROWS, D), jnp.float32) ** shard_levels(keys[11], (BACK_ROWS, D), ((0, 8), (1, 4)), -0.2, 0.2)), 2.048, 204.8),
        "vectors": draw_vectors(jax.random.fold_in(keys[17], 71), 0),
        "vector_first": bell_draw(keys[13], (VEC,), 10.0, 64.0, (), jnp.float32),
        "vector_second": jnp.clip(jnp.exp(jax.random.uniform(keys[14], (VEC,), jnp.float32, math.log(100.0), math.log(10000.0))), 100.0, 10000.0),
        "learn_rates": jnp.clip(jnp.exp(jax.random.uniform(keys[15], (3,), jnp.float32, math.log(0.02), math.log(0.2))), 0.02, 0.2),
        "adam_step": jax.random.randint(keys[16], (1,), 1, 9).astype(jnp.int32),
    }


@jax.custom_vjp
def low(v):
    return lax.optimization_barrier(v.astype(jnp.bfloat16)).astype(jnp.float32)

@jax.custom_vjp
def low_back(v):
    return v

def low_keep(v):
    return (low(v), None)

def low_pass(kept, grad):
    return (grad,)

def back_keep(v):
    return (v, None)

def back_low(kept, grad):
    return (low(grad),)
low.defvjp(low_keep, low_pass)
low_back.defvjp(back_keep, back_low)
norm_eps = 1e-05
beta_first = 0.9
beta_second = 0.95
adam_eps = 1e-08
weight_decay = 0.1
masked_score = -1e+30
top_precision = lax.Precision.HIGHEST

def query_block(length):
    for candidate in (512, 256, 128):
        if length % candidate == 0:
            return candidate
    return length

def rotary_tables(positions):
    half_rot = ROT // 2
    frequency = jnp.power(10000.0, -2.0 * jnp.arange(half_rot, dtype=jnp.float32) / ROT)
    angles = positions[:, None] * frequency[None, :]
    return (jnp.cos(angles), jnp.sin(angles))

def rotate(values, cosine, sine):
    half_rot = ROT // 2
    lower_half = values[..., :half_rot]
    upper_half = values[..., half_rot:ROT]
    cos_full = cosine[:, None, :]
    sin_full = sine[:, None, :]
    return jnp.concatenate([lower_half * cos_full - upper_half * sin_full, upper_half * cos_full + lower_half * sin_full, values[..., ROT:]], axis=-1)

def attention(query_rot, key_rot, value_low, doc_row):
    block_len = query_block(SEQ)
    score_scale = HEAD_DIM ** (-0.5)
    positions = jnp.arange(SEQ, dtype=jnp.int32)

    def one_block(inputs):
        query_part, query_pos, query_seg = inputs
        scores = jnp.einsum('qhd,khd->hqk', query_part, key_rot, precision=top_precision) * score_scale
        scores = low_back(scores)
        allowed = (positions[None, :] <= query_pos[:, None]) & (doc_row[None, :] == query_seg[:, None])
        masked = jnp.where(allowed[None], scores, masked_score)
        row_max = lax.optimization_barrier(jnp.max(masked, axis=-1, keepdims=True))
        weights = jnp.where(allowed[None], jnp.exp(masked - row_max), 0.0)
        weights = low(weights / lax.optimization_barrier(jnp.sum(weights, axis=-1, keepdims=True)))
        return jnp.einsum('hqk,khd->qhd', weights, value_low, precision=top_precision).reshape(block_len, D)
    blocks = SEQ // block_len
    pieces = (query_rot.reshape(blocks, block_len, HEADS, HEAD_DIM), positions.reshape(blocks, block_len), doc_row.reshape(blocks, block_len))
    return lax.map(jax.checkpoint(one_block), pieces).reshape(SEQ, D)

def layer(inputs, front_all, back_all, vector_all, doc_ids):
    bias_front = vector_all[:IN_COLS]
    bias_back = vector_all[IN_COLS:IN_COLS + D]
    norm_gain = vector_all[IN_COLS + D:IN_COLS + 2 * D]
    norm_shift = vector_all[IN_COLS + 2 * D:]

    def one_sequence(unused, sequence):
        values, doc_row = sequence
        row_mean = lax.optimization_barrier(jnp.mean(values, axis=-1, keepdims=True))
        centered = values - row_mean
        variance = lax.optimization_barrier(jnp.mean(centered * centered, axis=-1, keepdims=True))
        normed = low(centered * lax.rsqrt(variance + norm_eps) * norm_gain + norm_shift)
        hidden = low_back(jnp.dot(normed, front_all, precision=top_precision) + bias_front)
        cosine, sine = rotary_tables(jnp.arange(SEQ, dtype=jnp.float32))
        shaped = (SEQ, HEADS, HEAD_DIM)
        query_rot = low(rotate(hidden[:, :D].reshape(shaped), cosine, sine))
        key_rot = low(rotate(hidden[:, D:2 * D].reshape(shaped), cosine, sine))
        value_low = low(hidden[:, 2 * D:3 * D].reshape(shaped))
        attended = low(low_back(attention(query_rot, key_rot, value_low, doc_row)))
        activation = low(jax.nn.gelu(hidden[:, 3 * D:], approximate=True))
        mixed = jnp.concatenate([attended, activation], axis=1)
        return (unused, values + jnp.dot(mixed, back_all, precision=top_precision) + bias_back)
    unused, outputs = lax.scan(one_sequence, jnp.zeros((), jnp.float32), (inputs, doc_ids))
    return outputs

def to_natural(stored, block_order):
    block_tokens = SEQ // BLOCKS
    shaped = stored.reshape((stored.shape[0], BLOCKS, block_tokens) + stored.shape[2:])
    inverse = jnp.zeros((BLOCKS,), jnp.int32).at[block_order].set(jnp.arange(BLOCKS, dtype=jnp.int32))
    return jnp.take(shaped, inverse, axis=1).reshape(stored.shape)

def to_stored(natural, block_order):
    block_tokens = SEQ // BLOCKS
    shaped = natural.reshape((natural.shape[0], BLOCKS, block_tokens) + natural.shape[2:])
    return jnp.take(shaped, block_order, axis=1).reshape(natural.shape)

def adam_update(weight, first, second, grad, rate, count_now, decay):
    first_new = beta_first * first + (1.0 - beta_first) * grad
    second_new = beta_second * second + (1.0 - beta_second) * grad * grad
    steps_float = count_now.astype(jnp.float32)
    first_fix = 1.0 - jnp.power(beta_first, steps_float)
    second_fix = 1.0 - jnp.power(beta_second, steps_float)
    change = first_new / first_fix / (jnp.sqrt(second_new / second_fix) + adam_eps) + decay * weight
    return (weight - rate * change, first_new, second_new)

def reference(tokens, cotangent, doc_ids, block_order, front_weight, back_weight, front_master, back_master, front_first, back_first, front_second, back_second, vectors, vector_first, vector_second, learn_rates, adam_step):
    inputs = to_natural(tokens.astype(jnp.float32), block_order)
    grad_in = to_natural(cotangent.astype(jnp.float32), block_order)

    def forward(values, front_all, back_all, vector_all):
        return layer(values, front_all, back_all, vector_all, doc_ids)
    outputs, pullback = jax.vjp(forward, inputs, front_weight.astype(jnp.float32), back_weight.astype(jnp.float32), vectors)
    input_grad, front_grad, back_grad, vector_grad = pullback(grad_in)
    count_now = adam_step[0]
    front_new, front_first_new, front_second_new = adam_update(front_master, front_first, front_second, front_grad, learn_rates[0], count_now, weight_decay)
    back_new, back_first_new, back_second_new = adam_update(back_master, back_first, back_second, back_grad, learn_rates[1], count_now, weight_decay)
    vectors_new, vector_first_new, vector_second_new = adam_update(vectors, vector_first, vector_second, vector_grad, learn_rates[2], count_now, 0.0)
    layer_out = to_stored(outputs, block_order).astype(jnp.bfloat16)
    tokens_grad = to_stored(input_grad, block_order).astype(jnp.bfloat16)
    return (layer_out, tokens_grad, front_grad, back_grad, vector_grad, front_new, back_new, vectors_new, front_first_new, back_first_new, vector_first_new, front_second_new, back_second_new, vector_second_new, front_new.astype(jnp.bfloat16), back_new.astype(jnp.bfloat16))
```

```python
import functools

import jax
import jax.numpy as jnp
import numpy as np
from jax import lax
from jax.experimental import pallas as pl
from jax.experimental.pallas import tpu as pltpu
from jax.sharding import PartitionSpec as P

D = 2048
HEADS = 32
FF = 8192
ROT = 32
HEAD_DIM = 64
IN_COLS = 14336
BACK_ROWS = 10240

norm_eps = 1e-05
beta_first = 0.9
beta_second = 0.95
adam_eps = 1e-08
weight_decay = 0.1
masked_score = -1e30
bf16 = jnp.bfloat16
f32 = jnp.float32


class Layout:
    def __init__(self, ctx, fsdp):
        self.ctx, self.fsdp, self.planes, self.ranks = ctx, fsdp, ctx // 2, 2 * fsdp
        assert ctx % 2 == 0 and self.planes == fsdp
        self.unit = D // self.ranks
        self.per_shard = IN_COLS // self.unit // fsdp
        r = self.ranks
        first_up = 3 * r
        home = {f: [] for f in range(fsdp)}
        for g in range(first_up, 7 * r, 2):
            assert g // self.per_shard == (g + 1) // self.per_shard
            home[g // self.per_shard].append(g)
        pairs = {p: [None, None] for p in range(r)}
        for f in range(fsdp):
            if len(home[f]) >= 4:
                keep, home[f] = home[f][:4], home[f][4:]
                pairs[2 * f], pairs[2 * f + 1] = keep[:2], keep[2:]
            elif home[f]:
                keep, home[f] = home[f], []
                for i, g in enumerate(keep):
                    pairs[2 * f + i % 2][(i + i // 2) % 2] = g
        for s in range(2):
            for k in range(2):
                used = set()
                for f in range(fsdp):
                    p = 2 * f + k
                    if pairs[p][s] is not None:
                        continue
                    options = sorted(
                        (h for h in range(fsdp) if home[h]),
                        key=lambda h: (h in used, bin(h ^ f).count("1"), -len(home[h])),
                    )
                    used.add(options[0])
                    pairs[p][s] = home[options[0]].pop(0)
        self.pairs = pairs
        self.slots = [
            ([p for p in range(r)], 1),
            ([r + p for p in range(r)], 1),
            ([2 * r + p for p in range(r)], 1),
            ([pairs[p][0] for p in range(r)], 2),
            ([pairs[p][1] for p in range(r)], 2),
        ]
        self.rounds = []
        for units, _ in self.slots:
            rounds = []
            for k in range(2):
                for f in range(fsdp):
                    src = units[2 * f + k] // self.per_shard
                    if src == f:
                        continue
                    for one in rounds:
                        if all((src, k) != (a, c) for a, _, c in one):
                            one.append((src, f, k))
                            break
                    else:
                        rounds.append([(src, f, k)])
            self.rounds.append(rounds)
        self.rank_units = [
            [p, r + p, 2 * r + p, pairs[p][0], pairs[p][0] + 1, pairs[p][1], pairs[p][1] + 1]
            for p in range(r)
        ]
        self.back_units = [[p] + [g - 2 * r for g in self.rank_units[p][3:]] for p in range(r)]
        self.matchings = []
        left = {p: list(range(5)) for p in range(r)}
        own = lambda p, j: self.back_units[p][j] // 5
        for _ in range(5):
            match = {}

            def assign(p, seen):
                for j in left[p]:
                    c = own(p, j)
                    if c in seen:
                        continue
                    seen.add(c)
                    if c not in match or assign(match[c][0], seen):
                        match[c] = (p, j)
                        return True
                return False

            for p in range(r):
                assert assign(p, set())
            for c, (p, j) in match.items():
                left[p].remove(j)
            self.matchings.append(match)

    def device(self, z, k, f):
        return (2 * z + k) * self.fsdp + f


def pick(table, index):
    return jnp.asarray(np.asarray(table, np.int32))[index]


def rotation_tables(positions, width):
    half = ROT // 2
    lane = np.arange(width) % HEAD_DIM
    frequency = jnp.power(
        10000.0, -2.0 * jnp.asarray(lane % half, f32) / ROT
    )
    angles = positions.astype(f32)[:, None] * frequency[None, :]
    rotated = jnp.asarray(lane < ROT)
    lower = jnp.asarray(lane < half)
    cosine = jnp.where(rotated, jnp.cos(angles), 1.0)
    sine = jnp.where(rotated, jnp.sin(angles), 0.0)
    return cosine, jnp.where(lower, -sine, 0.0), jnp.where(lower, 0.0, sine)


def rotate(values, tables):
    half = ROT // 2
    cosine, from_above, from_below = tables
    return (
        values * cosine
        + jnp.roll(values, -half, axis=1) * from_above
        + jnp.roll(values, half, axis=1) * from_below
    )


def rotate_back(values, tables):
    half = ROT // 2
    cosine, from_above, from_below = tables
    return (
        values * cosine
        + jnp.roll(values * from_above, half, axis=1)
        + jnp.roll(values * from_below, -half, axis=1)
    )


def attention_kernel(
    q_ref, k_ref, v_ref, g_ref, pos_q, pos_k, seg_q, seg_k, att_ref, dq_ref, dk_ref, dv_ref
):
    scale = HEAD_DIM ** (-0.5)
    width = q_ref.shape[1]

    @pl.when(pl.program_id(0) == 0)
    def _():
        dk_ref[...] = jnp.zeros_like(dk_ref)
        dv_ref[...] = jnp.zeros_like(dv_ref)

    allowed = (pos_k[...] <= pos_q[...]) & (seg_k[...] == seg_q[...])
    bias = jnp.where(allowed, 0.0, masked_score)
    last = (((1,), (1,)), ((), ()))
    first = (((0,), (0,)), ((), ()))
    for head in range(width // HEAD_DIM):
        cols = slice(head * HEAD_DIM, (head + 1) * HEAD_DIM)
        q, g = q_ref[:, cols], g_ref[:, cols]
        k, v = k_ref[:, cols], v_ref[:, cols]
        scores = lax.dot_general(q, k, last, preferred_element_type=f32) * scale + bias
        weights = jnp.exp(scores - jnp.max(scores, axis=1, keepdims=True))
        probs = weights * (1.0 / jnp.sum(weights, axis=1, keepdims=True))
        probs_low = probs.astype(bf16)
        out = jnp.dot(probs_low, v, preferred_element_type=f32)
        att_ref[:, cols] = out.astype(bf16)
        prob_grad = lax.dot_general(g, v, last, preferred_element_type=f32)
        delta = jnp.sum(g.astype(f32) * out, axis=1, keepdims=True)
        score_grad = (probs * (prob_grad - delta)).astype(bf16)
        dq_ref[:, cols] = jnp.dot(score_grad, k, preferred_element_type=f32) * scale
        dk_ref[:, cols] += lax.dot_general(score_grad, q, first, preferred_element_type=f32) * scale
        dv_ref[:, cols] += lax.dot_general(probs_low, g, first, preferred_element_type=f32)


def attention(query, key, value, grad, positions, segments):
    length, width = query.shape
    block = 256
    rows = pl.BlockSpec((block, width), lambda i: (i, 0))
    whole = pl.BlockSpec((length, width), lambda i: (0, 0))
    column = pl.BlockSpec((block, 1), lambda i: (i, 0))
    line = pl.BlockSpec((1, length), lambda i: (0, 0))
    return pl.pallas_call(
        attention_kernel,
        grid=(length // block,),
        in_specs=[rows, whole, whole, rows, column, line, column, line],
        out_specs=[rows, rows, whole, whole],
        out_shape=[
            jax.ShapeDtypeStruct((length, width), bf16),
            jax.ShapeDtypeStruct((length, width), f32),
            jax.ShapeDtypeStruct((length, width), f32),
            jax.ShapeDtypeStruct((length, width), f32),
        ],
        cost_estimate=pl.CostEstimate(
            flops=14 * length * length * width,
            transcendentals=length * length * width // HEAD_DIM,
            bytes_accessed=20 * length * width,
        ),
    )(query, key, value, grad, positions[:, None], positions[None], segments[:, None], segments[None])


def gelu_parts(u):
    scale = np.float32(np.sqrt(2.0 / np.pi))
    square = u * u
    inner = scale * u * (1.0 + 0.044715 * square)
    t = jnp.tanh(inner)
    value = 0.5 * u * (1.0 + t)
    slope = 0.5 * (1.0 + t) + 0.5 * u * (1.0 - t * t) * scale * (1.0 + 3 * 0.044715 * square)
    return value, slope


def adam_update(weight, first, second, grad, rate, count_now, decay):
    first_new = beta_first * first + (1.0 - beta_first) * grad
    second_new = beta_second * second + (1.0 - beta_second) * grad * grad
    steps_float = count_now.astype(f32)
    first_fix = 1.0 - jnp.power(beta_first, steps_float)
    second_fix = 1.0 - jnp.power(beta_second, steps_float)
    change = first_new / first_fix / (jnp.sqrt(second_new / second_fix) + adam_eps) + decay * weight
    return (weight - rate * change, first_new, second_new)


def after(value, *others):
    return lax.optimization_barrier((value,) + others)[0]


def per_device(
    tokens,
    cotangent,
    doc_ids,
    block_order,
    front_weight,
    back_weight,
    front_master,
    back_master,
    front_first,
    back_first,
    front_second,
    back_second,
    vectors,
    vector_first,
    vector_second,
    learn_rates,
    adam_step,
    *,
    plan,
):
    planes, shards, ranks, unit = plan.planes, plan.fsdp, plan.ranks, plan.unit
    both = ("ctx", "fsdp")
    contract_last = (((1,), (1,)), ((), ()))
    contract_first = (((0,), (0,)), ((), ()))
    c_index, f = lax.axis_index("ctx"), lax.axis_index("fsdp")
    z, k = c_index // 2, c_index % 2
    p = 2 * f + k
    rows = tokens.shape[1]
    plane_rows = 2 * shards * rows
    share = 2 * rows

    bias_front = vectors[:IN_COLS].reshape(-1, unit)
    bias_back = vectors[IN_COLS : IN_COLS + D]
    norm_gain = vectors[IN_COLS + D : IN_COLS + 2 * D]
    norm_shift = vectors[IN_COLS + 2 * D :]

    swap_pairs = [(2 * i + j, 2 * i + 1 - j) for i in range(planes) for j in range(2)]

    def swap_core(value):
        return lax.ppermute(value, "ctx", swap_pairs)

    def to_shard(value, step):
        return lax.ppermute(value, "fsdp", [(i, i ^ step) for i in range(shards)])

    def to_plane(value, step):
        return lax.ppermute(
            value, "ctx", [(2 * i + j, 2 * (i ^ step) + j) for i in range(planes) for j in range(2)]
        )

    def gather_plane(value):
        mine = lax.all_gather(value, "fsdp")
        other = swap_core(mine)
        low = jnp.where(k == 0, mine, other)
        high = jnp.where(k == 0, other, mine)
        return jnp.stack([low, high], axis=1).reshape(plane_rows, D)

    def at(array, index):
        return lax.dynamic_index_in_dim(array, index, 0, keepdims=False)

    blocks = block_order.shape[0]
    block_tokens = doc_ids.shape[1] // blocks
    offsets = jnp.arange(block_tokens, dtype=jnp.int32)
    positions_all = (block_order[:, None] * block_tokens + offsets[None, :]).reshape(planes, share)
    own_positions = at(positions_all, z)
    plane_positions = jnp.tile(own_positions, shards)

    plane_tokens = gather_plane(tokens[0])

    def normalize(values):
        values = values.astype(f32)
        centered = values - jnp.mean(values, axis=-1, keepdims=True)
        factor = lax.rsqrt(jnp.mean(centered * centered, axis=-1, keepdims=True) + norm_eps)
        return centered * factor, factor

    normed = (normalize(plane_tokens)[0] * norm_gain + norm_shift).astype(bf16)

    def slot_weight(slot, gate):
        units, wide = plan.slots[slot]
        width = wide * unit
        table = np.asarray(units)
        source, place = table // plan.per_shard, table % plan.per_shard
        total = None
        for one in plan.rounds[slot]:
            sends = np.zeros(ranks, np.int32)
            links = []
            for src, dst, core in one:
                sends[2 * src + core] = place[2 * dst + core]
                links += [
                    (plan.device(i, core, src), plan.device(i, core, dst)) for i in range(planes)
                ]
            start = after(pick(sends, p) * unit, gate)
            block = lax.dynamic_slice(front_weight, (0, start), (D, width))
            block = lax.ppermute(block, both, links)
            total = block if total is None else total + block
        local = source == np.arange(ranks) // 2
        start = pick(np.where(local, place, 0), p) * unit
        own = lax.dynamic_slice(front_weight, (0, start), (D, width))
        if total is None:
            return own
        if not local.any():
            return total
        return jnp.where(pick(local, p) > 0, own, total)

    gate = normed[0, 0]
    weight_qkv = jnp.concatenate([slot_weight(i, gate) for i in range(3)], axis=1)
    gate = weight_qkv[0, 0]
    plane_grad = gather_plane(after(cotangent[0], gate))
    weight_up = jnp.concatenate([slot_weight(i, gate) for i in range(3, 5)], axis=1)

    def back_rows(rank):
        table = pick(plan.back_units, rank)
        return jnp.concatenate(
            [lax.dynamic_slice(back_weight, (table[j] * unit, 0), (unit, D // shards)) for j in range(5)],
            axis=0,
        )

    col_width = D // shards
    back_local = jnp.zeros((5 * unit, D), bf16)
    for step in range(shards):
        piece = back_rows(after(2 * (f ^ step) + k, gate))
        if step:
            piece = to_shard(piece, step)
        back_local = lax.dynamic_update_slice(back_local, piece, (0, (f ^ step) * col_width))

    unit_table = pick(plan.rank_units, p)
    bias_local = jnp.take(bias_front, unit_table, axis=0).reshape(-1)

    hidden = jnp.dot(normed, weight_qkv, preferred_element_type=f32) + bias_local[: 3 * unit]
    tables = rotation_tables(plane_positions, unit)
    query = rotate(hidden[:, :unit], tables).astype(bf16)
    key = rotate(hidden[:, unit : 2 * unit], tables).astype(bf16)
    qkv = jnp.concatenate([query, key, hidden[:, 2 * unit :].astype(bf16)], axis=1)

    def to_sequence(value):
        shaped = value.reshape(shards, share, -1)
        pieces = [at(shaped, z)]
        for step in range(1, planes):
            pieces.append(to_plane(at(shaped, z ^ step), step))
        return jnp.concatenate(pieces, axis=0)

    def to_plane_rows(value):
        shaped = value.reshape(planes, share, -1)
        pieces = [shaped[0]] + [to_plane(shaped[step], step) for step in range(1, planes)]
        stacked = jnp.stack(pieces)
        return jnp.concatenate([at(stacked, i ^ z) for i in range(planes)], axis=0)

    qkv_seq = to_sequence(qkv)

    mixed_grad = lax.dot_general(plane_grad, back_local, contract_last, preferred_element_type=f32)
    grad_seq = to_sequence(mixed_grad[:, :unit].astype(bf16))

    order = jnp.arange(planes, dtype=jnp.int32) ^ z
    seq_positions = jnp.take(positions_all, order, axis=0).reshape(-1)
    documents = lax.all_gather(doc_ids[0].astype(f32), "fsdp")
    doc_row = at(documents, z).astype(jnp.int32)
    seq_documents = jnp.take(
        jnp.take(doc_row.reshape(blocks, block_tokens), block_order, axis=0).reshape(planes, share),
        order,
        axis=0,
    ).reshape(-1)
    attended, query_grad, key_grad, value_grad = attention(
        qkv_seq[:, :unit],
        qkv_seq[:, unit : 2 * unit],
        qkv_seq[:, 2 * unit :],
        grad_seq,
        seq_positions,
        seq_documents,
    )
    seq_tables = rotation_tables(seq_positions, unit)
    returned = to_plane_rows(
        jnp.concatenate(
            [
                attended,
                rotate_back(query_grad, seq_tables).astype(bf16),
                rotate_back(key_grad, seq_tables).astype(bf16),
                value_grad.astype(bf16),
            ],
            axis=1,
        )
    )

    up = jnp.dot(normed, weight_up, preferred_element_type=f32) + bias_local[3 * unit :]
    activation, slope = gelu_parts(up)
    up_grad = (mixed_grad[:, unit:] * slope).astype(bf16)
    mixed = jnp.concatenate([returned[:, :unit], activation.astype(bf16)], axis=1)
    hidden_grad = jnp.concatenate([returned[:, unit:], up_grad], axis=1)

    def sum_to_owner(value):
        shaped = value.reshape(shards, 2, rows, D)
        kept = lax.dynamic_index_in_dim(shaped, k, 1, keepdims=False)
        sent = lax.dynamic_index_in_dim(shaped, 1 - k, 1, keepdims=False).astype(bf16)
        summed = kept + swap_core(sent).astype(f32)
        total = at(summed, f)
        for step in range(1, shards):
            total = total + to_shard(at(summed, f ^ step).astype(bf16), step).astype(f32)
        return total

    projected = sum_to_owner(jnp.dot(mixed, back_local, preferred_element_type=f32))
    inputs = tokens[0].astype(f32)
    layer_out = (inputs + projected + bias_back).astype(bf16)[None]

    weight_local = jnp.concatenate([weight_qkv, weight_up], axis=1)
    normed_grad = sum_to_owner(
        lax.dot_general(hidden_grad, weight_local, contract_last, preferred_element_type=f32)
    )
    unscaled, factor = normalize(inputs)
    scaled = normed_grad * norm_gain
    input_grad = factor * (
        scaled
        - jnp.mean(scaled, axis=-1, keepdims=True)
        - unscaled * jnp.mean(scaled * unscaled, axis=-1, keepdims=True)
    )
    tokens_grad = (cotangent[0].astype(f32) + input_grad).astype(bf16)[None]

    up_links = lambda s: [
        (2 * i + j, 2 * i + 2 + j) for i in range(min(s, planes - 1)) for j in range(2)
    ]
    mirror = lambda links: [
        (2 * (planes - 1 - a // 2) + a % 2, 2 * (planes - 1 - b // 2) + b % 2) for a, b in links
    ]

    def sum_over_planes(block_of):
        rising = falling = None
        for s in range(1, planes):
            a = jnp.clip(planes - s + z, 0, planes - 1)
            b = jnp.clip(s - 1 - (planes - 1 - z), 0, planes - 1)
            term_a, term_b = block_of(a), block_of(b)
            if rising is not None:
                term_a = (term_a.astype(f32) + rising.astype(f32)).astype(bf16)
                term_b = (term_b.astype(f32) + falling.astype(f32)).astype(bf16)
            rising = lax.ppermute(term_a, "ctx", up_links(s))
            falling = lax.ppermute(term_b, "ctx", mirror(up_links(s)))
        return block_of(z).astype(f32) + rising.astype(f32) + falling.astype(f32)

    back_partial = lax.dot_general(
        mixed, plane_grad, contract_first, preferred_element_type=f32
    ).astype(bf16)
    back_sum = sum_over_planes(
        lambda i: lax.dynamic_slice(back_partial, (0, i * col_width), (5 * unit, col_width))
    ).astype(bf16)
    front_partial = lax.dot_general(
        normed, hidden_grad, contract_first, preferred_element_type=f32
    ).astype(bf16)
    front_rows = D // planes
    front_sum = sum_over_planes(
        lambda i: lax.dynamic_slice(front_partial, (i * front_rows, 0), (front_rows, 7 * unit))
    ).astype(bf16)

    back_grad = jnp.zeros((5 * unit, col_width), bf16)
    for match in plan.matchings:
        slot = np.zeros(ranks, np.int32)
        place = np.zeros(ranks, np.int32)
        links = []
        for owner, (rank, j) in match.items():
            slot[rank] = j
            place[owner] = plan.back_units[rank][j] % 5
            for i in range(planes):
                links.append((plan.device(i, rank % 2, rank // 2), owner * shards + i))
        block = lax.dynamic_slice(back_sum, (pick(slot, p) * unit, 0), (unit, col_width))
        block = lax.ppermute(block, both, links)
        back_grad = lax.dynamic_update_slice(back_grad, block, (pick(place, c_index) * unit, 0))
    back_grad = back_grad.astype(f32)

    natural = jnp.zeros((front_rows, (plan.per_shard + 2) * unit), bf16)
    start = 0
    for (units, wide), rounds in zip(plan.slots, plan.rounds):
        table = np.asarray(units)
        source, place = table // plan.per_shard, table % plan.per_shard
        block = front_sum[:, start : start + wide * unit]
        start += wide * unit
        local = source == np.arange(ranks) // 2
        where = np.where(local, place, plan.per_shard)
        natural = lax.dynamic_update_slice(natural, block, (0, pick(where, p) * unit))
        for one in rounds:
            where = np.full(ranks, plan.per_shard, np.int32)
            links = []
            for src, dst, core in one:
                where[2 * src + core] = place[2 * dst + core]
                links += [
                    (plan.device(i, core, dst), plan.device(i, core, src)) for i in range(planes)
                ]
            moved = lax.ppermute(block, both, links)
            natural = lax.dynamic_update_slice(natural, moved, (0, pick(where, p) * unit))
    natural = natural[:, : plan.per_shard * unit].reshape(2, front_rows // 2, -1)
    front_grad = at(natural, k).astype(f32) + swap_core(at(natural, 1 - k)).astype(f32)

    spread = (jnp.arange(7 * ranks)[:, None] == unit_table[None, :]).astype(f32)
    hidden_sum = jnp.sum(hidden_grad, axis=0, dtype=f32).reshape(7, unit)
    front_vector = jnp.sum(spread[:, :, None] * hidden_sum[None], axis=1).reshape(-1)
    vector_term = jnp.concatenate(
        [
            front_vector,
            jnp.sum(cotangent[0], axis=0, dtype=f32),
            jnp.sum(normed_grad * unscaled, axis=0),
            jnp.sum(normed_grad, axis=0),
        ]
    )
    vector_grad = lax.psum(vector_term, both)

    count_now = adam_step[0]
    back_new, back_first_new, back_second_new = adam_update(
        back_master, back_first, back_second, back_grad, learn_rates[1], count_now, weight_decay
    )
    front_new, front_first_new, front_second_new = adam_update(
        front_master, front_first, front_second, front_grad, learn_rates[0], count_now, weight_decay
    )
    vectors_new, vector_first_new, vector_second_new = adam_update(
        vectors, vector_first, vector_second, vector_grad, learn_rates[2], count_now, 0.0
    )

    def gather_rows(value):
        height = value.shape[0]
        out = jnp.zeros((2 * planes * height, value.shape[1]), value.dtype)

        def place(out, piece, plane):
            valid = (plane >= 0) & (plane < planes)
            where = jnp.where(valid, plane, z)
            mine, other = piece
            out = lax.dynamic_update_slice(out, mine, ((2 * where + k) * height, 0))
            return lax.dynamic_update_slice(out, other, ((2 * where + 1 - k) * height, 0))

        rising = falling = value
        pieces = []
        for s in range(1, planes):
            links = [(2 * i + j, 2 * i + 2 + j) for i in range(s - 1, planes - 1) for j in range(2)]
            rising = lax.ppermute(rising, "ctx", links)
            falling = lax.ppermute(falling, "ctx", mirror(links))
            pieces.append(((rising, swap_core(rising)), z - s))
            pieces.append(((falling, swap_core(falling)), z + s))
        for piece, plane in pieces:
            out = place(out, piece, plane)
        return place(out, (value, swap_core(value)), z)

    back_next = gather_rows(back_new.astype(bf16))
    front_next = gather_rows(front_new.astype(bf16))
    return (
        layer_out,
        tokens_grad,
        front_grad,
        back_grad,
        vector_grad,
        front_new,
        back_new,
        vectors_new,
        front_first_new,
        back_first_new,
        vector_first_new,
        front_second_new,
        back_second_new,
        vector_second_new,
        front_next,
        back_next,
    )


def solution(mesh):
    plan = Layout(mesh.shape["ctx"], mesh.shape["fsdp"])
    tokens_spec = P("fsdp", "ctx", None)
    cols, owned, same = P(None, "fsdp"), P("ctx", "fsdp"), P()
    in_specs = (
        (tokens_spec, tokens_spec, P("fsdp", None), same, cols, cols)
        + (owned,) * 6
        + (same,) * 5
    )
    out_specs = (
        (tokens_spec, tokens_spec, owned, owned, same)
        + (owned, owned, same) * 3
        + (cols, cols)
    )
    return jax.shard_map(
        functools.partial(per_device, plan=plan),
        mesh=mesh,
        in_specs=in_specs,
        out_specs=out_specs,
        check_vma=False,
    )
```

```python
import functools

import jax
import jax.numpy as jnp
import numpy as np
from jax import lax
from jax.experimental import pallas as pl
from jax.experimental.pallas import tpu as pltpu
from jax.sharding import PartitionSpec as P

D = 2048
HEADS = 32
FF = 8192
ROT = 32
HEAD_DIM = 64
IN_COLS = 14336
BACK_ROWS = 10240

norm_eps = 1e-05
beta_first = 0.9
beta_second = 0.95
adam_eps = 1e-08
weight_decay = 0.1
masked_score = -1e30
bf16 = jnp.bfloat16
f32 = jnp.float32


class Layout:
    def __init__(self, ctx, fsdp):
        self.ctx, self.fsdp, self.planes, self.ranks = ctx, fsdp, ctx // 2, 2 * fsdp
        assert ctx % 2 == 0 and self.planes == fsdp
        self.unit = D // self.ranks
        self.per_shard = IN_COLS // self.unit // fsdp
        r = self.ranks
        first_up = 3 * r
        home = {f: [] for f in range(fsdp)}
        for g in range(first_up, 7 * r, 2):
            assert g // self.per_shard == (g + 1) // self.per_shard
            home[g // self.per_shard].append(g)
        pairs = {p: [None, None] for p in range(r)}
        for f in range(fsdp):
            if len(home[f]) >= 4:
                keep, home[f] = home[f][:4], home[f][4:]
                pairs[2 * f], pairs[2 * f + 1] = keep[:2], keep[2:]
            elif home[f]:
                keep, home[f] = home[f], []
                for i, g in enumerate(keep):
                    pairs[2 * f + i % 2][(i + i // 2) % 2] = g
        for s in range(2):
            for k in range(2):
                used = set()
                for f in range(fsdp):
                    p = 2 * f + k
                    if pairs[p][s] is not None:
                        continue
                    options = sorted(
                        (h for h in range(fsdp) if home[h]),
                        key=lambda h: (h in used, bin(h ^ f).count("1"), -len(home[h])),
                    )
                    used.add(options[0])
                    pairs[p][s] = home[options[0]].pop(0)
        self.pairs = pairs
        self.slots = [
            ([p for p in range(r)], 1),
            ([r + p for p in range(r)], 1),
            ([2 * r + p for p in range(r)], 1),
            ([pairs[p][0] for p in range(r)], 2),
            ([pairs[p][1] for p in range(r)], 2),
        ]
        self.rounds = []
        for units, _ in self.slots:
            rounds = []
            for k in range(2):
                for f in range(fsdp):
                    src = units[2 * f + k] // self.per_shard
                    if src == f:
                        continue
                    for one in rounds:
                        if all((src, k) != (a, c) for a, _, c in one):
                            one.append((src, f, k))
                            break
                    else:
                        rounds.append([(src, f, k)])
            self.rounds.append(rounds)
        self.rank_units = [
            [p, r + p, 2 * r + p, pairs[p][0], pairs[p][0] + 1, pairs[p][1], pairs[p][1] + 1]
            for p in range(r)
        ]
        self.back_units = [[p] + [g - 2 * r for g in self.rank_units[p][3:]] for p in range(r)]
        self.matchings = []
        left = {p: list(range(5)) for p in range(r)}
        own = lambda p, j: self.back_units[p][j] // 5
        for _ in range(5):
            match = {}

            def assign(p, seen):
                for j in left[p]:
                    c = own(p, j)
                    if c in seen:
                        continue
                    seen.add(c)
                    if c not in match or assign(match[c][0], seen):
                        match[c] = (p, j)
                        return True
                return False

            for p in range(r):
                assert assign(p, set())
            for c, (p, j) in match.items():
                left[p].remove(j)
            self.matchings.append(match)

    def device(self, z, k, f):
        return (2 * z + k) * self.fsdp + f


def pick(table, index):
    return jnp.asarray(np.asarray(table, np.int32))[index]


def normalize(values):
    values = values.astype(f32)
    centered = values - jnp.mean(values, axis=-1, keepdims=True)
    factor = lax.rsqrt(jnp.mean(centered * centered, axis=-1, keepdims=True) + norm_eps)
    return centered * factor, factor


def rotation_tables(positions, width):
    half = ROT // 2
    lane = np.arange(width) % HEAD_DIM
    frequency = jnp.power(
        10000.0, -2.0 * jnp.asarray(lane % half, f32) / ROT
    )
    angles = positions.astype(f32)[:, None] * frequency[None, :]
    rotated = jnp.asarray(lane < ROT)
    lower = jnp.asarray(lane < half)
    cosine = jnp.where(rotated, jnp.cos(angles), 1.0)
    sine = jnp.where(rotated, jnp.sin(angles), 0.0)
    return cosine, jnp.where(lower, -sine, 0.0), jnp.where(lower, 0.0, sine)


def rotate(values, tables):
    half = ROT // 2
    cosine, from_above, from_below = tables
    return (
        values * cosine
        + jnp.roll(values, -half, axis=1) * from_above
        + jnp.roll(values, half, axis=1) * from_below
    )


def rotate_back(values, tables):
    half = ROT // 2
    cosine, from_above, from_below = tables
    return (
        values * cosine
        + jnp.roll(values * from_above, half, axis=1)
        + jnp.roll(values * from_below, -half, axis=1)
    )


def attention_kernel(
    q_ref, k_ref, v_ref, g_ref, pos_q, pos_k, seg_q, seg_k, att_ref, dq_ref, dk_ref, dv_ref
):
    scale = HEAD_DIM ** (-0.5)
    width = q_ref.shape[1]

    @pl.when(pl.program_id(0) == 0)
    def _():
        dk_ref[...] = jnp.zeros_like(dk_ref)
        dv_ref[...] = jnp.zeros_like(dv_ref)

    allowed = (pos_k[...] <= pos_q[...]) & (seg_k[...] == seg_q[...])
    bias = jnp.where(allowed, 0.0, masked_score)
    last = (((1,), (1,)), ((), ()))
    first = (((0,), (0,)), ((), ()))
    for head in range(width // HEAD_DIM):
        cols = slice(head * HEAD_DIM, (head + 1) * HEAD_DIM)
        q, g = q_ref[:, cols], g_ref[:, cols]
        k, v = k_ref[:, cols], v_ref[:, cols]
        scores = lax.dot_general(q, k, last, preferred_element_type=f32) * scale + bias
        weights = jnp.exp(scores - jnp.max(scores, axis=1, keepdims=True))
        probs = weights * (1.0 / jnp.sum(weights, axis=1, keepdims=True))
        probs_low = probs.astype(bf16)
        out = jnp.dot(probs_low, v, preferred_element_type=f32)
        att_ref[:, cols] = out.astype(bf16)
        prob_grad = lax.dot_general(g, v, last, preferred_element_type=f32)
        delta = jnp.sum(g.astype(f32) * out, axis=1, keepdims=True)
        score_grad = (probs * (prob_grad - delta)).astype(bf16)
        dq_ref[:, cols] = jnp.dot(score_grad, k, preferred_element_type=f32) * scale
        dk_ref[:, cols] += lax.dot_general(score_grad, q, first, preferred_element_type=f32) * scale
        dv_ref[:, cols] += lax.dot_general(probs_low, g, first, preferred_element_type=f32)


def attention(query, key, value, grad, positions, segments):
    length, width = query.shape
    block = 256
    rows = pl.BlockSpec((block, width), lambda i: (i, 0))
    whole = pl.BlockSpec((length, width), lambda i: (0, 0))
    column = pl.BlockSpec((block, 1), lambda i: (i, 0))
    line = pl.BlockSpec((1, length), lambda i: (0, 0))
    return pl.pallas_call(
        attention_kernel,
        grid=(length // block,),
        in_specs=[rows, whole, whole, rows, column, line, column, line],
        out_specs=[rows, rows, whole, whole],
        out_shape=[
            jax.ShapeDtypeStruct((length, width), bf16),
            jax.ShapeDtypeStruct((length, width), f32),
            jax.ShapeDtypeStruct((length, width), f32),
            jax.ShapeDtypeStruct((length, width), f32),
        ],
        cost_estimate=pl.CostEstimate(
            flops=14 * length * length * width,
            transcendentals=length * length * width // HEAD_DIM,
            bytes_accessed=20 * length * width,
        ),
    )(query, key, value, grad, positions[:, None], positions[None], segments[:, None], segments[None])


MESH = pl.DeviceIdType.MESH


def place_in_mesh():
    c, f = lax.axis_index("ctx"), lax.axis_index("fsdp")
    z, k = lax.div(c, 2), lax.rem(c, 2)
    return c, f, z, k, 2 * f + k


def bounce(source, buffer, target, sem):
    one = pltpu.make_async_copy(source, buffer, sem)
    one.start()
    one.wait()
    two = pltpu.make_async_copy(buffer, target, sem)
    two.start()
    two.wait()


def gather_kernel(
    plan, tok, doc, front, back, tok_out, doc_out, w_out, b_out,
    w_buf, b_buf, tsend, trecv, csend, crecv, wsend, wrecv, bsend, brecv, dsend, drecv, lsem,
):
    shards, unit, ranks = plan.fsdp, plan.unit, plan.ranks
    c, f, z, k, p = place_in_mesh()
    other = c + 1 - 2 * k
    width = D // shards

    def cols(block):
        return pl.ds(pl.multiple_of(block * width, 128), width)

    def remote(src, dst, send, recv, device):
        return pltpu.make_async_remote_copy(
            src_ref=src, dst_ref=dst, send_sem=send, recv_sem=recv, device_id=device, device_id_type=MESH
        )

    def peer(step):
        return lax.rem(f + step, shards)

    def giver(step):
        return lax.rem(f + shards - step, shards)

    def send_tokens(step):
        return remote(tok, tok_out.at[f, k], tsend.at[step], trecv.at[step], (c, peer(step)))

    def get_tokens(step):
        here = tok_out.at[giver(step), k]
        return remote(here, here, tsend.at[step], trecv.at[step], (c, peer(step)))

    def share(step):
        here = tok_out.at[giver(step), k]
        src = tok if step == 0 else here
        return remote(src, here, csend.at[step], crecv.at[step], (other, f))

    def get_share(step):
        here = tok_out.at[giver(step), 1 - k]
        return remote(here, here, csend.at[step], crecv.at[step], (other, f))

    def rows_of(dst):
        return pl.ds(pl.multiple_of((2 * dst + k) * unit, unit), unit)

    def send_back(step):
        return remote(
            back.at[rows_of(peer(step)), :], b_out.at[:, cols(f)], bsend.at[step], brecv.at[step], (c, peer(step))
        )

    def get_back(step):
        here = b_out.at[:, cols(giver(step))]
        return remote(here, here, bsend.at[step], brecv.at[step], (c, peer(step)))

    def send_doc(step):
        return remote(doc, doc_out, dsend.at[step], drecv, (c, peer(step)))

    weights = []
    for slot in range(3):
        units, _ = plan.slots[slot]
        for dst in range(ranks):
            src, at = units[dst] // plan.per_shard, units[dst] % plan.per_shard
            weights.append((slot, dst, 2 * src + dst % 2, at))

    def send_weight(slot, dst, at):
        return remote(
            front.at[:, pl.ds(at * unit, unit)],
            w_out.at[:, pl.ds(slot * unit, unit)],
            wsend.at[slot, dst // 2],
            wrecv.at[slot],
            (c, dst // 2),
        )

    own_tok = pltpu.make_async_copy(tok, tok_out.at[f, k], lsem.at[0])
    own_doc = pltpu.make_async_copy(doc, doc_out, lsem.at[1])
    for step in range(1, shards):
        send_tokens(step).start()
    share(0).start()
    own_tok.start()
    for step in range(1, shards):
        send_back(step).start()

    @pl.when(f == z)
    def _():
        own_doc.start()
        for step in range(1, shards):
            send_doc(step).start()

    for slot, dst, src, at in weights:
        if src != dst:

            @pl.when(p == src)
            def _(slot=slot, dst=dst, at=at):
                send_weight(slot, dst, at).start()

    for step in range(1, shards):
        get_tokens(step).wait_recv()
        share(step).start()
    for slot, dst, src, at in weights:
        if src == dst:

            @pl.when(p == dst)
            def _(slot=slot, at=at):
                bounce(
                    front.at[:, pl.ds(at * unit, unit)], w_buf, w_out.at[:, pl.ds(slot * unit, unit)], lsem.at[2]
                )

    bounce(back.at[rows_of(f), :], b_buf, b_out.at[:, cols(f)], lsem.at[3])
    own_tok.wait()

    @pl.when(f == z)
    def _():
        own_doc.wait()
        for step in range(1, shards):
            send_doc(step).wait_send()

    @pl.when(f != z)
    def _():
        send_doc(1).wait_recv()

    for step in range(shards):
        get_share(step).wait_recv()
        share(step).wait_send()
    for step in range(1, shards):
        send_tokens(step).wait_send()
        send_back(step).wait_send()
        get_back(step).wait_recv()
    for slot, dst, src, at in weights:
        if src != dst:

            @pl.when(p == src)
            def _(slot=slot, dst=dst, at=at):
                send_weight(slot, dst, at).wait_send()

            @pl.when(p == dst)
            def _(slot=slot, dst=dst, at=at):
                send_weight(slot, dst, at).wait_recv()


def gather_first(plan, tokens, documents, front_weight, back_weight):
    shards, unit = plan.fsdp, plan.unit
    rows, length = tokens.shape[0], documents.shape[1]
    vmem, anywhere = pl.BlockSpec(memory_space=pltpu.VMEM), pl.BlockSpec(memory_space=pl.ANY)
    dma = pltpu.SemaphoreType.DMA
    return pl.pallas_call(
        functools.partial(gather_kernel, plan),
        in_specs=[vmem, vmem, anywhere, anywhere],
        out_specs=[anywhere] * 4,
        out_shape=[
            jax.ShapeDtypeStruct((shards, 2, rows, D), bf16),
            jax.ShapeDtypeStruct((1, length), f32),
            jax.ShapeDtypeStruct((D, 3 * unit), bf16),
            jax.ShapeDtypeStruct((unit, D), bf16),
        ],
        scratch_shapes=[
            pltpu.VMEM((D, unit), bf16),
            pltpu.VMEM((unit, D // shards), bf16),
            dma((shards,)),
            dma((shards,)),
            dma((shards,)),
            dma((shards,)),
            dma((3, shards)),
            dma((3,)),
            dma((shards,)),
            dma((shards,)),
            dma((shards,)),
            dma(()),
            dma((4,)),
        ],
        compiler_params=pltpu.CompilerParams(has_side_effects=True),
    )(tokens, documents, front_weight, back_weight)


def back_owner_kernel(plan, src, out, send, recv, lsem):
    unit, ranks = plan.unit, plan.ranks
    c, f, z, k, p = place_in_mesh()

    def copy(j, owner, place):
        return pltpu.make_async_remote_copy(
            src_ref=src.at[pl.ds(j * unit, unit), :],
            dst_ref=out.at[pl.ds(place * unit, unit), :],
            send_sem=send.at[j],
            recv_sem=recv.at[place],
            device_id=(owner, z),
            device_id_type=MESH,
        )

    blocks = [
        (rank, j, plan.back_units[rank][j] // 5, plan.back_units[rank][j] % 5)
        for rank in range(ranks)
        for j in range(5)
    ]
    for rank, j, owner, place in blocks:

        @pl.when((p == rank) & ~((c == owner) & (f == z)))
        def _(j=j, owner=owner, place=place):
            copy(j, owner, place).start()

        @pl.when((p == rank) & (c == owner) & (f == z))
        def _(j=j, place=place):
            pltpu.make_async_copy(
                src.at[pl.ds(j * unit, unit), :], out.at[pl.ds(place * unit, unit), :], lsem.at[place]
            ).start()

    for rank, j, owner, place in blocks:

        @pl.when((p == rank) & ~((c == owner) & (f == z)))
        def _(j=j, owner=owner, place=place):
            copy(j, owner, place).wait_send()

        @pl.when((c == owner) & ~((p == rank) & (f == z)))
        def _(j=j, owner=owner, place=place):
            copy(j, owner, place).wait_recv()

        @pl.when((p == rank) & (c == owner) & (f == z))
        def _(j=j, place=place):
            pltpu.make_async_copy(
                src.at[pl.ds(j * unit, unit), :], out.at[pl.ds(place * unit, unit), :], lsem.at[place]
            ).wait()


def back_to_owner(plan, value):
    dma = pltpu.SemaphoreType.DMA
    return pl.pallas_call(
        functools.partial(back_owner_kernel, plan),
        in_specs=[pl.BlockSpec(memory_space=pltpu.VMEM)],
        out_specs=pl.BlockSpec(memory_space=pl.ANY),
        out_shape=jax.ShapeDtypeStruct(value.shape, value.dtype),
        scratch_shapes=[dma((5,)), dma((5,)), dma((5,))],
        compiler_params=pltpu.CompilerParams(has_side_effects=True),
    )(value)


def front_owner_kernel(plan, src, out, send, recv, lsem):
    unit, ranks = plan.unit, plan.ranks
    c, f, z, k, p = place_in_mesh()
    moves, start = [], 0
    for slot, (units, wide) in enumerate(plan.slots):
        for rank in range(ranks):
            owner, place = units[rank] // plan.per_shard, units[rank] % plan.per_shard
            moves.append((slot, rank, owner, place, start, wide))
        start += wide

    def copy(slot, owner, place, begin, wide, half):
        return pltpu.make_async_remote_copy(
            src_ref=src.at[half, :, pl.ds(begin * unit, wide * unit)],
            dst_ref=out.at[:, pl.ds(place * unit, wide * unit)],
            send_sem=send.at[slot, half],
            recv_sem=recv.at[place],
            device_id=(2 * z + half, owner),
            device_id_type=MESH,
        )

    def local(place, begin, wide, half):
        return pltpu.make_async_copy(
            src.at[half, :, pl.ds(begin * unit, wide * unit)],
            out.at[:, pl.ds(place * unit, wide * unit)],
            lsem.at[place],
        )

    for slot, rank, owner, place, begin, wide in moves:
        for half in range(2):
            if 2 * owner + half == rank:

                @pl.when(p == rank)
                def _(place=place, begin=begin, wide=wide, half=half):
                    local(place, begin, wide, half).start()

            else:

                @pl.when(p == rank)
                def _(slot=slot, owner=owner, place=place, begin=begin, wide=wide, half=half):
                    copy(slot, owner, place, begin, wide, half).start()

    for slot, rank, owner, place, begin, wide in moves:
        for half in range(2):
            if 2 * owner + half == rank:

                @pl.when(p == rank)
                def _(place=place, begin=begin, wide=wide, half=half):
                    local(place, begin, wide, half).wait()

            else:

                @pl.when(p == rank)
                def _(slot=slot, owner=owner, place=place, begin=begin, wide=wide, half=half):
                    copy(slot, owner, place, begin, wide, half).wait_send()

                @pl.when(p == 2 * owner + half)
                def _(slot=slot, owner=owner, place=place, begin=begin, wide=wide, half=half):
                    copy(slot, owner, place, begin, wide, half).wait_recv()


def front_to_owner(plan, value):
    dma = pltpu.SemaphoreType.DMA
    return pl.pallas_call(
        functools.partial(front_owner_kernel, plan),
        in_specs=[pl.BlockSpec(memory_space=pltpu.VMEM)],
        out_specs=pl.BlockSpec(memory_space=pl.ANY),
        out_shape=jax.ShapeDtypeStruct((value.shape[1], plan.per_shard * plan.unit), value.dtype),
        scratch_shapes=[dma((5, 2)), dma((plan.per_shard,)), dma((plan.per_shard,))],
        compiler_params=pltpu.CompilerParams(has_side_effects=True),
    )(value)


def gelu_parts(u):
    scale = np.float32(np.sqrt(2.0 / np.pi))
    square = u * u
    inner = scale * u * (1.0 + 0.044715 * square)
    t = jnp.tanh(inner)
    value = 0.5 * u * (1.0 + t)
    slope = 0.5 * (1.0 + t) + 0.5 * u * (1.0 - t * t) * scale * (1.0 + 3 * 0.044715 * square)
    return value, slope


def adam_update(weight, first, second, grad, rate, count_now, decay):
    first_new = beta_first * first + (1.0 - beta_first) * grad
    second_new = beta_second * second + (1.0 - beta_second) * grad * grad
    steps_float = count_now.astype(f32)
    first_fix = 1.0 - jnp.power(beta_first, steps_float)
    second_fix = 1.0 - jnp.power(beta_second, steps_float)
    change = first_new / first_fix / (jnp.sqrt(second_new / second_fix) + adam_eps) + decay * weight
    return (weight - rate * change, first_new, second_new)


def after(value, *others):
    return lax.optimization_barrier((value,) + others)[0]


def per_device(
    tokens,
    cotangent,
    doc_ids,
    block_order,
    front_weight,
    back_weight,
    front_master,
    back_master,
    front_first,
    back_first,
    front_second,
    back_second,
    vectors,
    vector_first,
    vector_second,
    learn_rates,
    adam_step,
    *,
    plan,
):
    planes, shards, ranks, unit = plan.planes, plan.fsdp, plan.ranks, plan.unit
    both = ("ctx", "fsdp")
    contract_last = (((1,), (1,)), ((), ()))
    contract_first = (((0,), (0,)), ((), ()))
    c_index, f = lax.axis_index("ctx"), lax.axis_index("fsdp")
    z, k = c_index // 2, c_index % 2
    p = 2 * f + k
    rows = tokens.shape[1]
    plane_rows = 2 * shards * rows
    share = 2 * rows

    bias_front = vectors[:IN_COLS].reshape(-1, unit)
    bias_back = vectors[IN_COLS : IN_COLS + D]
    norm_gain = vectors[IN_COLS + D : IN_COLS + 2 * D]
    norm_shift = vectors[IN_COLS + 2 * D :]

    swap_pairs = [(2 * i + j, 2 * i + 1 - j) for i in range(planes) for j in range(2)]

    def swap_core(value):
        return lax.ppermute(value, "ctx", swap_pairs)

    def to_shard(value, step):
        return lax.ppermute(value, "fsdp", [(i, i ^ step) for i in range(shards)])

    def to_plane(value, step):
        return lax.ppermute(
            value, "ctx", [(2 * i + j, 2 * (i ^ step) + j) for i in range(planes) for j in range(2)]
        )

    def gather_plane(value):
        mine = lax.all_gather(value, "fsdp")
        other = swap_core(mine)
        low = jnp.where(k == 0, mine, other)
        high = jnp.where(k == 0, other, mine)
        return jnp.stack([low, high], axis=1).reshape(plane_rows, D)

    def at(array, index):
        return lax.dynamic_index_in_dim(array, index, 0, keepdims=False)

    blocks = block_order.shape[0]
    block_tokens = doc_ids.shape[1] // blocks
    offsets = jnp.arange(block_tokens, dtype=jnp.int32)
    positions_all = (block_order[:, None] * block_tokens + offsets[None, :]).reshape(planes, share)
    own_positions = at(positions_all, z)
    plane_positions = jnp.tile(own_positions, shards)

    plane_tokens, documents, weight_qkv, back_attention = gather_first(
        plan, tokens[0], doc_ids.astype(f32), front_weight, back_weight
    )
    plane_tokens = plane_tokens.reshape(plane_rows, D)

    normed = (normalize(plane_tokens)[0] * norm_gain + norm_shift).astype(bf16)

    def slot_weight(slot, gate):
        units, wide = plan.slots[slot]
        width = wide * unit
        table = np.asarray(units)
        source, place = table // plan.per_shard, table % plan.per_shard
        total = None
        for one in plan.rounds[slot]:
            sends = np.zeros(ranks, np.int32)
            links = []
            for src, dst, core in one:
                sends[2 * src + core] = place[2 * dst + core]
                links += [
                    (plan.device(i, core, src), plan.device(i, core, dst)) for i in range(planes)
                ]
            start = after(pick(sends, p) * unit, gate)
            block = lax.dynamic_slice(front_weight, (0, start), (D, width))
            block = lax.ppermute(block, both, links)
            total = block if total is None else total + block
        local = source == np.arange(ranks) // 2
        start = pick(np.where(local, place, 0), p) * unit
        own = lax.dynamic_slice(front_weight, (0, start), (D, width))
        if total is None:
            return own
        if not local.any():
            return total
        return jnp.where(pick(local, p) > 0, own, total)

    gate = weight_qkv[0, 0]
    plane_grad = gather_plane(after(cotangent[0], gate))
    weight_up = jnp.concatenate([slot_weight(i, gate) for i in range(3, 5)], axis=1)

    def back_rows(rank):
        table = pick(plan.back_units, rank)
        return jnp.concatenate(
            [
                lax.dynamic_slice(back_weight, (table[j] * unit, 0), (2 * unit, D // shards))
                for j in (1, 3)
            ],
            axis=0,
        )

    col_width = D // shards
    back_up = jnp.zeros((4 * unit, D), bf16)
    for step in range(shards):
        piece = back_rows(after(2 * (f ^ step) + k, gate))
        if step:
            piece = to_shard(piece, step)
        back_up = lax.dynamic_update_slice(back_up, piece, (0, (f ^ step) * col_width))
    back_local = jnp.concatenate([back_attention, back_up], axis=0)

    unit_table = pick(plan.rank_units, p)
    bias_local = jnp.take(bias_front, unit_table, axis=0).reshape(-1)

    hidden = jnp.dot(normed, weight_qkv, preferred_element_type=f32) + bias_local[: 3 * unit]
    tables = rotation_tables(plane_positions, unit)
    query = rotate(hidden[:, :unit], tables).astype(bf16)
    key = rotate(hidden[:, unit : 2 * unit], tables).astype(bf16)
    qkv = jnp.concatenate([query, key, hidden[:, 2 * unit :].astype(bf16)], axis=1)

    def to_sequence(value):
        shaped = value.reshape(shards, share, -1)
        pieces = [at(shaped, z)]
        for step in range(1, planes):
            pieces.append(to_plane(at(shaped, z ^ step), step))
        return jnp.concatenate(pieces, axis=0)

    def to_plane_rows(value):
        shaped = value.reshape(planes, share, -1)
        pieces = [shaped[0]] + [to_plane(shaped[step], step) for step in range(1, planes)]
        stacked = jnp.stack(pieces)
        return jnp.concatenate([at(stacked, i ^ z) for i in range(planes)], axis=0)

    qkv_seq = to_sequence(qkv)

    attended_grad = lax.dot_general(
        plane_grad, back_attention, contract_last, preferred_element_type=f32
    ).astype(bf16)
    grad_seq = to_sequence(attended_grad)

    order = jnp.arange(planes, dtype=jnp.int32) ^ z
    seq_positions = jnp.take(positions_all, order, axis=0).reshape(-1)
    doc_row = documents[0].astype(jnp.int32)
    seq_documents = jnp.take(
        jnp.take(doc_row.reshape(blocks, block_tokens), block_order, axis=0).reshape(planes, share),
        order,
        axis=0,
    ).reshape(-1)
    attended, query_grad, key_grad, value_grad = attention(
        qkv_seq[:, :unit],
        qkv_seq[:, unit : 2 * unit],
        qkv_seq[:, 2 * unit :],
        grad_seq,
        seq_positions,
        seq_documents,
    )
    seq_tables = rotation_tables(seq_positions, unit)
    returned = to_plane_rows(
        jnp.concatenate(
            [
                attended,
                rotate_back(query_grad, seq_tables).astype(bf16),
                rotate_back(key_grad, seq_tables).astype(bf16),
                value_grad.astype(bf16),
            ],
            axis=1,
        )
    )

    up = jnp.dot(normed, weight_up, preferred_element_type=f32) + bias_local[3 * unit :]
    activation, slope = gelu_parts(up)
    mixed_grad = lax.dot_general(plane_grad, back_up, contract_last, preferred_element_type=f32)
    up_grad = (mixed_grad * slope).astype(bf16)
    mixed = jnp.concatenate([returned[:, :unit], activation.astype(bf16)], axis=1)
    hidden_grad = jnp.concatenate([returned[:, unit:], up_grad], axis=1)

    def sum_to_owner(value):
        shaped = value.reshape(shards, 2, rows, D)
        kept = lax.dynamic_index_in_dim(shaped, k, 1, keepdims=False)
        sent = lax.dynamic_index_in_dim(shaped, 1 - k, 1, keepdims=False).astype(bf16)
        summed = kept + swap_core(sent).astype(f32)
        total = at(summed, f)
        for step in range(1, shards):
            total = total + to_shard(at(summed, f ^ step).astype(bf16), step).astype(f32)
        return total

    projected = sum_to_owner(jnp.dot(mixed, back_local, preferred_element_type=f32))
    inputs = tokens[0].astype(f32)
    layer_out = (inputs + projected + bias_back).astype(bf16)[None]

    weight_local = jnp.concatenate([weight_qkv, weight_up], axis=1)
    normed_grad = sum_to_owner(
        lax.dot_general(hidden_grad, weight_local, contract_last, preferred_element_type=f32)
    )
    unscaled, factor = normalize(inputs)
    scaled = normed_grad * norm_gain
    input_grad = factor * (
        scaled
        - jnp.mean(scaled, axis=-1, keepdims=True)
        - unscaled * jnp.mean(scaled * unscaled, axis=-1, keepdims=True)
    )
    tokens_grad = (cotangent[0].astype(f32) + input_grad).astype(bf16)[None]

    up_links = lambda s: [
        (2 * i + j, 2 * i + 2 + j) for i in range(min(s, planes - 1)) for j in range(2)
    ]
    mirror = lambda links: [
        (2 * (planes - 1 - a // 2) + a % 2, 2 * (planes - 1 - b // 2) + b % 2) for a, b in links
    ]

    def sum_over_planes(block_of):
        rising = falling = None
        for s in range(1, planes):
            a = jnp.clip(planes - s + z, 0, planes - 1)
            b = jnp.clip(s - 1 - (planes - 1 - z), 0, planes - 1)
            term_a, term_b = block_of(a), block_of(b)
            if rising is not None:
                term_a = (term_a.astype(f32) + rising.astype(f32)).astype(bf16)
                term_b = (term_b.astype(f32) + falling.astype(f32)).astype(bf16)
            rising = lax.ppermute(term_a, "ctx", up_links(s))
            falling = lax.ppermute(term_b, "ctx", mirror(up_links(s)))
        return block_of(z).astype(f32) + rising.astype(f32) + falling.astype(f32)

    back_partial = lax.dot_general(
        mixed, plane_grad, contract_first, preferred_element_type=f32
    ).astype(bf16)
    back_sum = sum_over_planes(
        lambda i: lax.dynamic_slice(back_partial, (0, i * col_width), (5 * unit, col_width))
    ).astype(bf16)
    front_partial = lax.dot_general(
        normed, hidden_grad, contract_first, preferred_element_type=f32
    ).astype(bf16)
    front_rows = D // planes
    front_sum = sum_over_planes(
        lambda i: lax.dynamic_slice(front_partial, (i * front_rows, 0), (front_rows, 7 * unit))
    ).astype(bf16)

    back_grad = back_to_owner(plan, back_sum).astype(f32)
    front_grad = front_to_owner(plan, front_sum.reshape(2, front_rows // 2, -1)).astype(f32)

    def column_sums(value):
        ones = jnp.ones((8, value.shape[0]), bf16)
        return jnp.dot(ones, value, preferred_element_type=f32)[0]

    spread = (jnp.arange(7 * ranks)[:, None] == unit_table[None, :]).astype(f32)
    hidden_sum = column_sums(hidden_grad).reshape(7, unit)
    front_vector = jnp.sum(spread[:, :, None] * hidden_sum[None], axis=1).reshape(-1)
    vector_term = jnp.concatenate(
        [
            front_vector,
            column_sums(cotangent[0]),
            jnp.sum(normed_grad * unscaled, axis=0),
            jnp.sum(normed_grad, axis=0),
        ]
    )
    vector_grad = vector_term.reshape(-1, 128)
    vector_grad = vector_grad + swap_core(vector_grad)
    step = 1
    while step < shards:
        vector_grad = vector_grad + to_shard(vector_grad, step)
        vector_grad = vector_grad + to_plane(vector_grad, step)
        step *= 2
    vector_grad = vector_grad.reshape(-1)

    count_now = adam_step[0]
    back_new, back_first_new, back_second_new = adam_update(
        back_master, back_first, back_second, back_grad, learn_rates[1], count_now, weight_decay
    )
    front_new, front_first_new, front_second_new = adam_update(
        front_master, front_first, front_second, front_grad, learn_rates[0], count_now, weight_decay
    )
    vectors_new, vector_first_new, vector_second_new = adam_update(
        vectors, vector_first, vector_second, vector_grad, learn_rates[2], count_now, 0.0
    )

    def gather_rows(value):
        height = value.shape[0]
        out = jnp.zeros((2 * planes * height, value.shape[1]), value.dtype)

        def place(out, piece, plane):
            valid = (plane >= 0) & (plane < planes)
            where = jnp.where(valid, plane, z)
            mine, other = piece
            out = lax.dynamic_update_slice(out, mine, ((2 * where + k) * height, 0))
            return lax.dynamic_update_slice(out, other, ((2 * where + 1 - k) * height, 0))

        rising = falling = value
        pieces = []
        for s in range(1, planes):
            links = [(2 * i + j, 2 * i + 2 + j) for i in range(s - 1, planes - 1) for j in range(2)]
            rising = lax.ppermute(rising, "ctx", links)
            falling = lax.ppermute(falling, "ctx", mirror(links))
            pieces.append(((rising, swap_core(rising)), z - s))
            pieces.append(((falling, swap_core(falling)), z + s))
        for piece, plane in pieces:
            out = place(out, piece, plane)
        return place(out, (value, swap_core(value)), z)

    back_next = gather_rows(back_new.astype(bf16))
    front_next = gather_rows(front_new.astype(bf16))
    return (
        layer_out,
        tokens_grad,
        front_grad,
        back_grad,
        vector_grad,
        front_new,
        back_new,
        vectors_new,
        front_first_new,
        back_first_new,
        vector_first_new,
        front_second_new,
        back_second_new,
        vector_second_new,
        front_next,
        back_next,
    )


def solution(mesh):
    plan = Layout(mesh.shape["ctx"], mesh.shape["fsdp"])
    tokens_spec = P("fsdp", "ctx", None)
    cols, owned, same = P(None, "fsdp"), P("ctx", "fsdp"), P()
    in_specs = (
        (tokens_spec, tokens_spec, P("fsdp", None), same, cols, cols)
        + (owned,) * 6
        + (same,) * 5
    )
    out_specs = (
        (tokens_spec, tokens_spec, owned, owned, same)
        + (owned, owned, same) * 3
        + (cols, cols)
    )
    return jax.shard_map(
        functools.partial(per_device, plan=plan),
        mesh=mesh,
        in_specs=in_specs,
        out_specs=out_specs,
        check_vma=False,
    )
```

```python
import functools

import jax
import jax.numpy as jnp
import numpy as np
from jax import lax
from jax.experimental import pallas as pl
from jax.experimental.pallas import tpu as pltpu
from jax.sharding import PartitionSpec as P

D = 2048
HEADS = 32
FF = 8192
ROT = 32
HEAD_DIM = 64
IN_COLS = 14336
BACK_ROWS = 10240

norm_eps = 1e-05
beta_first = 0.9
beta_second = 0.95
adam_eps = 1e-08
weight_decay = 0.1
masked_score = -1e30
bf16 = jnp.bfloat16
f32 = jnp.float32


class Layout:
    def __init__(self, ctx, fsdp):
        self.ctx, self.fsdp, self.planes, self.ranks = ctx, fsdp, ctx // 2, 2 * fsdp
        assert ctx % 2 == 0 and self.planes == fsdp
        self.unit = D // self.ranks
        self.per_shard = IN_COLS // self.unit // fsdp
        r = self.ranks
        first_up = 3 * r
        home = {f: [] for f in range(fsdp)}
        for g in range(first_up, 7 * r, 2):
            assert g // self.per_shard == (g + 1) // self.per_shard
            home[g // self.per_shard].append(g)
        pairs = {p: [None, None] for p in range(r)}
        for f in range(fsdp):
            if len(home[f]) >= 4:
                keep, home[f] = home[f][:4], home[f][4:]
                pairs[2 * f], pairs[2 * f + 1] = keep[:2], keep[2:]
            elif home[f]:
                keep, home[f] = home[f], []
                for i, g in enumerate(keep):
                    pairs[2 * f + i % 2][(i + i // 2) % 2] = g
        for s in range(2):
            for k in range(2):
                used = set()
                for f in range(fsdp):
                    p = 2 * f + k
                    if pairs[p][s] is not None:
                        continue
                    options = sorted(
                        (h for h in range(fsdp) if home[h]),
                        key=lambda h: (h in used, bin(h ^ f).count("1"), -len(home[h])),
                    )
                    used.add(options[0])
                    pairs[p][s] = home[options[0]].pop(0)
        self.pairs = pairs
        self.slots = [
            ([p for p in range(r)], 1),
            ([r + p for p in range(r)], 1),
            ([2 * r + p for p in range(r)], 1),
            ([pairs[p][0] for p in range(r)], 2),
            ([pairs[p][1] for p in range(r)], 2),
        ]
        self.rounds = []
        for units, _ in self.slots:
            rounds = []
            for k in range(2):
                for f in range(fsdp):
                    src = units[2 * f + k] // self.per_shard
                    if src == f:
                        continue
                    for one in rounds:
                        if all((src, k) != (a, c) for a, _, c in one):
                            one.append((src, f, k))
                            break
                    else:
                        rounds.append([(src, f, k)])
            self.rounds.append(rounds)
        self.rank_units = [
            [p, r + p, 2 * r + p, pairs[p][0], pairs[p][0] + 1, pairs[p][1], pairs[p][1] + 1]
            for p in range(r)
        ]
        self.back_units = [[p] + [g - 2 * r for g in self.rank_units[p][3:]] for p in range(r)]
        self.matchings = []
        left = {p: list(range(5)) for p in range(r)}
        own = lambda p, j: self.back_units[p][j] // 5
        for _ in range(5):
            match = {}

            def assign(p, seen):
                for j in left[p]:
                    c = own(p, j)
                    if c in seen:
                        continue
                    seen.add(c)
                    if c not in match or assign(match[c][0], seen):
                        match[c] = (p, j)
                        return True
                return False

            for p in range(r):
                assert assign(p, set())
            for c, (p, j) in match.items():
                left[p].remove(j)
            self.matchings.append(match)

    def device(self, z, k, f):
        return (2 * z + k) * self.fsdp + f


def pick(table, index):
    return jnp.asarray(np.asarray(table, np.int32))[index]


def normalize(values):
    values = values.astype(f32)
    centered = values - jnp.mean(values, axis=-1, keepdims=True)
    factor = lax.rsqrt(jnp.mean(centered * centered, axis=-1, keepdims=True) + norm_eps)
    return centered * factor, factor


def rotation_tables(positions, width):
    half = ROT // 2
    lane = np.arange(width) % HEAD_DIM
    frequency = jnp.power(
        10000.0, -2.0 * jnp.asarray(lane % half, f32) / ROT
    )
    angles = positions.astype(f32)[:, None] * frequency[None, :]
    rotated = jnp.asarray(lane < ROT)
    lower = jnp.asarray(lane < half)
    cosine = jnp.where(rotated, jnp.cos(angles), 1.0)
    sine = jnp.where(rotated, jnp.sin(angles), 0.0)
    return cosine, jnp.where(lower, -sine, 0.0), jnp.where(lower, 0.0, sine)


def rotate(values, tables):
    half = ROT // 2
    cosine, from_above, from_below = tables
    return (
        values * cosine
        + jnp.roll(values, -half, axis=1) * from_above
        + jnp.roll(values, half, axis=1) * from_below
    )


def rotate_back(values, tables):
    half = ROT // 2
    cosine, from_above, from_below = tables
    return (
        values * cosine
        + jnp.roll(values * from_above, half, axis=1)
        + jnp.roll(values * from_below, -half, axis=1)
    )


def attention_kernel(
    q_ref, k_ref, v_ref, g_ref, pos_q, pos_k, seg_q, seg_k, att_ref, dq_ref, dk_ref, dv_ref
):
    scale = HEAD_DIM ** (-0.5)
    width = q_ref.shape[1]

    @pl.when(pl.program_id(0) == 0)
    def _():
        dk_ref[...] = jnp.zeros_like(dk_ref)
        dv_ref[...] = jnp.zeros_like(dv_ref)

    allowed = (pos_k[...] <= pos_q[...]) & (seg_k[...] == seg_q[...])
    bias = jnp.where(allowed, 0.0, masked_score)
    last = (((1,), (1,)), ((), ()))
    first = (((0,), (0,)), ((), ()))
    for head in range(width // HEAD_DIM):
        cols = slice(head * HEAD_DIM, (head + 1) * HEAD_DIM)
        q, g = q_ref[:, cols], g_ref[:, cols]
        k, v = k_ref[:, cols], v_ref[:, cols]
        scores = lax.dot_general(q, k, last, preferred_element_type=f32) * scale + bias
        weights = jnp.exp(scores - jnp.max(scores, axis=1, keepdims=True))
        probs = weights * (1.0 / jnp.sum(weights, axis=1, keepdims=True))
        probs_low = probs.astype(bf16)
        out = jnp.dot(probs_low, v, preferred_element_type=f32)
        att_ref[:, cols] = out.astype(bf16)
        prob_grad = lax.dot_general(g, v, last, preferred_element_type=f32)
        delta = jnp.sum(g.astype(f32) * out, axis=1, keepdims=True)
        score_grad = (probs * (prob_grad - delta)).astype(bf16)
        dq_ref[:, cols] = jnp.dot(score_grad, k, preferred_element_type=f32) * scale
        dk_ref[:, cols] += lax.dot_general(score_grad, q, first, preferred_element_type=f32) * scale
        dv_ref[:, cols] += lax.dot_general(probs_low, g, first, preferred_element_type=f32)


def attention(query, key, value, grad, positions, segments):
    length, width = query.shape
    block = 256
    rows = pl.BlockSpec((block, width), lambda i: (i, 0))
    whole = pl.BlockSpec((length, width), lambda i: (0, 0))
    column = pl.BlockSpec((block, 1), lambda i: (i, 0))
    line = pl.BlockSpec((1, length), lambda i: (0, 0))
    return pl.pallas_call(
        attention_kernel,
        grid=(length // block,),
        in_specs=[rows, whole, whole, rows, column, line, column, line],
        out_specs=[rows, rows, whole, whole],
        out_shape=[
            jax.ShapeDtypeStruct((length, width), bf16),
            jax.ShapeDtypeStruct((length, width), f32),
            jax.ShapeDtypeStruct((length, width), f32),
            jax.ShapeDtypeStruct((length, width), f32),
        ],
        cost_estimate=pl.CostEstimate(
            flops=14 * length * length * width,
            transcendentals=length * length * width // HEAD_DIM,
            bytes_accessed=20 * length * width,
        ),
    )(query, key, value, grad, positions[:, None], positions[None], segments[:, None], segments[None])


MESH = pl.DeviceIdType.MESH


def place_in_mesh():
    c, f = lax.axis_index("ctx"), lax.axis_index("fsdp")
    z, k = lax.div(c, 2), lax.rem(c, 2)
    return c, f, z, k, 2 * f + k


def bounce(source, buffer, target, sem):
    one = pltpu.make_async_copy(source, buffer, sem)
    one.start()
    one.wait()
    two = pltpu.make_async_copy(buffer, target, sem)
    two.start()
    two.wait()


def gather_kernel(
    plan, tok, doc, front, back, tok_out, doc_out, w_out, b_out,
    w_buf, b_buf, tsend, trecv, csend, crecv, wsend, wrecv, bsend, brecv, dsend, drecv, lsem,
):
    shards, unit, ranks = plan.fsdp, plan.unit, plan.ranks
    c, f, z, k, p = place_in_mesh()
    other = c + 1 - 2 * k
    width = D // shards

    def cols(block):
        return pl.ds(pl.multiple_of(block * width, 128), width)

    def remote(src, dst, send, recv, device):
        return pltpu.make_async_remote_copy(
            src_ref=src, dst_ref=dst, send_sem=send, recv_sem=recv, device_id=device, device_id_type=MESH
        )

    def peer(step):
        return lax.rem(f + step, shards)

    def giver(step):
        return lax.rem(f + shards - step, shards)

    def send_tokens(step):
        return remote(tok, tok_out.at[f, k], tsend.at[step], trecv.at[step], (c, peer(step)))

    def get_tokens(step):
        here = tok_out.at[giver(step), k]
        return remote(here, here, tsend.at[step], trecv.at[step], (c, peer(step)))

    def share(step):
        here = tok_out.at[giver(step), k]
        src = tok if step == 0 else here
        return remote(src, here, csend.at[step], crecv.at[step], (other, f))

    def get_share(step):
        here = tok_out.at[giver(step), 1 - k]
        return remote(here, here, csend.at[step], crecv.at[step], (other, f))

    def rows_of(dst):
        return pl.ds(pl.multiple_of((2 * dst + k) * unit, unit), unit)

    def send_back(step):
        return remote(
            back.at[rows_of(peer(step)), :], b_out.at[:, cols(f)], bsend.at[step], brecv.at[step], (c, peer(step))
        )

    def get_back(step):
        here = b_out.at[:, cols(giver(step))]
        return remote(here, here, bsend.at[step], brecv.at[step], (c, peer(step)))

    def send_doc(step):
        return remote(doc, doc_out, dsend.at[step], drecv, (c, peer(step)))

    weights = []
    for slot in range(3):
        units, _ = plan.slots[slot]
        for dst in range(ranks):
            src, at = units[dst] // plan.per_shard, units[dst] % plan.per_shard
            weights.append((slot, dst, 2 * src + dst % 2, at))

    def send_weight(slot, dst, at):
        return remote(
            front.at[:, pl.ds(at * unit, unit)],
            w_out.at[:, pl.ds(slot * unit, unit)],
            wsend.at[slot, dst // 2],
            wrecv.at[slot],
            (c, dst // 2),
        )

    own_tok = pltpu.make_async_copy(tok, tok_out.at[f, k], lsem.at[0])
    own_doc = pltpu.make_async_copy(doc, doc_out, lsem.at[1])
    for step in range(1, shards):
        send_tokens(step).start()
    share(0).start()
    own_tok.start()
    for step in range(1, shards):
        send_back(step).start()

    @pl.when(f == z)
    def _():
        own_doc.start()
        for step in range(1, shards):
            send_doc(step).start()

    for slot, dst, src, at in weights:
        if src != dst:

            @pl.when(p == src)
            def _(slot=slot, dst=dst, at=at):
                send_weight(slot, dst, at).start()

    for step in range(1, shards):
        get_tokens(step).wait_recv()
        share(step).start()
    for slot, dst, src, at in weights:
        if src == dst:

            @pl.when(p == dst)
            def _(slot=slot, at=at):
                bounce(
                    front.at[:, pl.ds(at * unit, unit)], w_buf, w_out.at[:, pl.ds(slot * unit, unit)], lsem.at[2]
                )

    bounce(back.at[rows_of(f), :], b_buf, b_out.at[:, cols(f)], lsem.at[3])
    own_tok.wait()

    @pl.when(f == z)
    def _():
        own_doc.wait()
        for step in range(1, shards):
            send_doc(step).wait_send()

    @pl.when(f != z)
    def _():
        send_doc(1).wait_recv()

    for step in range(shards):
        get_share(step).wait_recv()
        share(step).wait_send()
    for step in range(1, shards):
        send_tokens(step).wait_send()
        send_back(step).wait_send()
        get_back(step).wait_recv()
    for slot, dst, src, at in weights:
        if src != dst:

            @pl.when(p == src)
            def _(slot=slot, dst=dst, at=at):
                send_weight(slot, dst, at).wait_send()

            @pl.when(p == dst)
            def _(slot=slot, dst=dst, at=at):
                send_weight(slot, dst, at).wait_recv()


def gather_first(plan, tokens, documents, front_weight, back_weight):
    shards, unit = plan.fsdp, plan.unit
    rows, length = tokens.shape[0], documents.shape[1]
    vmem, anywhere = pl.BlockSpec(memory_space=pltpu.VMEM), pl.BlockSpec(memory_space=pl.ANY)
    dma = pltpu.SemaphoreType.DMA
    return pl.pallas_call(
        functools.partial(gather_kernel, plan),
        in_specs=[vmem, vmem, anywhere, anywhere],
        out_specs=[anywhere] * 4,
        out_shape=[
            jax.ShapeDtypeStruct((shards, 2, rows, D), bf16),
            jax.ShapeDtypeStruct((1, length), f32),
            jax.ShapeDtypeStruct((D, 3 * unit), bf16),
            jax.ShapeDtypeStruct((unit, D), bf16),
        ],
        scratch_shapes=[
            pltpu.VMEM((D, unit), bf16),
            pltpu.VMEM((unit, D // shards), bf16),
            dma((shards,)),
            dma((shards,)),
            dma((shards,)),
            dma((shards,)),
            dma((3, shards)),
            dma((3,)),
            dma((shards,)),
            dma((shards,)),
            dma((shards,)),
            dma(()),
            dma((4,)),
        ],
        compiler_params=pltpu.CompilerParams(has_side_effects=True),
    )(tokens, documents, front_weight, back_weight)


def line_sum(plan, block, rising, falling, sends, gets, rows):
    planes, chunk = plan.planes, 64
    c, f, z, k, p = place_in_mesh()

    def copy(side, s, src):
        slots = (rising, falling)[side]
        return pltpu.make_async_remote_copy(
            src_ref=src,
            dst_ref=slots.at[s - 1],
            send_sem=sends.at[side, s - 1],
            recv_sem=gets.at[side, s - 1],
            device_id=(c + 2 - 4 * side, f),
            device_id_type=MESH,
        )

    def add(side, s, number):
        slots = (rising, falling)[side]
        term = block(number)

        def body(i, carry):
            at = pl.ds(pl.multiple_of(i * chunk, chunk), chunk)
            slots[s - 1, at, :] = (slots[s - 1, at, :].astype(f32) + term[at, :].astype(f32)).astype(bf16)
            return carry

        lax.fori_loop(0, rows // chunk, body, 0)

    def step(s):
        for side in range(2):
            place = z if side == 0 else planes - 1 - z
            number = planes - s + place
            number = number if side == 0 else planes - 1 - number

            @pl.when(place == 0)
            def _(side=side, number=number):
                copy(side, s, block(number)).start()

            if s > 1:

                @pl.when((place > 0) & (place < s) & (place < planes - 1))
                def _(side=side, number=number):
                    slots = (rising, falling)[side]
                    copy(side, s - 1, slots.at[s - 2]).wait_recv()
                    add(side, s - 1, number)
                    copy(side, s, slots.at[s - 2]).start()

    def finish(out):
        last = planes - 1
        for side in range(2):
            place = z if side == 0 else planes - 1 - z
            slots = (rising, falling)[side]

            @pl.when(place > 0)
            def _(side=side, slots=slots):
                copy(side, last, slots.at[last - 1]).wait_recv()

        mine = block(z)

        def total(ups, downs):
            def body(i, carry):
                at = pl.ds(pl.multiple_of(i * chunk, chunk), chunk)
                value = mine[at, :].astype(f32)
                if ups:
                    value = value + rising[last - 1, at, :].astype(f32)
                if downs:
                    value = value + falling[last - 1, at, :].astype(f32)
                out[at, :] = value.astype(out.dtype)
                return carry

            lax.fori_loop(0, rows // chunk, body, 0)

        @pl.when(z == 0)
        def _():
            total(False, True)

        @pl.when(z == planes - 1)
        def _():
            total(True, False)

        @pl.when((z > 0) & (z < planes - 1))
        def _():
            total(True, True)

        for side in range(2):
            place = z if side == 0 else planes - 1 - z
            slots = (rising, falling)[side]
            for s in range(1, planes):

                @pl.when((place < s) & (place < planes - 1))
                def _(side=side, slots=slots, s=s):
                    copy(side, s, slots.at[s - 1]).wait_send()

    return step, finish


def line_gather(plan, own, out, sends, gets, share_sends, share_gets, local, height):
    planes = plan.planes
    c, f, z, k, p = place_in_mesh()
    other = c + 1 - 2 * k

    def rows_of(plane, core):
        return out.at[pl.ds(pl.multiple_of((2 * plane + core) * height, height), height), :]

    def origin(side, s):
        return z - s if side == 0 else z + s

    def copy(side, s):
        plane = origin(side, s - 1)
        src = own if s == 1 else rows_of(plane, k)
        return pltpu.make_async_remote_copy(
            src_ref=src,
            dst_ref=rows_of(plane, k),
            send_sem=sends.at[side, s - 1],
            recv_sem=gets.at[side, s - 1],
            device_id=(c + 2 - 4 * side, f),
            device_id_type=MESH,
        )

    def arrival(side, s):
        here = rows_of(origin(side, s), k)
        return pltpu.make_async_remote_copy(
            src_ref=here,
            dst_ref=here,
            send_sem=sends.at[side, s - 1],
            recv_sem=gets.at[side, s - 1],
            device_id=(c + 2 - 4 * side, f),
            device_id_type=MESH,
        )

    def share(side, s, core):
        plane = origin(side, s)
        here = rows_of(plane, core)
        src = own if s == 0 else here
        return pltpu.make_async_remote_copy(
            src_ref=src,
            dst_ref=here,
            send_sem=share_sends.at[side, s],
            recv_sem=share_gets.at[side, s],
            device_id=(other, f),
            device_id_type=MESH,
        )

    keep = pltpu.make_async_copy(own, rows_of(z, k), local)

    def sends_at(side, s):
        place = z if side == 0 else planes - 1 - z
        return (place >= s - 1) & (place < planes - 1)

    def gets_at(side, s):
        place = z if side == 0 else planes - 1 - z
        return place >= s

    def take(s):
        for side in range(2):

            @pl.when(gets_at(side, s))
            def _(side=side):
                arrival(side, s).wait_recv()
                if s < planes - 1:

                    @pl.when(sends_at(side, s + 1))
                    def _():
                        copy(side, s + 1).start()

                share(side, s, k).start()

    def step(s):
        if s > 1:
            take(s - 1)
            return
        for side in range(2):

            @pl.when(sends_at(side, 1))
            def _(side=side):
                copy(side, 1).start()

        share(0, 0, k).start()
        keep.start()

    def finish():
        take(planes - 1)
        keep.wait()
        share(0, 0, k).wait_send()
        share(0, 0, 1 - k).wait_recv()
        for side in range(2):
            for s in range(1, planes):

                @pl.when(sends_at(side, s))
                def _(side=side, s=s):
                    copy(side, s).wait_send()

                @pl.when(gets_at(side, s))
                def _(side=side, s=s):
                    share(side, s, k).wait_send()
                    share(side, s, 1 - k).wait_recv()

    return step, finish


def back_owners(plan, src, out, send, recv, lsem):
    unit, ranks = plan.unit, plan.ranks
    c, f, z, k, p = place_in_mesh()

    def copy(j, owner, place):
        return pltpu.make_async_remote_copy(
            src_ref=src.at[pl.ds(j * unit, unit), :],
            dst_ref=out.at[pl.ds(place * unit, unit), :],
            send_sem=send.at[j],
            recv_sem=recv.at[place],
            device_id=(owner, z),
            device_id_type=MESH,
        )

    def local(j, place):
        return pltpu.make_async_copy(
            src.at[pl.ds(j * unit, unit), :], out.at[pl.ds(place * unit, unit), :], lsem.at[place]
        )

    blocks = [
        (rank, j, plan.back_units[rank][j] // 5, plan.back_units[rank][j] % 5)
        for rank in range(ranks)
        for j in range(5)
    ]

    def start():
        for rank, j, owner, place in blocks:

            @pl.when((p == rank) & ~((c == owner) & (f == z)))
            def _(j=j, owner=owner, place=place):
                copy(j, owner, place).start()

            @pl.when((p == rank) & (c == owner) & (f == z))
            def _(j=j, place=place):
                local(j, place).start()

    def finish():
        for rank, j, owner, place in blocks:

            @pl.when((p == rank) & ~((c == owner) & (f == z)))
            def _(j=j, owner=owner, place=place):
                copy(j, owner, place).wait_send()

            @pl.when((c == owner) & ~((p == rank) & (f == z)))
            def _(j=j, owner=owner, place=place):
                copy(j, owner, place).wait_recv()

            @pl.when((p == rank) & (c == owner) & (f == z))
            def _(j=j, place=place):
                local(j, place).wait()

    return start, finish


def front_owners(plan, src, out, send, recv, lsem):
    unit, ranks = plan.unit, plan.ranks
    c, f, z, k, p = place_in_mesh()
    height = src.shape[0] // 2
    moves, start_at = [], 0
    for slot, (units, wide) in enumerate(plan.slots):
        for rank in range(ranks):
            owner, place = units[rank] // plan.per_shard, units[rank] % plan.per_shard
            moves.append((slot, rank, owner, place, start_at, wide))
        start_at += wide

    def copy(slot, owner, place, begin, wide, half):
        return pltpu.make_async_remote_copy(
            src_ref=src.at[pl.ds(half * height, height), pl.ds(begin * unit, wide * unit)],
            dst_ref=out.at[:, pl.ds(place * unit, wide * unit)],
            send_sem=send.at[slot, half],
            recv_sem=recv.at[place],
            device_id=(2 * z + half, owner),
            device_id_type=MESH,
        )

    def local(place, begin, wide, half):
        return pltpu.make_async_copy(
            src.at[pl.ds(half * height, height), pl.ds(begin * unit, wide * unit)],
            out.at[:, pl.ds(place * unit, wide * unit)],
            lsem.at[place],
        )

    def start():
        for slot, rank, owner, place, begin, wide in moves:
            for half in range(2):
                if 2 * owner + half == rank:

                    @pl.when(p == rank)
                    def _(place=place, begin=begin, wide=wide, half=half):
                        local(place, begin, wide, half).start()

                else:

                    @pl.when(p == rank)
                    def _(slot=slot, owner=owner, place=place, begin=begin, wide=wide, half=half):
                        copy(slot, owner, place, begin, wide, half).start()

    def finish():
        for slot, rank, owner, place, begin, wide in moves:
            for half in range(2):
                if 2 * owner + half == rank:

                    @pl.when(p == rank)
                    def _(place=place, begin=begin, wide=wide, half=half):
                        local(place, begin, wide, half).wait()

                else:

                    @pl.when(p == rank)
                    def _(slot=slot, owner=owner, place=place, begin=begin, wide=wide, half=half):
                        copy(slot, owner, place, begin, wide, half).wait_send()

                    @pl.when(p == 2 * owner + half)
                    def _(slot=slot, owner=owner, place=place, begin=begin, wide=wide, half=half):
                        copy(slot, owner, place, begin, wide, half).wait_recv()

    return start, finish


VMEM_BLOCK = pl.BlockSpec(memory_space=pltpu.VMEM)
ANY_BLOCK = pl.BlockSpec(memory_space=pl.ANY)


def sum_scratch(plan, rows, columns):
    dma = pltpu.SemaphoreType.DMA
    steps = plan.planes - 1
    slots = pltpu.VMEM((steps, rows, columns), bf16)
    return [slots, slots, dma((2, steps)), dma((2, steps))]


def gather_scratch(plan):
    dma = pltpu.SemaphoreType.DMA
    return [dma((2, plan.planes - 1))] * 2 + [dma((2, plan.planes))] * 2 + [dma(())]


def busy(microseconds):
    return pl.CostEstimate(flops=int(microseconds * 900e6), transcendentals=0, bytes_accessed=0)


def back_sum_kernel(plan, width, src, out, *scratch):
    def block(i):
        return src.at[:, pl.ds(pl.multiple_of(i * width, 128), width)]

    step, finish = line_sum(plan, block, *scratch, src.shape[0])
    for s in range(1, plan.planes):
        step(s)
    finish(out)


def back_sums(plan, partial):
    rows, width = partial.shape[0], D // plan.planes
    return pl.pallas_call(
        functools.partial(back_sum_kernel, plan, width),
        in_specs=[VMEM_BLOCK],
        out_specs=VMEM_BLOCK,
        out_shape=jax.ShapeDtypeStruct((rows, width), bf16),
        scratch_shapes=sum_scratch(plan, rows, width),
        compiler_params=pltpu.CompilerParams(has_side_effects=True),
        cost_estimate=busy(90),
    )(partial)


def front_sum_kernel(plan, rows, src, back, out, owned, *scratch):
    start, done = back_owners(plan, back, owned, *scratch[:3])
    step, finish = line_sum(
        plan, lambda i: src.at[pl.ds(pl.multiple_of(i * rows, rows), rows), :], *scratch[3:], rows
    )
    step(1)
    start()
    for s in range(2, plan.planes):
        step(s)
    finish(out)
    done()


def front_sums(plan, partial, back_sum):
    dma = pltpu.SemaphoreType.DMA
    rows, width = partial.shape[0] // plan.planes, partial.shape[1]
    return pl.pallas_call(
        functools.partial(front_sum_kernel, plan, rows),
        in_specs=[VMEM_BLOCK, VMEM_BLOCK],
        out_specs=[VMEM_BLOCK, ANY_BLOCK],
        out_shape=[
            jax.ShapeDtypeStruct((rows, width), bf16),
            jax.ShapeDtypeStruct(back_sum.shape, bf16),
        ],
        scratch_shapes=[dma((5,))] * 3 + sum_scratch(plan, rows, width),
        compiler_params=pltpu.CompilerParams(has_side_effects=True),
        cost_estimate=busy(120),
    )(partial, back_sum)


def back_next_kernel(plan, own, src, out, owned, *scratch):
    start, done = front_owners(plan, src, owned, *scratch[:3])
    step, finish = line_gather(plan, own, out, *scratch[3:], own.shape[0])
    step(1)
    start()
    for s in range(2, plan.planes):
        step(s)
    finish()
    done()


def back_nexts(plan, own, front_sum):
    dma = pltpu.SemaphoreType.DMA
    return pl.pallas_call(
        functools.partial(back_next_kernel, plan),
        in_specs=[VMEM_BLOCK, VMEM_BLOCK],
        out_specs=[ANY_BLOCK, ANY_BLOCK],
        out_shape=[
            jax.ShapeDtypeStruct((2 * plan.planes * own.shape[0], own.shape[1]), bf16),
            jax.ShapeDtypeStruct((front_sum.shape[0] // 2, plan.per_shard * plan.unit), bf16),
        ],
        scratch_shapes=[dma((5, 2)), dma((plan.per_shard,)), dma((plan.per_shard,))] + gather_scratch(plan),
        compiler_params=pltpu.CompilerParams(has_side_effects=True),
        cost_estimate=busy(90),
    )(own, front_sum)


def front_next_kernel(plan, own, out, *scratch):
    step, finish = line_gather(plan, own, out, *scratch, own.shape[0])
    for s in range(1, plan.planes):
        step(s)
    finish()


def front_nexts(plan, own):
    return pl.pallas_call(
        functools.partial(front_next_kernel, plan),
        in_specs=[VMEM_BLOCK],
        out_specs=ANY_BLOCK,
        out_shape=jax.ShapeDtypeStruct((2 * plan.planes * own.shape[0], own.shape[1]), bf16),
        scratch_shapes=gather_scratch(plan),
        compiler_params=pltpu.CompilerParams(has_side_effects=True),
        cost_estimate=busy(120),
    )(own)


def gelu_parts(u):
    scale = np.float32(np.sqrt(2.0 / np.pi))
    square = u * u
    inner = scale * u * (1.0 + 0.044715 * square)
    t = jnp.tanh(inner)
    value = 0.5 * u * (1.0 + t)
    slope = 0.5 * (1.0 + t) + 0.5 * u * (1.0 - t * t) * scale * (1.0 + 3 * 0.044715 * square)
    return value, slope


def adam_update(weight, first, second, grad, rate, count_now, decay):
    first_new = beta_first * first + (1.0 - beta_first) * grad
    second_new = beta_second * second + (1.0 - beta_second) * grad * grad
    steps_float = count_now.astype(f32)
    first_fix = 1.0 - jnp.power(beta_first, steps_float)
    second_fix = 1.0 - jnp.power(beta_second, steps_float)
    change = first_new / first_fix / (jnp.sqrt(second_new / second_fix) + adam_eps) + decay * weight
    return (weight - rate * change, first_new, second_new)


def after(value, *others):
    return lax.optimization_barrier((value,) + others)[0]


def per_device(
    tokens,
    cotangent,
    doc_ids,
    block_order,
    front_weight,
    back_weight,
    front_master,
    back_master,
    front_first,
    back_first,
    front_second,
    back_second,
    vectors,
    vector_first,
    vector_second,
    learn_rates,
    adam_step,
    *,
    plan,
):
    planes, shards, ranks, unit = plan.planes, plan.fsdp, plan.ranks, plan.unit
    both = ("ctx", "fsdp")
    contract_last = (((1,), (1,)), ((), ()))
    contract_first = (((0,), (0,)), ((), ()))
    c_index, f = lax.axis_index("ctx"), lax.axis_index("fsdp")
    z, k = c_index // 2, c_index % 2
    p = 2 * f + k
    rows = tokens.shape[1]
    plane_rows = 2 * shards * rows
    share = 2 * rows

    bias_front = vectors[:IN_COLS].reshape(-1, unit)
    bias_back = vectors[IN_COLS : IN_COLS + D]
    norm_gain = vectors[IN_COLS + D : IN_COLS + 2 * D]
    norm_shift = vectors[IN_COLS + 2 * D :]

    swap_pairs = [(2 * i + j, 2 * i + 1 - j) for i in range(planes) for j in range(2)]

    def swap_core(value):
        return lax.ppermute(value, "ctx", swap_pairs)

    def to_shard(value, step):
        return lax.ppermute(value, "fsdp", [(i, i ^ step) for i in range(shards)])

    def to_plane(value, step):
        return lax.ppermute(
            value, "ctx", [(2 * i + j, 2 * (i ^ step) + j) for i in range(planes) for j in range(2)]
        )

    def gather_plane(value):
        mine = lax.all_gather(value, "fsdp")
        other = swap_core(mine)
        low = jnp.where(k == 0, mine, other)
        high = jnp.where(k == 0, other, mine)
        return jnp.stack([low, high], axis=1).reshape(plane_rows, D)

    def at(array, index):
        return lax.dynamic_index_in_dim(array, index, 0, keepdims=False)

    blocks = block_order.shape[0]
    block_tokens = doc_ids.shape[1] // blocks
    offsets = jnp.arange(block_tokens, dtype=jnp.int32)
    positions_all = (block_order[:, None] * block_tokens + offsets[None, :]).reshape(planes, share)
    own_positions = at(positions_all, z)
    plane_positions = jnp.tile(own_positions, shards)

    plane_tokens, documents, weight_qkv, back_attention = gather_first(
        plan, tokens[0], doc_ids.astype(f32), front_weight, back_weight
    )
    plane_tokens = plane_tokens.reshape(plane_rows, D)

    normed = (normalize(plane_tokens)[0] * norm_gain + norm_shift).astype(bf16)

    def slot_weight(slot, gate):
        units, wide = plan.slots[slot]
        width = wide * unit
        table = np.asarray(units)
        source, place = table // plan.per_shard, table % plan.per_shard
        total = None
        for one in plan.rounds[slot]:
            sends = np.zeros(ranks, np.int32)
            links = []
            for src, dst, core in one:
                sends[2 * src + core] = place[2 * dst + core]
                links += [
                    (plan.device(i, core, src), plan.device(i, core, dst)) for i in range(planes)
                ]
            start = after(pick(sends, p) * unit, gate)
            block = lax.dynamic_slice(front_weight, (0, start), (D, width))
            block = lax.ppermute(block, both, links)
            total = block if total is None else total + block
        local = source == np.arange(ranks) // 2
        start = pick(np.where(local, place, 0), p) * unit
        own = lax.dynamic_slice(front_weight, (0, start), (D, width))
        if total is None:
            return own
        if not local.any():
            return total
        return jnp.where(pick(local, p) > 0, own, total)

    gate = weight_qkv[0, 0]
    plane_grad = gather_plane(after(cotangent[0], gate))
    weight_up = jnp.concatenate([slot_weight(i, gate) for i in range(3, 5)], axis=1)

    def back_rows(rank):
        table = pick(plan.back_units, rank)
        return jnp.concatenate(
            [
                lax.dynamic_slice(back_weight, (table[j] * unit, 0), (2 * unit, D // shards))
                for j in (1, 3)
            ],
            axis=0,
        )

    col_width = D // shards
    back_up = jnp.zeros((4 * unit, D), bf16)
    for step in range(shards):
        piece = back_rows(after(2 * (f ^ step) + k, gate))
        if step:
            piece = to_shard(piece, step)
        back_up = lax.dynamic_update_slice(back_up, piece, (0, (f ^ step) * col_width))
    back_local = jnp.concatenate([back_attention, back_up], axis=0)

    unit_table = pick(plan.rank_units, p)
    bias_local = jnp.take(bias_front, unit_table, axis=0).reshape(-1)

    hidden = jnp.dot(normed, weight_qkv, preferred_element_type=f32) + bias_local[: 3 * unit]
    tables = rotation_tables(plane_positions, unit)
    query = rotate(hidden[:, :unit], tables).astype(bf16)
    key = rotate(hidden[:, unit : 2 * unit], tables).astype(bf16)
    qkv = jnp.concatenate([query, key, hidden[:, 2 * unit :].astype(bf16)], axis=1)

    def to_sequence(value):
        shaped = value.reshape(shards, share, -1)
        pieces = [at(shaped, z)]
        for step in range(1, planes):
            pieces.append(to_plane(at(shaped, z ^ step), step))
        return jnp.concatenate(pieces, axis=0)

    def to_plane_rows(value):
        shaped = value.reshape(planes, share, -1)
        pieces = [shaped[0]] + [to_plane(shaped[step], step) for step in range(1, planes)]
        stacked = jnp.stack(pieces)
        return jnp.concatenate([at(stacked, i ^ z) for i in range(planes)], axis=0)

    qkv_seq = to_sequence(qkv)

    attended_grad = lax.dot_general(
        plane_grad, back_attention, contract_last, preferred_element_type=f32
    ).astype(bf16)
    grad_seq = to_sequence(attended_grad)

    order = jnp.arange(planes, dtype=jnp.int32) ^ z
    seq_positions = jnp.take(positions_all, order, axis=0).reshape(-1)
    doc_row = documents[0].astype(jnp.int32)
    seq_documents = jnp.take(
        jnp.take(doc_row.reshape(blocks, block_tokens), block_order, axis=0).reshape(planes, share),
        order,
        axis=0,
    ).reshape(-1)
    attended, query_grad, key_grad, value_grad = attention(
        qkv_seq[:, :unit],
        qkv_seq[:, unit : 2 * unit],
        qkv_seq[:, 2 * unit :],
        grad_seq,
        seq_positions,
        seq_documents,
    )
    seq_tables = rotation_tables(seq_positions, unit)
    returned = to_plane_rows(
        jnp.concatenate(
            [
                attended,
                rotate_back(query_grad, seq_tables).astype(bf16),
                rotate_back(key_grad, seq_tables).astype(bf16),
                value_grad.astype(bf16),
            ],
            axis=1,
        )
    )

    up = jnp.dot(normed, weight_up, preferred_element_type=f32) + bias_local[3 * unit :]
    activation, slope = gelu_parts(up)
    mixed_grad = lax.dot_general(plane_grad, back_up, contract_last, preferred_element_type=f32)
    up_grad = (mixed_grad * slope).astype(bf16)
    mixed = jnp.concatenate([returned[:, :unit], activation.astype(bf16)], axis=1)
    hidden_grad = jnp.concatenate([returned[:, unit:], up_grad], axis=1)

    def sum_to_owner(value):
        shaped = value.reshape(shards, 2, rows, D)
        kept = lax.dynamic_index_in_dim(shaped, k, 1, keepdims=False)
        sent = lax.dynamic_index_in_dim(shaped, 1 - k, 1, keepdims=False).astype(bf16)
        summed = kept + swap_core(sent).astype(f32)
        total = at(summed, f)
        for step in range(1, shards):
            total = total + to_shard(at(summed, f ^ step).astype(bf16), step).astype(f32)
        return total

    projected = sum_to_owner(jnp.dot(mixed, back_local, preferred_element_type=f32))
    inputs = tokens[0].astype(f32)
    layer_out = (inputs + projected + bias_back).astype(bf16)[None]

    weight_local = jnp.concatenate([weight_qkv, weight_up], axis=1)
    normed_grad = sum_to_owner(
        lax.dot_general(hidden_grad, weight_local, contract_last, preferred_element_type=f32)
    )
    unscaled, factor = normalize(inputs)
    scaled = normed_grad * norm_gain
    input_grad = factor * (
        scaled
        - jnp.mean(scaled, axis=-1, keepdims=True)
        - unscaled * jnp.mean(scaled * unscaled, axis=-1, keepdims=True)
    )
    tokens_grad = (cotangent[0].astype(f32) + input_grad).astype(bf16)[None]

    back_partial = lax.dot_general(
        mixed, plane_grad, contract_first, preferred_element_type=f32
    ).astype(bf16)
    front_partial = lax.dot_general(
        normed, hidden_grad, contract_first, preferred_element_type=f32
    ).astype(bf16)
    back_sum = back_sums(plan, back_partial)
    front_sum, back_owned = front_sums(plan, front_partial, back_sum)
    back_grad = back_owned.astype(f32)
    back_new, back_first_new, back_second_new = adam_update(
        back_master, back_first, back_second, back_grad, learn_rates[1], adam_step[0], weight_decay
    )
    back_next, front_owned = back_nexts(plan, back_new.astype(bf16), front_sum)
    front_grad = front_owned.astype(f32)
    front_new, front_first_new, front_second_new = adam_update(
        front_master, front_first, front_second, front_grad, learn_rates[0], adam_step[0], weight_decay
    )
    front_next = front_nexts(plan, front_new.astype(bf16))

    def column_sums(value):
        ones = jnp.ones((8, value.shape[0]), bf16)
        return jnp.dot(ones, value, preferred_element_type=f32)[0]

    spread = (jnp.arange(7 * ranks)[:, None] == unit_table[None, :]).astype(f32)
    hidden_sum = column_sums(hidden_grad).reshape(7, unit)
    front_vector = jnp.sum(spread[:, :, None] * hidden_sum[None], axis=1).reshape(-1)
    vector_term = jnp.concatenate(
        [
            front_vector,
            column_sums(cotangent[0]),
            jnp.sum(normed_grad * unscaled, axis=0),
            jnp.sum(normed_grad, axis=0),
        ]
    )
    vector_grad = vector_term.reshape(-1, 128)
    vector_grad = vector_grad + swap_core(vector_grad)
    step = 1
    while step < shards:
        vector_grad = vector_grad + to_shard(vector_grad, step)
        vector_grad = vector_grad + to_plane(vector_grad, step)
        step *= 2
    vector_grad = vector_grad.reshape(-1)

    count_now = adam_step[0]
    vectors_new, vector_first_new, vector_second_new = adam_update(
        vectors, vector_first, vector_second, vector_grad, learn_rates[2], count_now, 0.0
    )

    return (
        layer_out,
        tokens_grad,
        front_grad,
        back_grad,
        vector_grad,
        front_new,
        back_new,
        vectors_new,
        front_first_new,
        back_first_new,
        vector_first_new,
        front_second_new,
        back_second_new,
        vector_second_new,
        front_next,
        back_next,
    )


def solution(mesh):
    plan = Layout(mesh.shape["ctx"], mesh.shape["fsdp"])
    tokens_spec = P("fsdp", "ctx", None)
    cols, owned, same = P(None, "fsdp"), P("ctx", "fsdp"), P()
    in_specs = (
        (tokens_spec, tokens_spec, P("fsdp", None), same, cols, cols)
        + (owned,) * 6
        + (same,) * 5
    )
    out_specs = (
        (tokens_spec, tokens_spec, owned, owned, same)
        + (owned, owned, same) * 3
        + (cols, cols)
    )
    return jax.shard_map(
        functools.partial(per_device, plan=plan),
        mesh=mesh,
        in_specs=in_specs,
        out_specs=out_specs,
        check_vma=False,
    )
```

```python
import functools

import jax
import jax.numpy as jnp
import numpy as np
from jax import lax
from jax.experimental import pallas as pl
from jax.experimental.pallas import tpu as pltpu
from jax.sharding import PartitionSpec as P

D = 2048
HEADS = 32
FF = 8192
ROT = 32
HEAD_DIM = 64
IN_COLS = 14336
BACK_ROWS = 10240

norm_eps = 1e-05
beta_first = 0.9
beta_second = 0.95
adam_eps = 1e-08
weight_decay = 0.1
masked_score = -1e30
bf16 = jnp.bfloat16
f32 = jnp.float32


class Layout:
    def __init__(self, ctx, fsdp):
        self.ctx, self.fsdp, self.planes, self.ranks = ctx, fsdp, ctx // 2, 2 * fsdp
        assert ctx % 2 == 0 and self.planes == fsdp
        self.unit = D // self.ranks
        self.per_shard = IN_COLS // self.unit // fsdp
        r = self.ranks
        first_up = 3 * r
        home = {f: [] for f in range(fsdp)}
        for g in range(first_up, 7 * r, 2):
            assert g // self.per_shard == (g + 1) // self.per_shard
            home[g // self.per_shard].append(g)
        pairs = {p: [None, None] for p in range(r)}
        for f in range(fsdp):
            if len(home[f]) >= 4:
                keep, home[f] = home[f][:4], home[f][4:]
                pairs[2 * f], pairs[2 * f + 1] = keep[:2], keep[2:]
            elif home[f]:
                keep, home[f] = home[f], []
                for i, g in enumerate(keep):
                    pairs[2 * f + i % 2][(i + i // 2) % 2] = g
        for s in range(2):
            for k in range(2):
                used = set()
                for f in range(fsdp):
                    p = 2 * f + k
                    if pairs[p][s] is not None:
                        continue
                    options = sorted(
                        (h for h in range(fsdp) if home[h]),
                        key=lambda h: (h in used, bin(h ^ f).count("1"), -len(home[h])),
                    )
                    used.add(options[0])
                    pairs[p][s] = home[options[0]].pop(0)
        self.pairs = pairs
        self.slots = [
            ([p for p in range(r)], 1),
            ([r + p for p in range(r)], 1),
            ([2 * r + p for p in range(r)], 1),
            ([pairs[p][0] for p in range(r)], 2),
            ([pairs[p][1] for p in range(r)], 2),
        ]
        self.rounds = []
        for units, _ in self.slots:
            rounds = []
            for k in range(2):
                for f in range(fsdp):
                    src = units[2 * f + k] // self.per_shard
                    if src == f:
                        continue
                    for one in rounds:
                        if all((src, k) != (a, c) for a, _, c in one):
                            one.append((src, f, k))
                            break
                    else:
                        rounds.append([(src, f, k)])
            self.rounds.append(rounds)
        self.rank_units = [
            [p, r + p, 2 * r + p, pairs[p][0], pairs[p][0] + 1, pairs[p][1], pairs[p][1] + 1]
            for p in range(r)
        ]
        self.back_units = [[p] + [g - 2 * r for g in self.rank_units[p][3:]] for p in range(r)]
        self.matchings = []
        left = {p: list(range(5)) for p in range(r)}
        own = lambda p, j: self.back_units[p][j] // 5
        for _ in range(5):
            match = {}

            def assign(p, seen):
                for j in left[p]:
                    c = own(p, j)
                    if c in seen:
                        continue
                    seen.add(c)
                    if c not in match or assign(match[c][0], seen):
                        match[c] = (p, j)
                        return True
                return False

            for p in range(r):
                assert assign(p, set())
            for c, (p, j) in match.items():
                left[p].remove(j)
            self.matchings.append(match)

    def device(self, z, k, f):
        return (2 * z + k) * self.fsdp + f


def pick(table, index):
    return jnp.asarray(np.asarray(table, np.int32))[index]


def normalize(values):
    values = values.astype(f32)
    centered = values - jnp.mean(values, axis=-1, keepdims=True)
    factor = lax.rsqrt(jnp.mean(centered * centered, axis=-1, keepdims=True) + norm_eps)
    return centered * factor, factor


def rotation_tables(positions, width):
    half = ROT // 2
    lane = np.arange(width) % HEAD_DIM
    frequency = jnp.power(
        10000.0, -2.0 * jnp.asarray(lane % half, f32) / ROT
    )
    angles = positions.astype(f32)[:, None] * frequency[None, :]
    rotated = jnp.asarray(lane < ROT)
    lower = jnp.asarray(lane < half)
    cosine = jnp.where(rotated, jnp.cos(angles), 1.0)
    sine = jnp.where(rotated, jnp.sin(angles), 0.0)
    return cosine, jnp.where(lower, -sine, 0.0), jnp.where(lower, 0.0, sine)


def rotate(values, tables):
    half = ROT // 2
    cosine, from_above, from_below = tables
    return (
        values * cosine
        + jnp.roll(values, -half, axis=1) * from_above
        + jnp.roll(values, half, axis=1) * from_below
    )


def rotate_back(values, tables):
    half = ROT // 2
    cosine, from_above, from_below = tables
    return (
        values * cosine
        + jnp.roll(values * from_above, half, axis=1)
        + jnp.roll(values * from_below, -half, axis=1)
    )


def attention_kernel(
    q_ref, k_ref, v_ref, g_ref, pos_q, pos_k, seg_q, seg_k, att_ref, dq_ref, dk_ref, dv_ref
):
    scale = HEAD_DIM ** (-0.5)
    width = q_ref.shape[1]

    @pl.when(pl.program_id(0) == 0)
    def _():
        dk_ref[...] = jnp.zeros_like(dk_ref)
        dv_ref[...] = jnp.zeros_like(dv_ref)

    allowed = (pos_k[...] <= pos_q[...]) & (seg_k[...] == seg_q[...])
    bias = jnp.where(allowed, 0.0, masked_score)
    last = (((1,), (1,)), ((), ()))
    first = (((0,), (0,)), ((), ()))
    for head in range(width // HEAD_DIM):
        cols = slice(head * HEAD_DIM, (head + 1) * HEAD_DIM)
        q, g = q_ref[:, cols], g_ref[:, cols]
        k, v = k_ref[:, cols], v_ref[:, cols]
        scores = lax.dot_general(q, k, last, preferred_element_type=f32) * scale + bias
        weights = jnp.exp(scores - jnp.max(scores, axis=1, keepdims=True))
        probs = weights * (1.0 / jnp.sum(weights, axis=1, keepdims=True))
        probs_low = probs.astype(bf16)
        out = jnp.dot(probs_low, v, preferred_element_type=f32)
        att_ref[:, cols] = out.astype(bf16)
        prob_grad = lax.dot_general(g, v, last, preferred_element_type=f32)
        delta = jnp.sum(g.astype(f32) * out, axis=1, keepdims=True)
        score_grad = (probs * (prob_grad - delta)).astype(bf16)
        dq_ref[:, cols] = jnp.dot(score_grad, k, preferred_element_type=f32) * scale
        dk_ref[:, cols] += lax.dot_general(score_grad, q, first, preferred_element_type=f32) * scale
        dv_ref[:, cols] += lax.dot_general(probs_low, g, first, preferred_element_type=f32)


def attention(query, key, value, grad, positions, segments):
    length, width = query.shape
    block = 256
    rows = pl.BlockSpec((block, width), lambda i: (i, 0))
    whole = pl.BlockSpec((length, width), lambda i: (0, 0))
    column = pl.BlockSpec((block, 1), lambda i: (i, 0))
    line = pl.BlockSpec((1, length), lambda i: (0, 0))
    return pl.pallas_call(
        attention_kernel,
        grid=(length // block,),
        in_specs=[rows, whole, whole, rows, column, line, column, line],
        out_specs=[rows, rows, whole, whole],
        out_shape=[
            jax.ShapeDtypeStruct((length, width), bf16),
            jax.ShapeDtypeStruct((length, width), f32),
            jax.ShapeDtypeStruct((length, width), f32),
            jax.ShapeDtypeStruct((length, width), f32),
        ],
        cost_estimate=pl.CostEstimate(
            flops=14 * length * length * width,
            transcendentals=length * length * width // HEAD_DIM,
            bytes_accessed=20 * length * width,
        ),
    )(query, key, value, grad, positions[:, None], positions[None], segments[:, None], segments[None])


MESH = pl.DeviceIdType.MESH


VMEM_BLOCK = pl.BlockSpec(memory_space=pltpu.VMEM)
ANY_BLOCK = pl.BlockSpec(memory_space=pl.ANY)


def busy(microseconds):
    return pl.CostEstimate(flops=int(microseconds * 900e6), transcendentals=0, bytes_accessed=0)


def place_in_mesh():
    c, f = lax.axis_index("ctx"), lax.axis_index("fsdp")
    z, k = lax.div(c, 2), lax.rem(c, 2)
    return c, f, z, k, 2 * f + k


def bounce(source, buffer, target, sem):
    one = pltpu.make_async_copy(source, buffer, sem)
    one.start()
    one.wait()
    two = pltpu.make_async_copy(buffer, target, sem)
    two.start()
    two.wait()


def gather_kernel(
    plan, tok, cot, doc, front, back, tok_out, cot_out, doc_out, w_out, b_out,
    w_buf, b_buf, tsend, trecv, csend, crecv, wsend, wrecv, bsend, brecv, dsend, drecv, lsem,
):
    shards, unit, ranks = plan.fsdp, plan.unit, plan.ranks
    c, f, z, k, p = place_in_mesh()
    other = c + 1 - 2 * k
    width = D // shards
    both = ((tok, tok_out), (cot, cot_out))

    def cols(block):
        return pl.ds(pl.multiple_of(block * width, 128), width)

    def remote(src, dst, send, recv, device):
        return pltpu.make_async_remote_copy(
            src_ref=src, dst_ref=dst, send_sem=send, recv_sem=recv, device_id=device, device_id_type=MESH
        )

    def peer(step):
        return lax.rem(f + step, shards)

    def giver(step):
        return lax.rem(f + shards - step, shards)

    def send_tokens(n, step):
        src, out = both[n]
        return remote(src, out.at[f, k], tsend.at[n, step], trecv.at[n, step], (c, peer(step)))

    def get_tokens(n, step):
        here = both[n][1].at[giver(step), k]
        return remote(here, here, tsend.at[n, step], trecv.at[n, step], (c, peer(step)))

    def share(n, step):
        src, out = both[n]
        here = out.at[giver(step), k]
        return remote(src if step == 0 else here, here, csend.at[n, step], crecv.at[n, step], (other, f))

    def get_share(n, step):
        here = both[n][1].at[giver(step), 1 - k]
        return remote(here, here, csend.at[n, step], crecv.at[n, step], (other, f))

    def rows_of(dst):
        return pl.ds(pl.multiple_of((2 * dst + k) * unit, unit), unit)

    def send_back(step):
        return remote(
            back.at[rows_of(peer(step)), :], b_out.at[:, cols(f)], bsend.at[step], brecv.at[step], (c, peer(step))
        )

    def get_back(step):
        here = b_out.at[:, cols(giver(step))]
        return remote(here, here, bsend.at[step], brecv.at[step], (c, peer(step)))

    def send_doc(step):
        return remote(doc, doc_out, dsend.at[step], drecv, (c, peer(step)))

    start_weights, finish_weights = weight_moves(plan, range(3), front, w_out, w_buf, wsend, wrecv, lsem.at[2])
    own = [pltpu.make_async_copy(src, out.at[f, k], lsem.at[4 * n]) for n, (src, out) in enumerate(both)]
    own_doc = pltpu.make_async_copy(doc, doc_out, lsem.at[1])
    for n in range(2):
        for step in range(1, shards):
            send_tokens(n, step).start()
        share(n, 0).start()
        own[n].start()
    for step in range(1, shards):
        send_back(step).start()

    @pl.when(f == z)
    def _():
        own_doc.start()
        for step in range(1, shards):
            send_doc(step).start()

    start_weights()
    for n in range(2):
        for step in range(1, shards):
            get_tokens(n, step).wait_recv()
            share(n, step).start()
    bounce(back.at[rows_of(f), :], b_buf, b_out.at[:, cols(f)], lsem.at[3])
    for n in range(2):
        own[n].wait()

    @pl.when(f == z)
    def _():
        own_doc.wait()
        for step in range(1, shards):
            send_doc(step).wait_send()

    @pl.when(f != z)
    def _():
        send_doc(1).wait_recv()

    for n in range(2):
        for step in range(shards):
            get_share(n, step).wait_recv()
            share(n, step).wait_send()
        for step in range(1, shards):
            send_tokens(n, step).wait_send()
    for step in range(1, shards):
        send_back(step).wait_send()
        get_back(step).wait_recv()
    finish_weights()


def moves_between(moves, device_of):
    c, f, z, k, p = place_in_mesh()

    def remote(move):
        src, dst, source, target, send, recv, _, _ = move
        return pltpu.make_async_remote_copy(
            src_ref=source, dst_ref=target, send_sem=send, recv_sem=recv, device_id=device_of(c, dst), device_id_type=MESH
        )

    def start():
        for move in moves:
            if move[0] != move[1]:

                @pl.when(p == move[0])
                def _(move=move):
                    remote(move).start()

        for move in moves:
            if move[0] == move[1]:

                @pl.when(p == move[0])
                def _(move=move):
                    bounce(move[2], move[6], move[3], move[7])

    def finish():
        for move in moves:
            if move[0] != move[1]:

                @pl.when(p == move[0])
                def _(move=move):
                    remote(move).wait_send()

                @pl.when(p == move[1])
                def _(move=move):
                    remote(move).wait_recv()

    return start, finish


def weight_moves(plan, slots, front, out, buffer, send, recv, local):
    unit, moves, begin = plan.unit, [], 0
    for number, slot in enumerate(slots):
        units, wide = plan.slots[slot]
        for dst in range(plan.ranks):
            src, at = units[dst] // plan.per_shard, units[dst] % plan.per_shard
            moves.append(
                (
                    2 * src + dst % 2,
                    dst,
                    front.at[:, pl.ds(at * unit, wide * unit)],
                    out.at[:, pl.ds(begin * unit, wide * unit)],
                    send.at[number, dst // 2],
                    recv.at[number],
                    buffer,
                    local,
                )
            )
        begin += wide
    return moves_between(moves, lambda c, dst: (c, dst // 2))


def back_moves(plan, back, out, buffer, send, recv, local):
    unit, width, moves = plan.unit, D // plan.fsdp, []
    for dst in range(plan.ranks):
        for src in range(plan.fsdp):
            for number in range(2):
                row = plan.back_units[dst][1 + 2 * number]
                moves.append(
                    (
                        2 * src + dst % 2,
                        dst,
                        back.at[pl.ds(row * unit, 2 * unit), :],
                        out.at[pl.ds(2 * number * unit, 2 * unit), pl.ds(src * width, width)],
                        send.at[number, dst // 2],
                        recv.at[number, src],
                        buffer,
                        local,
                    )
                )
    return moves_between(moves, lambda c, dst: (c, dst // 2))


def line_exchange(plan, src, out, send, recv, local):
    planes = plan.planes
    c, f, z, k, p = place_in_mesh()

    def copy(step):
        to = lax.rem(z + step, planes)
        return pltpu.make_async_remote_copy(
            src_ref=src.at[to],
            dst_ref=out.at[z],
            send_sem=send.at[step],
            recv_sem=recv.at[step],
            device_id=(2 * to + k, f),
            device_id_type=MESH,
        )

    def arrival(step):
        here = out.at[lax.rem(z + planes - step, planes)]
        return pltpu.make_async_remote_copy(
            src_ref=here,
            dst_ref=here,
            send_sem=send.at[step],
            recv_sem=recv.at[step],
            device_id=(2 * lax.rem(z + step, planes) + k, f),
            device_id_type=MESH,
        )

    keep = pltpu.make_async_copy(src.at[z], out.at[z], local)

    def start():
        for step in range(planes - 1, 0, -1):
            copy(step).start()
        keep.start()

    def finish():
        keep.wait()
        for step in range(1, planes):
            copy(step).wait_send()
            arrival(step).wait_recv()

    return start, finish


def gather_first(plan, tokens, cotangent, documents, front_weight, back_weight):
    shards, unit = plan.fsdp, plan.unit
    rows, length = tokens.shape[0], documents.shape[1]
    dma = pltpu.SemaphoreType.DMA
    return pl.pallas_call(
        functools.partial(gather_kernel, plan),
        in_specs=[VMEM_BLOCK] * 3 + [ANY_BLOCK] * 2,
        out_specs=[ANY_BLOCK] * 5,
        out_shape=[
            jax.ShapeDtypeStruct((shards, 2, rows, D), bf16),
            jax.ShapeDtypeStruct((shards, 2, rows, D), bf16),
            jax.ShapeDtypeStruct((1, length), f32),
            jax.ShapeDtypeStruct((D, 3 * unit), bf16),
            jax.ShapeDtypeStruct((unit, D), bf16),
        ],
        scratch_shapes=[
            pltpu.VMEM((D, unit), bf16),
            pltpu.VMEM((unit, D // shards), bf16),
            dma((2, shards)),
            dma((2, shards)),
            dma((2, shards)),
            dma((2, shards)),
            dma((3, shards)),
            dma((3,)),
            dma((shards,)),
            dma((shards,)),
            dma((shards,)),
            dma(()),
            dma((5,)),
        ],
        compiler_params=pltpu.CompilerParams(has_side_effects=True),
        cost_estimate=busy(130),
    )(tokens, cotangent, documents, front_weight, back_weight)


def exchange_kernel(plan, make, src, weight, out, w_out, buffer, send, recv, local, wsend, wrecv):
    start, finish = line_exchange(plan, src, out, send, recv, local.at[0])
    start_weights, finish_weights = make(weight, w_out, buffer, wsend, wrecv, local.at[1])
    start()
    start_weights()
    finish()
    finish_weights()


def exchange_with(plan, values, weight, moves, shape, buffer, recv_shape):
    dma = pltpu.SemaphoreType.DMA
    return pl.pallas_call(
        functools.partial(exchange_kernel, plan, moves),
        in_specs=[VMEM_BLOCK, ANY_BLOCK],
        out_specs=[ANY_BLOCK, ANY_BLOCK],
        out_shape=[jax.ShapeDtypeStruct(values.shape, bf16), jax.ShapeDtypeStruct(shape, bf16)],
        scratch_shapes=[
            pltpu.VMEM(buffer, bf16),
            dma((plan.planes,)),
            dma((plan.planes,)),
            dma((2,)),
            dma((2, plan.fsdp)),
            dma(recv_shape),
        ],
        compiler_params=pltpu.CompilerParams(has_side_effects=True),
        cost_estimate=busy(50),
    )(values, weight)


def line_sum(plan, block, rising, falling, sends, gets, rows):
    planes, chunk = plan.planes, 64
    c, f, z, k, p = place_in_mesh()

    def copy(side, s, src):
        slots = (rising, falling)[side]
        return pltpu.make_async_remote_copy(
            src_ref=src,
            dst_ref=slots.at[s - 1],
            send_sem=sends.at[side, s - 1],
            recv_sem=gets.at[side, s - 1],
            device_id=(c + 2 - 4 * side, f),
            device_id_type=MESH,
        )

    def add(side, s, number):
        slots = (rising, falling)[side]
        term = block(number)

        def body(i, carry):
            at = pl.ds(pl.multiple_of(i * chunk, chunk), chunk)
            slots[s - 1, at, :] = (slots[s - 1, at, :].astype(f32) + term[at, :].astype(f32)).astype(bf16)
            return carry

        lax.fori_loop(0, rows // chunk, body, 0)

    def step(s):
        for side in range(2):
            place = z if side == 0 else planes - 1 - z
            number = planes - s + place
            number = number if side == 0 else planes - 1 - number

            @pl.when(place == 0)
            def _(side=side, number=number):
                copy(side, s, block(number)).start()

            if s > 1:

                @pl.when((place > 0) & (place < s) & (place < planes - 1))
                def _(side=side, number=number):
                    slots = (rising, falling)[side]
                    copy(side, s - 1, slots.at[s - 2]).wait_recv()
                    add(side, s - 1, number)
                    copy(side, s, slots.at[s - 2]).start()

    def finish(out):
        last = planes - 1
        for side in range(2):
            place = z if side == 0 else planes - 1 - z
            slots = (rising, falling)[side]

            @pl.when(place > 0)
            def _(side=side, slots=slots):
                copy(side, last, slots.at[last - 1]).wait_recv()

        mine = block(z)

        def total(ups, downs):
            def body(i, carry):
                at = pl.ds(pl.multiple_of(i * chunk, chunk), chunk)
                value = mine[at, :].astype(f32)
                if ups:
                    value = value + rising[last - 1, at, :].astype(f32)
                if downs:
                    value = value + falling[last - 1, at, :].astype(f32)
                out[at, :] = value.astype(out.dtype)
                return carry

            lax.fori_loop(0, rows // chunk, body, 0)

        @pl.when(z == 0)
        def _():
            total(False, True)

        @pl.when(z == planes - 1)
        def _():
            total(True, False)

        @pl.when((z > 0) & (z < planes - 1))
        def _():
            total(True, True)

        for side in range(2):
            place = z if side == 0 else planes - 1 - z
            slots = (rising, falling)[side]
            for s in range(1, planes):

                @pl.when((place < s) & (place < planes - 1))
                def _(side=side, slots=slots, s=s):
                    copy(side, s, slots.at[s - 1]).wait_send()

    return step, finish


def line_gather(plan, own, out, sends, gets, share_sends, share_gets, local, height):
    planes = plan.planes
    c, f, z, k, p = place_in_mesh()
    other = c + 1 - 2 * k

    def rows_of(plane, core):
        return out.at[pl.ds(pl.multiple_of((2 * plane + core) * height, height), height), :]

    def origin(side, s):
        return z - s if side == 0 else z + s

    def copy(side, s):
        plane = origin(side, s - 1)
        src = own if s == 1 else rows_of(plane, k)
        return pltpu.make_async_remote_copy(
            src_ref=src,
            dst_ref=rows_of(plane, k),
            send_sem=sends.at[side, s - 1],
            recv_sem=gets.at[side, s - 1],
            device_id=(c + 2 - 4 * side, f),
            device_id_type=MESH,
        )

    def arrival(side, s):
        here = rows_of(origin(side, s), k)
        return pltpu.make_async_remote_copy(
            src_ref=here,
            dst_ref=here,
            send_sem=sends.at[side, s - 1],
            recv_sem=gets.at[side, s - 1],
            device_id=(c + 2 - 4 * side, f),
            device_id_type=MESH,
        )

    def share(side, s, core):
        plane = origin(side, s)
        here = rows_of(plane, core)
        src = own if s == 0 else here
        return pltpu.make_async_remote_copy(
            src_ref=src,
            dst_ref=here,
            send_sem=share_sends.at[side, s],
            recv_sem=share_gets.at[side, s],
            device_id=(other, f),
            device_id_type=MESH,
        )

    keep = pltpu.make_async_copy(own, rows_of(z, k), local)

    def sends_at(side, s):
        place = z if side == 0 else planes - 1 - z
        return (place >= s - 1) & (place < planes - 1)

    def gets_at(side, s):
        place = z if side == 0 else planes - 1 - z
        return place >= s

    def take(s):
        for side in range(2):

            @pl.when(gets_at(side, s))
            def _(side=side):
                arrival(side, s).wait_recv()
                if s < planes - 1:

                    @pl.when(sends_at(side, s + 1))
                    def _():
                        copy(side, s + 1).start()

                share(side, s, k).start()

    def step(s):
        if s > 1:
            take(s - 1)
            return
        for side in range(2):

            @pl.when(sends_at(side, 1))
            def _(side=side):
                copy(side, 1).start()

        share(0, 0, k).start()
        keep.start()

    def finish():
        take(planes - 1)
        keep.wait()
        share(0, 0, k).wait_send()
        share(0, 0, 1 - k).wait_recv()
        for side in range(2):
            for s in range(1, planes):

                @pl.when(sends_at(side, s))
                def _(side=side, s=s):
                    copy(side, s).wait_send()

                @pl.when(gets_at(side, s))
                def _(side=side, s=s):
                    share(side, s, k).wait_send()
                    share(side, s, 1 - k).wait_recv()

    return step, finish


def back_owners(plan, src, out, send, recv, lsem):
    unit, ranks = plan.unit, plan.ranks
    c, f, z, k, p = place_in_mesh()

    def copy(j, owner, place):
        return pltpu.make_async_remote_copy(
            src_ref=src.at[pl.ds(j * unit, unit), :],
            dst_ref=out.at[pl.ds(place * unit, unit), :],
            send_sem=send.at[j],
            recv_sem=recv.at[place],
            device_id=(owner, z),
            device_id_type=MESH,
        )

    def local(j, place):
        return pltpu.make_async_copy(
            src.at[pl.ds(j * unit, unit), :], out.at[pl.ds(place * unit, unit), :], lsem.at[place]
        )

    blocks = [
        (rank, j, plan.back_units[rank][j] // 5, plan.back_units[rank][j] % 5)
        for rank in range(ranks)
        for j in range(5)
    ]

    def start():
        for rank, j, owner, place in blocks:

            @pl.when((p == rank) & ~((c == owner) & (f == z)))
            def _(j=j, owner=owner, place=place):
                copy(j, owner, place).start()

            @pl.when((p == rank) & (c == owner) & (f == z))
            def _(j=j, place=place):
                local(j, place).start()

    def finish():
        for rank, j, owner, place in blocks:

            @pl.when((p == rank) & ~((c == owner) & (f == z)))
            def _(j=j, owner=owner, place=place):
                copy(j, owner, place).wait_send()

            @pl.when((c == owner) & ~((p == rank) & (f == z)))
            def _(j=j, owner=owner, place=place):
                copy(j, owner, place).wait_recv()

            @pl.when((p == rank) & (c == owner) & (f == z))
            def _(j=j, place=place):
                local(j, place).wait()

    return start, finish


def front_owners(plan, src, out, send, recv, lsem):
    unit, ranks = plan.unit, plan.ranks
    c, f, z, k, p = place_in_mesh()
    height = src.shape[0] // 2
    moves, start_at = [], 0
    for slot, (units, wide) in enumerate(plan.slots):
        for rank in range(ranks):
            owner, place = units[rank] // plan.per_shard, units[rank] % plan.per_shard
            moves.append((slot, rank, owner, place, start_at, wide))
        start_at += wide

    def copy(slot, owner, place, begin, wide, half):
        return pltpu.make_async_remote_copy(
            src_ref=src.at[pl.ds(half * height, height), pl.ds(begin * unit, wide * unit)],
            dst_ref=out.at[:, pl.ds(place * unit, wide * unit)],
            send_sem=send.at[slot, half],
            recv_sem=recv.at[place],
            device_id=(2 * z + half, owner),
            device_id_type=MESH,
        )

    def local(place, begin, wide, half):
        return pltpu.make_async_copy(
            src.at[pl.ds(half * height, height), pl.ds(begin * unit, wide * unit)],
            out.at[:, pl.ds(place * unit, wide * unit)],
            lsem.at[place],
        )

    def start():
        for slot, rank, owner, place, begin, wide in moves:
            for half in range(2):
                if 2 * owner + half == rank:

                    @pl.when(p == rank)
                    def _(place=place, begin=begin, wide=wide, half=half):
                        local(place, begin, wide, half).start()

                else:

                    @pl.when(p == rank)
                    def _(slot=slot, owner=owner, place=place, begin=begin, wide=wide, half=half):
                        copy(slot, owner, place, begin, wide, half).start()

    def finish():
        for slot, rank, owner, place, begin, wide in moves:
            for half in range(2):
                if 2 * owner + half == rank:

                    @pl.when(p == rank)
                    def _(place=place, begin=begin, wide=wide, half=half):
                        local(place, begin, wide, half).wait()

                else:

                    @pl.when(p == rank)
                    def _(slot=slot, owner=owner, place=place, begin=begin, wide=wide, half=half):
                        copy(slot, owner, place, begin, wide, half).wait_send()

                    @pl.when(p == 2 * owner + half)
                    def _(slot=slot, owner=owner, place=place, begin=begin, wide=wide, half=half):
                        copy(slot, owner, place, begin, wide, half).wait_recv()

    return start, finish


def sum_scratch(plan, rows, columns):
    dma = pltpu.SemaphoreType.DMA
    steps = plan.planes - 1
    slots = pltpu.VMEM((steps, rows, columns), bf16)
    return [slots, slots, dma((2, steps)), dma((2, steps))]


def gather_scratch(plan):
    dma = pltpu.SemaphoreType.DMA
    return [dma((2, plan.planes - 1))] * 2 + [dma((2, plan.planes))] * 2 + [dma(())]


def back_sum_kernel(plan, width, src, out, *scratch):
    def block(i):
        return src.at[:, pl.ds(pl.multiple_of(i * width, 128), width)]

    step, finish = line_sum(plan, block, *scratch, src.shape[0])
    for s in range(1, plan.planes):
        step(s)
    finish(out)


def back_sums(plan, partial):
    rows, width = partial.shape[0], D // plan.planes
    return pl.pallas_call(
        functools.partial(back_sum_kernel, plan, width),
        in_specs=[VMEM_BLOCK],
        out_specs=VMEM_BLOCK,
        out_shape=jax.ShapeDtypeStruct((rows, width), bf16),
        scratch_shapes=sum_scratch(plan, rows, width),
        compiler_params=pltpu.CompilerParams(has_side_effects=True),
        cost_estimate=busy(90),
    )(partial)


def front_sum_kernel(plan, rows, src, back, out, owned, *scratch):
    start, done = back_owners(plan, back, owned, *scratch[:3])
    step, finish = line_sum(
        plan, lambda i: src.at[pl.ds(pl.multiple_of(i * rows, rows), rows), :], *scratch[3:], rows
    )
    step(1)
    start()
    for s in range(2, plan.planes):
        step(s)
    finish(out)
    done()


def front_sums(plan, partial, back_sum):
    dma = pltpu.SemaphoreType.DMA
    rows, width = partial.shape[0] // plan.planes, partial.shape[1]
    return pl.pallas_call(
        functools.partial(front_sum_kernel, plan, rows),
        in_specs=[VMEM_BLOCK, VMEM_BLOCK],
        out_specs=[VMEM_BLOCK, ANY_BLOCK],
        out_shape=[
            jax.ShapeDtypeStruct((rows, width), bf16),
            jax.ShapeDtypeStruct(back_sum.shape, bf16),
        ],
        scratch_shapes=[dma((5,))] * 3 + sum_scratch(plan, rows, width),
        compiler_params=pltpu.CompilerParams(has_side_effects=True),
        cost_estimate=busy(120),
    )(partial, back_sum)


def back_next_kernel(plan, own, src, out, owned, *scratch):
    start, done = front_owners(plan, src, owned, *scratch[:3])
    step, finish = line_gather(plan, own, out, *scratch[3:], own.shape[0])
    step(1)
    start()
    for s in range(2, plan.planes):
        step(s)
    finish()
    done()


def back_nexts(plan, own, front_sum):
    dma = pltpu.SemaphoreType.DMA
    return pl.pallas_call(
        functools.partial(back_next_kernel, plan),
        in_specs=[VMEM_BLOCK, VMEM_BLOCK],
        out_specs=[ANY_BLOCK, ANY_BLOCK],
        out_shape=[
            jax.ShapeDtypeStruct((2 * plan.planes * own.shape[0], own.shape[1]), bf16),
            jax.ShapeDtypeStruct((front_sum.shape[0] // 2, plan.per_shard * plan.unit), bf16),
        ],
        scratch_shapes=[dma((5, 2)), dma((plan.per_shard,)), dma((plan.per_shard,))] + gather_scratch(plan),
        compiler_params=pltpu.CompilerParams(has_side_effects=True),
        cost_estimate=busy(90),
    )(own, front_sum)


def vector_sum(plan, own, out, terms, sums, send, recv):
    planes, ranks = plan.planes, plan.ranks
    c, f, z, k, p = place_in_mesh()

    def in_plane(step, target):
        to = lax.rem(p + step, ranks)
        return pltpu.make_async_remote_copy(
            src_ref=own,
            dst_ref=terms.at[target],
            send_sem=send.at[step],
            recv_sem=recv.at[step],
            device_id=(2 * z + lax.rem(to, 2), lax.div(to, 2)),
            device_id_type=MESH,
        )

    def over_planes(step, target):
        to = lax.rem(z + step, planes)
        return pltpu.make_async_remote_copy(
            src_ref=out,
            dst_ref=sums.at[target],
            send_sem=send.at[ranks + step],
            recv_sem=recv.at[ranks + step],
            device_id=(2 * to + k, f),
            device_id_type=MESH,
        )

    def start():
        for step in range(1, ranks):
            in_plane(step, p).start()
        terms[p] = own[...]

    def middle():
        for step in range(1, ranks):
            in_plane(step, lax.rem(p + ranks - step, ranks)).wait_recv()
        total = terms[0]
        for rank in range(1, ranks):
            total = total + terms[rank]
        out[...] = total
        sums[z] = total
        for step in range(1, planes):
            over_planes(step, z).start()

    def finish():
        for step in range(1, ranks):
            in_plane(step, p).wait_send()
        for step in range(1, planes):
            over_planes(step, z).wait_send()
            over_planes(step, lax.rem(z + planes - step, planes)).wait_recv()
        total = sums[0]
        for plane in range(1, planes):
            total = total + sums[plane]
        out[...] = total

    return start, middle, finish


def front_next_kernel(plan, own, vector, out, vector_out, terms, sums, vsend, vrecv, *scratch):
    begin, middle, end = vector_sum(plan, vector, vector_out, terms, sums, vsend, vrecv)
    step, finish = line_gather(plan, own, out, *scratch, own.shape[0])
    begin()
    step(1)
    middle()
    for s in range(2, plan.planes):
        step(s)
    finish()
    end()


def front_nexts(plan, own, vector):
    dma = pltpu.SemaphoreType.DMA
    return pl.pallas_call(
        functools.partial(front_next_kernel, plan),
        in_specs=[VMEM_BLOCK, VMEM_BLOCK],
        out_specs=[ANY_BLOCK, VMEM_BLOCK],
        out_shape=[
            jax.ShapeDtypeStruct((2 * plan.planes * own.shape[0], own.shape[1]), bf16),
            jax.ShapeDtypeStruct(vector.shape, f32),
        ],
        scratch_shapes=[
            pltpu.VMEM((plan.ranks,) + vector.shape, f32),
            pltpu.VMEM((plan.planes,) + vector.shape, f32),
            dma((plan.ranks + plan.planes,)),
            dma((plan.ranks + plan.planes,)),
        ]
        + gather_scratch(plan),
        compiler_params=pltpu.CompilerParams(has_side_effects=True),
        cost_estimate=busy(120),
    )(own, vector)


def gelu_parts(u):
    scale = np.float32(np.sqrt(2.0 / np.pi))
    square = u * u
    inner = scale * u * (1.0 + 0.044715 * square)
    t = jnp.tanh(inner)
    value = 0.5 * u * (1.0 + t)
    slope = 0.5 * (1.0 + t) + 0.5 * u * (1.0 - t * t) * scale * (1.0 + 3 * 0.044715 * square)
    return value, slope


def adam_update(weight, first, second, grad, rate, count_now, decay):
    first_new = beta_first * first + (1.0 - beta_first) * grad
    second_new = beta_second * second + (1.0 - beta_second) * grad * grad
    steps_float = count_now.astype(f32)
    first_fix = 1.0 - jnp.power(beta_first, steps_float)
    second_fix = 1.0 - jnp.power(beta_second, steps_float)
    change = first_new / first_fix / (jnp.sqrt(second_new / second_fix) + adam_eps) + decay * weight
    return (weight - rate * change, first_new, second_new)


def after(value, *others):
    return lax.optimization_barrier((value,) + others)[0]


def per_device(
    tokens,
    cotangent,
    doc_ids,
    block_order,
    front_weight,
    back_weight,
    front_master,
    back_master,
    front_first,
    back_first,
    front_second,
    back_second,
    vectors,
    vector_first,
    vector_second,
    learn_rates,
    adam_step,
    *,
    plan,
):
    planes, shards, ranks, unit = plan.planes, plan.fsdp, plan.ranks, plan.unit
    both = ("ctx", "fsdp")
    contract_last = (((1,), (1,)), ((), ()))
    contract_first = (((0,), (0,)), ((), ()))
    c_index, f = lax.axis_index("ctx"), lax.axis_index("fsdp")
    z, k = c_index // 2, c_index % 2
    p = 2 * f + k
    rows = tokens.shape[1]
    plane_rows = 2 * shards * rows
    share = 2 * rows

    bias_front = vectors[:IN_COLS].reshape(-1, unit)
    bias_back = vectors[IN_COLS : IN_COLS + D]
    norm_gain = vectors[IN_COLS + D : IN_COLS + 2 * D]
    norm_shift = vectors[IN_COLS + 2 * D :]

    swap_pairs = [(2 * i + j, 2 * i + 1 - j) for i in range(planes) for j in range(2)]

    def swap_core(value):
        return lax.ppermute(value, "ctx", swap_pairs)

    def to_shard(value, step):
        return lax.ppermute(value, "fsdp", [(i, i ^ step) for i in range(shards)])

    def at(array, index):
        return lax.dynamic_index_in_dim(array, index, 0, keepdims=False)

    blocks = block_order.shape[0]
    block_tokens = doc_ids.shape[1] // blocks
    offsets = jnp.arange(block_tokens, dtype=jnp.int32)
    positions_all = (block_order[:, None] * block_tokens + offsets[None, :]).reshape(planes, share)
    own_positions = at(positions_all, z)
    plane_positions = jnp.tile(own_positions, shards)

    plane_tokens, plane_grad, documents, weight_qkv, back_attention = gather_first(
        plan, tokens[0], cotangent[0], doc_ids.astype(f32), front_weight, back_weight
    )
    plane_tokens = plane_tokens.reshape(plane_rows, D)
    plane_grad = plane_grad.reshape(plane_rows, D)

    normed = (normalize(plane_tokens)[0] * norm_gain + norm_shift).astype(bf16)

    unit_table = pick(plan.rank_units, p)
    bias_local = jnp.take(bias_front, unit_table, axis=0).reshape(-1)

    hidden = jnp.dot(normed, weight_qkv, preferred_element_type=f32) + bias_local[: 3 * unit]
    tables = rotation_tables(plane_positions, unit)
    query = rotate(hidden[:, :unit], tables).astype(bf16)
    key = rotate(hidden[:, unit : 2 * unit], tables).astype(bf16)
    attended_grad = lax.dot_general(
        plane_grad, back_attention, contract_last, preferred_element_type=f32
    ).astype(bf16)
    qkvg = jnp.concatenate([query, key, hidden[:, 2 * unit :].astype(bf16), attended_grad], axis=1)
    qkvg, weight_up = exchange_with(
        plan,
        qkvg.reshape(planes, share, -1),
        front_weight,
        functools.partial(weight_moves, plan, range(3, 5)),
        (D, 4 * unit),
        (D, 2 * unit),
        (2,),
    )
    qkvg = qkvg.reshape(planes * share, -1)

    seq_positions = positions_all.reshape(-1)
    doc_row = documents[0].astype(jnp.int32)
    seq_documents = jnp.take(doc_row.reshape(blocks, block_tokens), block_order, axis=0).reshape(-1)
    attended, query_grad, key_grad, value_grad = attention(
        qkvg[:, :unit],
        qkvg[:, unit : 2 * unit],
        qkvg[:, 2 * unit : 3 * unit],
        qkvg[:, 3 * unit :],
        seq_positions,
        seq_documents,
    )
    seq_tables = rotation_tables(seq_positions, unit)
    returned = jnp.concatenate(
        [
            attended,
            rotate_back(query_grad, seq_tables).astype(bf16),
            rotate_back(key_grad, seq_tables).astype(bf16),
            value_grad.astype(bf16),
        ],
        axis=1,
    )
    returned, back_up = exchange_with(
        plan,
        returned.reshape(planes, share, -1),
        back_weight,
        functools.partial(back_moves, plan),
        (4 * unit, D),
        (2 * unit, D // shards),
        (2, shards),
    )
    returned = returned.reshape(plane_rows, -1)
    back_local = jnp.concatenate([back_attention, back_up], axis=0)

    up = jnp.dot(normed, weight_up, preferred_element_type=f32) + bias_local[3 * unit :]
    activation, slope = gelu_parts(up)
    mixed_grad = lax.dot_general(plane_grad, back_up, contract_last, preferred_element_type=f32)
    up_grad = (mixed_grad * slope).astype(bf16)
    mixed = jnp.concatenate([returned[:, :unit], activation.astype(bf16)], axis=1)
    hidden_grad = jnp.concatenate([returned[:, unit:], up_grad], axis=1)

    def sum_to_owner(value):
        shaped = value.reshape(shards, 2, rows, D)
        kept = lax.dynamic_index_in_dim(shaped, k, 1, keepdims=False)
        sent = lax.dynamic_index_in_dim(shaped, 1 - k, 1, keepdims=False).astype(bf16)
        summed = kept + swap_core(sent).astype(f32)
        total = at(summed, f)
        for step in range(1, shards):
            total = total + to_shard(at(summed, f ^ step).astype(bf16), step).astype(f32)
        return total

    projected = sum_to_owner(jnp.dot(mixed, back_local, preferred_element_type=f32))
    inputs = tokens[0].astype(f32)
    layer_out = (inputs + projected + bias_back).astype(bf16)[None]

    weight_local = jnp.concatenate([weight_qkv, weight_up], axis=1)
    normed_grad = sum_to_owner(
        lax.dot_general(hidden_grad, weight_local, contract_last, preferred_element_type=f32)
    )
    unscaled, factor = normalize(inputs)
    scaled = normed_grad * norm_gain
    input_grad = factor * (
        scaled
        - jnp.mean(scaled, axis=-1, keepdims=True)
        - unscaled * jnp.mean(scaled * unscaled, axis=-1, keepdims=True)
    )
    tokens_grad = (cotangent[0].astype(f32) + input_grad).astype(bf16)[None]

    back_partial = lax.dot_general(
        mixed, plane_grad, contract_first, preferred_element_type=f32
    ).astype(bf16)
    front_partial = lax.dot_general(
        normed, hidden_grad, contract_first, preferred_element_type=f32
    ).astype(bf16)
    back_sum = back_sums(plan, back_partial)
    front_sum, back_owned = front_sums(plan, front_partial, back_sum)
    back_grad = back_owned.astype(f32)
    back_new, back_first_new, back_second_new = adam_update(
        back_master, back_first, back_second, back_grad, learn_rates[1], adam_step[0], weight_decay
    )
    back_next, front_owned = back_nexts(plan, back_new.astype(bf16), front_sum)
    front_grad = front_owned.astype(f32)
    front_new, front_first_new, front_second_new = adam_update(
        front_master, front_first, front_second, front_grad, learn_rates[0], adam_step[0], weight_decay
    )
    def column_sums(value):
        ones = jnp.ones((8, value.shape[0]), bf16)
        return jnp.dot(ones, value, preferred_element_type=f32)[0]

    spread = (jnp.arange(7 * ranks)[:, None] == unit_table[None, :]).astype(f32)
    hidden_sum = column_sums(hidden_grad).reshape(7, unit)
    front_vector = jnp.sum(spread[:, :, None] * hidden_sum[None], axis=1).reshape(-1)
    vector_term = jnp.concatenate(
        [
            front_vector,
            column_sums(cotangent[0]),
            jnp.sum(normed_grad * unscaled, axis=0),
            jnp.sum(normed_grad, axis=0),
        ]
    )
    front_next, vector_grad = front_nexts(plan, front_new.astype(bf16), vector_term.reshape(-1, 128))
    vector_grad = vector_grad.reshape(-1)

    count_now = adam_step[0]
    vectors_new, vector_first_new, vector_second_new = adam_update(
        vectors, vector_first, vector_second, vector_grad, learn_rates[2], count_now, 0.0
    )

    return (
        layer_out,
        tokens_grad,
        front_grad,
        back_grad,
        vector_grad,
        front_new,
        back_new,
        vectors_new,
        front_first_new,
        back_first_new,
        vector_first_new,
        front_second_new,
        back_second_new,
        vector_second_new,
        front_next,
        back_next,
    )


def solution(mesh):
    plan = Layout(mesh.shape["ctx"], mesh.shape["fsdp"])
    tokens_spec = P("fsdp", "ctx", None)
    cols, owned, same = P(None, "fsdp"), P("ctx", "fsdp"), P()
    in_specs = (
        (tokens_spec, tokens_spec, P("fsdp", None), same, cols, cols)
        + (owned,) * 6
        + (same,) * 5
    )
    out_specs = (
        (tokens_spec, tokens_spec, owned, owned, same)
        + (owned, owned, same) * 3
        + (cols, cols)
    )
    return jax.shard_map(
        functools.partial(per_device, plan=plan),
        mesh=mesh,
        in_specs=in_specs,
        out_specs=out_specs,
        check_vma=False,
    )
```

```python
import functools

import jax
import jax.numpy as jnp
import numpy as np
from jax import lax
from jax.experimental import pallas as pl
from jax.experimental.pallas import tpu as pltpu
from jax.sharding import PartitionSpec as P

D = 2048
HEADS = 32
FF = 8192
ROT = 32
HEAD_DIM = 64
IN_COLS = 14336
BACK_ROWS = 10240

norm_eps = 1e-05
beta_first = 0.9
beta_second = 0.95
adam_eps = 1e-08
weight_decay = 0.1
masked_score = -1e30
bf16 = jnp.bfloat16
f32 = jnp.float32


class Layout:
    def __init__(self, ctx, fsdp):
        self.ctx, self.fsdp, self.planes, self.ranks = ctx, fsdp, ctx // 2, 2 * fsdp
        assert ctx % 2 == 0 and self.planes == fsdp
        self.unit = D // self.ranks
        self.per_shard = IN_COLS // self.unit // fsdp
        r = self.ranks
        first_up = 3 * r
        home = {f: [] for f in range(fsdp)}
        for g in range(first_up, 7 * r, 2):
            assert g // self.per_shard == (g + 1) // self.per_shard
            home[g // self.per_shard].append(g)
        pairs = {p: [None, None] for p in range(r)}
        for f in range(fsdp):
            if len(home[f]) >= 4:
                keep, home[f] = home[f][:4], home[f][4:]
                pairs[2 * f], pairs[2 * f + 1] = keep[:2], keep[2:]
            elif home[f]:
                keep, home[f] = home[f], []
                for i, g in enumerate(keep):
                    pairs[2 * f + i % 2][(i + i // 2) % 2] = g
        for s in range(2):
            for k in range(2):
                used = set()
                for f in range(fsdp):
                    p = 2 * f + k
                    if pairs[p][s] is not None:
                        continue
                    options = sorted(
                        (h for h in range(fsdp) if home[h]),
                        key=lambda h: (h in used, bin(h ^ f).count("1"), -len(home[h])),
                    )
                    used.add(options[0])
                    pairs[p][s] = home[options[0]].pop(0)
        self.pairs = pairs
        self.slots = [
            ([p for p in range(r)], 1),
            ([r + p for p in range(r)], 1),
            ([2 * r + p for p in range(r)], 1),
            ([pairs[p][0] for p in range(r)], 2),
            ([pairs[p][1] for p in range(r)], 2),
        ]
        self.rounds = []
        for units, _ in self.slots:
            rounds = []
            for k in range(2):
                for f in range(fsdp):
                    src = units[2 * f + k] // self.per_shard
                    if src == f:
                        continue
                    for one in rounds:
                        if all((src, k) != (a, c) for a, _, c in one):
                            one.append((src, f, k))
                            break
                    else:
                        rounds.append([(src, f, k)])
            self.rounds.append(rounds)
        self.rank_units = [
            [p, r + p, 2 * r + p, pairs[p][0], pairs[p][0] + 1, pairs[p][1], pairs[p][1] + 1]
            for p in range(r)
        ]
        self.back_units = [[p] + [g - 2 * r for g in self.rank_units[p][3:]] for p in range(r)]
        self.matchings = []
        left = {p: list(range(5)) for p in range(r)}
        own = lambda p, j: self.back_units[p][j] // 5
        for _ in range(5):
            match = {}

            def assign(p, seen):
                for j in left[p]:
                    c = own(p, j)
                    if c in seen:
                        continue
                    seen.add(c)
                    if c not in match or assign(match[c][0], seen):
                        match[c] = (p, j)
                        return True
                return False

            for p in range(r):
                assert assign(p, set())
            for c, (p, j) in match.items():
                left[p].remove(j)
            self.matchings.append(match)

    def device(self, z, k, f):
        return (2 * z + k) * self.fsdp + f


def pick(table, index):
    return jnp.asarray(np.asarray(table, np.int32))[index]


def normalize(values):
    values = values.astype(f32)
    centered = values - jnp.mean(values, axis=-1, keepdims=True)
    factor = lax.rsqrt(jnp.mean(centered * centered, axis=-1, keepdims=True) + norm_eps)
    return centered * factor, factor


def rotation_tables(positions, width):
    half = ROT // 2
    lane = np.arange(width) % HEAD_DIM
    frequency = jnp.power(
        10000.0, -2.0 * jnp.asarray(lane % half, f32) / ROT
    )
    angles = positions.astype(f32)[:, None] * frequency[None, :]
    rotated = jnp.asarray(lane < ROT)
    lower = jnp.asarray(lane < half)
    cosine = jnp.where(rotated, jnp.cos(angles), 1.0)
    sine = jnp.where(rotated, jnp.sin(angles), 0.0)
    return cosine, jnp.where(lower, -sine, 0.0), jnp.where(lower, 0.0, sine)


def rotate(values, tables):
    half = ROT // 2
    cosine, from_above, from_below = tables
    return (
        values * cosine
        + jnp.roll(values, -half, axis=1) * from_above
        + jnp.roll(values, half, axis=1) * from_below
    )


def rotate_back(values, tables):
    half = ROT // 2
    cosine, from_above, from_below = tables
    return (
        values * cosine
        + jnp.roll(values * from_above, half, axis=1)
        + jnp.roll(values * from_below, -half, axis=1)
    )


def attention_kernel(
    q_ref, k_ref, v_ref, g_ref, pos_q, pos_k, seg_q, seg_k, att_ref, dq_ref, dk_ref, dv_ref
):
    scale = HEAD_DIM ** (-0.5)
    width = q_ref.shape[1]

    @pl.when(pl.program_id(0) == 0)
    def _():
        dk_ref[...] = jnp.zeros_like(dk_ref)
        dv_ref[...] = jnp.zeros_like(dv_ref)

    allowed = (pos_k[...] <= pos_q[...]) & (seg_k[...] == seg_q[...])
    bias = jnp.where(allowed, 0.0, masked_score)
    last = (((1,), (1,)), ((), ()))
    first = (((0,), (0,)), ((), ()))
    for head in range(width // HEAD_DIM):
        cols = slice(head * HEAD_DIM, (head + 1) * HEAD_DIM)
        q, g = q_ref[:, cols], g_ref[:, cols]
        k, v = k_ref[:, cols], v_ref[:, cols]
        scores = lax.dot_general(q, k, last, preferred_element_type=f32) * scale + bias
        weights = jnp.exp(scores - jnp.max(scores, axis=1, keepdims=True))
        probs = weights * (1.0 / jnp.sum(weights, axis=1, keepdims=True))
        probs_low = probs.astype(bf16)
        out = jnp.dot(probs_low, v, preferred_element_type=f32)
        att_ref[:, cols] = out.astype(bf16)
        prob_grad = lax.dot_general(g, v, last, preferred_element_type=f32)
        delta = jnp.sum(g.astype(f32) * out, axis=1, keepdims=True)
        score_grad = (probs * (prob_grad - delta)).astype(bf16)
        dq_ref[:, cols] = jnp.dot(score_grad, k, preferred_element_type=f32) * scale
        dk_ref[:, cols] += lax.dot_general(score_grad, q, first, preferred_element_type=f32) * scale
        dv_ref[:, cols] += lax.dot_general(probs_low, g, first, preferred_element_type=f32)


def attention(query, key, value, grad, positions, segments):
    length, width = query.shape
    block = 256
    rows = pl.BlockSpec((block, width), lambda i: (i, 0))
    whole = pl.BlockSpec((length, width), lambda i: (0, 0))
    column = pl.BlockSpec((block, 1), lambda i: (i, 0))
    line = pl.BlockSpec((1, length), lambda i: (0, 0))
    return pl.pallas_call(
        attention_kernel,
        grid=(length // block,),
        in_specs=[rows, whole, whole, rows, column, line, column, line],
        out_specs=[rows, rows, whole, whole],
        out_shape=[
            jax.ShapeDtypeStruct((length, width), bf16),
            jax.ShapeDtypeStruct((length, width), f32),
            jax.ShapeDtypeStruct((length, width), f32),
            jax.ShapeDtypeStruct((length, width), f32),
        ],
        cost_estimate=pl.CostEstimate(
            flops=14 * length * length * width,
            transcendentals=length * length * width // HEAD_DIM,
            bytes_accessed=20 * length * width,
        ),
    )(query, key, value, grad, positions[:, None], positions[None], segments[:, None], segments[None])


MESH = pl.DeviceIdType.MESH


VMEM_BLOCK = pl.BlockSpec(memory_space=pltpu.VMEM)
ANY_BLOCK = pl.BlockSpec(memory_space=pl.ANY)


def busy(microseconds):
    return pl.CostEstimate(flops=int(microseconds * 900e6), transcendentals=0, bytes_accessed=0)


def place_in_mesh():
    c, f = lax.axis_index("ctx"), lax.axis_index("fsdp")
    z, k = lax.div(c, 2), lax.rem(c, 2)
    return c, f, z, k, 2 * f + k


def bounce(source, buffer, target, sem):
    one = pltpu.make_async_copy(source, buffer, sem)
    one.start()
    one.wait()
    two = pltpu.make_async_copy(buffer, target, sem)
    two.start()
    two.wait()


def gather_kernel(
    plan, tok, cot, doc, front, back, tok_out, cot_out, doc_out, w_out, b_out,
    w_buf, b_buf, tsend, trecv, csend, crecv, wsend, wrecv, rsend, rrecv, bsend, brecv, dsend, drecv, lsem,
):
    shards, unit, ranks = plan.fsdp, plan.unit, plan.ranks
    c, f, z, k, p = place_in_mesh()
    other = c + 1 - 2 * k
    width = D // shards
    both = ((tok, tok_out), (cot, cot_out))

    def cols(block):
        return pl.ds(pl.multiple_of(block * width, 128), width)

    def remote(src, dst, send, recv, device):
        return pltpu.make_async_remote_copy(
            src_ref=src, dst_ref=dst, send_sem=send, recv_sem=recv, device_id=device, device_id_type=MESH
        )

    def peer(step):
        return lax.rem(f + step, shards)

    def giver(step):
        return lax.rem(f + shards - step, shards)

    def send_tokens(n, step):
        src, out = both[n]
        return remote(src, out.at[f, k], tsend.at[n, step], trecv.at[n, step], (c, peer(step)))

    def get_tokens(n, step):
        here = both[n][1].at[giver(step), k]
        return remote(here, here, tsend.at[n, step], trecv.at[n, step], (c, peer(step)))

    def share(n, step):
        src, out = both[n]
        here = out.at[giver(step), k]
        return remote(src if step == 0 else here, here, csend.at[n, step], crecv.at[n, step], (other, f))

    def get_share(n, step):
        here = both[n][1].at[giver(step), 1 - k]
        return remote(here, here, csend.at[n, step], crecv.at[n, step], (other, f))

    def rows_of(dst):
        return pl.ds(pl.multiple_of((2 * dst + k) * unit, unit), unit)

    def send_back(step):
        return remote(
            back.at[rows_of(peer(step)), :], b_out.at[:, cols(f)], bsend.at[step], brecv.at[step], (c, peer(step))
        )

    def get_back(step):
        here = b_out.at[:, cols(giver(step))]
        return remote(here, here, bsend.at[step], brecv.at[step], (c, peer(step)))

    def send_doc(step):
        return remote(doc, doc_out, dsend.at[step], drecv, (c, peer(step)))

    start_weights, relay_weights, finish_weights = weight_moves(
        plan, front, w_out, w_buf, wsend, wrecv, rsend, rrecv, lsem.at[2]
    )
    own = [pltpu.make_async_copy(src, out.at[f, k], lsem.at[4 * n]) for n, (src, out) in enumerate(both)]
    own_doc = pltpu.make_async_copy(doc, doc_out, lsem.at[1])
    for n in range(2):
        for step in range(1, shards):
            send_tokens(n, step).start()
        share(n, 0).start()
        own[n].start()
    for step in range(1, shards):
        send_back(step).start()

    @pl.when(f == z)
    def _():
        own_doc.start()
        for step in range(1, shards):
            send_doc(step).start()

    start_weights()
    for n in range(2):
        for step in range(1, shards):
            get_tokens(n, step).wait_recv()
            share(n, step).start()
    relay_weights()
    bounce(back.at[rows_of(f), :], b_buf, b_out.at[:, cols(f)], lsem.at[3])
    for n in range(2):
        own[n].wait()

    @pl.when(f == z)
    def _():
        own_doc.wait()
        for step in range(1, shards):
            send_doc(step).wait_send()

    @pl.when(f != z)
    def _():
        send_doc(1).wait_recv()

    for n in range(2):
        for step in range(shards):
            get_share(n, step).wait_recv()
            share(n, step).wait_send()
        for step in range(1, shards):
            send_tokens(n, step).wait_send()
    for step in range(1, shards):
        send_back(step).wait_send()
        get_back(step).wait_recv()
    finish_weights()


def moves_between(moves, device_of):
    c, f, z, k, p = place_in_mesh()

    def remote(move):
        src, dst, source, target, send, recv, _, _ = move
        return pltpu.make_async_remote_copy(
            src_ref=source, dst_ref=target, send_sem=send, recv_sem=recv, device_id=device_of(c, dst), device_id_type=MESH
        )

    def start():
        for move in moves:
            if move[0] != move[1]:

                @pl.when(p == move[0])
                def _(move=move):
                    remote(move).start()

        for move in moves:
            if move[0] == move[1]:

                @pl.when(p == move[0])
                def _(move=move):
                    bounce(move[2], move[6], move[3], move[7])

    def finish():
        for move in moves:
            if move[0] != move[1]:

                @pl.when(p == move[0])
                def _(move=move):
                    remote(move).wait_send()

                @pl.when(p == move[1])
                def _(move=move):
                    remote(move).wait_recv()

    return start, finish


def weight_moves(plan, front, out, buffer, send, recv, relay_send, relay_recv, local):
    unit, moves, begin = plan.unit, [], 0
    c, f, z, k, p = place_in_mesh()
    half, parity = D // 2, lax.rem(z, 2)

    def rows(part):
        return pl.ds(pl.multiple_of(part * half, half), half)

    for slot, (units, wide) in enumerate(plan.slots):
        for dst in range(plan.ranks):
            src, at = units[dst] // plan.per_shard, units[dst] % plan.per_shard
            moves.append(
                (slot, 2 * src + dst % 2, dst, pl.ds(at * unit, wide * unit), pl.ds(begin * unit, wide * unit), wide * unit)
            )
        begin += wide

    def copy(move):
        slot, _, dst, source, target, _ = move
        return pltpu.make_async_remote_copy(
            src_ref=front.at[rows(parity), source],
            dst_ref=out.at[rows(parity), target],
            send_sem=send.at[slot, dst // 2],
            recv_sem=recv.at[slot],
            device_id=(c, dst // 2),
            device_id_type=MESH,
        )

    def pass_on(move, part):
        slot, _, _, _, target, _ = move
        here = out.at[rows(part), target]
        return pltpu.make_async_remote_copy(
            src_ref=here,
            dst_ref=here,
            send_sem=relay_send.at[slot],
            recv_sem=relay_recv.at[slot],
            device_id=(c + 2 - 4 * parity, f),
            device_id_type=MESH,
        )

    def start():
        for move in moves:
            if move[1] != move[2]:

                @pl.when(p == move[1])
                def _(move=move):
                    copy(move).start()

    def relay():
        for move in moves:
            if move[1] != move[2]:

                @pl.when(p == move[2])
                def _(move=move):
                    copy(move).wait_recv()
                    pass_on(move, parity).start()

    def finish():
        for move in moves:
            if move[1] == move[2]:

                @pl.when(p == move[2])
                def _(move=move):
                    bounce(front.at[:, move[3]], buffer.at[:, pl.ds(0, move[5])], out.at[:, move[4]], local)

        for move in moves:
            if move[1] != move[2]:

                @pl.when(p == move[1])
                def _(move=move):
                    copy(move).wait_send()

                @pl.when(p == move[2])
                def _(move=move):
                    pass_on(move, parity).wait_send()
                    pass_on(move, 1 - parity).wait_recv()

    return start, relay, finish


def back_moves(plan, back, out, buffer, send, recv, local):
    unit, width, moves = plan.unit, D // plan.fsdp, []
    for dst in range(plan.ranks):
        for src in range(plan.fsdp):
            for number in range(2):
                row = plan.back_units[dst][1 + 2 * number]
                moves.append(
                    (
                        2 * src + dst % 2,
                        dst,
                        back.at[pl.ds(row * unit, 2 * unit), :],
                        out.at[pl.ds(2 * number * unit, 2 * unit), pl.ds(src * width, width)],
                        send.at[number, dst // 2],
                        recv.at[number, src],
                        buffer,
                        local,
                    )
                )
    return moves_between(moves, lambda c, dst: (c, dst // 2))


def line_exchange(plan, src, out, send, recv, local):
    planes = plan.planes
    c, f, z, k, p = place_in_mesh()

    def copy(step):
        to = lax.rem(z + step, planes)
        return pltpu.make_async_remote_copy(
            src_ref=src.at[to],
            dst_ref=out.at[z],
            send_sem=send.at[step],
            recv_sem=recv.at[step],
            device_id=(2 * to + k, f),
            device_id_type=MESH,
        )

    def arrival(step):
        here = out.at[lax.rem(z + planes - step, planes)]
        return pltpu.make_async_remote_copy(
            src_ref=here,
            dst_ref=here,
            send_sem=send.at[step],
            recv_sem=recv.at[step],
            device_id=(2 * lax.rem(z + step, planes) + k, f),
            device_id_type=MESH,
        )

    keep = pltpu.make_async_copy(src.at[z], out.at[z], local)

    def start():
        for step in range(planes - 1, 0, -1):
            copy(step).start()
        keep.start()

    def finish():
        keep.wait()
        for step in range(1, planes):
            copy(step).wait_send()
            arrival(step).wait_recv()

    return start, finish


def gather_first(plan, tokens, cotangent, documents, front_weight, back_weight):
    shards, unit = plan.fsdp, plan.unit
    rows, length = tokens.shape[0], documents.shape[1]
    dma = pltpu.SemaphoreType.DMA
    return pl.pallas_call(
        functools.partial(gather_kernel, plan),
        in_specs=[VMEM_BLOCK] * 3 + [ANY_BLOCK] * 2,
        out_specs=[ANY_BLOCK] * 5,
        out_shape=[
            jax.ShapeDtypeStruct((shards, 2, rows, D), bf16),
            jax.ShapeDtypeStruct((shards, 2, rows, D), bf16),
            jax.ShapeDtypeStruct((1, length), f32),
            jax.ShapeDtypeStruct((D, 7 * unit), bf16),
            jax.ShapeDtypeStruct((unit, D), bf16),
        ],
        scratch_shapes=[
            pltpu.VMEM((D, 2 * unit), bf16),
            pltpu.VMEM((unit, D // shards), bf16),
            dma((2, shards)),
            dma((2, shards)),
            dma((2, shards)),
            dma((2, shards)),
            dma((5, shards)),
            dma((5,)),
            dma((5,)),
            dma((5,)),
            dma((shards,)),
            dma((shards,)),
            dma((shards,)),
            dma(()),
            dma((5,)),
        ],
        compiler_params=pltpu.CompilerParams(has_side_effects=True),
        cost_estimate=busy(130),
    )(tokens, cotangent, documents, front_weight, back_weight)


def exchange_kernel(plan, src, back, out, b_out, buffer, send, recv, local, bsend, brecv):
    start, finish = line_exchange(plan, src, out, send, recv, local.at[0])
    start_rows, finish_rows = back_moves(plan, back, b_out, buffer, bsend, brecv, local.at[1])
    start()
    start_rows()
    finish()
    finish_rows()


def exchange_first(plan, values, back_weight):
    dma = pltpu.SemaphoreType.DMA
    unit, shards = plan.unit, plan.fsdp
    return pl.pallas_call(
        functools.partial(exchange_kernel, plan),
        in_specs=[VMEM_BLOCK, ANY_BLOCK],
        out_specs=[ANY_BLOCK, ANY_BLOCK],
        out_shape=[jax.ShapeDtypeStruct(values.shape, bf16), jax.ShapeDtypeStruct((4 * unit, D), bf16)],
        scratch_shapes=[
            pltpu.VMEM((2 * unit, D // shards), bf16),
            dma((plan.planes,)),
            dma((plan.planes,)),
            dma((2,)),
            dma((2, shards)),
            dma((2, shards)),
        ],
        compiler_params=pltpu.CompilerParams(has_side_effects=True),
        cost_estimate=busy(50),
    )(values, back_weight)


def exchange_back_kernel(plan, src, out, send, recv, local):
    start, finish = line_exchange(plan, src, out, send, recv, local)
    start()
    finish()


def exchange_back(plan, values):
    dma = pltpu.SemaphoreType.DMA
    return pl.pallas_call(
        functools.partial(exchange_back_kernel, plan),
        in_specs=[VMEM_BLOCK],
        out_specs=ANY_BLOCK,
        out_shape=jax.ShapeDtypeStruct(values.shape, bf16),
        scratch_shapes=[dma((plan.planes,)), dma((plan.planes,)), dma(())],
        compiler_params=pltpu.CompilerParams(has_side_effects=True),
        cost_estimate=busy(50),
    )(values)


def line_sum(plan, block, rising, falling, sends, gets, rows):
    planes, chunk = plan.planes, 64
    c, f, z, k, p = place_in_mesh()

    def copy(side, s, src):
        slots = (rising, falling)[side]
        return pltpu.make_async_remote_copy(
            src_ref=src,
            dst_ref=slots.at[s - 1],
            send_sem=sends.at[side, s - 1],
            recv_sem=gets.at[side, s - 1],
            device_id=(c + 2 - 4 * side, f),
            device_id_type=MESH,
        )

    def add(side, s, number):
        slots = (rising, falling)[side]
        term = block(number)

        def body(i, carry):
            at = pl.ds(pl.multiple_of(i * chunk, chunk), chunk)
            slots[s - 1, at, :] = (slots[s - 1, at, :].astype(f32) + term[at, :].astype(f32)).astype(bf16)
            return carry

        lax.fori_loop(0, rows // chunk, body, 0)

    def step(s):
        for side in range(2):
            place = z if side == 0 else planes - 1 - z
            number = planes - s + place
            number = number if side == 0 else planes - 1 - number

            @pl.when(place == 0)
            def _(side=side, number=number):
                copy(side, s, block(number)).start()

            if s > 1:

                @pl.when((place > 0) & (place < s) & (place < planes - 1))
                def _(side=side, number=number):
                    slots = (rising, falling)[side]
                    copy(side, s - 1, slots.at[s - 2]).wait_recv()
                    add(side, s - 1, number)
                    copy(side, s, slots.at[s - 2]).start()

    def finish(out):
        last = planes - 1
        for side in range(2):
            place = z if side == 0 else planes - 1 - z
            slots = (rising, falling)[side]

            @pl.when(place > 0)
            def _(side=side, slots=slots):
                copy(side, last, slots.at[last - 1]).wait_recv()

        mine = block(z)

        def total(ups, downs):
            def body(i, carry):
                at = pl.ds(pl.multiple_of(i * chunk, chunk), chunk)
                value = mine[at, :].astype(f32)
                if ups:
                    value = value + rising[last - 1, at, :].astype(f32)
                if downs:
                    value = value + falling[last - 1, at, :].astype(f32)
                out[at, :] = value.astype(out.dtype)
                return carry

            lax.fori_loop(0, rows // chunk, body, 0)

        @pl.when(z == 0)
        def _():
            total(False, True)

        @pl.when(z == planes - 1)
        def _():
            total(True, False)

        @pl.when((z > 0) & (z < planes - 1))
        def _():
            total(True, True)

        for side in range(2):
            place = z if side == 0 else planes - 1 - z
            slots = (rising, falling)[side]
            for s in range(1, planes):

                @pl.when((place < s) & (place < planes - 1))
                def _(side=side, slots=slots, s=s):
                    copy(side, s, slots.at[s - 1]).wait_send()

    return step, finish


def line_gather(plan, own, out, sends, gets, share_sends, share_gets, local, height):
    planes = plan.planes
    c, f, z, k, p = place_in_mesh()
    other = c + 1 - 2 * k

    def rows_of(plane, core):
        return out.at[pl.ds(pl.multiple_of((2 * plane + core) * height, height), height), :]

    def origin(side, s):
        return z - s if side == 0 else z + s

    def copy(side, s):
        plane = origin(side, s - 1)
        src = own if s == 1 else rows_of(plane, k)
        return pltpu.make_async_remote_copy(
            src_ref=src,
            dst_ref=rows_of(plane, k),
            send_sem=sends.at[side, s - 1],
            recv_sem=gets.at[side, s - 1],
            device_id=(c + 2 - 4 * side, f),
            device_id_type=MESH,
        )

    def arrival(side, s):
        here = rows_of(origin(side, s), k)
        return pltpu.make_async_remote_copy(
            src_ref=here,
            dst_ref=here,
            send_sem=sends.at[side, s - 1],
            recv_sem=gets.at[side, s - 1],
            device_id=(c + 2 - 4 * side, f),
            device_id_type=MESH,
        )

    def share(side, s, core):
        plane = origin(side, s)
        here = rows_of(plane, core)
        src = own if s == 0 else here
        return pltpu.make_async_remote_copy(
            src_ref=src,
            dst_ref=here,
            send_sem=share_sends.at[side, s],
            recv_sem=share_gets.at[side, s],
            device_id=(other, f),
            device_id_type=MESH,
        )

    keep = pltpu.make_async_copy(own, rows_of(z, k), local)

    def sends_at(side, s):
        place = z if side == 0 else planes - 1 - z
        return (place >= s - 1) & (place < planes - 1)

    def gets_at(side, s):
        place = z if side == 0 else planes - 1 - z
        return place >= s

    def take(s):
        for side in range(2):

            @pl.when(gets_at(side, s))
            def _(side=side):
                arrival(side, s).wait_recv()
                if s < planes - 1:

                    @pl.when(sends_at(side, s + 1))
                    def _():
                        copy(side, s + 1).start()

                share(side, s, k).start()

    def step(s):
        if s > 1:
            take(s - 1)
            return
        for side in range(2):

            @pl.when(sends_at(side, 1))
            def _(side=side):
                copy(side, 1).start()

        share(0, 0, k).start()
        keep.start()

    def finish():
        take(planes - 1)
        keep.wait()
        share(0, 0, k).wait_send()
        share(0, 0, 1 - k).wait_recv()
        for side in range(2):
            for s in range(1, planes):

                @pl.when(sends_at(side, s))
                def _(side=side, s=s):
                    copy(side, s).wait_send()

                @pl.when(gets_at(side, s))
                def _(side=side, s=s):
                    share(side, s, k).wait_send()
                    share(side, s, 1 - k).wait_recv()

    return step, finish


def back_owners(plan, src, out, send, recv, lsem):
    unit, ranks = plan.unit, plan.ranks
    c, f, z, k, p = place_in_mesh()

    def copy(j, owner, place):
        return pltpu.make_async_remote_copy(
            src_ref=src.at[pl.ds(j * unit, unit), :],
            dst_ref=out.at[pl.ds(place * unit, unit), :],
            send_sem=send.at[j],
            recv_sem=recv.at[place],
            device_id=(owner, z),
            device_id_type=MESH,
        )

    def local(j, place):
        return pltpu.make_async_copy(
            src.at[pl.ds(j * unit, unit), :], out.at[pl.ds(place * unit, unit), :], lsem.at[place]
        )

    blocks = [
        (rank, j, plan.back_units[rank][j] // 5, plan.back_units[rank][j] % 5)
        for rank in range(ranks)
        for j in range(5)
    ]

    def start():
        for rank, j, owner, place in blocks:

            @pl.when((p == rank) & ~((c == owner) & (f == z)))
            def _(j=j, owner=owner, place=place):
                copy(j, owner, place).start()

            @pl.when((p == rank) & (c == owner) & (f == z))
            def _(j=j, place=place):
                local(j, place).start()

    def finish():
        for rank, j, owner, place in blocks:

            @pl.when((p == rank) & ~((c == owner) & (f == z)))
            def _(j=j, owner=owner, place=place):
                copy(j, owner, place).wait_send()

            @pl.when((c == owner) & ~((p == rank) & (f == z)))
            def _(j=j, owner=owner, place=place):
                copy(j, owner, place).wait_recv()

            @pl.when((p == rank) & (c == owner) & (f == z))
            def _(j=j, place=place):
                local(j, place).wait()

    return start, finish


def front_owners(plan, src, out, send, recv, lsem):
    unit, ranks = plan.unit, plan.ranks
    c, f, z, k, p = place_in_mesh()
    height = src.shape[0] // 2
    moves, start_at = [], 0
    for slot, (units, wide) in enumerate(plan.slots):
        for rank in range(ranks):
            owner, place = units[rank] // plan.per_shard, units[rank] % plan.per_shard
            moves.append((slot, rank, owner, place, start_at, wide))
        start_at += wide

    def copy(slot, owner, place, begin, wide, half):
        return pltpu.make_async_remote_copy(
            src_ref=src.at[pl.ds(half * height, height), pl.ds(begin * unit, wide * unit)],
            dst_ref=out.at[:, pl.ds(place * unit, wide * unit)],
            send_sem=send.at[slot, half],
            recv_sem=recv.at[place],
            device_id=(2 * z + half, owner),
            device_id_type=MESH,
        )

    def local(place, begin, wide, half):
        return pltpu.make_async_copy(
            src.at[pl.ds(half * height, height), pl.ds(begin * unit, wide * unit)],
            out.at[:, pl.ds(place * unit, wide * unit)],
            lsem.at[place],
        )

    def start():
        for slot, rank, owner, place, begin, wide in moves:
            for half in range(2):
                if 2 * owner + half == rank:

                    @pl.when(p == rank)
                    def _(place=place, begin=begin, wide=wide, half=half):
                        local(place, begin, wide, half).start()

                else:

                    @pl.when(p == rank)
                    def _(slot=slot, owner=owner, place=place, begin=begin, wide=wide, half=half):
                        copy(slot, owner, place, begin, wide, half).start()

    def finish():
        for slot, rank, owner, place, begin, wide in moves:
            for half in range(2):
                if 2 * owner + half == rank:

                    @pl.when(p == rank)
                    def _(place=place, begin=begin, wide=wide, half=half):
                        local(place, begin, wide, half).wait()

                else:

                    @pl.when(p == rank)
                    def _(slot=slot, owner=owner, place=place, begin=begin, wide=wide, half=half):
                        copy(slot, owner, place, begin, wide, half).wait_send()

                    @pl.when(p == 2 * owner + half)
                    def _(slot=slot, owner=owner, place=place, begin=begin, wide=wide, half=half):
                        copy(slot, owner, place, begin, wide, half).wait_recv()

    return start, finish


def sum_scratch(plan, rows, columns):
    dma = pltpu.SemaphoreType.DMA
    steps = plan.planes - 1
    slots = pltpu.VMEM((steps, rows, columns), bf16)
    return [slots, slots, dma((2, steps)), dma((2, steps))]


def gather_scratch(plan):
    dma = pltpu.SemaphoreType.DMA
    return [dma((2, plan.planes - 1))] * 2 + [dma((2, plan.planes))] * 2 + [dma(())]


def back_sum_kernel(plan, width, src, out, *scratch):
    def block(i):
        return src.at[:, pl.ds(pl.multiple_of(i * width, 128), width)]

    step, finish = line_sum(plan, block, *scratch, src.shape[0])
    for s in range(1, plan.planes):
        step(s)
    finish(out)


def back_sums(plan, partial):
    rows, width = partial.shape[0], D // plan.planes
    return pl.pallas_call(
        functools.partial(back_sum_kernel, plan, width),
        in_specs=[VMEM_BLOCK],
        out_specs=VMEM_BLOCK,
        out_shape=jax.ShapeDtypeStruct((rows, width), bf16),
        scratch_shapes=sum_scratch(plan, rows, width),
        compiler_params=pltpu.CompilerParams(has_side_effects=True),
        cost_estimate=busy(90),
    )(partial)


def front_sum_kernel(plan, rows, src, back, out, owned, *scratch):
    start, done = back_owners(plan, back, owned, *scratch[:3])
    step, finish = line_sum(
        plan, lambda i: src.at[pl.ds(pl.multiple_of(i * rows, rows), rows), :], *scratch[3:], rows
    )
    step(1)
    start()
    for s in range(2, plan.planes):
        step(s)
    finish(out)
    done()


def front_sums(plan, partial, back_sum):
    dma = pltpu.SemaphoreType.DMA
    rows, width = partial.shape[0] // plan.planes, partial.shape[1]
    return pl.pallas_call(
        functools.partial(front_sum_kernel, plan, rows),
        in_specs=[VMEM_BLOCK, VMEM_BLOCK],
        out_specs=[VMEM_BLOCK, ANY_BLOCK],
        out_shape=[
            jax.ShapeDtypeStruct((rows, width), bf16),
            jax.ShapeDtypeStruct(back_sum.shape, bf16),
        ],
        scratch_shapes=[dma((5,))] * 3 + sum_scratch(plan, rows, width),
        compiler_params=pltpu.CompilerParams(has_side_effects=True),
        cost_estimate=busy(120),
    )(partial, back_sum)


def back_next_kernel(plan, own, src, out, owned, *scratch):
    start, done = front_owners(plan, src, owned, *scratch[:3])
    step, finish = line_gather(plan, own, out, *scratch[3:], own.shape[0])
    step(1)
    start()
    for s in range(2, plan.planes):
        step(s)
    finish()
    done()


def back_nexts(plan, own, front_sum):
    dma = pltpu.SemaphoreType.DMA
    return pl.pallas_call(
        functools.partial(back_next_kernel, plan),
        in_specs=[VMEM_BLOCK, VMEM_BLOCK],
        out_specs=[ANY_BLOCK, ANY_BLOCK],
        out_shape=[
            jax.ShapeDtypeStruct((2 * plan.planes * own.shape[0], own.shape[1]), bf16),
            jax.ShapeDtypeStruct((front_sum.shape[0] // 2, plan.per_shard * plan.unit), bf16),
        ],
        scratch_shapes=[dma((5, 2)), dma((plan.per_shard,)), dma((plan.per_shard,))] + gather_scratch(plan),
        compiler_params=pltpu.CompilerParams(has_side_effects=True),
        cost_estimate=busy(90),
    )(own, front_sum)


def vector_sum(plan, own, out, terms, sums, send, recv):
    planes, ranks = plan.planes, plan.ranks
    c, f, z, k, p = place_in_mesh()

    def in_plane(step, target):
        to = lax.rem(p + step, ranks)
        return pltpu.make_async_remote_copy(
            src_ref=own,
            dst_ref=terms.at[target],
            send_sem=send.at[step],
            recv_sem=recv.at[step],
            device_id=(2 * z + lax.rem(to, 2), lax.div(to, 2)),
            device_id_type=MESH,
        )

    def over_planes(step, target):
        to = lax.rem(z + step, planes)
        return pltpu.make_async_remote_copy(
            src_ref=out,
            dst_ref=sums.at[target],
            send_sem=send.at[ranks + step],
            recv_sem=recv.at[ranks + step],
            device_id=(2 * to + k, f),
            device_id_type=MESH,
        )

    def start():
        for step in range(1, ranks):
            in_plane(step, p).start()
        terms[p] = own[...]

    def middle():
        for step in range(1, ranks):
            in_plane(step, lax.rem(p + ranks - step, ranks)).wait_recv()
        total = terms[0]
        for rank in range(1, ranks):
            total = total + terms[rank]
        out[...] = total
        sums[z] = total
        for step in range(1, planes):
            over_planes(step, z).start()

    def finish():
        for step in range(1, ranks):
            in_plane(step, p).wait_send()
        for step in range(1, planes):
            over_planes(step, z).wait_send()
            over_planes(step, lax.rem(z + planes - step, planes)).wait_recv()
        total = sums[0]
        for plane in range(1, planes):
            total = total + sums[plane]
        out[...] = total

    return start, middle, finish


def front_next_kernel(plan, own, vector, out, vector_out, terms, sums, vsend, vrecv, *scratch):
    begin, middle, end = vector_sum(plan, vector, vector_out, terms, sums, vsend, vrecv)
    step, finish = line_gather(plan, own, out, *scratch, own.shape[0])
    begin()
    step(1)
    middle()
    for s in range(2, plan.planes):
        step(s)
    finish()
    end()


def front_nexts(plan, own, vector):
    dma = pltpu.SemaphoreType.DMA
    return pl.pallas_call(
        functools.partial(front_next_kernel, plan),
        in_specs=[VMEM_BLOCK, VMEM_BLOCK],
        out_specs=[ANY_BLOCK, VMEM_BLOCK],
        out_shape=[
            jax.ShapeDtypeStruct((2 * plan.planes * own.shape[0], own.shape[1]), bf16),
            jax.ShapeDtypeStruct(vector.shape, f32),
        ],
        scratch_shapes=[
            pltpu.VMEM((plan.ranks,) + vector.shape, f32),
            pltpu.VMEM((plan.planes,) + vector.shape, f32),
            dma((plan.ranks + plan.planes,)),
            dma((plan.ranks + plan.planes,)),
        ]
        + gather_scratch(plan),
        compiler_params=pltpu.CompilerParams(has_side_effects=True),
        cost_estimate=busy(120),
    )(own, vector)


def gelu_parts(u):
    scale = np.float32(np.sqrt(2.0 / np.pi))
    square = u * u
    inner = scale * u * (1.0 + 0.044715 * square)
    t = jnp.tanh(inner)
    value = 0.5 * u * (1.0 + t)
    slope = 0.5 * (1.0 + t) + 0.5 * u * (1.0 - t * t) * scale * (1.0 + 3 * 0.044715 * square)
    return value, slope


def adam_update(weight, first, second, grad, rate, count_now, decay):
    first_new = beta_first * first + (1.0 - beta_first) * grad
    second_new = beta_second * second + (1.0 - beta_second) * grad * grad
    steps_float = count_now.astype(f32)
    first_fix = 1.0 - jnp.power(beta_first, steps_float)
    second_fix = 1.0 - jnp.power(beta_second, steps_float)
    change = first_new / first_fix / (jnp.sqrt(second_new / second_fix) + adam_eps) + decay * weight
    return (weight - rate * change, first_new, second_new)


def after(value, *others):
    return lax.optimization_barrier((value,) + others)[0]


def per_device(
    tokens,
    cotangent,
    doc_ids,
    block_order,
    front_weight,
    back_weight,
    front_master,
    back_master,
    front_first,
    back_first,
    front_second,
    back_second,
    vectors,
    vector_first,
    vector_second,
    learn_rates,
    adam_step,
    *,
    plan,
):
    planes, shards, ranks, unit = plan.planes, plan.fsdp, plan.ranks, plan.unit
    both = ("ctx", "fsdp")
    contract_last = (((1,), (1,)), ((), ()))
    contract_first = (((0,), (0,)), ((), ()))
    c_index, f = lax.axis_index("ctx"), lax.axis_index("fsdp")
    z, k = c_index // 2, c_index % 2
    p = 2 * f + k
    rows = tokens.shape[1]
    plane_rows = 2 * shards * rows
    share = 2 * rows

    bias_front = vectors[:IN_COLS].reshape(-1, unit)
    bias_back = vectors[IN_COLS : IN_COLS + D]
    norm_gain = vectors[IN_COLS + D : IN_COLS + 2 * D]
    norm_shift = vectors[IN_COLS + 2 * D :]

    swap_pairs = [(2 * i + j, 2 * i + 1 - j) for i in range(planes) for j in range(2)]

    def swap_core(value):
        return lax.ppermute(value, "ctx", swap_pairs)

    def to_shard(value, step):
        return lax.ppermute(value, "fsdp", [(i, i ^ step) for i in range(shards)])

    def at(array, index):
        return lax.dynamic_index_in_dim(array, index, 0, keepdims=False)

    blocks = block_order.shape[0]
    block_tokens = doc_ids.shape[1] // blocks
    offsets = jnp.arange(block_tokens, dtype=jnp.int32)
    positions_all = (block_order[:, None] * block_tokens + offsets[None, :]).reshape(planes, share)
    own_positions = at(positions_all, z)
    plane_positions = jnp.tile(own_positions, shards)

    plane_tokens, plane_grad, documents, weight_local, back_attention = gather_first(
        plan, tokens[0], cotangent[0], doc_ids.astype(f32), front_weight, back_weight
    )
    plane_tokens = plane_tokens.reshape(plane_rows, D)
    plane_grad = plane_grad.reshape(plane_rows, D)

    normed = (normalize(plane_tokens)[0] * norm_gain + norm_shift).astype(bf16)

    unit_table = pick(plan.rank_units, p)
    bias_local = jnp.take(bias_front, unit_table, axis=0).reshape(-1)

    hidden = jnp.dot(normed, weight_local[:, : 3 * unit], preferred_element_type=f32) + bias_local[: 3 * unit]
    tables = rotation_tables(plane_positions, unit)
    query = rotate(hidden[:, :unit], tables).astype(bf16)
    key = rotate(hidden[:, unit : 2 * unit], tables).astype(bf16)
    attended_grad = lax.dot_general(
        plane_grad, back_attention, contract_last, preferred_element_type=f32
    ).astype(bf16)
    qkvg = jnp.concatenate([query, key, hidden[:, 2 * unit :].astype(bf16), attended_grad], axis=1)
    qkvg, back_up = exchange_first(plan, qkvg.reshape(planes, share, -1), back_weight)
    qkvg = qkvg.reshape(planes * share, -1)

    seq_positions = positions_all.reshape(-1)
    doc_row = documents[0].astype(jnp.int32)
    seq_documents = jnp.take(doc_row.reshape(blocks, block_tokens), block_order, axis=0).reshape(-1)
    attended, query_grad, key_grad, value_grad = attention(
        qkvg[:, :unit],
        qkvg[:, unit : 2 * unit],
        qkvg[:, 2 * unit : 3 * unit],
        qkvg[:, 3 * unit :],
        seq_positions,
        seq_documents,
    )
    seq_tables = rotation_tables(seq_positions, unit)
    returned = jnp.concatenate(
        [
            attended,
            rotate_back(query_grad, seq_tables).astype(bf16),
            rotate_back(key_grad, seq_tables).astype(bf16),
            value_grad.astype(bf16),
        ],
        axis=1,
    )
    returned = exchange_back(plan, returned.reshape(planes, share, -1))
    returned = returned.reshape(plane_rows, -1)
    back_local = jnp.concatenate([back_attention, back_up], axis=0)

    up = jnp.dot(normed, weight_local[:, 3 * unit :], preferred_element_type=f32) + bias_local[3 * unit :]
    activation, slope = gelu_parts(up)
    mixed_grad = lax.dot_general(plane_grad, back_up, contract_last, preferred_element_type=f32)
    up_grad = (mixed_grad * slope).astype(bf16)
    mixed = jnp.concatenate([returned[:, :unit], activation.astype(bf16)], axis=1)
    hidden_grad = jnp.concatenate([returned[:, unit:], up_grad], axis=1)

    def sum_over_cores(value):
        shaped = value.reshape(shards, 2, rows, D)
        kept = lax.dynamic_index_in_dim(shaped, k, 1, keepdims=False)
        sent = lax.dynamic_index_in_dim(shaped, 1 - k, 1, keepdims=False).astype(bf16)
        return kept + swap_core(sent).astype(f32)

    def sum_over_shards(*values):
        totals = [at(value, f) for value in values]
        for step in range(1, shards):
            pieces = jnp.stack([at(value, f ^ step).astype(bf16) for value in values])
            pieces = to_shard(pieces, step).astype(f32)
            totals = [total + piece for total, piece in zip(totals, pieces)]
        return totals

    projected_cores = sum_over_cores(jnp.dot(mixed, back_local, preferred_element_type=f32))
    normed_grad_cores = sum_over_cores(
        lax.dot_general(hidden_grad, weight_local, contract_last, preferred_element_type=f32)
    )

    back_partial = lax.dot_general(
        mixed, plane_grad, contract_first, preferred_element_type=f32
    ).astype(bf16)
    front_partial = lax.dot_general(
        normed, hidden_grad, contract_first, preferred_element_type=f32
    ).astype(bf16)
    back_sum = back_sums(plan, back_partial)
    back_sum, projected_cores, normed_grad_cores = lax.optimization_barrier(
        (back_sum, projected_cores, normed_grad_cores)
    )
    projected, normed_grad = sum_over_shards(projected_cores, normed_grad_cores)
    front_sum, back_owned = front_sums(plan, front_partial, back_sum)
    front_sum, projected, normed_grad = lax.optimization_barrier((front_sum, projected, normed_grad))

    inputs = tokens[0].astype(f32)
    layer_out = (inputs + projected + bias_back).astype(bf16)[None]
    unscaled, factor = normalize(inputs)
    scaled = normed_grad * norm_gain
    input_grad = factor * (
        scaled
        - jnp.mean(scaled, axis=-1, keepdims=True)
        - unscaled * jnp.mean(scaled * unscaled, axis=-1, keepdims=True)
    )
    tokens_grad = (cotangent[0].astype(f32) + input_grad).astype(bf16)[None]

    back_grad = back_owned.astype(f32)
    back_new, back_first_new, back_second_new = adam_update(
        back_master, back_first, back_second, back_grad, learn_rates[1], adam_step[0], weight_decay
    )
    back_next, front_owned = back_nexts(plan, back_new.astype(bf16), front_sum)
    front_grad = front_owned.astype(f32)
    front_new, front_first_new, front_second_new = adam_update(
        front_master, front_first, front_second, front_grad, learn_rates[0], adam_step[0], weight_decay
    )
    def column_sums(value):
        ones = jnp.ones((8, value.shape[0]), bf16)
        return jnp.dot(ones, value, preferred_element_type=f32)[0]

    spread = (jnp.arange(7 * ranks)[:, None] == unit_table[None, :]).astype(f32)
    hidden_sum = column_sums(hidden_grad).reshape(7, unit)
    front_vector = jnp.sum(spread[:, :, None] * hidden_sum[None], axis=1).reshape(-1)
    vector_term = jnp.concatenate(
        [
            front_vector,
            column_sums(cotangent[0]),
            jnp.sum(normed_grad * unscaled, axis=0),
            jnp.sum(normed_grad, axis=0),
        ]
    )
    front_next, vector_grad = front_nexts(plan, front_new.astype(bf16), vector_term.reshape(-1, 128))
    vector_grad = vector_grad.reshape(-1)

    count_now = adam_step[0]
    vectors_new, vector_first_new, vector_second_new = adam_update(
        vectors, vector_first, vector_second, vector_grad, learn_rates[2], count_now, 0.0
    )

    return (
        layer_out,
        tokens_grad,
        front_grad,
        back_grad,
        vector_grad,
        front_new,
        back_new,
        vectors_new,
        front_first_new,
        back_first_new,
        vector_first_new,
        front_second_new,
        back_second_new,
        vector_second_new,
        front_next,
        back_next,
    )


def solution(mesh):
    plan = Layout(mesh.shape["ctx"], mesh.shape["fsdp"])
    tokens_spec = P("fsdp", "ctx", None)
    cols, owned, same = P(None, "fsdp"), P("ctx", "fsdp"), P()
    in_specs = (
        (tokens_spec, tokens_spec, P("fsdp", None), same, cols, cols)
        + (owned,) * 6
        + (same,) * 5
    )
    out_specs = (
        (tokens_spec, tokens_spec, owned, owned, same)
        + (owned, owned, same) * 3
        + (cols, cols)
    )
    return jax.shard_map(
        functools.partial(per_device, plan=plan),
        mesh=mesh,
        in_specs=in_specs,
        out_specs=out_specs,
        check_vma=False,
    )
```

```python
import functools

import jax
import jax.numpy as jnp
import numpy as np
from jax import lax
from jax.experimental import pallas as pl
from jax.experimental.pallas import tpu as pltpu
from jax.sharding import PartitionSpec as P

D = 2048
HEADS = 32
FF = 8192
ROT = 32
HEAD_DIM = 64
IN_COLS = 14336
BACK_ROWS = 10240

norm_eps = 1e-05
beta_first = 0.9
beta_second = 0.95
adam_eps = 1e-08
weight_decay = 0.1
masked_score = -1e30
bf16 = jnp.bfloat16
f32 = jnp.float32


class Layout:
    def __init__(self, ctx, fsdp):
        self.ctx, self.fsdp, self.planes, self.ranks = ctx, fsdp, ctx // 2, 2 * fsdp
        assert ctx % 2 == 0 and self.planes == fsdp
        self.unit = D // self.ranks
        self.per_shard = IN_COLS // self.unit // fsdp
        r = self.ranks
        first_up = 3 * r
        home = {f: [] for f in range(fsdp)}
        for g in range(first_up, 7 * r, 2):
            assert g // self.per_shard == (g + 1) // self.per_shard
            home[g // self.per_shard].append(g)
        pairs = {p: [None, None] for p in range(r)}
        for f in range(fsdp):
            if len(home[f]) >= 4:
                keep, home[f] = home[f][:4], home[f][4:]
                pairs[2 * f], pairs[2 * f + 1] = keep[:2], keep[2:]
            elif home[f]:
                keep, home[f] = home[f], []
                for i, g in enumerate(keep):
                    pairs[2 * f + i % 2][(i + i // 2) % 2] = g
        for s in range(2):
            for k in range(2):
                used = set()
                for f in range(fsdp):
                    p = 2 * f + k
                    if pairs[p][s] is not None:
                        continue
                    options = sorted(
                        (h for h in range(fsdp) if home[h]),
                        key=lambda h: (h in used, bin(h ^ f).count("1"), -len(home[h])),
                    )
                    used.add(options[0])
                    pairs[p][s] = home[options[0]].pop(0)
        self.pairs = pairs
        self.slots = [
            ([p for p in range(r)], 1),
            ([r + p for p in range(r)], 1),
            ([2 * r + p for p in range(r)], 1),
            ([pairs[p][0] for p in range(r)], 2),
            ([pairs[p][1] for p in range(r)], 2),
        ]
        self.rounds = []
        for units, _ in self.slots:
            rounds = []
            for k in range(2):
                for f in range(fsdp):
                    src = units[2 * f + k] // self.per_shard
                    if src == f:
                        continue
                    for one in rounds:
                        if all((src, k) != (a, c) for a, _, c in one):
                            one.append((src, f, k))
                            break
                    else:
                        rounds.append([(src, f, k)])
            self.rounds.append(rounds)
        self.rank_units = [
            [p, r + p, 2 * r + p, pairs[p][0], pairs[p][0] + 1, pairs[p][1], pairs[p][1] + 1]
            for p in range(r)
        ]
        self.back_units = [[p] + [g - 2 * r for g in self.rank_units[p][3:]] for p in range(r)]
        self.matchings = []
        left = {p: list(range(5)) for p in range(r)}
        own = lambda p, j: self.back_units[p][j] // 5
        for _ in range(5):
            match = {}

            def assign(p, seen):
                for j in left[p]:
                    c = own(p, j)
                    if c in seen:
                        continue
                    seen.add(c)
                    if c not in match or assign(match[c][0], seen):
                        match[c] = (p, j)
                        return True
                return False

            for p in range(r):
                assert assign(p, set())
            for c, (p, j) in match.items():
                left[p].remove(j)
            self.matchings.append(match)

    def device(self, z, k, f):
        return (2 * z + k) * self.fsdp + f


def pick(table, index):
    return jnp.asarray(np.asarray(table, np.int32))[index]


def normalize(values):
    values = values.astype(f32)
    centered = values - jnp.mean(values, axis=-1, keepdims=True)
    factor = lax.rsqrt(jnp.mean(centered * centered, axis=-1, keepdims=True) + norm_eps)
    return centered * factor, factor


def rotation_tables(positions, width):
    half = ROT // 2
    lane = np.arange(width) % HEAD_DIM
    frequency = jnp.power(
        10000.0, -2.0 * jnp.asarray(lane % half, f32) / ROT
    )
    angles = positions.astype(f32)[:, None] * frequency[None, :]
    rotated = jnp.asarray(lane < ROT)
    lower = jnp.asarray(lane < half)
    cosine = jnp.where(rotated, jnp.cos(angles), 1.0)
    sine = jnp.where(rotated, jnp.sin(angles), 0.0)
    return cosine, jnp.where(lower, -sine, 0.0), jnp.where(lower, 0.0, sine)


def rotate(values, tables):
    half = ROT // 2
    cosine, from_above, from_below = tables
    return (
        values * cosine
        + jnp.roll(values, -half, axis=1) * from_above
        + jnp.roll(values, half, axis=1) * from_below
    )


def rotate_back(values, tables):
    half = ROT // 2
    cosine, from_above, from_below = tables
    return (
        values * cosine
        + jnp.roll(values * from_above, half, axis=1)
        + jnp.roll(values * from_below, -half, axis=1)
    )


def attention_kernel(
    q_ref, k_ref, v_ref, g_ref, pos_q, pos_k, seg_q, seg_k, att_ref, dq_ref, dk_ref, dv_ref
):
    scale = HEAD_DIM ** (-0.5)
    width = q_ref.shape[1]

    @pl.when(pl.program_id(0) == 0)
    def _():
        dk_ref[...] = jnp.zeros_like(dk_ref)
        dv_ref[...] = jnp.zeros_like(dv_ref)

    allowed = (pos_k[...] <= pos_q[...]) & (seg_k[...] == seg_q[...])
    bias = jnp.where(allowed, 0.0, masked_score)
    last = (((1,), (1,)), ((), ()))
    first = (((0,), (0,)), ((), ()))
    for head in range(width // HEAD_DIM):
        cols = slice(head * HEAD_DIM, (head + 1) * HEAD_DIM)
        q, g = q_ref[:, cols], g_ref[:, cols]
        k, v = k_ref[:, cols], v_ref[:, cols]
        scores = lax.dot_general(q, k, last, preferred_element_type=f32) * scale + bias
        weights = jnp.exp(scores - jnp.max(scores, axis=1, keepdims=True))
        probs = weights * (1.0 / jnp.sum(weights, axis=1, keepdims=True))
        probs_low = probs.astype(bf16)
        out = jnp.dot(probs_low, v, preferred_element_type=f32)
        att_ref[:, cols] = out.astype(bf16)
        prob_grad = lax.dot_general(g, v, last, preferred_element_type=f32)
        delta = jnp.sum(g.astype(f32) * out, axis=1, keepdims=True)
        score_grad = (probs * (prob_grad - delta)).astype(bf16)
        dq_ref[:, cols] = jnp.dot(score_grad, k, preferred_element_type=f32) * scale
        dk_ref[:, cols] += lax.dot_general(score_grad, q, first, preferred_element_type=f32) * scale
        dv_ref[:, cols] += lax.dot_general(probs_low, g, first, preferred_element_type=f32)


def attention(query, key, value, grad, positions, segments):
    length, width = query.shape
    block = 256
    rows = pl.BlockSpec((block, width), lambda i: (i, 0))
    whole = pl.BlockSpec((length, width), lambda i: (0, 0))
    column = pl.BlockSpec((block, 1), lambda i: (i, 0))
    line = pl.BlockSpec((1, length), lambda i: (0, 0))
    return pl.pallas_call(
        attention_kernel,
        grid=(length // block,),
        in_specs=[rows, whole, whole, rows, column, line, column, line],
        out_specs=[rows, rows, whole, whole],
        out_shape=[
            jax.ShapeDtypeStruct((length, width), bf16),
            jax.ShapeDtypeStruct((length, width), f32),
            jax.ShapeDtypeStruct((length, width), f32),
            jax.ShapeDtypeStruct((length, width), f32),
        ],
        cost_estimate=pl.CostEstimate(
            flops=14 * length * length * width,
            transcendentals=length * length * width // HEAD_DIM,
            bytes_accessed=20 * length * width,
        ),
    )(query, key, value, grad, positions[:, None], positions[None], segments[:, None], segments[None])


MESH = pl.DeviceIdType.MESH


VMEM_BLOCK = pl.BlockSpec(memory_space=pltpu.VMEM)
ANY_BLOCK = pl.BlockSpec(memory_space=pl.ANY)


def busy(microseconds):
    return pl.CostEstimate(flops=int(microseconds * 900e6), transcendentals=0, bytes_accessed=0)


def place_in_mesh():
    c, f = lax.axis_index("ctx"), lax.axis_index("fsdp")
    z, k = lax.div(c, 2), lax.rem(c, 2)
    return c, f, z, k, 2 * f + k


def bounce(source, buffer, target, sem):
    one = pltpu.make_async_copy(source, buffer, sem)
    one.start()
    one.wait()
    two = pltpu.make_async_copy(buffer, target, sem)
    two.start()
    two.wait()


def gather_kernel(
    plan, tok, cot, doc, front, back, tok_out, cot_out, doc_out, w_out, b_out,
    w_buf, b_buf, tsend, trecv, csend, crecv, wsend, wrecv, rsend, rrecv, bsend, brecv, dsend, drecv, lsem,
):
    shards, unit, ranks = plan.fsdp, plan.unit, plan.ranks
    c, f, z, k, p = place_in_mesh()
    other = c + 1 - 2 * k
    width = D // shards
    both = ((tok, tok_out), (cot, cot_out))

    def cols(block):
        return pl.ds(pl.multiple_of(block * width, 128), width)

    def remote(src, dst, send, recv, device):
        return pltpu.make_async_remote_copy(
            src_ref=src, dst_ref=dst, send_sem=send, recv_sem=recv, device_id=device, device_id_type=MESH
        )

    def peer(step):
        return lax.rem(f + step, shards)

    def giver(step):
        return lax.rem(f + shards - step, shards)

    def send_tokens(n, step):
        src, out = both[n]
        return remote(src, out.at[f, k], tsend.at[n, step], trecv.at[n, step], (c, peer(step)))

    def get_tokens(n, step):
        here = both[n][1].at[giver(step), k]
        return remote(here, here, tsend.at[n, step], trecv.at[n, step], (c, peer(step)))

    def share(n, step):
        src, out = both[n]
        here = out.at[giver(step), k]
        return remote(src if step == 0 else here, here, csend.at[n, step], crecv.at[n, step], (other, f))

    def get_share(n, step):
        here = both[n][1].at[giver(step), 1 - k]
        return remote(here, here, csend.at[n, step], crecv.at[n, step], (other, f))

    def rows_of(dst):
        return pl.ds(pl.multiple_of((2 * dst + k) * unit, unit), unit)

    def send_back(step):
        return remote(
            back.at[rows_of(peer(step)), :], b_out.at[:, cols(f)], bsend.at[step], brecv.at[step], (c, peer(step))
        )

    def get_back(step):
        here = b_out.at[:, cols(giver(step))]
        return remote(here, here, bsend.at[step], brecv.at[step], (c, peer(step)))

    def send_doc(step):
        return remote(doc, doc_out, dsend.at[step], drecv, (c, peer(step)))

    start_weights, relay_weights, finish_weights = weight_moves(
        plan, front, w_out, w_buf, wsend, wrecv, rsend, rrecv, lsem.at[2]
    )
    own = [pltpu.make_async_copy(src, out.at[f, k], lsem.at[4 * n]) for n, (src, out) in enumerate(both)]
    own_doc = pltpu.make_async_copy(doc, doc_out, lsem.at[1])
    start_weights()
    for n in range(2):
        for step in range(1, shards):
            send_tokens(n, step).start()
        share(n, 0).start()
        own[n].start()
    for step in range(1, shards):
        send_back(step).start()

    @pl.when(f == z)
    def _():
        own_doc.start()
        for step in range(1, shards):
            send_doc(step).start()

    relay_weights()
    for n in range(2):
        for step in range(1, shards):
            get_tokens(n, step).wait_recv()
            share(n, step).start()
    bounce(back.at[rows_of(f), :], b_buf, b_out.at[:, cols(f)], lsem.at[3])
    for n in range(2):
        own[n].wait()

    @pl.when(f == z)
    def _():
        own_doc.wait()
        for step in range(1, shards):
            send_doc(step).wait_send()

    @pl.when(f != z)
    def _():
        send_doc(1).wait_recv()

    for n in range(2):
        for step in range(shards):
            get_share(n, step).wait_recv()
            share(n, step).wait_send()
        for step in range(1, shards):
            send_tokens(n, step).wait_send()
    for step in range(1, shards):
        send_back(step).wait_send()
        get_back(step).wait_recv()
    finish_weights()


def moves_between(moves, device_of):
    c, f, z, k, p = place_in_mesh()

    def remote(move):
        src, dst, source, target, send, recv, _, _ = move
        return pltpu.make_async_remote_copy(
            src_ref=source, dst_ref=target, send_sem=send, recv_sem=recv, device_id=device_of(c, dst), device_id_type=MESH
        )

    def start():
        for move in moves:
            if move[0] != move[1]:

                @pl.when(p == move[0])
                def _(move=move):
                    remote(move).start()

        for move in moves:
            if move[0] == move[1]:

                @pl.when(p == move[0])
                def _(move=move):
                    bounce(move[2], move[6], move[3], move[7])

    def finish():
        for move in moves:
            if move[0] != move[1]:

                @pl.when(p == move[0])
                def _(move=move):
                    remote(move).wait_send()

                @pl.when(p == move[1])
                def _(move=move):
                    remote(move).wait_recv()

    return start, finish


def weight_moves(plan, front, out, buffer, send, recv, relay_send, relay_recv, local):
    unit, moves, begin = plan.unit, [], 0
    c, f, z, k, p = place_in_mesh()
    half, parity = D // 2, lax.rem(z, 2)

    def rows(part):
        return pl.ds(pl.multiple_of(part * half, half), half)

    for slot, (units, wide) in enumerate(plan.slots):
        for dst in range(plan.ranks):
            src, at = units[dst] // plan.per_shard, units[dst] % plan.per_shard
            moves.append(
                (slot, 2 * src + dst % 2, dst, pl.ds(at * unit, wide * unit), pl.ds(begin * unit, wide * unit), wide * unit)
            )
        begin += wide

    def copy(move):
        slot, _, dst, source, target, _ = move
        return pltpu.make_async_remote_copy(
            src_ref=front.at[rows(parity), source],
            dst_ref=out.at[rows(parity), target],
            send_sem=send.at[slot, dst // 2],
            recv_sem=recv.at[slot],
            device_id=(c, dst // 2),
            device_id_type=MESH,
        )

    def pass_on(move, part):
        slot, _, _, _, target, _ = move
        here = out.at[rows(part), target]
        return pltpu.make_async_remote_copy(
            src_ref=here,
            dst_ref=here,
            send_sem=relay_send.at[slot],
            recv_sem=relay_recv.at[slot],
            device_id=(c + 2 - 4 * parity, f),
            device_id_type=MESH,
        )

    def start():
        for move in moves:
            if move[1] != move[2]:

                @pl.when(p == move[1])
                def _(move=move):
                    copy(move).start()

    def relay():
        for move in moves:
            if move[1] != move[2]:

                @pl.when(p == move[2])
                def _(move=move):
                    copy(move).wait_recv()
                    pass_on(move, parity).start()

    def finish():
        for move in moves:
            if move[1] == move[2]:

                @pl.when(p == move[2])
                def _(move=move):
                    bounce(front.at[:, move[3]], buffer.at[:, pl.ds(0, move[5])], out.at[:, move[4]], local)

        for move in moves:
            if move[1] != move[2]:

                @pl.when(p == move[1])
                def _(move=move):
                    copy(move).wait_send()

                @pl.when(p == move[2])
                def _(move=move):
                    pass_on(move, parity).wait_send()
                    pass_on(move, 1 - parity).wait_recv()

    return start, relay, finish


def back_moves(plan, back, out, buffer, send, recv, local):
    unit, width, moves = plan.unit, D // plan.fsdp, []
    for dst in range(plan.ranks):
        for src in range(plan.fsdp):
            for number in range(2):
                row = plan.back_units[dst][1 + 2 * number]
                moves.append(
                    (
                        2 * src + dst % 2,
                        dst,
                        back.at[pl.ds(row * unit, 2 * unit), :],
                        out.at[pl.ds(2 * number * unit, 2 * unit), pl.ds(src * width, width)],
                        send.at[number, dst // 2],
                        recv.at[number, src],
                        buffer,
                        local,
                    )
                )
    return moves_between(moves, lambda c, dst: (c, dst // 2))


def line_exchange(plan, src, out, send, recv, local):
    planes = plan.planes
    c, f, z, k, p = place_in_mesh()

    def copy(step):
        to = lax.rem(z + step, planes)
        return pltpu.make_async_remote_copy(
            src_ref=src.at[to],
            dst_ref=out.at[z],
            send_sem=send.at[step],
            recv_sem=recv.at[step],
            device_id=(2 * to + k, f),
            device_id_type=MESH,
        )

    def arrival(step):
        here = out.at[lax.rem(z + planes - step, planes)]
        return pltpu.make_async_remote_copy(
            src_ref=here,
            dst_ref=here,
            send_sem=send.at[step],
            recv_sem=recv.at[step],
            device_id=(2 * lax.rem(z + step, planes) + k, f),
            device_id_type=MESH,
        )

    keep = pltpu.make_async_copy(src.at[z], out.at[z], local)

    def start():
        for step in range(planes - 1, 0, -1):
            copy(step).start()
        keep.start()

    def finish():
        keep.wait()
        for step in range(1, planes):
            copy(step).wait_send()
            arrival(step).wait_recv()

    return start, finish


def gather_first(plan, tokens, cotangent, documents, front_weight, back_weight):
    shards, unit = plan.fsdp, plan.unit
    rows, length = tokens.shape[0], documents.shape[1]
    dma = pltpu.SemaphoreType.DMA
    return pl.pallas_call(
        functools.partial(gather_kernel, plan),
        in_specs=[VMEM_BLOCK] * 3 + [ANY_BLOCK] * 2,
        out_specs=[ANY_BLOCK] * 5,
        out_shape=[
            jax.ShapeDtypeStruct((shards, 2, rows, D), bf16),
            jax.ShapeDtypeStruct((shards, 2, rows, D), bf16),
            jax.ShapeDtypeStruct((1, length), f32),
            jax.ShapeDtypeStruct((D, 7 * unit), bf16),
            jax.ShapeDtypeStruct((unit, D), bf16),
        ],
        scratch_shapes=[
            pltpu.VMEM((D, 2 * unit), bf16),
            pltpu.VMEM((unit, D // shards), bf16),
            dma((2, shards)),
            dma((2, shards)),
            dma((2, shards)),
            dma((2, shards)),
            dma((5, shards)),
            dma((5,)),
            dma((5,)),
            dma((5,)),
            dma((shards,)),
            dma((shards,)),
            dma((shards,)),
            dma(()),
            dma((5,)),
        ],
        compiler_params=pltpu.CompilerParams(has_side_effects=True),
        cost_estimate=busy(130),
    )(tokens, cotangent, documents, front_weight, back_weight)


def tiles(rows, columns, tall, wide, first, last, body):
    across = columns // wide

    def one(i, carry):
        row = pl.multiple_of(lax.div(i, across) * tall, tall)
        column = pl.multiple_of(lax.rem(i, across) * wide, wide)
        body(row, column)
        return carry

    lax.fori_loop(first, last, one, 0)


def exchange_kernel(
    plan, src, normed, weight, bias, back, out, b_out, act, slope, buffer, send, recv, local, bsend, brecv
):
    unit = plan.unit
    start, finish = line_exchange(plan, src, out, send, recv, local.at[0])
    start_rows, finish_rows = back_moves(plan, back, b_out, buffer, bsend, brecv, local.at[1])
    start()
    start_rows()
    tall = 512

    def units(row, column):
        at, here = pl.ds(row, tall), pl.ds(column, unit)
        u = jnp.dot(
            normed[at, :],
            weight[:, pl.ds(pl.multiple_of(column + 3 * unit, unit), unit)],
            preferred_element_type=f32,
        )
        value, steep = gelu_parts(u + bias[:, here])
        act[at, here] = value.astype(bf16)
        slope[at, here] = steep

    tiles(act.shape[0], 4 * unit, tall, unit, 0, act.shape[0] // tall * 4, units)
    finish()
    finish_rows()


def exchange_first(plan, values, normed, weight, bias, back_weight):
    dma = pltpu.SemaphoreType.DMA
    unit, shards = plan.unit, plan.fsdp
    length = normed.shape[0]
    return pl.pallas_call(
        functools.partial(exchange_kernel, plan),
        in_specs=[VMEM_BLOCK] * 4 + [ANY_BLOCK],
        out_specs=[ANY_BLOCK, ANY_BLOCK, VMEM_BLOCK, VMEM_BLOCK],
        out_shape=[
            jax.ShapeDtypeStruct(values.shape, bf16),
            jax.ShapeDtypeStruct((4 * unit, D), bf16),
            jax.ShapeDtypeStruct((length, 4 * unit), bf16),
            jax.ShapeDtypeStruct((length, 4 * unit), f32),
        ],
        scratch_shapes=[
            pltpu.VMEM((2 * unit, D // shards), bf16),
            dma((plan.planes,)),
            dma((plan.planes,)),
            dma((2,)),
            dma((2, shards)),
            dma((2, shards)),
        ],
        compiler_params=pltpu.CompilerParams(has_side_effects=True),
        cost_estimate=busy(50),
    )(values, normed, weight, bias, back_weight)


def exchange_back_kernel(plan, src, grad, rows, slope, out, up_grad, send, recv, local):
    unit, tall = plan.unit, 512
    start, finish = line_exchange(plan, src, out, send, recv, local)
    start()

    def units(row, column):
        at, here = pl.ds(row, tall), pl.ds(column, unit)
        mixed_grad = lax.dot_general(
            grad[at, :], rows[here, :], (((1,), (1,)), ((), ())), preferred_element_type=f32
        )
        up_grad[at, here] = (mixed_grad * slope[at, here]).astype(bf16)

    tiles(grad.shape[0], 4 * unit, tall, unit, 0, grad.shape[0] // tall * 4, units)
    finish()


def exchange_back(plan, values, grad, rows, slope):
    dma = pltpu.SemaphoreType.DMA
    return pl.pallas_call(
        functools.partial(exchange_back_kernel, plan),
        in_specs=[VMEM_BLOCK] * 4,
        out_specs=[ANY_BLOCK, VMEM_BLOCK],
        out_shape=[
            jax.ShapeDtypeStruct(values.shape, bf16),
            jax.ShapeDtypeStruct(slope.shape, bf16),
        ],
        scratch_shapes=[dma((plan.planes,)), dma((plan.planes,)), dma(())],
        compiler_params=pltpu.CompilerParams(has_side_effects=True),
        cost_estimate=busy(50),
    )(values, grad, rows, slope)


def line_sum(plan, block, rising, falling, sends, gets, rows):
    planes, chunk = plan.planes, 64
    c, f, z, k, p = place_in_mesh()

    def copy(side, s, src):
        slots = (rising, falling)[side]
        return pltpu.make_async_remote_copy(
            src_ref=src,
            dst_ref=slots.at[s - 1],
            send_sem=sends.at[side, s - 1],
            recv_sem=gets.at[side, s - 1],
            device_id=(c + 2 - 4 * side, f),
            device_id_type=MESH,
        )

    def add(side, s, number):
        slots = (rising, falling)[side]
        term = block(number)

        def body(i, carry):
            at = pl.ds(pl.multiple_of(i * chunk, chunk), chunk)
            slots[s - 1, at, :] = (slots[s - 1, at, :].astype(f32) + term[at, :].astype(f32)).astype(bf16)
            return carry

        lax.fori_loop(0, rows // chunk, body, 0)

    def step(s):
        for side in range(2):
            place = z if side == 0 else planes - 1 - z
            number = planes - s + place
            number = number if side == 0 else planes - 1 - number

            @pl.when(place == 0)
            def _(side=side, number=number):
                copy(side, s, block(number)).start()

            if s > 1:

                @pl.when((place > 0) & (place < s) & (place < planes - 1))
                def _(side=side, number=number):
                    slots = (rising, falling)[side]
                    copy(side, s - 1, slots.at[s - 2]).wait_recv()
                    add(side, s - 1, number)
                    copy(side, s, slots.at[s - 2]).start()

    def finish(out):
        last = planes - 1
        for side in range(2):
            place = z if side == 0 else planes - 1 - z
            slots = (rising, falling)[side]

            @pl.when(place > 0)
            def _(side=side, slots=slots):
                copy(side, last, slots.at[last - 1]).wait_recv()

        mine = block(z)

        def total(ups, downs):
            def body(i, carry):
                at = pl.ds(pl.multiple_of(i * chunk, chunk), chunk)
                value = mine[at, :].astype(f32)
                if ups:
                    value = value + rising[last - 1, at, :].astype(f32)
                if downs:
                    value = value + falling[last - 1, at, :].astype(f32)
                out[at, :] = value.astype(out.dtype)
                return carry

            lax.fori_loop(0, rows // chunk, body, 0)

        @pl.when(z == 0)
        def _():
            total(False, True)

        @pl.when(z == planes - 1)
        def _():
            total(True, False)

        @pl.when((z > 0) & (z < planes - 1))
        def _():
            total(True, True)

        for side in range(2):
            place = z if side == 0 else planes - 1 - z
            slots = (rising, falling)[side]
            for s in range(1, planes):

                @pl.when((place < s) & (place < planes - 1))
                def _(side=side, slots=slots, s=s):
                    copy(side, s, slots.at[s - 1]).wait_send()

    return step, finish


def line_gather(plan, own, out, sends, gets, share_sends, share_gets, local, height):
    planes = plan.planes
    c, f, z, k, p = place_in_mesh()
    other = c + 1 - 2 * k

    def rows_of(plane, core):
        return out.at[pl.ds(pl.multiple_of((2 * plane + core) * height, height), height), :]

    def origin(side, s):
        return z - s if side == 0 else z + s

    def copy(side, s):
        plane = origin(side, s - 1)
        src = own if s == 1 else rows_of(plane, k)
        return pltpu.make_async_remote_copy(
            src_ref=src,
            dst_ref=rows_of(plane, k),
            send_sem=sends.at[side, s - 1],
            recv_sem=gets.at[side, s - 1],
            device_id=(c + 2 - 4 * side, f),
            device_id_type=MESH,
        )

    def arrival(side, s):
        here = rows_of(origin(side, s), k)
        return pltpu.make_async_remote_copy(
            src_ref=here,
            dst_ref=here,
            send_sem=sends.at[side, s - 1],
            recv_sem=gets.at[side, s - 1],
            device_id=(c + 2 - 4 * side, f),
            device_id_type=MESH,
        )

    def share(side, s, core):
        plane = origin(side, s)
        here = rows_of(plane, core)
        src = own if s == 0 else here
        return pltpu.make_async_remote_copy(
            src_ref=src,
            dst_ref=here,
            send_sem=share_sends.at[side, s],
            recv_sem=share_gets.at[side, s],
            device_id=(other, f),
            device_id_type=MESH,
        )

    keep = pltpu.make_async_copy(own, rows_of(z, k), local)

    def sends_at(side, s):
        place = z if side == 0 else planes - 1 - z
        return (place >= s - 1) & (place < planes - 1)

    def gets_at(side, s):
        place = z if side == 0 else planes - 1 - z
        return place >= s

    def take(s):
        for side in range(2):

            @pl.when(gets_at(side, s))
            def _(side=side):
                arrival(side, s).wait_recv()
                if s < planes - 1:

                    @pl.when(sends_at(side, s + 1))
                    def _():
                        copy(side, s + 1).start()

                share(side, s, k).start()

    def step(s):
        if s > 1:
            take(s - 1)
            return
        for side in range(2):

            @pl.when(sends_at(side, 1))
            def _(side=side):
                copy(side, 1).start()

        share(0, 0, k).start()
        keep.start()

    def finish():
        take(planes - 1)
        keep.wait()
        share(0, 0, k).wait_send()
        share(0, 0, 1 - k).wait_recv()
        for side in range(2):
            for s in range(1, planes):

                @pl.when(sends_at(side, s))
                def _(side=side, s=s):
                    copy(side, s).wait_send()

                @pl.when(gets_at(side, s))
                def _(side=side, s=s):
                    share(side, s, k).wait_send()
                    share(side, s, 1 - k).wait_recv()

    return step, finish


def back_owners(plan, src, out, send, recv, lsem):
    unit, ranks = plan.unit, plan.ranks
    c, f, z, k, p = place_in_mesh()

    def copy(j, owner, place):
        return pltpu.make_async_remote_copy(
            src_ref=src.at[pl.ds(j * unit, unit), :],
            dst_ref=out.at[pl.ds(place * unit, unit), :],
            send_sem=send.at[j],
            recv_sem=recv.at[place],
            device_id=(owner, z),
            device_id_type=MESH,
        )

    def local(j, place):
        return pltpu.make_async_copy(
            src.at[pl.ds(j * unit, unit), :], out.at[pl.ds(place * unit, unit), :], lsem.at[place]
        )

    blocks = [
        (rank, j, plan.back_units[rank][j] // 5, plan.back_units[rank][j] % 5)
        for rank in range(ranks)
        for j in range(5)
    ]

    def start():
        for rank, j, owner, place in blocks:

            @pl.when((p == rank) & ~((c == owner) & (f == z)))
            def _(j=j, owner=owner, place=place):
                copy(j, owner, place).start()

            @pl.when((p == rank) & (c == owner) & (f == z))
            def _(j=j, place=place):
                local(j, place).start()

    def finish():
        for rank, j, owner, place in blocks:

            @pl.when((p == rank) & ~((c == owner) & (f == z)))
            def _(j=j, owner=owner, place=place):
                copy(j, owner, place).wait_send()

            @pl.when((c == owner) & ~((p == rank) & (f == z)))
            def _(j=j, owner=owner, place=place):
                copy(j, owner, place).wait_recv()

            @pl.when((p == rank) & (c == owner) & (f == z))
            def _(j=j, place=place):
                local(j, place).wait()

    return start, finish


def front_owners(plan, src, out, send, recv, lsem):
    unit, ranks = plan.unit, plan.ranks
    c, f, z, k, p = place_in_mesh()
    height = src.shape[0] // 2
    moves, start_at = [], 0
    for slot, (units, wide) in enumerate(plan.slots):
        for rank in range(ranks):
            owner, place = units[rank] // plan.per_shard, units[rank] % plan.per_shard
            moves.append((slot, rank, owner, place, start_at, wide))
        start_at += wide

    def copy(slot, owner, place, begin, wide, half):
        return pltpu.make_async_remote_copy(
            src_ref=src.at[pl.ds(half * height, height), pl.ds(begin * unit, wide * unit)],
            dst_ref=out.at[:, pl.ds(place * unit, wide * unit)],
            send_sem=send.at[slot, half],
            recv_sem=recv.at[place],
            device_id=(2 * z + half, owner),
            device_id_type=MESH,
        )

    def local(place, begin, wide, half):
        return pltpu.make_async_copy(
            src.at[pl.ds(half * height, height), pl.ds(begin * unit, wide * unit)],
            out.at[:, pl.ds(place * unit, wide * unit)],
            lsem.at[place],
        )

    def start():
        for slot, rank, owner, place, begin, wide in moves:
            for half in range(2):
                if 2 * owner + half == rank:

                    @pl.when(p == rank)
                    def _(place=place, begin=begin, wide=wide, half=half):
                        local(place, begin, wide, half).start()

                else:

                    @pl.when(p == rank)
                    def _(slot=slot, owner=owner, place=place, begin=begin, wide=wide, half=half):
                        copy(slot, owner, place, begin, wide, half).start()

    def finish():
        for slot, rank, owner, place, begin, wide in moves:
            for half in range(2):
                if 2 * owner + half == rank:

                    @pl.when(p == rank)
                    def _(place=place, begin=begin, wide=wide, half=half):
                        local(place, begin, wide, half).wait()

                else:

                    @pl.when(p == rank)
                    def _(slot=slot, owner=owner, place=place, begin=begin, wide=wide, half=half):
                        copy(slot, owner, place, begin, wide, half).wait_send()

                    @pl.when(p == 2 * owner + half)
                    def _(slot=slot, owner=owner, place=place, begin=begin, wide=wide, half=half):
                        copy(slot, owner, place, begin, wide, half).wait_recv()

    return start, finish


def sum_scratch(plan, rows, columns):
    dma = pltpu.SemaphoreType.DMA
    steps = plan.planes - 1
    slots = pltpu.VMEM((steps, rows, columns), bf16)
    return [slots, slots, dma((2, steps)), dma((2, steps))]


def gather_scratch(plan):
    dma = pltpu.SemaphoreType.DMA
    return [dma((2, plan.planes - 1))] * 2 + [dma((2, plan.planes))] * 2 + [dma(())]


def back_sum_kernel(plan, width, src, normed, grad, out, partial, *scratch):
    unit, tall = plan.unit, 512

    def block(i):
        return src.at[:, pl.ds(pl.multiple_of(i * width, 128), width)]

    def term(row, column):
        here = pl.ds(column, unit)
        partial[pl.ds(row, tall), here] = lax.dot_general(
            normed[:, pl.ds(row, tall)], grad[:, here], (((0,), (0,)), ((), ())), preferred_element_type=f32
        ).astype(bf16)

    count = D // tall * 7
    step, finish = line_sum(plan, block, *scratch, src.shape[0])
    for s in range(1, plan.planes):
        step(s)
        tiles(
            D,
            7 * unit,
            tall,
            unit,
            count * (s - 1) // (plan.planes - 1),
            count * s // (plan.planes - 1),
            term,
        )
    finish(out)


def back_sums(plan, partial, normed, hidden_grad):
    rows, width = partial.shape[0], D // plan.planes
    return pl.pallas_call(
        functools.partial(back_sum_kernel, plan, width),
        in_specs=[VMEM_BLOCK] * 3,
        out_specs=[VMEM_BLOCK] * 2,
        out_shape=[
            jax.ShapeDtypeStruct((rows, width), bf16),
            jax.ShapeDtypeStruct((D, hidden_grad.shape[1]), bf16),
        ],
        scratch_shapes=sum_scratch(plan, rows, width),
        compiler_params=pltpu.CompilerParams(has_side_effects=True),
        cost_estimate=busy(90),
    )(partial, normed, hidden_grad)


def front_sum_kernel(plan, rows, src, back, out, owned, *scratch):
    start, done = back_owners(plan, back, owned, *scratch[:3])
    step, finish = line_sum(
        plan, lambda i: src.at[pl.ds(pl.multiple_of(i * rows, rows), rows), :], *scratch[3:], rows
    )
    step(1)
    start()
    for s in range(2, plan.planes):
        step(s)
    finish(out)
    done()


def front_sums(plan, partial, back_sum):
    dma = pltpu.SemaphoreType.DMA
    rows, width = partial.shape[0] // plan.planes, partial.shape[1]
    return pl.pallas_call(
        functools.partial(front_sum_kernel, plan, rows),
        in_specs=[VMEM_BLOCK, VMEM_BLOCK],
        out_specs=[VMEM_BLOCK, ANY_BLOCK],
        out_shape=[
            jax.ShapeDtypeStruct((rows, width), bf16),
            jax.ShapeDtypeStruct(back_sum.shape, bf16),
        ],
        scratch_shapes=[dma((5,))] * 3 + sum_scratch(plan, rows, width),
        compiler_params=pltpu.CompilerParams(has_side_effects=True),
        cost_estimate=busy(120),
    )(partial, back_sum)


def back_next_kernel(plan, own, src, out, owned, *scratch):
    start, done = front_owners(plan, src, owned, *scratch[:3])
    step, finish = line_gather(plan, own, out, *scratch[3:], own.shape[0])
    step(1)
    start()
    for s in range(2, plan.planes):
        step(s)
    finish()
    done()


def back_nexts(plan, own, front_sum):
    dma = pltpu.SemaphoreType.DMA
    return pl.pallas_call(
        functools.partial(back_next_kernel, plan),
        in_specs=[VMEM_BLOCK, VMEM_BLOCK],
        out_specs=[ANY_BLOCK, ANY_BLOCK],
        out_shape=[
            jax.ShapeDtypeStruct((2 * plan.planes * own.shape[0], own.shape[1]), bf16),
            jax.ShapeDtypeStruct((front_sum.shape[0] // 2, plan.per_shard * plan.unit), bf16),
        ],
        scratch_shapes=[dma((5, 2)), dma((plan.per_shard,)), dma((plan.per_shard,))] + gather_scratch(plan),
        compiler_params=pltpu.CompilerParams(has_side_effects=True),
        cost_estimate=busy(90),
    )(own, front_sum)


def vector_sum(plan, own, out, terms, sums, send, recv):
    planes, ranks = plan.planes, plan.ranks
    c, f, z, k, p = place_in_mesh()

    def in_plane(step, target):
        to = lax.rem(p + step, ranks)
        return pltpu.make_async_remote_copy(
            src_ref=own,
            dst_ref=terms.at[target],
            send_sem=send.at[step],
            recv_sem=recv.at[step],
            device_id=(2 * z + lax.rem(to, 2), lax.div(to, 2)),
            device_id_type=MESH,
        )

    def over_planes(step, target):
        to = lax.rem(z + step, planes)
        return pltpu.make_async_remote_copy(
            src_ref=out,
            dst_ref=sums.at[target],
            send_sem=send.at[ranks + step],
            recv_sem=recv.at[ranks + step],
            device_id=(2 * to + k, f),
            device_id_type=MESH,
        )

    def start():
        for step in range(1, ranks):
            in_plane(step, p).start()
        terms[p] = own[...]

    def middle():
        for step in range(1, ranks):
            in_plane(step, lax.rem(p + ranks - step, ranks)).wait_recv()
        total = terms[0]
        for rank in range(1, ranks):
            total = total + terms[rank]
        out[...] = total
        sums[z] = total
        for step in range(1, planes):
            over_planes(step, z).start()

    def finish():
        for step in range(1, ranks):
            in_plane(step, p).wait_send()
        for step in range(1, planes):
            over_planes(step, z).wait_send()
            over_planes(step, lax.rem(z + planes - step, planes)).wait_recv()
        total = sums[0]
        for plane in range(1, planes):
            total = total + sums[plane]
        out[...] = total

    return start, middle, finish


def front_next_kernel(plan, own, vector, out, vector_out, terms, sums, vsend, vrecv, *scratch):
    begin, middle, end = vector_sum(plan, vector, vector_out, terms, sums, vsend, vrecv)
    step, finish = line_gather(plan, own, out, *scratch, own.shape[0])
    begin()
    step(1)
    middle()
    for s in range(2, plan.planes):
        step(s)
    finish()
    end()


def front_nexts(plan, own, vector):
    dma = pltpu.SemaphoreType.DMA
    return pl.pallas_call(
        functools.partial(front_next_kernel, plan),
        in_specs=[VMEM_BLOCK, VMEM_BLOCK],
        out_specs=[ANY_BLOCK, VMEM_BLOCK],
        out_shape=[
            jax.ShapeDtypeStruct((2 * plan.planes * own.shape[0], own.shape[1]), bf16),
            jax.ShapeDtypeStruct(vector.shape, f32),
        ],
        scratch_shapes=[
            pltpu.VMEM((plan.ranks,) + vector.shape, f32),
            pltpu.VMEM((plan.planes,) + vector.shape, f32),
            dma((plan.ranks + plan.planes,)),
            dma((plan.ranks + plan.planes,)),
        ]
        + gather_scratch(plan),
        compiler_params=pltpu.CompilerParams(has_side_effects=True),
        cost_estimate=busy(120),
    )(own, vector)


def gelu_parts(u):
    scale = np.float32(np.sqrt(2.0 / np.pi))
    square = u * u
    inner = scale * u * (1.0 + 0.044715 * square)
    t = jnp.tanh(inner)
    value = 0.5 * u * (1.0 + t)
    slope = 0.5 * (1.0 + t) + 0.5 * u * (1.0 - t * t) * scale * (1.0 + 3 * 0.044715 * square)
    return value, slope


def adam_update(weight, first, second, grad, rate, count_now, decay):
    first_new = beta_first * first + (1.0 - beta_first) * grad
    second_new = beta_second * second + (1.0 - beta_second) * grad * grad
    steps_float = count_now.astype(f32)
    first_fix = 1.0 - jnp.power(beta_first, steps_float)
    second_fix = 1.0 - jnp.power(beta_second, steps_float)
    change = first_new / first_fix / (jnp.sqrt(second_new / second_fix) + adam_eps) + decay * weight
    return (weight - rate * change, first_new, second_new)


def after(value, *others):
    return lax.optimization_barrier((value,) + others)[0]


def per_device(
    tokens,
    cotangent,
    doc_ids,
    block_order,
    front_weight,
    back_weight,
    front_master,
    back_master,
    front_first,
    back_first,
    front_second,
    back_second,
    vectors,
    vector_first,
    vector_second,
    learn_rates,
    adam_step,
    *,
    plan,
):
    planes, shards, ranks, unit = plan.planes, plan.fsdp, plan.ranks, plan.unit
    both = ("ctx", "fsdp")
    contract_last = (((1,), (1,)), ((), ()))
    contract_first = (((0,), (0,)), ((), ()))
    c_index, f = lax.axis_index("ctx"), lax.axis_index("fsdp")
    z, k = c_index // 2, c_index % 2
    p = 2 * f + k
    rows = tokens.shape[1]
    plane_rows = 2 * shards * rows
    share = 2 * rows

    bias_front = vectors[:IN_COLS].reshape(-1, unit)
    bias_back = vectors[IN_COLS : IN_COLS + D]
    norm_gain = vectors[IN_COLS + D : IN_COLS + 2 * D]
    norm_shift = vectors[IN_COLS + 2 * D :]

    swap_pairs = [(2 * i + j, 2 * i + 1 - j) for i in range(planes) for j in range(2)]

    def swap_core(value):
        return lax.ppermute(value, "ctx", swap_pairs)

    def to_shard(value, step):
        return lax.ppermute(value, "fsdp", [(i, i ^ step) for i in range(shards)])

    def at(array, index):
        return lax.dynamic_index_in_dim(array, index, 0, keepdims=False)

    blocks = block_order.shape[0]
    block_tokens = doc_ids.shape[1] // blocks
    offsets = jnp.arange(block_tokens, dtype=jnp.int32)
    positions_all = (block_order[:, None] * block_tokens + offsets[None, :]).reshape(planes, share)
    own_positions = at(positions_all, z)
    plane_positions = jnp.tile(own_positions, shards)

    plane_tokens, plane_grad, documents, weight_local, back_attention = gather_first(
        plan, tokens[0], cotangent[0], doc_ids.astype(f32), front_weight, back_weight
    )
    plane_tokens = plane_tokens.reshape(plane_rows, D)
    plane_grad = plane_grad.reshape(plane_rows, D)

    normed = (normalize(plane_tokens)[0] * norm_gain + norm_shift).astype(bf16)

    unit_table = pick(plan.rank_units, p)
    bias_local = jnp.take(bias_front, unit_table, axis=0).reshape(-1)

    hidden = jnp.dot(normed, weight_local[:, : 3 * unit], preferred_element_type=f32) + bias_local[: 3 * unit]
    tables = rotation_tables(plane_positions, unit)
    query = rotate(hidden[:, :unit], tables).astype(bf16)
    key = rotate(hidden[:, unit : 2 * unit], tables).astype(bf16)
    attended_grad = lax.dot_general(
        plane_grad, back_attention, contract_last, preferred_element_type=f32
    ).astype(bf16)
    qkvg = jnp.concatenate([query, key, hidden[:, 2 * unit :].astype(bf16), attended_grad], axis=1)
    qkvg, back_up, activation, slope = exchange_first(
        plan, qkvg.reshape(planes, share, -1), normed, weight_local, bias_local[None, 3 * unit :], back_weight
    )
    qkvg = qkvg.reshape(planes * share, -1)

    seq_positions = positions_all.reshape(-1)
    doc_row = documents[0].astype(jnp.int32)
    seq_documents = jnp.take(doc_row.reshape(blocks, block_tokens), block_order, axis=0).reshape(-1)
    attended, query_grad, key_grad, value_grad = attention(
        qkvg[:, :unit],
        qkvg[:, unit : 2 * unit],
        qkvg[:, 2 * unit : 3 * unit],
        qkvg[:, 3 * unit :],
        seq_positions,
        seq_documents,
    )
    seq_tables = rotation_tables(seq_positions, unit)
    returned = jnp.concatenate(
        [
            attended,
            rotate_back(query_grad, seq_tables).astype(bf16),
            rotate_back(key_grad, seq_tables).astype(bf16),
            value_grad.astype(bf16),
        ],
        axis=1,
    )
    returned, up_grad = exchange_back(
        plan, returned.reshape(planes, share, -1), plane_grad, back_up, slope
    )
    returned = returned.reshape(plane_rows, -1)
    back_local = jnp.concatenate([back_attention, back_up], axis=0)

    mixed = jnp.concatenate([returned[:, :unit], activation], axis=1)
    hidden_grad = jnp.concatenate([returned[:, unit:], up_grad], axis=1)

    def sum_over_cores(value):
        shaped = value.reshape(shards, 2, rows, D)
        kept = lax.dynamic_index_in_dim(shaped, k, 1, keepdims=False)
        sent = lax.dynamic_index_in_dim(shaped, 1 - k, 1, keepdims=False).astype(bf16)
        return kept + swap_core(sent).astype(f32)

    def sum_over_shards(*values):
        totals = [at(value, f) for value in values]
        for step in range(1, shards):
            pieces = jnp.stack([at(value, f ^ step).astype(bf16) for value in values])
            pieces = to_shard(pieces, step).astype(f32)
            totals = [total + piece for total, piece in zip(totals, pieces)]
        return totals

    projected_cores = sum_over_cores(jnp.dot(mixed, back_local, preferred_element_type=f32))
    normed_grad_cores = sum_over_cores(
        lax.dot_general(hidden_grad, weight_local, contract_last, preferred_element_type=f32)
    )

    back_partial = lax.dot_general(
        mixed, plane_grad, contract_first, preferred_element_type=f32
    ).astype(bf16)
    back_sum, front_partial = back_sums(plan, back_partial, normed, hidden_grad)
    back_sum, projected_cores, normed_grad_cores = lax.optimization_barrier(
        (back_sum, projected_cores, normed_grad_cores)
    )
    projected, normed_grad = sum_over_shards(projected_cores, normed_grad_cores)
    front_sum, back_owned = front_sums(plan, front_partial, back_sum)
    front_sum, projected, normed_grad = lax.optimization_barrier((front_sum, projected, normed_grad))

    inputs = tokens[0].astype(f32)
    layer_out = (inputs + projected + bias_back).astype(bf16)[None]
    unscaled, factor = normalize(inputs)
    scaled = normed_grad * norm_gain
    input_grad = factor * (
        scaled
        - jnp.mean(scaled, axis=-1, keepdims=True)
        - unscaled * jnp.mean(scaled * unscaled, axis=-1, keepdims=True)
    )
    tokens_grad = (cotangent[0].astype(f32) + input_grad).astype(bf16)[None]

    back_grad = back_owned.astype(f32)
    back_new, back_first_new, back_second_new = adam_update(
        back_master, back_first, back_second, back_grad, learn_rates[1], adam_step[0], weight_decay
    )
    back_next, front_owned = back_nexts(plan, back_new.astype(bf16), front_sum)
    front_grad = front_owned.astype(f32)
    front_new, front_first_new, front_second_new = adam_update(
        front_master, front_first, front_second, front_grad, learn_rates[0], adam_step[0], weight_decay
    )
    def column_sums(value):
        ones = jnp.ones((8, value.shape[0]), bf16)
        return jnp.dot(ones, value, preferred_element_type=f32)[0]

    spread = (jnp.arange(7 * ranks)[:, None] == unit_table[None, :]).astype(f32)
    hidden_sum = column_sums(hidden_grad).reshape(7, unit)
    front_vector = jnp.sum(spread[:, :, None] * hidden_sum[None], axis=1).reshape(-1)
    vector_term = jnp.concatenate(
        [
            front_vector,
            column_sums(cotangent[0]),
            jnp.sum(normed_grad * unscaled, axis=0),
            jnp.sum(normed_grad, axis=0),
        ]
    )
    front_next, vector_grad = front_nexts(plan, front_new.astype(bf16), vector_term.reshape(-1, 128))
    vector_grad = vector_grad.reshape(-1)

    count_now = adam_step[0]
    vectors_new, vector_first_new, vector_second_new = adam_update(
        vectors, vector_first, vector_second, vector_grad, learn_rates[2], count_now, 0.0
    )

    return (
        layer_out,
        tokens_grad,
        front_grad,
        back_grad,
        vector_grad,
        front_new,
        back_new,
        vectors_new,
        front_first_new,
        back_first_new,
        vector_first_new,
        front_second_new,
        back_second_new,
        vector_second_new,
        front_next,
        back_next,
    )


def solution(mesh):
    plan = Layout(mesh.shape["ctx"], mesh.shape["fsdp"])
    tokens_spec = P("fsdp", "ctx", None)
    cols, owned, same = P(None, "fsdp"), P("ctx", "fsdp"), P()
    in_specs = (
        (tokens_spec, tokens_spec, P("fsdp", None), same, cols, cols)
        + (owned,) * 6
        + (same,) * 5
    )
    out_specs = (
        (tokens_spec, tokens_spec, owned, owned, same)
        + (owned, owned, same) * 3
        + (cols, cols)
    )
    return jax.shard_map(
        functools.partial(per_device, plan=plan),
        mesh=mesh,
        in_specs=in_specs,
        out_specs=out_specs,
        check_vma=False,
    )
```

```python
import functools

import jax
import jax.numpy as jnp
import numpy as np
from jax import lax
from jax.experimental import pallas as pl
from jax.experimental.pallas import tpu as pltpu
from jax.sharding import PartitionSpec as P

D = 2048
HEADS = 32
FF = 8192
ROT = 32
HEAD_DIM = 64
IN_COLS = 14336
BACK_ROWS = 10240

norm_eps = 1e-05
beta_first = 0.9
beta_second = 0.95
adam_eps = 1e-08
weight_decay = 0.1
masked_score = -1e30
bf16 = jnp.bfloat16
f32 = jnp.float32


class Layout:
    def __init__(self, ctx, fsdp):
        self.ctx, self.fsdp, self.planes, self.ranks = ctx, fsdp, ctx // 2, 2 * fsdp
        assert ctx % 2 == 0 and self.planes == fsdp
        self.unit = D // self.ranks
        self.per_shard = IN_COLS // self.unit // fsdp
        r = self.ranks
        first_up = 3 * r
        home = {f: [] for f in range(fsdp)}
        for g in range(first_up, 7 * r, 2):
            assert g // self.per_shard == (g + 1) // self.per_shard
            home[g // self.per_shard].append(g)
        pairs = {p: [None, None] for p in range(r)}
        for f in range(fsdp):
            if len(home[f]) >= 4:
                keep, home[f] = home[f][:4], home[f][4:]
                pairs[2 * f], pairs[2 * f + 1] = keep[:2], keep[2:]
            elif home[f]:
                keep, home[f] = home[f], []
                for i, g in enumerate(keep):
                    pairs[2 * f + i % 2][(i + i // 2) % 2] = g
        for s in range(2):
            for k in range(2):
                used = set()
                for f in range(fsdp):
                    p = 2 * f + k
                    if pairs[p][s] is not None:
                        continue
                    options = sorted(
                        (h for h in range(fsdp) if home[h]),
                        key=lambda h: (h in used, bin(h ^ f).count("1"), -len(home[h])),
                    )
                    used.add(options[0])
                    pairs[p][s] = home[options[0]].pop(0)
        self.pairs = pairs
        self.slots = [
            ([p for p in range(r)], 1),
            ([r + p for p in range(r)], 1),
            ([2 * r + p for p in range(r)], 1),
            ([pairs[p][0] for p in range(r)], 2),
            ([pairs[p][1] for p in range(r)], 2),
        ]
        self.rounds = []
        for units, _ in self.slots:
            rounds = []
            for k in range(2):
                for f in range(fsdp):
                    src = units[2 * f + k] // self.per_shard
                    if src == f:
                        continue
                    for one in rounds:
                        if all((src, k) != (a, c) for a, _, c in one):
                            one.append((src, f, k))
                            break
                    else:
                        rounds.append([(src, f, k)])
            self.rounds.append(rounds)
        self.rank_units = [
            [p, r + p, 2 * r + p, pairs[p][0], pairs[p][0] + 1, pairs[p][1], pairs[p][1] + 1]
            for p in range(r)
        ]
        self.back_units = [[p] + [g - 2 * r for g in self.rank_units[p][3:]] for p in range(r)]
        self.matchings = []
        left = {p: list(range(5)) for p in range(r)}
        own = lambda p, j: self.back_units[p][j] // 5
        for _ in range(5):
            match = {}

            def assign(p, seen):
                for j in left[p]:
                    c = own(p, j)
                    if c in seen:
                        continue
                    seen.add(c)
                    if c not in match or assign(match[c][0], seen):
                        match[c] = (p, j)
                        return True
                return False

            for p in range(r):
                assert assign(p, set())
            for c, (p, j) in match.items():
                left[p].remove(j)
            self.matchings.append(match)

    def device(self, z, k, f):
        return (2 * z + k) * self.fsdp + f


def pick(table, index):
    return jnp.asarray(np.asarray(table, np.int32))[index]


def normalize(values):
    values = values.astype(f32)
    centered = values - jnp.mean(values, axis=-1, keepdims=True)
    factor = lax.rsqrt(jnp.mean(centered * centered, axis=-1, keepdims=True) + norm_eps)
    return centered * factor, factor


def rotation_tables(positions, width):
    half = ROT // 2
    lane = np.arange(width) % HEAD_DIM
    frequency = jnp.power(
        10000.0, -2.0 * jnp.asarray(lane % half, f32) / ROT
    )
    angles = positions.astype(f32)[:, None] * frequency[None, :]
    rotated = jnp.asarray(lane < ROT)
    lower = jnp.asarray(lane < half)
    cosine = jnp.where(rotated, jnp.cos(angles), 1.0)
    sine = jnp.where(rotated, jnp.sin(angles), 0.0)
    return cosine, jnp.where(lower, -sine, 0.0), jnp.where(lower, 0.0, sine)


def rotate(values, tables):
    half = ROT // 2
    cosine, from_above, from_below = tables
    return (
        values * cosine
        + jnp.roll(values, -half, axis=1) * from_above
        + jnp.roll(values, half, axis=1) * from_below
    )


def rotate_back(values, tables):
    half = ROT // 2
    cosine, from_above, from_below = tables
    return (
        values * cosine
        + jnp.roll(values * from_above, half, axis=1)
        + jnp.roll(values * from_below, -half, axis=1)
    )


def attention_kernel(
    q_ref, k_ref, v_ref, g_ref, pos_q, pos_k, seg_q, seg_k, att_ref, dq_ref, dk_ref, dv_ref
):
    scale = HEAD_DIM ** (-0.5)
    width = q_ref.shape[1]

    @pl.when(pl.program_id(0) == 0)
    def _():
        dk_ref[...] = jnp.zeros_like(dk_ref)
        dv_ref[...] = jnp.zeros_like(dv_ref)

    allowed = (pos_k[...] <= pos_q[...]) & (seg_k[...] == seg_q[...])
    bias = jnp.where(allowed, 0.0, masked_score)
    last = (((1,), (1,)), ((), ()))
    first = (((0,), (0,)), ((), ()))
    for head in range(width // HEAD_DIM):
        cols = slice(head * HEAD_DIM, (head + 1) * HEAD_DIM)
        q, g = q_ref[:, cols], g_ref[:, cols]
        k, v = k_ref[:, cols], v_ref[:, cols]
        scores = lax.dot_general(q, k, last, preferred_element_type=f32) * scale + bias
        weights = jnp.exp(scores - jnp.max(scores, axis=1, keepdims=True))
        probs = weights * (1.0 / jnp.sum(weights, axis=1, keepdims=True))
        probs_low = probs.astype(bf16)
        out = jnp.dot(probs_low, v, preferred_element_type=f32)
        att_ref[:, cols] = out.astype(bf16)
        prob_grad = lax.dot_general(g, v, last, preferred_element_type=f32)
        delta = jnp.sum(g.astype(f32) * out, axis=1, keepdims=True)
        score_grad = (probs * (prob_grad - delta)).astype(bf16)
        dq_ref[:, cols] = jnp.dot(score_grad, k, preferred_element_type=f32) * scale
        dk_ref[:, cols] += lax.dot_general(score_grad, q, first, preferred_element_type=f32) * scale
        dv_ref[:, cols] += lax.dot_general(probs_low, g, first, preferred_element_type=f32)


def attention(query, key, value, grad, positions, segments):
    length, width = query.shape
    block = 256
    rows = pl.BlockSpec((block, width), lambda i: (i, 0))
    whole = pl.BlockSpec((length, width), lambda i: (0, 0))
    column = pl.BlockSpec((block, 1), lambda i: (i, 0))
    line = pl.BlockSpec((1, length), lambda i: (0, 0))
    return pl.pallas_call(
        attention_kernel,
        grid=(length // block,),
        in_specs=[rows, whole, whole, rows, column, line, column, line],
        out_specs=[rows, rows, whole, whole],
        out_shape=[
            jax.ShapeDtypeStruct((length, width), bf16),
            jax.ShapeDtypeStruct((length, width), f32),
            jax.ShapeDtypeStruct((length, width), f32),
            jax.ShapeDtypeStruct((length, width), f32),
        ],
        cost_estimate=pl.CostEstimate(
            flops=14 * length * length * width,
            transcendentals=length * length * width // HEAD_DIM,
            bytes_accessed=20 * length * width,
        ),
    )(query, key, value, grad, positions[:, None], positions[None], segments[:, None], segments[None])


MESH = pl.DeviceIdType.MESH


VMEM_BLOCK = pl.BlockSpec(memory_space=pltpu.VMEM)
ANY_BLOCK = pl.BlockSpec(memory_space=pl.ANY)


def busy(microseconds):
    return pl.CostEstimate(flops=int(microseconds * 900e6), transcendentals=0, bytes_accessed=0)


def place_in_mesh():
    c, f = lax.axis_index("ctx"), lax.axis_index("fsdp")
    z, k = lax.div(c, 2), lax.rem(c, 2)
    return c, f, z, k, 2 * f + k


def bounce(source, buffer, target, sem):
    one = pltpu.make_async_copy(source, buffer, sem)
    one.start()
    one.wait()
    two = pltpu.make_async_copy(buffer, target, sem)
    two.start()
    two.wait()


def gather_kernel(
    plan, tok, cot, doc, front, back, tok_out, cot_out, doc_out, w_out, b_out,
    w_buf, b_buf, tsend, trecv, csend, crecv, wsend, wrecv, rsend, rrecv, bsend, brecv, dsend, drecv, lsem,
):
    shards, unit, ranks = plan.fsdp, plan.unit, plan.ranks
    c, f, z, k, p = place_in_mesh()
    other = c + 1 - 2 * k
    width = D // shards
    both = ((tok, tok_out), (cot, cot_out))

    def cols(block):
        return pl.ds(pl.multiple_of(block * width, 128), width)

    def remote(src, dst, send, recv, device):
        return pltpu.make_async_remote_copy(
            src_ref=src, dst_ref=dst, send_sem=send, recv_sem=recv, device_id=device, device_id_type=MESH
        )

    def peer(step):
        return lax.rem(f + step, shards)

    def giver(step):
        return lax.rem(f + shards - step, shards)

    def send_tokens(n, step):
        src, out = both[n]
        return remote(src, out.at[f, k], tsend.at[n, step], trecv.at[n, step], (c, peer(step)))

    def get_tokens(n, step):
        here = both[n][1].at[giver(step), k]
        return remote(here, here, tsend.at[n, step], trecv.at[n, step], (c, peer(step)))

    def share(n, step):
        src, out = both[n]
        here = out.at[giver(step), k]
        return remote(src if step == 0 else here, here, csend.at[n, step], crecv.at[n, step], (other, f))

    def get_share(n, step):
        here = both[n][1].at[giver(step), 1 - k]
        return remote(here, here, csend.at[n, step], crecv.at[n, step], (other, f))

    def rows_of(dst):
        return pl.ds(pl.multiple_of((2 * dst + k) * unit, unit), unit)

    def send_back(step):
        return remote(
            back.at[rows_of(peer(step)), :], b_out.at[:, cols(f)], bsend.at[step], brecv.at[step], (c, peer(step))
        )

    def get_back(step):
        here = b_out.at[:, cols(giver(step))]
        return remote(here, here, bsend.at[step], brecv.at[step], (c, peer(step)))

    def send_doc(step):
        return remote(doc, doc_out, dsend.at[step], drecv, (c, peer(step)))

    start_weights, relay_weights, finish_weights = weight_moves(
        plan, front, w_out, w_buf, wsend, wrecv, rsend, rrecv, lsem.at[2]
    )
    own = [pltpu.make_async_copy(src, out.at[f, k], lsem.at[4 * n]) for n, (src, out) in enumerate(both)]
    own_doc = pltpu.make_async_copy(doc, doc_out, lsem.at[1])
    start_weights()
    for n in range(2):
        for step in range(1, shards):
            send_tokens(n, step).start()
        share(n, 0).start()
        own[n].start()
    for step in range(1, shards):
        send_back(step).start()

    @pl.when(f == z)
    def _():
        own_doc.start()
        for step in range(1, shards):
            send_doc(step).start()

    relay_weights()
    for n in range(2):
        for step in range(1, shards):
            get_tokens(n, step).wait_recv()
            share(n, step).start()
    bounce(back.at[rows_of(f), :], b_buf, b_out.at[:, cols(f)], lsem.at[3])
    for n in range(2):
        own[n].wait()

    @pl.when(f == z)
    def _():
        own_doc.wait()
        for step in range(1, shards):
            send_doc(step).wait_send()

    @pl.when(f != z)
    def _():
        send_doc(1).wait_recv()

    for n in range(2):
        for step in range(shards):
            get_share(n, step).wait_recv()
            share(n, step).wait_send()
        for step in range(1, shards):
            send_tokens(n, step).wait_send()
    for step in range(1, shards):
        send_back(step).wait_send()
        get_back(step).wait_recv()
    finish_weights()


def moves_between(moves, device_of):
    c, f, z, k, p = place_in_mesh()

    def remote(move):
        src, dst, source, target, send, recv, _, _ = move
        return pltpu.make_async_remote_copy(
            src_ref=source, dst_ref=target, send_sem=send, recv_sem=recv, device_id=device_of(c, dst), device_id_type=MESH
        )

    def start():
        for move in moves:
            if move[0] != move[1]:

                @pl.when(p == move[0])
                def _(move=move):
                    remote(move).start()

        for move in moves:
            if move[0] == move[1]:

                @pl.when(p == move[0])
                def _(move=move):
                    bounce(move[2], move[6], move[3], move[7])

    def finish():
        for move in moves:
            if move[0] != move[1]:

                @pl.when(p == move[0])
                def _(move=move):
                    remote(move).wait_send()

                @pl.when(p == move[1])
                def _(move=move):
                    remote(move).wait_recv()

    return start, finish


def weight_moves(plan, front, out, buffer, send, recv, relay_send, relay_recv, local):
    unit, moves, begin = plan.unit, [], 0
    c, f, z, k, p = place_in_mesh()
    half, parity = D // 2, lax.rem(z, 2)

    def rows(part):
        return pl.ds(pl.multiple_of(part * half, half), half)

    for slot, (units, wide) in enumerate(plan.slots):
        for dst in range(plan.ranks):
            src, at = units[dst] // plan.per_shard, units[dst] % plan.per_shard
            moves.append(
                (slot, 2 * src + dst % 2, dst, pl.ds(at * unit, wide * unit), pl.ds(begin * unit, wide * unit), wide * unit)
            )
        begin += wide

    def copy(move):
        slot, _, dst, source, target, _ = move
        return pltpu.make_async_remote_copy(
            src_ref=front.at[rows(parity), source],
            dst_ref=out.at[rows(parity), target],
            send_sem=send.at[slot, dst // 2],
            recv_sem=recv.at[slot],
            device_id=(c, dst // 2),
            device_id_type=MESH,
        )

    def pass_on(move, part):
        slot, _, _, _, target, _ = move
        here = out.at[rows(part), target]
        return pltpu.make_async_remote_copy(
            src_ref=here,
            dst_ref=here,
            send_sem=relay_send.at[slot],
            recv_sem=relay_recv.at[slot],
            device_id=(c + 2 - 4 * parity, f),
            device_id_type=MESH,
        )

    def start():
        for move in moves:
            if move[1] != move[2]:

                @pl.when(p == move[1])
                def _(move=move):
                    copy(move).start()

    def relay():
        for move in moves:
            if move[1] != move[2]:

                @pl.when(p == move[2])
                def _(move=move):
                    copy(move).wait_recv()
                    pass_on(move, parity).start()

    def finish():
        for move in moves:
            if move[1] == move[2]:

                @pl.when(p == move[2])
                def _(move=move):
                    bounce(front.at[:, move[3]], buffer.at[:, pl.ds(0, move[5])], out.at[:, move[4]], local)

        for move in moves:
            if move[1] != move[2]:

                @pl.when(p == move[1])
                def _(move=move):
                    copy(move).wait_send()

                @pl.when(p == move[2])
                def _(move=move):
                    pass_on(move, parity).wait_send()
                    pass_on(move, 1 - parity).wait_recv()

    return start, relay, finish


def back_moves(plan, back, out, buffer, send, recv, local):
    unit, width, moves = plan.unit, D // plan.fsdp, []
    for dst in range(plan.ranks):
        for src in range(plan.fsdp):
            for number in range(2):
                row = plan.back_units[dst][1 + 2 * number]
                moves.append(
                    (
                        2 * src + dst % 2,
                        dst,
                        back.at[pl.ds(row * unit, 2 * unit), :],
                        out.at[pl.ds(2 * number * unit, 2 * unit), pl.ds(src * width, width)],
                        send.at[number, dst // 2],
                        recv.at[number, src],
                        buffer,
                        local,
                    )
                )
    return moves_between(moves, lambda c, dst: (c, dst // 2))


def line_exchange(plan, src, out, send, recv, local):
    planes = plan.planes
    c, f, z, k, p = place_in_mesh()

    def copy(step):
        to = lax.rem(z + step, planes)
        return pltpu.make_async_remote_copy(
            src_ref=src.at[to],
            dst_ref=out.at[z],
            send_sem=send.at[step],
            recv_sem=recv.at[step],
            device_id=(2 * to + k, f),
            device_id_type=MESH,
        )

    def arrival(step):
        here = out.at[lax.rem(z + planes - step, planes)]
        return pltpu.make_async_remote_copy(
            src_ref=here,
            dst_ref=here,
            send_sem=send.at[step],
            recv_sem=recv.at[step],
            device_id=(2 * lax.rem(z + step, planes) + k, f),
            device_id_type=MESH,
        )

    keep = pltpu.make_async_copy(src.at[z], out.at[z], local)

    def start():
        for step in range(planes - 1, 0, -1):
            copy(step).start()
        keep.start()

    def finish():
        keep.wait()
        for step in range(1, planes):
            copy(step).wait_send()
            arrival(step).wait_recv()

    return start, finish


def gather_first(plan, tokens, cotangent, documents, front_weight, back_weight):
    shards, unit = plan.fsdp, plan.unit
    rows, length = tokens.shape[0], documents.shape[1]
    dma = pltpu.SemaphoreType.DMA
    return pl.pallas_call(
        functools.partial(gather_kernel, plan),
        in_specs=[VMEM_BLOCK] * 3 + [ANY_BLOCK] * 2,
        out_specs=[ANY_BLOCK] * 5,
        out_shape=[
            jax.ShapeDtypeStruct((shards, 2, rows, D), bf16),
            jax.ShapeDtypeStruct((shards, 2, rows, D), bf16),
            jax.ShapeDtypeStruct((1, length), f32),
            jax.ShapeDtypeStruct((D, 7 * unit), bf16),
            jax.ShapeDtypeStruct((unit, D), bf16),
        ],
        scratch_shapes=[
            pltpu.VMEM((D, 2 * unit), bf16),
            pltpu.VMEM((unit, D // shards), bf16),
            dma((2, shards)),
            dma((2, shards)),
            dma((2, shards)),
            dma((2, shards)),
            dma((5, shards)),
            dma((5,)),
            dma((5,)),
            dma((5,)),
            dma((shards,)),
            dma((shards,)),
            dma((shards,)),
            dma(()),
            dma((5,)),
        ],
        compiler_params=pltpu.CompilerParams(has_side_effects=True),
        cost_estimate=busy(130),
    )(tokens, cotangent, documents, front_weight, back_weight)


def tiles(rows, columns, tall, wide, first, last, body):
    across = columns // wide

    def one(i, carry):
        row = pl.multiple_of(lax.div(i, across) * tall, tall)
        column = pl.multiple_of(lax.rem(i, across) * wide, wide)
        body(row, column)
        return carry

    lax.fori_loop(first, last, one, 0)


def exchange_kernel(
    plan, src, normed, weight, bias, back, out, b_out, act, slope, buffer, send, recv, local, bsend, brecv
):
    unit = plan.unit
    start, finish = line_exchange(plan, src, out, send, recv, local.at[0])
    start_rows, finish_rows = back_moves(plan, back, b_out, buffer, bsend, brecv, local.at[1])
    start()
    start_rows()
    tall = 512

    def units(row, column):
        at, here = pl.ds(row, tall), pl.ds(column, unit)
        u = jnp.dot(
            normed[at, :],
            weight[:, pl.ds(pl.multiple_of(column + 3 * unit, unit), unit)],
            preferred_element_type=f32,
        )
        value, steep = gelu_parts(u + bias[:, here])
        act[at, here] = value.astype(bf16)
        slope[at, here] = steep

    tiles(act.shape[0], 4 * unit, tall, unit, 0, act.shape[0] // tall * 4, units)
    finish()
    finish_rows()


def exchange_first(plan, values, normed, weight, bias, back_weight):
    dma = pltpu.SemaphoreType.DMA
    unit, shards = plan.unit, plan.fsdp
    length = normed.shape[0]
    return pl.pallas_call(
        functools.partial(exchange_kernel, plan),
        in_specs=[VMEM_BLOCK] * 4 + [ANY_BLOCK],
        out_specs=[ANY_BLOCK, ANY_BLOCK, VMEM_BLOCK, VMEM_BLOCK],
        out_shape=[
            jax.ShapeDtypeStruct(values.shape, bf16),
            jax.ShapeDtypeStruct((4 * unit, D), bf16),
            jax.ShapeDtypeStruct((length, 4 * unit), bf16),
            jax.ShapeDtypeStruct((length, 4 * unit), f32),
        ],
        scratch_shapes=[
            pltpu.VMEM((2 * unit, D // shards), bf16),
            dma((plan.planes,)),
            dma((plan.planes,)),
            dma((2,)),
            dma((2, shards)),
            dma((2, shards)),
        ],
        compiler_params=pltpu.CompilerParams(has_side_effects=True),
        cost_estimate=busy(50),
    )(values, normed, weight, bias, back_weight)


def exchange_back_kernel(plan, src, grad, rows, slope, out, up_grad, send, recv, local):
    unit, tall = plan.unit, 512
    start, finish = line_exchange(plan, src, out, send, recv, local)
    start()

    def units(row, column):
        at, here = pl.ds(row, tall), pl.ds(column, unit)
        mixed_grad = lax.dot_general(
            grad[at, :], rows[here, :], (((1,), (1,)), ((), ())), preferred_element_type=f32
        )
        up_grad[at, here] = (mixed_grad * slope[at, here]).astype(bf16)

    tiles(grad.shape[0], 4 * unit, tall, unit, 0, grad.shape[0] // tall * 4, units)
    finish()


def exchange_back(plan, values, grad, rows, slope):
    dma = pltpu.SemaphoreType.DMA
    return pl.pallas_call(
        functools.partial(exchange_back_kernel, plan),
        in_specs=[VMEM_BLOCK] * 4,
        out_specs=[ANY_BLOCK, VMEM_BLOCK],
        out_shape=[
            jax.ShapeDtypeStruct(values.shape, bf16),
            jax.ShapeDtypeStruct(slope.shape, bf16),
        ],
        scratch_shapes=[dma((plan.planes,)), dma((plan.planes,)), dma(())],
        compiler_params=pltpu.CompilerParams(has_side_effects=True),
        cost_estimate=busy(50),
    )(values, grad, rows, slope)


def line_sum(plan, block, rising, falling, sends, gets, rows):
    planes, chunk = plan.planes, 64
    c, f, z, k, p = place_in_mesh()

    def copy(side, s, src):
        slots = (rising, falling)[side]
        return pltpu.make_async_remote_copy(
            src_ref=src,
            dst_ref=slots.at[s - 1],
            send_sem=sends.at[side, s - 1],
            recv_sem=gets.at[side, s - 1],
            device_id=(c + 2 - 4 * side, f),
            device_id_type=MESH,
        )

    def add(side, s, number):
        slots = (rising, falling)[side]
        term = block(number)

        def body(i, carry):
            at = pl.ds(pl.multiple_of(i * chunk, chunk), chunk)
            slots[s - 1, at, :] = (slots[s - 1, at, :].astype(f32) + term[at, :].astype(f32)).astype(bf16)
            return carry

        lax.fori_loop(0, rows // chunk, body, 0)

    def step(s):
        for side in range(2):
            place = z if side == 0 else planes - 1 - z
            number = planes - s + place
            number = number if side == 0 else planes - 1 - number

            @pl.when(place == 0)
            def _(side=side, number=number):
                copy(side, s, block(number)).start()

            if s > 1:

                @pl.when((place > 0) & (place < s) & (place < planes - 1))
                def _(side=side, number=number):
                    slots = (rising, falling)[side]
                    copy(side, s - 1, slots.at[s - 2]).wait_recv()
                    add(side, s - 1, number)
                    copy(side, s, slots.at[s - 2]).start()

    def finish(out):
        last = planes - 1
        for side in range(2):
            place = z if side == 0 else planes - 1 - z
            slots = (rising, falling)[side]

            @pl.when(place > 0)
            def _(side=side, slots=slots):
                copy(side, last, slots.at[last - 1]).wait_recv()

        mine = block(z)

        def total(ups, downs):
            def body(i, carry):
                at = pl.ds(pl.multiple_of(i * chunk, chunk), chunk)
                value = mine[at, :].astype(f32)
                if ups:
                    value = value + rising[last - 1, at, :].astype(f32)
                if downs:
                    value = value + falling[last - 1, at, :].astype(f32)
                out[at, :] = value.astype(out.dtype)
                return carry

            lax.fori_loop(0, rows // chunk, body, 0)

        @pl.when(z == 0)
        def _():
            total(False, True)

        @pl.when(z == planes - 1)
        def _():
            total(True, False)

        @pl.when((z > 0) & (z < planes - 1))
        def _():
            total(True, True)

        for side in range(2):
            place = z if side == 0 else planes - 1 - z
            slots = (rising, falling)[side]
            for s in range(1, planes):

                @pl.when((place < s) & (place < planes - 1))
                def _(side=side, slots=slots, s=s):
                    copy(side, s, slots.at[s - 1]).wait_send()

    return step, finish


def line_gather(plan, own, out, sends, gets, share_sends, share_gets, local, pitch, offset=0):
    planes, height = plan.planes, own.shape[0]
    c, f, z, k, p = place_in_mesh()
    other = c + 1 - 2 * k

    def rows_of(plane, core):
        return out.at[pl.ds(pl.multiple_of((2 * plane + core) * pitch + offset, height), height), :]

    def origin(side, s):
        return z - s if side == 0 else z + s

    def copy(side, s):
        plane = origin(side, s - 1)
        src = own if s == 1 else rows_of(plane, k)
        return pltpu.make_async_remote_copy(
            src_ref=src,
            dst_ref=rows_of(plane, k),
            send_sem=sends.at[side, s - 1],
            recv_sem=gets.at[side, s - 1],
            device_id=(c + 2 - 4 * side, f),
            device_id_type=MESH,
        )

    def arrival(side, s):
        here = rows_of(origin(side, s), k)
        return pltpu.make_async_remote_copy(
            src_ref=here,
            dst_ref=here,
            send_sem=sends.at[side, s - 1],
            recv_sem=gets.at[side, s - 1],
            device_id=(c + 2 - 4 * side, f),
            device_id_type=MESH,
        )

    def share(side, s, core):
        plane = origin(side, s)
        here = rows_of(plane, core)
        src = own if s == 0 else here
        return pltpu.make_async_remote_copy(
            src_ref=src,
            dst_ref=here,
            send_sem=share_sends.at[side, s],
            recv_sem=share_gets.at[side, s],
            device_id=(other, f),
            device_id_type=MESH,
        )

    keep = pltpu.make_async_copy(own, rows_of(z, k), local)

    def sends_at(side, s):
        place = z if side == 0 else planes - 1 - z
        return (place >= s - 1) & (place < planes - 1)

    def gets_at(side, s):
        place = z if side == 0 else planes - 1 - z
        return place >= s

    def take(s):
        for side in range(2):

            @pl.when(gets_at(side, s))
            def _(side=side):
                arrival(side, s).wait_recv()
                if s < planes - 1:

                    @pl.when(sends_at(side, s + 1))
                    def _():
                        copy(side, s + 1).start()

                share(side, s, k).start()

    def step(s):
        if s > 1:
            take(s - 1)
            return
        for side in range(2):

            @pl.when(sends_at(side, 1))
            def _(side=side):
                copy(side, 1).start()

        share(0, 0, k).start()
        keep.start()

    def finish():
        take(planes - 1)
        keep.wait()
        share(0, 0, k).wait_send()
        share(0, 0, 1 - k).wait_recv()
        for side in range(2):
            for s in range(1, planes):

                @pl.when(sends_at(side, s))
                def _(side=side, s=s):
                    copy(side, s).wait_send()

                @pl.when(gets_at(side, s))
                def _(side=side, s=s):
                    share(side, s, k).wait_send()
                    share(side, s, 1 - k).wait_recv()

    return step, finish


def back_owners(plan, src, out, send, recv, lsem):
    unit, ranks = plan.unit, plan.ranks
    c, f, z, k, p = place_in_mesh()

    def copy(j, owner, place):
        return pltpu.make_async_remote_copy(
            src_ref=src.at[pl.ds(j * unit, unit), :],
            dst_ref=out.at[pl.ds(place * unit, unit), :],
            send_sem=send.at[j],
            recv_sem=recv.at[place],
            device_id=(owner, z),
            device_id_type=MESH,
        )

    def local(j, place):
        return pltpu.make_async_copy(
            src.at[pl.ds(j * unit, unit), :], out.at[pl.ds(place * unit, unit), :], lsem.at[place]
        )

    blocks = [
        (rank, j, plan.back_units[rank][j] // 5, plan.back_units[rank][j] % 5)
        for rank in range(ranks)
        for j in range(5)
    ]

    def start():
        for rank, j, owner, place in blocks:

            @pl.when((p == rank) & ~((c == owner) & (f == z)))
            def _(j=j, owner=owner, place=place):
                copy(j, owner, place).start()

            @pl.when((p == rank) & (c == owner) & (f == z))
            def _(j=j, place=place):
                local(j, place).start()

    def finish():
        for rank, j, owner, place in blocks:

            @pl.when((p == rank) & ~((c == owner) & (f == z)))
            def _(j=j, owner=owner, place=place):
                copy(j, owner, place).wait_send()

            @pl.when((c == owner) & ~((p == rank) & (f == z)))
            def _(j=j, owner=owner, place=place):
                copy(j, owner, place).wait_recv()

            @pl.when((p == rank) & (c == owner) & (f == z))
            def _(j=j, place=place):
                local(j, place).wait()

    return start, finish


def front_owners(plan, src, out, send, recv, lsem):
    unit, ranks = plan.unit, plan.ranks
    c, f, z, k, p = place_in_mesh()
    height = src.shape[0] // 2
    moves, start_at = [], 0
    for slot, (units, wide) in enumerate(plan.slots):
        for rank in range(ranks):
            owner, place = units[rank] // plan.per_shard, units[rank] % plan.per_shard
            moves.append((slot, rank, owner, place, start_at, wide))
        start_at += wide

    def copy(slot, owner, place, begin, wide, half):
        return pltpu.make_async_remote_copy(
            src_ref=src.at[pl.ds(half * height, height), pl.ds(begin * unit, wide * unit)],
            dst_ref=out.at[:, pl.ds(place * unit, wide * unit)],
            send_sem=send.at[slot, half],
            recv_sem=recv.at[place],
            device_id=(2 * z + half, owner),
            device_id_type=MESH,
        )

    def local(place, begin, wide, half):
        return pltpu.make_async_copy(
            src.at[pl.ds(half * height, height), pl.ds(begin * unit, wide * unit)],
            out.at[:, pl.ds(place * unit, wide * unit)],
            lsem.at[place],
        )

    def start():
        for slot, rank, owner, place, begin, wide in moves:
            for half in range(2):
                if 2 * owner + half == rank:

                    @pl.when(p == rank)
                    def _(place=place, begin=begin, wide=wide, half=half):
                        local(place, begin, wide, half).start()

                else:

                    @pl.when(p == rank)
                    def _(slot=slot, owner=owner, place=place, begin=begin, wide=wide, half=half):
                        copy(slot, owner, place, begin, wide, half).start()

    def finish():
        for slot, rank, owner, place, begin, wide in moves:
            for half in range(2):
                if 2 * owner + half == rank:

                    @pl.when(p == rank)
                    def _(place=place, begin=begin, wide=wide, half=half):
                        local(place, begin, wide, half).wait()

                else:

                    @pl.when(p == rank)
                    def _(slot=slot, owner=owner, place=place, begin=begin, wide=wide, half=half):
                        copy(slot, owner, place, begin, wide, half).wait_send()

                    @pl.when(p == 2 * owner + half)
                    def _(slot=slot, owner=owner, place=place, begin=begin, wide=wide, half=half):
                        copy(slot, owner, place, begin, wide, half).wait_recv()

    return start, finish


def sum_scratch(plan, rows, columns):
    dma = pltpu.SemaphoreType.DMA
    steps = plan.planes - 1
    slots = pltpu.VMEM((steps, rows, columns), bf16)
    return [slots, slots, dma((2, steps)), dma((2, steps))]


def gather_scratch(plan):
    dma = pltpu.SemaphoreType.DMA
    return [dma((2, plan.planes - 1))] * 2 + [dma((2, plan.planes))] * 2 + [dma(())]


def back_sum_kernel(plan, width, src, normed, grad, out, upper, lower, *scratch):
    unit, tall = plan.unit, D // (2 * plan.planes)
    half = tall // 2

    def block(i):
        return src.at[:, pl.ds(pl.multiple_of(i * width, 128), width)]

    def term(row, column):
        here = pl.ds(column, unit)
        value = lax.dot_general(
            normed[:, pl.ds(row, tall)], grad[:, here], (((0,), (0,)), ((), ())), preferred_element_type=f32
        ).astype(bf16)
        at = pl.ds(pl.multiple_of(lax.div(row, 2), half), half)
        upper[at, here] = value[:half]
        lower[at, here] = value[half:]

    count = D // tall * 7
    step, finish = line_sum(plan, block, *scratch, src.shape[0])
    for s in range(1, plan.planes):
        step(s)
        tiles(
            D,
            7 * unit,
            tall,
            unit,
            count * (s - 1) // (plan.planes - 1),
            count * s // (plan.planes - 1),
            term,
        )
    finish(out)


def back_sums(plan, partial, normed, hidden_grad):
    rows, width = partial.shape[0], D // plan.planes
    half = jax.ShapeDtypeStruct((D // 2, hidden_grad.shape[1]), bf16)
    return pl.pallas_call(
        functools.partial(back_sum_kernel, plan, width),
        in_specs=[VMEM_BLOCK] * 3,
        out_specs=[VMEM_BLOCK] * 3,
        out_shape=[jax.ShapeDtypeStruct((rows, width), bf16), half, half],
        scratch_shapes=sum_scratch(plan, rows, width),
        compiler_params=pltpu.CompilerParams(has_side_effects=True),
        cost_estimate=busy(90),
    )(partial, normed, hidden_grad)


def front_block(plan, src, rows):
    return lambda i: src.at[pl.ds(pl.multiple_of(i * rows, rows), rows), :]


def front_sum_kernel(plan, rows, src, back, out, owned, *scratch):
    start, done = back_owners(plan, back, owned, *scratch[:3])
    step, finish = line_sum(plan, front_block(plan, src, rows), *scratch[3:], rows)
    step(1)
    start()
    for s in range(2, plan.planes):
        step(s)
    finish(out)
    done()


def front_sums(plan, partial, back_sum):
    dma = pltpu.SemaphoreType.DMA
    rows, width = partial.shape[0] // plan.planes, partial.shape[1]
    return pl.pallas_call(
        functools.partial(front_sum_kernel, plan, rows),
        in_specs=[VMEM_BLOCK, VMEM_BLOCK],
        out_specs=[VMEM_BLOCK, ANY_BLOCK],
        out_shape=[
            jax.ShapeDtypeStruct((rows, width), bf16),
            jax.ShapeDtypeStruct(back_sum.shape, bf16),
        ],
        scratch_shapes=[dma((5,))] * 3 + sum_scratch(plan, rows, width),
        compiler_params=pltpu.CompilerParams(has_side_effects=True),
        cost_estimate=busy(80),
    )(partial, back_sum)


def owner_scratch(plan):
    dma = pltpu.SemaphoreType.DMA
    return [dma((5, 2)), dma((plan.per_shard,)), dma((plan.per_shard,))]


def back_next_kernel(plan, rows, own, upper, src, out, owned, total, *scratch):
    start, done = front_owners(plan, upper, owned, *scratch[:3])
    step, finish = line_gather(plan, own, out, *scratch[3:8], own.shape[0])
    step_sum, finish_sum = line_sum(plan, front_block(plan, src, rows), *scratch[8:], rows)
    step_sum(1)
    step(1)
    start()
    for s in range(2, plan.planes):
        step_sum(s)
        step(s)
    finish_sum(total)
    finish()
    done()


def back_nexts(plan, own, upper, partial):
    rows, width = partial.shape[0] // plan.planes, partial.shape[1]
    return pl.pallas_call(
        functools.partial(back_next_kernel, plan, rows),
        in_specs=[VMEM_BLOCK] * 3,
        out_specs=[ANY_BLOCK, ANY_BLOCK, VMEM_BLOCK],
        out_shape=[
            jax.ShapeDtypeStruct((2 * plan.planes * own.shape[0], own.shape[1]), bf16),
            jax.ShapeDtypeStruct((rows // 2, plan.per_shard * plan.unit), bf16),
            jax.ShapeDtypeStruct((rows, width), bf16),
        ],
        scratch_shapes=owner_scratch(plan) + gather_scratch(plan) + sum_scratch(plan, rows, width),
        compiler_params=pltpu.CompilerParams(has_side_effects=True),
        cost_estimate=busy(110),
    )(own, upper, partial)


def upper_next_kernel(plan, own, src, out, owned, *scratch):
    start, done = front_owners(plan, src, owned, *scratch[:3])
    step, finish = line_gather(plan, own, out, *scratch[3:], 2 * own.shape[0])
    step(1)
    start()
    for s in range(2, plan.planes):
        step(s)
    finish()
    done()


def upper_nexts(plan, own, lower):
    return pl.pallas_call(
        functools.partial(upper_next_kernel, plan),
        in_specs=[VMEM_BLOCK, VMEM_BLOCK],
        out_specs=[ANY_BLOCK, ANY_BLOCK],
        out_shape=[
            jax.ShapeDtypeStruct((4 * plan.planes * own.shape[0], own.shape[1]), bf16),
            jax.ShapeDtypeStruct((lower.shape[0] // 2, plan.per_shard * plan.unit), bf16),
        ],
        scratch_shapes=owner_scratch(plan) + gather_scratch(plan),
        compiler_params=pltpu.CompilerParams(has_side_effects=True),
        cost_estimate=busy(70),
    )(own, lower)


def vector_sum(plan, own, out, terms, sums, send, recv):
    planes, ranks = plan.planes, plan.ranks
    c, f, z, k, p = place_in_mesh()

    def in_plane(step, target):
        to = lax.rem(p + step, ranks)
        return pltpu.make_async_remote_copy(
            src_ref=own,
            dst_ref=terms.at[target],
            send_sem=send.at[step],
            recv_sem=recv.at[step],
            device_id=(2 * z + lax.rem(to, 2), lax.div(to, 2)),
            device_id_type=MESH,
        )

    def over_planes(step, target):
        to = lax.rem(z + step, planes)
        return pltpu.make_async_remote_copy(
            src_ref=out,
            dst_ref=sums.at[target],
            send_sem=send.at[ranks + step],
            recv_sem=recv.at[ranks + step],
            device_id=(2 * to + k, f),
            device_id_type=MESH,
        )

    def start():
        for step in range(1, ranks):
            in_plane(step, p).start()
        terms[p] = own[...]

    def middle():
        for step in range(1, ranks):
            in_plane(step, lax.rem(p + ranks - step, ranks)).wait_recv()
        total = terms[0]
        for rank in range(1, ranks):
            total = total + terms[rank]
        out[...] = total
        sums[z] = total
        for step in range(1, planes):
            over_planes(step, z).start()

    def finish():
        for step in range(1, ranks):
            in_plane(step, p).wait_send()
        for step in range(1, planes):
            over_planes(step, z).wait_send()
            over_planes(step, lax.rem(z + planes - step, planes)).wait_recv()
        total = sums[0]
        for plane in range(1, planes):
            total = total + sums[plane]
        out[...] = total

    return start, middle, finish


def front_next_kernel(plan, own, vector, upper, out, vector_out, terms, sums, vsend, vrecv, *scratch):
    begin, middle, end = vector_sum(plan, vector, vector_out, terms, sums, vsend, vrecv)
    step, finish = line_gather(plan, own, out, *scratch, 2 * own.shape[0], own.shape[0])
    begin()
    step(1)
    middle()
    for s in range(2, plan.planes):
        step(s)
    finish()
    end()


def front_nexts(plan, own, vector, upper):
    dma = pltpu.SemaphoreType.DMA
    return pl.pallas_call(
        functools.partial(front_next_kernel, plan),
        in_specs=[VMEM_BLOCK, VMEM_BLOCK, ANY_BLOCK],
        out_specs=[ANY_BLOCK, VMEM_BLOCK],
        out_shape=[
            jax.ShapeDtypeStruct((4 * plan.planes * own.shape[0], own.shape[1]), bf16),
            jax.ShapeDtypeStruct(vector.shape, f32),
        ],
        scratch_shapes=[
            pltpu.VMEM((plan.ranks,) + vector.shape, f32),
            pltpu.VMEM((plan.planes,) + vector.shape, f32),
            dma((plan.ranks + plan.planes,)),
            dma((plan.ranks + plan.planes,)),
        ]
        + gather_scratch(plan),
        input_output_aliases={2: 0},
        compiler_params=pltpu.CompilerParams(has_side_effects=True),
        cost_estimate=busy(120),
    )(own, vector, upper)


def gelu_parts(u):
    scale = np.float32(np.sqrt(2.0 / np.pi))
    square = u * u
    inner = scale * u * (1.0 + 0.044715 * square)
    t = jnp.tanh(inner)
    value = 0.5 * u * (1.0 + t)
    slope = 0.5 * (1.0 + t) + 0.5 * u * (1.0 - t * t) * scale * (1.0 + 3 * 0.044715 * square)
    return value, slope


def adam_update(weight, first, second, grad, rate, count_now, decay):
    first_new = beta_first * first + (1.0 - beta_first) * grad
    second_new = beta_second * second + (1.0 - beta_second) * grad * grad
    steps_float = count_now.astype(f32)
    first_fix = 1.0 - jnp.power(beta_first, steps_float)
    second_fix = 1.0 - jnp.power(beta_second, steps_float)
    change = first_new / first_fix / (jnp.sqrt(second_new / second_fix) + adam_eps) + decay * weight
    return (weight - rate * change, first_new, second_new)


def after(value, *others):
    return lax.optimization_barrier((value,) + others)[0]


def per_device(
    tokens,
    cotangent,
    doc_ids,
    block_order,
    front_weight,
    back_weight,
    front_master,
    back_master,
    front_first,
    back_first,
    front_second,
    back_second,
    vectors,
    vector_first,
    vector_second,
    learn_rates,
    adam_step,
    *,
    plan,
):
    planes, shards, ranks, unit = plan.planes, plan.fsdp, plan.ranks, plan.unit
    both = ("ctx", "fsdp")
    contract_last = (((1,), (1,)), ((), ()))
    contract_first = (((0,), (0,)), ((), ()))
    c_index, f = lax.axis_index("ctx"), lax.axis_index("fsdp")
    z, k = c_index // 2, c_index % 2
    p = 2 * f + k
    rows = tokens.shape[1]
    plane_rows = 2 * shards * rows
    share = 2 * rows

    bias_front = vectors[:IN_COLS].reshape(-1, unit)
    bias_back = vectors[IN_COLS : IN_COLS + D]
    norm_gain = vectors[IN_COLS + D : IN_COLS + 2 * D]
    norm_shift = vectors[IN_COLS + 2 * D :]

    swap_pairs = [(2 * i + j, 2 * i + 1 - j) for i in range(planes) for j in range(2)]

    def swap_core(value):
        return lax.ppermute(value, "ctx", swap_pairs)

    def to_shard(value, step):
        return lax.ppermute(value, "fsdp", [(i, i ^ step) for i in range(shards)])

    def at(array, index):
        return lax.dynamic_index_in_dim(array, index, 0, keepdims=False)

    blocks = block_order.shape[0]
    block_tokens = doc_ids.shape[1] // blocks
    offsets = jnp.arange(block_tokens, dtype=jnp.int32)
    positions_all = (block_order[:, None] * block_tokens + offsets[None, :]).reshape(planes, share)
    own_positions = at(positions_all, z)
    plane_positions = jnp.tile(own_positions, shards)

    plane_tokens, plane_grad, documents, weight_local, back_attention = gather_first(
        plan, tokens[0], cotangent[0], doc_ids.astype(f32), front_weight, back_weight
    )
    plane_tokens = plane_tokens.reshape(plane_rows, D)
    plane_grad = plane_grad.reshape(plane_rows, D)

    normed = (normalize(plane_tokens)[0] * norm_gain + norm_shift).astype(bf16)

    unit_table = pick(plan.rank_units, p)
    bias_local = jnp.take(bias_front, unit_table, axis=0).reshape(-1)

    hidden = jnp.dot(normed, weight_local[:, : 3 * unit], preferred_element_type=f32) + bias_local[: 3 * unit]
    tables = rotation_tables(plane_positions, unit)
    query = rotate(hidden[:, :unit], tables).astype(bf16)
    key = rotate(hidden[:, unit : 2 * unit], tables).astype(bf16)
    attended_grad = lax.dot_general(
        plane_grad, back_attention, contract_last, preferred_element_type=f32
    ).astype(bf16)
    qkvg = jnp.concatenate([query, key, hidden[:, 2 * unit :].astype(bf16), attended_grad], axis=1)
    qkvg, back_up, activation, slope = exchange_first(
        plan, qkvg.reshape(planes, share, -1), normed, weight_local, bias_local[None, 3 * unit :], back_weight
    )
    qkvg = qkvg.reshape(planes * share, -1)

    seq_positions = positions_all.reshape(-1)
    doc_row = documents[0].astype(jnp.int32)
    seq_documents = jnp.take(doc_row.reshape(blocks, block_tokens), block_order, axis=0).reshape(-1)
    attended, query_grad, key_grad, value_grad = attention(
        qkvg[:, :unit],
        qkvg[:, unit : 2 * unit],
        qkvg[:, 2 * unit : 3 * unit],
        qkvg[:, 3 * unit :],
        seq_positions,
        seq_documents,
    )
    seq_tables = rotation_tables(seq_positions, unit)
    returned = jnp.concatenate(
        [
            attended,
            rotate_back(query_grad, seq_tables).astype(bf16),
            rotate_back(key_grad, seq_tables).astype(bf16),
            value_grad.astype(bf16),
        ],
        axis=1,
    )
    returned, up_grad = exchange_back(
        plan, returned.reshape(planes, share, -1), plane_grad, back_up, slope
    )
    returned = returned.reshape(plane_rows, -1)
    back_local = jnp.concatenate([back_attention, back_up], axis=0)

    mixed = jnp.concatenate([returned[:, :unit], activation], axis=1)
    hidden_grad = jnp.concatenate([returned[:, unit:], up_grad], axis=1)

    def sum_over_cores(value):
        shaped = value.reshape(shards, 2, rows, D)
        kept = lax.dynamic_index_in_dim(shaped, k, 1, keepdims=False)
        sent = lax.dynamic_index_in_dim(shaped, 1 - k, 1, keepdims=False).astype(bf16)
        return kept + swap_core(sent).astype(f32)

    def sum_over_shards(*values):
        totals = [at(value, f) for value in values]
        for step in range(1, shards):
            pieces = jnp.stack([at(value, f ^ step).astype(bf16) for value in values])
            pieces = to_shard(pieces, step).astype(f32)
            totals = [total + piece for total, piece in zip(totals, pieces)]
        return totals

    projected_cores = sum_over_cores(jnp.dot(mixed, back_local, preferred_element_type=f32))
    normed_grad_cores = sum_over_cores(
        lax.dot_general(hidden_grad, weight_local, contract_last, preferred_element_type=f32)
    )

    back_partial = lax.dot_general(
        mixed, plane_grad, contract_first, preferred_element_type=f32
    ).astype(bf16)
    back_sum, upper_partial, lower_partial = back_sums(plan, back_partial, normed, hidden_grad)
    back_sum, projected_cores, normed_grad_cores = lax.optimization_barrier(
        (back_sum, projected_cores, normed_grad_cores)
    )
    projected, normed_grad = sum_over_shards(projected_cores, normed_grad_cores)
    upper_sum, back_owned = front_sums(plan, upper_partial, back_sum)
    upper_sum, projected, normed_grad = lax.optimization_barrier((upper_sum, projected, normed_grad))

    inputs = tokens[0].astype(f32)
    layer_out = (inputs + projected + bias_back).astype(bf16)[None]
    unscaled, factor = normalize(inputs)
    scaled = normed_grad * norm_gain
    input_grad = factor * (
        scaled
        - jnp.mean(scaled, axis=-1, keepdims=True)
        - unscaled * jnp.mean(scaled * unscaled, axis=-1, keepdims=True)
    )
    tokens_grad = (cotangent[0].astype(f32) + input_grad).astype(bf16)[None]

    back_grad = back_owned.astype(f32)
    back_new, back_first_new, back_second_new = adam_update(
        back_master, back_first, back_second, back_grad, learn_rates[1], adam_step[0], weight_decay
    )
    back_next, upper_owned, lower_sum = back_nexts(plan, back_new.astype(bf16), upper_sum, lower_partial)
    half = upper_owned.shape[0]
    upper_new = adam_update(
        front_master[:half],
        front_first[:half],
        front_second[:half],
        upper_owned.astype(f32),
        learn_rates[0],
        adam_step[0],
        weight_decay,
    )[0]
    upper_next, lower_owned = upper_nexts(plan, upper_new.astype(bf16), lower_sum)
    front_grad = jnp.concatenate([upper_owned, lower_owned], axis=0).astype(f32)
    front_new, front_first_new, front_second_new = adam_update(
        front_master, front_first, front_second, front_grad, learn_rates[0], adam_step[0], weight_decay
    )

    def column_sums(value):
        ones = jnp.ones((8, value.shape[0]), bf16)
        return jnp.dot(ones, value, preferred_element_type=f32)[0]

    spread = (jnp.arange(7 * ranks)[:, None] == unit_table[None, :]).astype(f32)
    hidden_sum = column_sums(hidden_grad).reshape(7, unit)
    front_vector = jnp.sum(spread[:, :, None] * hidden_sum[None], axis=1).reshape(-1)
    vector_term = jnp.concatenate(
        [
            front_vector,
            column_sums(cotangent[0]),
            jnp.sum(normed_grad * unscaled, axis=0),
            jnp.sum(normed_grad, axis=0),
        ]
    )
    front_next, vector_grad = front_nexts(
        plan, front_new[half:].astype(bf16), vector_term.reshape(-1, 128), upper_next
    )
    vector_grad = vector_grad.reshape(-1)

    count_now = adam_step[0]
    vectors_new, vector_first_new, vector_second_new = adam_update(
        vectors, vector_first, vector_second, vector_grad, learn_rates[2], count_now, 0.0
    )

    return (
        layer_out,
        tokens_grad,
        front_grad,
        back_grad,
        vector_grad,
        front_new,
        back_new,
        vectors_new,
        front_first_new,
        back_first_new,
        vector_first_new,
        front_second_new,
        back_second_new,
        vector_second_new,
        front_next,
        back_next,
    )


def solution(mesh):
    plan = Layout(mesh.shape["ctx"], mesh.shape["fsdp"])
    tokens_spec = P("fsdp", "ctx", None)
    cols, owned, same = P(None, "fsdp"), P("ctx", "fsdp"), P()
    in_specs = (
        (tokens_spec, tokens_spec, P("fsdp", None), same, cols, cols)
        + (owned,) * 6
        + (same,) * 5
    )
    out_specs = (
        (tokens_spec, tokens_spec, owned, owned, same)
        + (owned, owned, same) * 3
        + (cols, cols)
    )
    return jax.shard_map(
        functools.partial(per_device, plan=plan),
        mesh=mesh,
        in_specs=in_specs,
        out_specs=out_specs,
        check_vma=False,
    )
```

```python
import functools

import jax
import jax.numpy as jnp
import numpy as np
from jax import lax
from jax.experimental import pallas as pl
from jax.experimental.pallas import tpu as pltpu
from jax.sharding import PartitionSpec as P

D = 2048
HEADS = 32
FF = 8192
ROT = 32
HEAD_DIM = 64
IN_COLS = 14336
BACK_ROWS = 10240

norm_eps = 1e-05
beta_first = 0.9
beta_second = 0.95
adam_eps = 1e-08
weight_decay = 0.1
masked_score = -1e30
bf16 = jnp.bfloat16
f32 = jnp.float32


class Layout:
    def __init__(self, ctx, fsdp):
        self.ctx, self.fsdp, self.planes, self.ranks = ctx, fsdp, ctx // 2, 2 * fsdp
        assert ctx % 2 == 0 and self.planes == fsdp
        self.unit = D // self.ranks
        self.per_shard = IN_COLS // self.unit // fsdp
        r = self.ranks
        first_up = 3 * r
        home = {f: [] for f in range(fsdp)}
        for g in range(first_up, 7 * r, 2):
            assert g // self.per_shard == (g + 1) // self.per_shard
            home[g // self.per_shard].append(g)
        pairs = {p: [None, None] for p in range(r)}
        for f in range(fsdp):
            if len(home[f]) >= 4:
                keep, home[f] = home[f][:4], home[f][4:]
                pairs[2 * f], pairs[2 * f + 1] = keep[:2], keep[2:]
            elif home[f]:
                keep, home[f] = home[f], []
                for i, g in enumerate(keep):
                    pairs[2 * f + i % 2][(i + i // 2) % 2] = g
        for s in range(2):
            for k in range(2):
                used = set()
                for f in range(fsdp):
                    p = 2 * f + k
                    if pairs[p][s] is not None:
                        continue
                    options = sorted(
                        (h for h in range(fsdp) if home[h]),
                        key=lambda h: (h in used, bin(h ^ f).count("1"), -len(home[h])),
                    )
                    used.add(options[0])
                    pairs[p][s] = home[options[0]].pop(0)
        self.pairs = pairs
        self.slots = [
            ([p for p in range(r)], 1),
            ([r + p for p in range(r)], 1),
            ([2 * r + p for p in range(r)], 1),
            ([pairs[p][0] for p in range(r)], 2),
            ([pairs[p][1] for p in range(r)], 2),
        ]
        self.rounds = []
        for units, _ in self.slots:
            rounds = []
            for k in range(2):
                for f in range(fsdp):
                    src = units[2 * f + k] // self.per_shard
                    if src == f:
                        continue
                    for one in rounds:
                        if all((src, k) != (a, c) for a, _, c in one):
                            one.append((src, f, k))
                            break
                    else:
                        rounds.append([(src, f, k)])
            self.rounds.append(rounds)
        self.rank_units = [
            [p, r + p, 2 * r + p, pairs[p][0], pairs[p][0] + 1, pairs[p][1], pairs[p][1] + 1]
            for p in range(r)
        ]
        self.back_units = [[p] + [g - 2 * r for g in self.rank_units[p][3:]] for p in range(r)]
        self.matchings = []
        left = {p: list(range(5)) for p in range(r)}
        own = lambda p, j: self.back_units[p][j] // 5
        for _ in range(5):
            match = {}

            def assign(p, seen):
                for j in left[p]:
                    c = own(p, j)
                    if c in seen:
                        continue
                    seen.add(c)
                    if c not in match or assign(match[c][0], seen):
                        match[c] = (p, j)
                        return True
                return False

            for p in range(r):
                assert assign(p, set())
            for c, (p, j) in match.items():
                left[p].remove(j)
            self.matchings.append(match)

    def device(self, z, k, f):
        return (2 * z + k) * self.fsdp + f


def pick(table, index):
    return jnp.asarray(np.asarray(table, np.int32))[index]


def normalize(values):
    values = values.astype(f32)
    centered = values - jnp.mean(values, axis=-1, keepdims=True)
    factor = lax.rsqrt(jnp.mean(centered * centered, axis=-1, keepdims=True) + norm_eps)
    return centered * factor, factor


def rotation_tables(positions, width):
    half = ROT // 2
    lane = np.arange(width) % HEAD_DIM
    frequency = jnp.power(
        10000.0, -2.0 * jnp.asarray(lane % half, f32) / ROT
    )
    angles = positions.astype(f32)[:, None] * frequency[None, :]
    rotated = jnp.asarray(lane < ROT)
    lower = jnp.asarray(lane < half)
    cosine = jnp.where(rotated, jnp.cos(angles), 1.0)
    sine = jnp.where(rotated, jnp.sin(angles), 0.0)
    return cosine, jnp.where(lower, -sine, 0.0), jnp.where(lower, 0.0, sine)


def rotate(values, tables):
    half = ROT // 2
    cosine, from_above, from_below = tables
    return (
        values * cosine
        + jnp.roll(values, -half, axis=1) * from_above
        + jnp.roll(values, half, axis=1) * from_below
    )


def attention_kernel(
    x_ref, pos_q, pos_k, seg_q, seg_k, cosine, from_above, from_below, out_ref, dq_ref, dk_ref, dv_ref
):
    scale = HEAD_DIM ** (-0.5)
    half = ROT // 2
    block, width = dq_ref.shape
    length = dk_ref.shape[0]
    rows = pl.ds(pl.multiple_of(pl.program_id(0) * block, block), block)

    @pl.when(pl.program_id(0) == 0)
    def _():
        dk_ref[...] = jnp.zeros_like(dk_ref)
        dv_ref[...] = jnp.zeros_like(dv_ref)

    def turn_back(values, at):
        return (
            values * cosine[at, :]
            + pltpu.roll(values * from_above[at, :], half, 1)
            + pltpu.roll(values * from_below[at, :], width - half, 1)
        ).astype(bf16)

    allowed = (pos_k[...] <= pos_q[...]) & (seg_k[...] == seg_q[...])
    bias = jnp.where(allowed, 0.0, masked_score)
    last = (((1,), (1,)), ((), ()))
    first = (((0,), (0,)), ((), ()))
    for head in range(width // HEAD_DIM):
        q_cols, k_cols, v_cols, g_cols = (
            slice(n * width + head * HEAD_DIM, n * width + (head + 1) * HEAD_DIM) for n in range(4)
        )
        q, g = x_ref[rows, q_cols], x_ref[rows, g_cols]
        k, v = x_ref[:, k_cols], x_ref[:, v_cols]
        scores = lax.dot_general(q, k, last, preferred_element_type=f32) * scale + bias
        weights = jnp.exp(scores - jnp.max(scores, axis=1, keepdims=True))
        probs = weights * (1.0 / jnp.sum(weights, axis=1, keepdims=True))
        probs_low = probs.astype(bf16)
        out = jnp.dot(probs_low, v, preferred_element_type=f32)
        out_ref[rows, q_cols] = out.astype(bf16)
        prob_grad = lax.dot_general(g, v, last, preferred_element_type=f32)
        delta = jnp.sum(g.astype(f32) * out, axis=1, keepdims=True)
        score_grad = (probs * (prob_grad - delta)).astype(bf16)
        dq_ref[:, q_cols] = jnp.dot(score_grad, k, preferred_element_type=f32) * scale
        dk_ref[:, q_cols] += lax.dot_general(score_grad, q, first, preferred_element_type=f32) * scale
        dv_ref[:, q_cols] += lax.dot_general(probs_low, g, first, preferred_element_type=f32)
    out_ref[rows, width : 2 * width] = turn_back(dq_ref[...], rows)

    @pl.when(pl.program_id(0) == pl.num_programs(0) - 1)
    def _():
        for number in range(length // block):
            at = slice(number * block, (number + 1) * block)
            out_ref[at, 2 * width : 3 * width] = turn_back(dk_ref[at, :], at)
            out_ref[at, 3 * width :] = dv_ref[at, :].astype(bf16)


def attention(values, positions, segments, tables):
    length, width = values.shape[0], values.shape[1] // 4
    block = 256
    whole = lambda columns: pl.BlockSpec((length, columns), lambda i: (0, 0))
    column = pl.BlockSpec((block, 1), lambda i: (i, 0))
    line = pl.BlockSpec((1, length), lambda i: (0, 0))
    return pl.pallas_call(
        attention_kernel,
        grid=(length // block,),
        in_specs=[whole(4 * width), column, line, column, line] + [whole(width)] * 3,
        out_specs=whole(4 * width),
        out_shape=jax.ShapeDtypeStruct((length, 4 * width), bf16),
        scratch_shapes=[
            pltpu.VMEM((block, width), f32),
            pltpu.VMEM((length, width), f32),
            pltpu.VMEM((length, width), f32),
        ],
        cost_estimate=pl.CostEstimate(
            flops=14 * length * length * width,
            transcendentals=length * length * width // HEAD_DIM,
            bytes_accessed=20 * length * width,
        ),
    )(values, positions[:, None], positions[None], segments[:, None], segments[None], *tables)


MESH = pl.DeviceIdType.MESH


VMEM_BLOCK = pl.BlockSpec(memory_space=pltpu.VMEM)
ANY_BLOCK = pl.BlockSpec(memory_space=pl.ANY)


def busy(microseconds):
    return pl.CostEstimate(flops=int(microseconds * 900e6), transcendentals=0, bytes_accessed=0)


def place_in_mesh():
    c, f = lax.axis_index("ctx"), lax.axis_index("fsdp")
    z, k = lax.div(c, 2), lax.rem(c, 2)
    return c, f, z, k, 2 * f + k


def bounce(source, buffer, target, sem):
    one = pltpu.make_async_copy(source, buffer, sem)
    one.start()
    one.wait()
    two = pltpu.make_async_copy(buffer, target, sem)
    two.start()
    two.wait()


def gather_kernel(
    plan, tok, cot, doc, front, back, tok_out, cot_out, doc_out, w_out, b_out,
    w_buf, b_buf, tsend, trecv, csend, crecv, wsend, wrecv, rsend, rrecv, bsend, brecv, dsend, drecv, lsem,
):
    shards, unit, ranks = plan.fsdp, plan.unit, plan.ranks
    c, f, z, k, p = place_in_mesh()
    other = c + 1 - 2 * k
    width = D // shards
    both = ((tok, tok_out), (cot, cot_out))

    def cols(block):
        return pl.ds(pl.multiple_of(block * width, 128), width)

    def remote(src, dst, send, recv, device):
        return pltpu.make_async_remote_copy(
            src_ref=src, dst_ref=dst, send_sem=send, recv_sem=recv, device_id=device, device_id_type=MESH
        )

    def peer(step):
        return lax.rem(f + step, shards)

    def giver(step):
        return lax.rem(f + shards - step, shards)

    def send_tokens(n, step):
        src, out = both[n]
        return remote(src, out.at[f, k], tsend.at[n, step], trecv.at[n, step], (c, peer(step)))

    def get_tokens(n, step):
        here = both[n][1].at[giver(step), k]
        return remote(here, here, tsend.at[n, step], trecv.at[n, step], (c, peer(step)))

    def share(n, step):
        src, out = both[n]
        here = out.at[giver(step), k]
        return remote(src if step == 0 else here, here, csend.at[n, step], crecv.at[n, step], (other, f))

    def get_share(n, step):
        here = both[n][1].at[giver(step), 1 - k]
        return remote(here, here, csend.at[n, step], crecv.at[n, step], (other, f))

    def rows_of(dst):
        return pl.ds(pl.multiple_of((2 * dst + k) * unit, unit), unit)

    def send_back(step):
        return remote(
            back.at[rows_of(peer(step)), :], b_out.at[:, cols(f)], bsend.at[step], brecv.at[step], (c, peer(step))
        )

    def get_back(step):
        here = b_out.at[:, cols(giver(step))]
        return remote(here, here, bsend.at[step], brecv.at[step], (c, peer(step)))

    def send_doc(step):
        return remote(doc, doc_out, dsend.at[step], drecv, (c, peer(step)))

    start_weights, relay_weights, finish_weights = weight_moves(
        plan, front, w_out, w_buf, wsend, wrecv, rsend, rrecv, lsem.at[2]
    )
    own = [pltpu.make_async_copy(src, out.at[f, k], lsem.at[4 * n]) for n, (src, out) in enumerate(both)]
    own_doc = pltpu.make_async_copy(doc, doc_out, lsem.at[1])
    start_weights()
    for n in range(2):
        for step in range(1, shards):
            send_tokens(n, step).start()
        share(n, 0).start()
        own[n].start()
    for step in range(1, shards):
        send_back(step).start()

    @pl.when(f == z)
    def _():
        own_doc.start()
        for step in range(1, shards):
            send_doc(step).start()

    relay_weights()
    for n in range(2):
        for step in range(1, shards):
            get_tokens(n, step).wait_recv()
            share(n, step).start()
    bounce(back.at[rows_of(f), :], b_buf, b_out.at[:, cols(f)], lsem.at[3])
    for n in range(2):
        own[n].wait()

    @pl.when(f == z)
    def _():
        own_doc.wait()
        for step in range(1, shards):
            send_doc(step).wait_send()

    @pl.when(f != z)
    def _():
        send_doc(1).wait_recv()

    for n in range(2):
        for step in range(shards):
            get_share(n, step).wait_recv()
            share(n, step).wait_send()
        for step in range(1, shards):
            send_tokens(n, step).wait_send()
    for step in range(1, shards):
        send_back(step).wait_send()
        get_back(step).wait_recv()
    finish_weights()


def moves_between(moves, device_of):
    c, f, z, k, p = place_in_mesh()

    def remote(move):
        src, dst, source, target, send, recv, _, _ = move
        return pltpu.make_async_remote_copy(
            src_ref=source, dst_ref=target, send_sem=send, recv_sem=recv, device_id=device_of(c, dst), device_id_type=MESH
        )

    def start():
        for move in moves:
            if move[0] != move[1]:

                @pl.when(p == move[0])
                def _(move=move):
                    remote(move).start()

        for move in moves:
            if move[0] == move[1]:

                @pl.when(p == move[0])
                def _(move=move):
                    bounce(move[2], move[6], move[3], move[7])

    def finish():
        for move in moves:
            if move[0] != move[1]:

                @pl.when(p == move[0])
                def _(move=move):
                    remote(move).wait_send()

                @pl.when(p == move[1])
                def _(move=move):
                    remote(move).wait_recv()

    return start, finish


def weight_moves(plan, front, out, buffer, send, recv, relay_send, relay_recv, local):
    unit, moves, begin = plan.unit, [], 0
    c, f, z, k, p = place_in_mesh()
    half, parity = D // 2, lax.rem(z, 2)

    def rows(part):
        return pl.ds(pl.multiple_of(part * half, half), half)

    for slot, (units, wide) in enumerate(plan.slots):
        for dst in range(plan.ranks):
            src, at = units[dst] // plan.per_shard, units[dst] % plan.per_shard
            moves.append(
                (slot, 2 * src + dst % 2, dst, pl.ds(at * unit, wide * unit), pl.ds(begin * unit, wide * unit), wide * unit)
            )
        begin += wide

    def copy(move):
        slot, _, dst, source, target, _ = move
        return pltpu.make_async_remote_copy(
            src_ref=front.at[rows(parity), source],
            dst_ref=out.at[rows(parity), target],
            send_sem=send.at[slot, dst // 2],
            recv_sem=recv.at[slot],
            device_id=(c, dst // 2),
            device_id_type=MESH,
        )

    def pass_on(move, part):
        slot, _, _, _, target, _ = move
        here = out.at[rows(part), target]
        return pltpu.make_async_remote_copy(
            src_ref=here,
            dst_ref=here,
            send_sem=relay_send.at[slot],
            recv_sem=relay_recv.at[slot],
            device_id=(c + 2 - 4 * parity, f),
            device_id_type=MESH,
        )

    def start():
        for move in moves:
            if move[1] != move[2]:

                @pl.when(p == move[1])
                def _(move=move):
                    copy(move).start()

    def relay():
        for move in moves:
            if move[1] != move[2]:

                @pl.when(p == move[2])
                def _(move=move):
                    copy(move).wait_recv()
                    pass_on(move, parity).start()

    def finish():
        for move in moves:
            if move[1] == move[2]:

                @pl.when(p == move[2])
                def _(move=move):
                    bounce(front.at[:, move[3]], buffer.at[:, pl.ds(0, move[5])], out.at[:, move[4]], local)

        for move in moves:
            if move[1] != move[2]:

                @pl.when(p == move[1])
                def _(move=move):
                    copy(move).wait_send()

                @pl.when(p == move[2])
                def _(move=move):
                    pass_on(move, parity).wait_send()
                    pass_on(move, 1 - parity).wait_recv()

    return start, relay, finish


def back_moves(plan, back, out, buffer, send, recv, local):
    unit, width, moves = plan.unit, D // plan.fsdp, []
    for dst in range(plan.ranks):
        for src in range(plan.fsdp):
            for number in range(2):
                row = plan.back_units[dst][1 + 2 * number]
                moves.append(
                    (
                        2 * src + dst % 2,
                        dst,
                        back.at[pl.ds(row * unit, 2 * unit), :],
                        out.at[pl.ds(2 * number * unit, 2 * unit), pl.ds(src * width, width)],
                        send.at[number, dst // 2],
                        recv.at[number, src],
                        buffer,
                        local,
                    )
                )
    return moves_between(moves, lambda c, dst: (c, dst // 2))


def line_exchange(plan, src, out, send, recv, local):
    planes = plan.planes
    c, f, z, k, p = place_in_mesh()

    def copy(step):
        to = lax.rem(z + step, planes)
        return pltpu.make_async_remote_copy(
            src_ref=src.at[to],
            dst_ref=out.at[z],
            send_sem=send.at[step],
            recv_sem=recv.at[step],
            device_id=(2 * to + k, f),
            device_id_type=MESH,
        )

    def arrival(step):
        here = out.at[lax.rem(z + planes - step, planes)]
        return pltpu.make_async_remote_copy(
            src_ref=here,
            dst_ref=here,
            send_sem=send.at[step],
            recv_sem=recv.at[step],
            device_id=(2 * lax.rem(z + step, planes) + k, f),
            device_id_type=MESH,
        )

    keep = pltpu.make_async_copy(src.at[z], out.at[z], local)

    def start():
        for step in range(planes - 1, 0, -1):
            copy(step).start()
        keep.start()

    def finish():
        keep.wait()
        for step in range(1, planes):
            copy(step).wait_send()
            arrival(step).wait_recv()

    return start, finish


def gather_first(plan, tokens, cotangent, documents, front_weight, back_weight):
    shards, unit = plan.fsdp, plan.unit
    rows, length = tokens.shape[0], documents.shape[1]
    dma = pltpu.SemaphoreType.DMA
    return pl.pallas_call(
        functools.partial(gather_kernel, plan),
        in_specs=[VMEM_BLOCK] * 3 + [ANY_BLOCK] * 2,
        out_specs=[ANY_BLOCK] * 5,
        out_shape=[
            jax.ShapeDtypeStruct((shards, 2, rows, D), bf16),
            jax.ShapeDtypeStruct((shards, 2, rows, D), bf16),
            jax.ShapeDtypeStruct((1, length), f32),
            jax.ShapeDtypeStruct((D, 7 * unit), bf16),
            jax.ShapeDtypeStruct((unit, D), bf16),
        ],
        scratch_shapes=[
            pltpu.VMEM((D, 2 * unit), bf16),
            pltpu.VMEM((unit, D // shards), bf16),
            dma((2, shards)),
            dma((2, shards)),
            dma((2, shards)),
            dma((2, shards)),
            dma((5, shards)),
            dma((5,)),
            dma((5,)),
            dma((5,)),
            dma((shards,)),
            dma((shards,)),
            dma((shards,)),
            dma(()),
            dma((5,)),
        ],
        compiler_params=pltpu.CompilerParams(has_side_effects=True),
        cost_estimate=busy(130),
    )(tokens, cotangent, documents, front_weight, back_weight)


def tiles(rows, columns, tall, wide, first, last, body):
    across = columns // wide

    def one(i, carry):
        row = pl.multiple_of(lax.div(i, across) * tall, tall)
        column = pl.multiple_of(lax.rem(i, across) * wide, wide)
        body(row, column)
        return carry

    lax.fori_loop(first, last, one, 0)


def exchange_kernel(
    plan, src, normed, weight, bias, back, out, b_out, act, slope, buffer, send, recv, local, bsend, brecv
):
    unit = plan.unit
    start, finish = line_exchange(plan, src, out, send, recv, local.at[0])
    start_rows, finish_rows = back_moves(plan, back, b_out, buffer, bsend, brecv, local.at[1])
    start()
    start_rows()
    tall = 512

    def units(row, column):
        at, here = pl.ds(row, tall), pl.ds(column, unit)
        u = jnp.dot(
            normed[at, :],
            weight[:, pl.ds(pl.multiple_of(column + 3 * unit, unit), unit)],
            preferred_element_type=f32,
        )
        value, steep = gelu_parts(u + bias[:, here])
        act[at, here] = value.astype(bf16)
        slope[at, here] = steep

    tiles(act.shape[0], 4 * unit, tall, unit, 0, act.shape[0] // tall * 4, units)
    finish()
    finish_rows()


def exchange_first(plan, values, normed, weight, bias, back_weight):
    dma = pltpu.SemaphoreType.DMA
    unit, shards = plan.unit, plan.fsdp
    length = normed.shape[0]
    return pl.pallas_call(
        functools.partial(exchange_kernel, plan),
        in_specs=[VMEM_BLOCK] * 4 + [ANY_BLOCK],
        out_specs=[ANY_BLOCK, ANY_BLOCK, VMEM_BLOCK, VMEM_BLOCK],
        out_shape=[
            jax.ShapeDtypeStruct(values.shape, bf16),
            jax.ShapeDtypeStruct((4 * unit, D), bf16),
            jax.ShapeDtypeStruct((length, 4 * unit), bf16),
            jax.ShapeDtypeStruct((length, 4 * unit), f32),
        ],
        scratch_shapes=[
            pltpu.VMEM((2 * unit, D // shards), bf16),
            dma((plan.planes,)),
            dma((plan.planes,)),
            dma((2,)),
            dma((2, shards)),
            dma((2, shards)),
        ],
        compiler_params=pltpu.CompilerParams(has_side_effects=True),
        cost_estimate=busy(50),
    )(values, normed, weight, bias, back_weight)


def exchange_back_kernel(plan, src, grad, rows, slope, out, up_grad, send, recv, local):
    unit, tall = plan.unit, 512
    start, finish = line_exchange(plan, src, out, send, recv, local)
    start()

    def units(row, column):
        at, here = pl.ds(row, tall), pl.ds(column, unit)
        mixed_grad = lax.dot_general(
            grad[at, :], rows[here, :], (((1,), (1,)), ((), ())), preferred_element_type=f32
        )
        up_grad[at, here] = (mixed_grad * slope[at, here]).astype(bf16)

    tiles(grad.shape[0], 4 * unit, tall, unit, 0, grad.shape[0] // tall * 4, units)
    finish()


def exchange_back(plan, values, grad, rows, slope):
    dma = pltpu.SemaphoreType.DMA
    return pl.pallas_call(
        functools.partial(exchange_back_kernel, plan),
        in_specs=[VMEM_BLOCK] * 4,
        out_specs=[ANY_BLOCK, VMEM_BLOCK],
        out_shape=[
            jax.ShapeDtypeStruct(values.shape, bf16),
            jax.ShapeDtypeStruct(slope.shape, bf16),
        ],
        scratch_shapes=[dma((plan.planes,)), dma((plan.planes,)), dma(())],
        compiler_params=pltpu.CompilerParams(has_side_effects=True),
        cost_estimate=busy(50),
    )(values, grad, rows, slope)


def line_sum(plan, block, rising, falling, sends, gets, rows):
    planes, chunk = plan.planes, 64
    c, f, z, k, p = place_in_mesh()

    def copy(side, s, src):
        slots = (rising, falling)[side]
        return pltpu.make_async_remote_copy(
            src_ref=src,
            dst_ref=slots.at[s - 1],
            send_sem=sends.at[side, s - 1],
            recv_sem=gets.at[side, s - 1],
            device_id=(c + 2 - 4 * side, f),
            device_id_type=MESH,
        )

    def add(side, s, number):
        slots = (rising, falling)[side]
        term = block(number)

        def body(i, carry):
            at = pl.ds(pl.multiple_of(i * chunk, chunk), chunk)
            slots[s - 1, at, :] = (slots[s - 1, at, :].astype(f32) + term[at, :].astype(f32)).astype(bf16)
            return carry

        lax.fori_loop(0, rows // chunk, body, 0)

    def step(s):
        for side in range(2):
            place = z if side == 0 else planes - 1 - z
            number = planes - s + place
            number = number if side == 0 else planes - 1 - number

            @pl.when(place == 0)
            def _(side=side, number=number):
                copy(side, s, block(number)).start()

            if s > 1:

                @pl.when((place > 0) & (place < s) & (place < planes - 1))
                def _(side=side, number=number):
                    slots = (rising, falling)[side]
                    copy(side, s - 1, slots.at[s - 2]).wait_recv()
                    add(side, s - 1, number)
                    copy(side, s, slots.at[s - 2]).start()

    def finish(out):
        last = planes - 1
        for side in range(2):
            place = z if side == 0 else planes - 1 - z
            slots = (rising, falling)[side]

            @pl.when(place > 0)
            def _(side=side, slots=slots):
                copy(side, last, slots.at[last - 1]).wait_recv()

        mine = block(z)

        def total(ups, downs):
            def body(i, carry):
                at = pl.ds(pl.multiple_of(i * chunk, chunk), chunk)
                value = mine[at, :].astype(f32)
                if ups:
                    value = value + rising[last - 1, at, :].astype(f32)
                if downs:
                    value = value + falling[last - 1, at, :].astype(f32)
                out[at, :] = value.astype(out.dtype)
                return carry

            lax.fori_loop(0, rows // chunk, body, 0)

        @pl.when(z == 0)
        def _():
            total(False, True)

        @pl.when(z == planes - 1)
        def _():
            total(True, False)

        @pl.when((z > 0) & (z < planes - 1))
        def _():
            total(True, True)

        for side in range(2):
            place = z if side == 0 else planes - 1 - z
            slots = (rising, falling)[side]
            for s in range(1, planes):

                @pl.when((place < s) & (place < planes - 1))
                def _(side=side, slots=slots, s=s):
                    copy(side, s, slots.at[s - 1]).wait_send()

    return step, finish


def line_gather(plan, own, out, sends, gets, share_sends, share_gets, local, height):
    planes = plan.planes
    c, f, z, k, p = place_in_mesh()
    other = c + 1 - 2 * k

    def rows_of(plane, core):
        return out.at[pl.ds(pl.multiple_of((2 * plane + core) * height, height), height), :]

    def origin(side, s):
        return z - s if side == 0 else z + s

    def copy(side, s):
        plane = origin(side, s - 1)
        src = own if s == 1 else rows_of(plane, k)
        return pltpu.make_async_remote_copy(
            src_ref=src,
            dst_ref=rows_of(plane, k),
            send_sem=sends.at[side, s - 1],
            recv_sem=gets.at[side, s - 1],
            device_id=(c + 2 - 4 * side, f),
            device_id_type=MESH,
        )

    def arrival(side, s):
        here = rows_of(origin(side, s), k)
        return pltpu.make_async_remote_copy(
            src_ref=here,
            dst_ref=here,
            send_sem=sends.at[side, s - 1],
            recv_sem=gets.at[side, s - 1],
            device_id=(c + 2 - 4 * side, f),
            device_id_type=MESH,
        )

    def share(side, s, core):
        plane = origin(side, s)
        here = rows_of(plane, core)
        src = own if s == 0 else here
        return pltpu.make_async_remote_copy(
            src_ref=src,
            dst_ref=here,
            send_sem=share_sends.at[side, s],
            recv_sem=share_gets.at[side, s],
            device_id=(other, f),
            device_id_type=MESH,
        )

    keep = pltpu.make_async_copy(own, rows_of(z, k), local)

    def sends_at(side, s):
        place = z if side == 0 else planes - 1 - z
        return (place >= s - 1) & (place < planes - 1)

    def gets_at(side, s):
        place = z if side == 0 else planes - 1 - z
        return place >= s

    def take(s):
        for side in range(2):

            @pl.when(gets_at(side, s))
            def _(side=side):
                arrival(side, s).wait_recv()
                if s < planes - 1:

                    @pl.when(sends_at(side, s + 1))
                    def _():
                        copy(side, s + 1).start()

                share(side, s, k).start()

    def step(s):
        if s > 1:
            take(s - 1)
            return
        for side in range(2):

            @pl.when(sends_at(side, 1))
            def _(side=side):
                copy(side, 1).start()

        share(0, 0, k).start()
        keep.start()

    def finish():
        take(planes - 1)
        keep.wait()
        share(0, 0, k).wait_send()
        share(0, 0, 1 - k).wait_recv()
        for side in range(2):
            for s in range(1, planes):

                @pl.when(sends_at(side, s))
                def _(side=side, s=s):
                    copy(side, s).wait_send()

                @pl.when(gets_at(side, s))
                def _(side=side, s=s):
                    share(side, s, k).wait_send()
                    share(side, s, 1 - k).wait_recv()

    return step, finish


def back_owners(plan, src, out, send, recv, lsem):
    unit, ranks = plan.unit, plan.ranks
    c, f, z, k, p = place_in_mesh()

    def copy(j, owner, place):
        return pltpu.make_async_remote_copy(
            src_ref=src.at[pl.ds(j * unit, unit), :],
            dst_ref=out.at[pl.ds(place * unit, unit), :],
            send_sem=send.at[j],
            recv_sem=recv.at[place],
            device_id=(owner, z),
            device_id_type=MESH,
        )

    def local(j, place):
        return pltpu.make_async_copy(
            src.at[pl.ds(j * unit, unit), :], out.at[pl.ds(place * unit, unit), :], lsem.at[place]
        )

    blocks = [
        (rank, j, plan.back_units[rank][j] // 5, plan.back_units[rank][j] % 5)
        for rank in range(ranks)
        for j in range(5)
    ]

    def start():
        for rank, j, owner, place in blocks:

            @pl.when((p == rank) & ~((c == owner) & (f == z)))
            def _(j=j, owner=owner, place=place):
                copy(j, owner, place).start()

            @pl.when((p == rank) & (c == owner) & (f == z))
            def _(j=j, place=place):
                local(j, place).start()

    def finish():
        for rank, j, owner, place in blocks:

            @pl.when((p == rank) & ~((c == owner) & (f == z)))
            def _(j=j, owner=owner, place=place):
                copy(j, owner, place).wait_send()

            @pl.when((c == owner) & ~((p == rank) & (f == z)))
            def _(j=j, owner=owner, place=place):
                copy(j, owner, place).wait_recv()

            @pl.when((p == rank) & (c == owner) & (f == z))
            def _(j=j, place=place):
                local(j, place).wait()

    return start, finish


def front_owners(plan, src, out, send, recv, lsem):
    unit, ranks = plan.unit, plan.ranks
    c, f, z, k, p = place_in_mesh()
    height = src.shape[0] // 2
    moves, start_at = [], 0
    for slot, (units, wide) in enumerate(plan.slots):
        for rank in range(ranks):
            owner, place = units[rank] // plan.per_shard, units[rank] % plan.per_shard
            moves.append((slot, rank, owner, place, start_at, wide))
        start_at += wide

    def copy(slot, owner, place, begin, wide, half):
        return pltpu.make_async_remote_copy(
            src_ref=src.at[pl.ds(half * height, height), pl.ds(begin * unit, wide * unit)],
            dst_ref=out.at[:, pl.ds(place * unit, wide * unit)],
            send_sem=send.at[slot, half],
            recv_sem=recv.at[place],
            device_id=(2 * z + half, owner),
            device_id_type=MESH,
        )

    def local(place, begin, wide, half):
        return pltpu.make_async_copy(
            src.at[pl.ds(half * height, height), pl.ds(begin * unit, wide * unit)],
            out.at[:, pl.ds(place * unit, wide * unit)],
            lsem.at[place],
        )

    def start():
        for slot, rank, owner, place, begin, wide in moves:
            for half in range(2):
                if 2 * owner + half == rank:

                    @pl.when(p == rank)
                    def _(place=place, begin=begin, wide=wide, half=half):
                        local(place, begin, wide, half).start()

                else:

                    @pl.when(p == rank)
                    def _(slot=slot, owner=owner, place=place, begin=begin, wide=wide, half=half):
                        copy(slot, owner, place, begin, wide, half).start()

    def finish():
        for slot, rank, owner, place, begin, wide in moves:
            for half in range(2):
                if 2 * owner + half == rank:

                    @pl.when(p == rank)
                    def _(place=place, begin=begin, wide=wide, half=half):
                        local(place, begin, wide, half).wait()

                else:

                    @pl.when(p == rank)
                    def _(slot=slot, owner=owner, place=place, begin=begin, wide=wide, half=half):
                        copy(slot, owner, place, begin, wide, half).wait_send()

                    @pl.when(p == 2 * owner + half)
                    def _(slot=slot, owner=owner, place=place, begin=begin, wide=wide, half=half):
                        copy(slot, owner, place, begin, wide, half).wait_recv()

    return start, finish


def sum_scratch(plan, rows, columns):
    dma = pltpu.SemaphoreType.DMA
    steps = plan.planes - 1
    slots = pltpu.VMEM((steps, rows, columns), bf16)
    return [slots, slots, dma((2, steps)), dma((2, steps))]


def gather_scratch(plan):
    dma = pltpu.SemaphoreType.DMA
    return [dma((2, plan.planes - 1))] * 2 + [dma((2, plan.planes))] * 2 + [dma(())]


def back_sum_kernel(plan, width, src, normed, grad, out, partial, *scratch):
    unit, tall = plan.unit, 512

    def block(i):
        return src.at[:, pl.ds(pl.multiple_of(i * width, 128), width)]

    def term(row, column):
        here = pl.ds(column, unit)
        partial[pl.ds(row, tall), here] = lax.dot_general(
            normed[:, pl.ds(row, tall)], grad[:, here], (((0,), (0,)), ((), ())), preferred_element_type=f32
        ).astype(bf16)

    count = D // tall * 7
    step, finish = line_sum(plan, block, *scratch, src.shape[0])
    for s in range(1, plan.planes):
        step(s)
        tiles(
            D,
            7 * unit,
            tall,
            unit,
            count * (s - 1) // (plan.planes - 1),
            count * s // (plan.planes - 1),
            term,
        )
    finish(out)


def back_sums(plan, partial, normed, hidden_grad):
    rows, width = partial.shape[0], D // plan.planes
    return pl.pallas_call(
        functools.partial(back_sum_kernel, plan, width),
        in_specs=[VMEM_BLOCK] * 3,
        out_specs=[VMEM_BLOCK] * 2,
        out_shape=[
            jax.ShapeDtypeStruct((rows, width), bf16),
            jax.ShapeDtypeStruct((D, hidden_grad.shape[1]), bf16),
        ],
        scratch_shapes=sum_scratch(plan, rows, width),
        compiler_params=pltpu.CompilerParams(has_side_effects=True),
        cost_estimate=busy(90),
    )(partial, normed, hidden_grad)


def front_sum_kernel(plan, rows, src, back, out, owned, *scratch):
    start, done = back_owners(plan, back, owned, *scratch[:3])
    step, finish = line_sum(
        plan, lambda i: src.at[pl.ds(pl.multiple_of(i * rows, rows), rows), :], *scratch[3:], rows
    )
    step(1)
    start()
    for s in range(2, plan.planes):
        step(s)
    finish(out)
    done()


def front_sums(plan, partial, back_sum):
    dma = pltpu.SemaphoreType.DMA
    rows, width = partial.shape[0] // plan.planes, partial.shape[1]
    return pl.pallas_call(
        functools.partial(front_sum_kernel, plan, rows),
        in_specs=[VMEM_BLOCK, VMEM_BLOCK],
        out_specs=[VMEM_BLOCK, ANY_BLOCK],
        out_shape=[
            jax.ShapeDtypeStruct((rows, width), bf16),
            jax.ShapeDtypeStruct(back_sum.shape, bf16),
        ],
        scratch_shapes=[dma((5,))] * 3 + sum_scratch(plan, rows, width),
        compiler_params=pltpu.CompilerParams(has_side_effects=True),
        cost_estimate=busy(120),
    )(partial, back_sum)


def back_next_kernel(plan, own, src, out, owned, *scratch):
    start, done = front_owners(plan, src, owned, *scratch[:3])
    step, finish = line_gather(plan, own, out, *scratch[3:], own.shape[0])
    step(1)
    start()
    for s in range(2, plan.planes):
        step(s)
    finish()
    done()


def back_nexts(plan, own, front_sum):
    dma = pltpu.SemaphoreType.DMA
    return pl.pallas_call(
        functools.partial(back_next_kernel, plan),
        in_specs=[VMEM_BLOCK, VMEM_BLOCK],
        out_specs=[ANY_BLOCK, ANY_BLOCK],
        out_shape=[
            jax.ShapeDtypeStruct((2 * plan.planes * own.shape[0], own.shape[1]), bf16),
            jax.ShapeDtypeStruct((front_sum.shape[0] // 2, plan.per_shard * plan.unit), bf16),
        ],
        scratch_shapes=[dma((5, 2)), dma((plan.per_shard,)), dma((plan.per_shard,))] + gather_scratch(plan),
        compiler_params=pltpu.CompilerParams(has_side_effects=True),
        cost_estimate=busy(90),
    )(own, front_sum)


def vector_sum(plan, own, out, terms, sums, send, recv):
    planes, ranks = plan.planes, plan.ranks
    c, f, z, k, p = place_in_mesh()

    def in_plane(step, target):
        to = lax.rem(p + step, ranks)
        return pltpu.make_async_remote_copy(
            src_ref=own,
            dst_ref=terms.at[target],
            send_sem=send.at[step],
            recv_sem=recv.at[step],
            device_id=(2 * z + lax.rem(to, 2), lax.div(to, 2)),
            device_id_type=MESH,
        )

    def over_planes(step, target):
        to = lax.rem(z + step, planes)
        return pltpu.make_async_remote_copy(
            src_ref=out,
            dst_ref=sums.at[target],
            send_sem=send.at[ranks + step],
            recv_sem=recv.at[ranks + step],
            device_id=(2 * to + k, f),
            device_id_type=MESH,
        )

    def start():
        for step in range(1, ranks):
            in_plane(step, p).start()
        terms[p] = own[...]

    def middle():
        for step in range(1, ranks):
            in_plane(step, lax.rem(p + ranks - step, ranks)).wait_recv()
        total = terms[0]
        for rank in range(1, ranks):
            total = total + terms[rank]
        out[...] = total
        sums[z] = total
        for step in range(1, planes):
            over_planes(step, z).start()

    def finish():
        for step in range(1, ranks):
            in_plane(step, p).wait_send()
        for step in range(1, planes):
            over_planes(step, z).wait_send()
            over_planes(step, lax.rem(z + planes - step, planes)).wait_recv()
        total = sums[0]
        for plane in range(1, planes):
            total = total + sums[plane]
        out[...] = total

    return start, middle, finish


def front_next_kernel(plan, own, vector, out, vector_out, terms, sums, vsend, vrecv, *scratch):
    begin, middle, end = vector_sum(plan, vector, vector_out, terms, sums, vsend, vrecv)
    step, finish = line_gather(plan, own, out, *scratch, own.shape[0])
    begin()
    step(1)
    middle()
    for s in range(2, plan.planes):
        step(s)
    finish()
    end()


def front_nexts(plan, own, vector):
    dma = pltpu.SemaphoreType.DMA
    return pl.pallas_call(
        functools.partial(front_next_kernel, plan),
        in_specs=[VMEM_BLOCK, VMEM_BLOCK],
        out_specs=[ANY_BLOCK, VMEM_BLOCK],
        out_shape=[
            jax.ShapeDtypeStruct((2 * plan.planes * own.shape[0], own.shape[1]), bf16),
            jax.ShapeDtypeStruct(vector.shape, f32),
        ],
        scratch_shapes=[
            pltpu.VMEM((plan.ranks,) + vector.shape, f32),
            pltpu.VMEM((plan.planes,) + vector.shape, f32),
            dma((plan.ranks + plan.planes,)),
            dma((plan.ranks + plan.planes,)),
        ]
        + gather_scratch(plan),
        compiler_params=pltpu.CompilerParams(has_side_effects=True),
        cost_estimate=busy(120),
    )(own, vector)


def gelu_parts(u):
    scale = np.float32(np.sqrt(2.0 / np.pi))
    square = u * u
    inner = scale * u * (1.0 + 0.044715 * square)
    t = jnp.tanh(inner)
    value = 0.5 * u * (1.0 + t)
    slope = 0.5 * (1.0 + t) + 0.5 * u * (1.0 - t * t) * scale * (1.0 + 3 * 0.044715 * square)
    return value, slope


def adam_update(weight, first, second, grad, rate, count_now, decay):
    first_new = beta_first * first + (1.0 - beta_first) * grad
    second_new = beta_second * second + (1.0 - beta_second) * grad * grad
    steps_float = count_now.astype(f32)
    first_fix = 1.0 - jnp.power(beta_first, steps_float)
    second_fix = 1.0 - jnp.power(beta_second, steps_float)
    change = first_new / first_fix / (jnp.sqrt(second_new / second_fix) + adam_eps) + decay * weight
    return (weight - rate * change, first_new, second_new)


def after(value, *others):
    return lax.optimization_barrier((value,) + others)[0]


def per_device(
    tokens,
    cotangent,
    doc_ids,
    block_order,
    front_weight,
    back_weight,
    front_master,
    back_master,
    front_first,
    back_first,
    front_second,
    back_second,
    vectors,
    vector_first,
    vector_second,
    learn_rates,
    adam_step,
    *,
    plan,
):
    planes, shards, ranks, unit = plan.planes, plan.fsdp, plan.ranks, plan.unit
    both = ("ctx", "fsdp")
    contract_last = (((1,), (1,)), ((), ()))
    contract_first = (((0,), (0,)), ((), ()))
    c_index, f = lax.axis_index("ctx"), lax.axis_index("fsdp")
    z, k = c_index // 2, c_index % 2
    p = 2 * f + k
    rows = tokens.shape[1]
    plane_rows = 2 * shards * rows
    share = 2 * rows

    bias_front = vectors[:IN_COLS].reshape(-1, unit)
    bias_back = vectors[IN_COLS : IN_COLS + D]
    norm_gain = vectors[IN_COLS + D : IN_COLS + 2 * D]
    norm_shift = vectors[IN_COLS + 2 * D :]

    swap_pairs = [(2 * i + j, 2 * i + 1 - j) for i in range(planes) for j in range(2)]

    def swap_core(value):
        return lax.ppermute(value, "ctx", swap_pairs)

    def to_shard(value, step):
        return lax.ppermute(value, "fsdp", [(i, i ^ step) for i in range(shards)])

    def at(array, index):
        return lax.dynamic_index_in_dim(array, index, 0, keepdims=False)

    blocks = block_order.shape[0]
    block_tokens = doc_ids.shape[1] // blocks
    offsets = jnp.arange(block_tokens, dtype=jnp.int32)
    positions_all = (block_order[:, None] * block_tokens + offsets[None, :]).reshape(planes, share)
    own_positions = at(positions_all, z)
    plane_positions = jnp.tile(own_positions, shards)

    plane_tokens, plane_grad, documents, weight_local, back_attention = gather_first(
        plan, tokens[0], cotangent[0], doc_ids.astype(f32), front_weight, back_weight
    )
    plane_tokens = plane_tokens.reshape(plane_rows, D)
    plane_grad = plane_grad.reshape(plane_rows, D)

    normed = (normalize(plane_tokens)[0] * norm_gain + norm_shift).astype(bf16)

    unit_table = pick(plan.rank_units, p)
    bias_local = jnp.take(bias_front, unit_table, axis=0).reshape(-1)

    hidden = jnp.dot(normed, weight_local[:, : 3 * unit], preferred_element_type=f32) + bias_local[: 3 * unit]
    tables = rotation_tables(plane_positions, unit)
    query = rotate(hidden[:, :unit], tables).astype(bf16)
    key = rotate(hidden[:, unit : 2 * unit], tables).astype(bf16)
    attended_grad = lax.dot_general(
        plane_grad, back_attention, contract_last, preferred_element_type=f32
    ).astype(bf16)
    qkvg = jnp.concatenate([query, key, hidden[:, 2 * unit :].astype(bf16), attended_grad], axis=1)
    qkvg, back_up, activation, slope = exchange_first(
        plan, qkvg.reshape(planes, share, -1), normed, weight_local, bias_local[None, 3 * unit :], back_weight
    )
    qkvg = qkvg.reshape(planes * share, -1)

    seq_positions = positions_all.reshape(-1)
    doc_row = documents[0].astype(jnp.int32)
    seq_documents = jnp.take(doc_row.reshape(blocks, block_tokens), block_order, axis=0).reshape(-1)
    returned = attention(qkvg, seq_positions, seq_documents, rotation_tables(seq_positions, unit))
    returned, up_grad = exchange_back(
        plan, returned.reshape(planes, share, -1), plane_grad, back_up, slope
    )
    returned = returned.reshape(plane_rows, -1)
    back_local = jnp.concatenate([back_attention, back_up], axis=0)

    mixed = jnp.concatenate([returned[:, :unit], activation], axis=1)
    hidden_grad = jnp.concatenate([returned[:, unit:], up_grad], axis=1)

    def sum_over_cores(value):
        shaped = value.reshape(shards, 2, rows, D)
        kept = lax.dynamic_index_in_dim(shaped, k, 1, keepdims=False)
        sent = lax.dynamic_index_in_dim(shaped, 1 - k, 1, keepdims=False).astype(bf16)
        return kept + swap_core(sent).astype(f32)

    def sum_over_shards(*values):
        totals = [at(value, f) for value in values]
        for step in range(1, shards):
            pieces = jnp.stack([at(value, f ^ step).astype(bf16) for value in values])
            pieces = to_shard(pieces, step).astype(f32)
            totals = [total + piece for total, piece in zip(totals, pieces)]
        return totals

    projected_cores = sum_over_cores(jnp.dot(mixed, back_local, preferred_element_type=f32))
    normed_grad_cores = sum_over_cores(
        lax.dot_general(hidden_grad, weight_local, contract_last, preferred_element_type=f32)
    )

    back_partial = lax.dot_general(
        mixed, plane_grad, contract_first, preferred_element_type=f32
    ).astype(bf16)
    back_sum, front_partial = back_sums(plan, back_partial, normed, hidden_grad)
    back_sum, projected_cores, normed_grad_cores = lax.optimization_barrier(
        (back_sum, projected_cores, normed_grad_cores)
    )
    projected, normed_grad = sum_over_shards(projected_cores, normed_grad_cores)
    front_sum, back_owned = front_sums(plan, front_partial, back_sum)
    front_sum, projected, normed_grad = lax.optimization_barrier((front_sum, projected, normed_grad))

    inputs = tokens[0].astype(f32)
    layer_out = (inputs + projected + bias_back).astype(bf16)[None]
    unscaled, factor = normalize(inputs)
    scaled = normed_grad * norm_gain
    input_grad = factor * (
        scaled
        - jnp.mean(scaled, axis=-1, keepdims=True)
        - unscaled * jnp.mean(scaled * unscaled, axis=-1, keepdims=True)
    )
    tokens_grad = (cotangent[0].astype(f32) + input_grad).astype(bf16)[None]

    back_grad = back_owned.astype(f32)
    back_new, back_first_new, back_second_new = adam_update(
        back_master, back_first, back_second, back_grad, learn_rates[1], adam_step[0], weight_decay
    )
    back_next, front_owned = back_nexts(plan, back_new.astype(bf16), front_sum)
    front_grad = front_owned.astype(f32)
    front_new, front_first_new, front_second_new = adam_update(
        front_master, front_first, front_second, front_grad, learn_rates[0], adam_step[0], weight_decay
    )
    def column_sums(value):
        ones = jnp.ones((8, value.shape[0]), bf16)
        return jnp.dot(ones, value, preferred_element_type=f32)[0]

    spread = (jnp.arange(7 * ranks)[:, None] == unit_table[None, :]).astype(f32)
    hidden_sum = column_sums(hidden_grad).reshape(7, unit)
    front_vector = jnp.sum(spread[:, :, None] * hidden_sum[None], axis=1).reshape(-1)
    vector_term = jnp.concatenate(
        [
            front_vector,
            column_sums(cotangent[0]),
            jnp.sum(normed_grad * unscaled, axis=0),
            jnp.sum(normed_grad, axis=0),
        ]
    )
    front_next, vector_grad = front_nexts(plan, front_new.astype(bf16), vector_term.reshape(-1, 128))
    vector_grad = vector_grad.reshape(-1)

    count_now = adam_step[0]
    vectors_new, vector_first_new, vector_second_new = adam_update(
        vectors, vector_first, vector_second, vector_grad, learn_rates[2], count_now, 0.0
    )

    return (
        layer_out,
        tokens_grad,
        front_grad,
        back_grad,
        vector_grad,
        front_new,
        back_new,
        vectors_new,
        front_first_new,
        back_first_new,
        vector_first_new,
        front_second_new,
        back_second_new,
        vector_second_new,
        front_next,
        back_next,
    )


def solution(mesh):
    plan = Layout(mesh.shape["ctx"], mesh.shape["fsdp"])
    tokens_spec = P("fsdp", "ctx", None)
    cols, owned, same = P(None, "fsdp"), P("ctx", "fsdp"), P()
    in_specs = (
        (tokens_spec, tokens_spec, P("fsdp", None), same, cols, cols)
        + (owned,) * 6
        + (same,) * 5
    )
    out_specs = (
        (tokens_spec, tokens_spec, owned, owned, same)
        + (owned, owned, same) * 3
        + (cols, cols)
    )
    return jax.shard_map(
        functools.partial(per_device, plan=plan),
        mesh=mesh,
        in_specs=in_specs,
        out_specs=out_specs,
        check_vma=False,
    )
```

```python
import functools

import jax
import jax.numpy as jnp
import numpy as np
from jax import lax
from jax.experimental import pallas as pl
from jax.experimental.pallas import tpu as pltpu
from jax.sharding import PartitionSpec as P

D = 2048
HEADS = 32
FF = 8192
ROT = 32
HEAD_DIM = 64
IN_COLS = 14336
BACK_ROWS = 10240

norm_eps = 1e-05
beta_first = 0.9
beta_second = 0.95
adam_eps = 1e-08
weight_decay = 0.1
masked_score = -1e30
bf16 = jnp.bfloat16
f32 = jnp.float32


class Layout:
    def __init__(self, ctx, fsdp):
        self.ctx, self.fsdp, self.planes, self.ranks = ctx, fsdp, ctx // 2, 2 * fsdp
        assert ctx % 2 == 0 and self.planes == fsdp
        self.unit = D // self.ranks
        self.per_shard = IN_COLS // self.unit // fsdp
        r = self.ranks
        first_up = 3 * r
        home = {f: [] for f in range(fsdp)}
        for g in range(first_up, 7 * r, 2):
            assert g // self.per_shard == (g + 1) // self.per_shard
            home[g // self.per_shard].append(g)
        pairs = {p: [None, None] for p in range(r)}
        for f in range(fsdp):
            if len(home[f]) >= 4:
                keep, home[f] = home[f][:4], home[f][4:]
                pairs[2 * f], pairs[2 * f + 1] = keep[:2], keep[2:]
            elif home[f]:
                keep, home[f] = home[f], []
                for i, g in enumerate(keep):
                    pairs[2 * f + i % 2][(i + i // 2) % 2] = g
        for s in range(2):
            for k in range(2):
                used = set()
                for f in range(fsdp):
                    p = 2 * f + k
                    if pairs[p][s] is not None:
                        continue
                    options = sorted(
                        (h for h in range(fsdp) if home[h]),
                        key=lambda h: (h in used, bin(h ^ f).count("1"), -len(home[h])),
                    )
                    used.add(options[0])
                    pairs[p][s] = home[options[0]].pop(0)
        self.pairs = pairs
        self.slots = [
            ([p for p in range(r)], 1),
            ([r + p for p in range(r)], 1),
            ([2 * r + p for p in range(r)], 1),
            ([pairs[p][0] for p in range(r)], 2),
            ([pairs[p][1] for p in range(r)], 2),
        ]
        self.rounds = []
        for units, _ in self.slots:
            rounds = []
            for k in range(2):
                for f in range(fsdp):
                    src = units[2 * f + k] // self.per_shard
                    if src == f:
                        continue
                    for one in rounds:
                        if all((src, k) != (a, c) for a, _, c in one):
                            one.append((src, f, k))
                            break
                    else:
                        rounds.append([(src, f, k)])
            self.rounds.append(rounds)
        self.rank_units = [
            [p, r + p, 2 * r + p, pairs[p][0], pairs[p][0] + 1, pairs[p][1], pairs[p][1] + 1]
            for p in range(r)
        ]
        self.back_units = [[p] + [g - 2 * r for g in self.rank_units[p][3:]] for p in range(r)]
        self.matchings = []
        left = {p: list(range(5)) for p in range(r)}
        own = lambda p, j: self.back_units[p][j] // 5
        for _ in range(5):
            match = {}

            def assign(p, seen):
                for j in left[p]:
                    c = own(p, j)
                    if c in seen:
                        continue
                    seen.add(c)
                    if c not in match or assign(match[c][0], seen):
                        match[c] = (p, j)
                        return True
                return False

            for p in range(r):
                assert assign(p, set())
            for c, (p, j) in match.items():
                left[p].remove(j)
            self.matchings.append(match)

    def device(self, z, k, f):
        return (2 * z + k) * self.fsdp + f


def pick(table, index):
    return jnp.asarray(np.asarray(table, np.int32))[index]


def normalize(values):
    values = values.astype(f32)
    centered = values - jnp.mean(values, axis=-1, keepdims=True)
    factor = lax.rsqrt(jnp.mean(centered * centered, axis=-1, keepdims=True) + norm_eps)
    return centered * factor, factor


def rotation_tables(positions, width):
    half = ROT // 2
    lane = np.arange(width) % HEAD_DIM
    frequency = jnp.power(
        10000.0, -2.0 * jnp.asarray(lane % half, f32) / ROT
    )
    angles = positions.astype(f32)[:, None] * frequency[None, :]
    rotated = jnp.asarray(lane < ROT)
    lower = jnp.asarray(lane < half)
    cosine = jnp.where(rotated, jnp.cos(angles), 1.0)
    sine = jnp.where(rotated, jnp.sin(angles), 0.0)
    return cosine, jnp.where(lower, -sine, 0.0), jnp.where(lower, 0.0, sine)


def across(table, width):
    return jnp.concatenate([table] * (width // table.shape[1]), axis=1)


def prepare_kernel(
    tok, grad, weight, back, bias, gain, shift, cosine, from_above, from_below, normed_ref, out_ref
):
    half, width = ROT // 2, back.shape[0]
    contract_last = (((1,), (1,)), ((), ()))
    normed = (normalize(tok[...])[0] * gain[...] + shift[...]).astype(bf16)
    normed_ref[...] = normed
    hidden = jnp.dot(normed, weight[...], preferred_element_type=f32) + bias[...]
    tables = [across(ref[...], width) for ref in (cosine, from_above, from_below)]
    for number in range(2):
        values = hidden[:, number * width : (number + 1) * width]
        out_ref[:, number * width : (number + 1) * width] = (
            values * tables[0]
            + pltpu.roll(values, width - half, 1) * tables[1]
            + pltpu.roll(values, half, 1) * tables[2]
        ).astype(bf16)
    out_ref[:, 2 * width : 3 * width] = hidden[:, 2 * width :].astype(bf16)
    out_ref[:, 3 * width :] = lax.dot_general(
        grad[...], back[...], contract_last, preferred_element_type=f32
    ).astype(bf16)


def prepare(tokens, grad, weight, back, bias, gain, shift, tables):
    length, width, block = tokens.shape[0], back.shape[0], tables[0].shape[0]
    rows = lambda columns: pl.BlockSpec((block, columns), lambda i: (i, 0))
    fixed = lambda height, columns: pl.BlockSpec((height, columns), lambda i: (0, 0))
    return pl.pallas_call(
        prepare_kernel,
        grid=(length // block,),
        in_specs=[
            rows(D),
            rows(D),
            fixed(D, 3 * width),
            fixed(width, D),
            fixed(1, 3 * width),
            fixed(1, D),
            fixed(1, D),
        ]
        + [fixed(block, tables[0].shape[1])] * 3,
        out_specs=[rows(D), rows(4 * width)],
        out_shape=[
            jax.ShapeDtypeStruct((length, D), bf16),
            jax.ShapeDtypeStruct((length, 4 * width), bf16),
        ],
        cost_estimate=pl.CostEstimate(
            flops=8 * length * width * D, transcendentals=0, bytes_accessed=16 * length * D
        ),
    )(tokens, grad, weight, back, bias, gain, shift, *tables)


def attention_kernel(
    x_ref, pos_q, pos_k, seg_q, seg_k, cosine, from_above, from_below, out_ref, dq_ref, dk_ref, dv_ref
):
    scale = HEAD_DIM ** (-0.5)
    half = ROT // 2
    block, width = dq_ref.shape
    length = dk_ref.shape[0]
    rows = pl.ds(pl.multiple_of(pl.program_id(0) * block, block), block)

    @pl.when(pl.program_id(0) == 0)
    def _():
        dk_ref[...] = jnp.zeros_like(dk_ref)
        dv_ref[...] = jnp.zeros_like(dv_ref)

    def turn_back(values, at):
        return (
            values * across(cosine[at, :], width)
            + pltpu.roll(values * across(from_above[at, :], width), half, 1)
            + pltpu.roll(values * across(from_below[at, :], width), width - half, 1)
        ).astype(bf16)

    allowed = (pos_k[...] <= pos_q[...]) & (seg_k[...] == seg_q[...])
    bias = jnp.where(allowed, 0.0, masked_score)
    last = (((1,), (1,)), ((), ()))
    first = (((0,), (0,)), ((), ()))
    for head in range(width // HEAD_DIM):
        q_cols, k_cols, v_cols, g_cols = (
            slice(n * width + head * HEAD_DIM, n * width + (head + 1) * HEAD_DIM) for n in range(4)
        )
        q, g = x_ref[rows, q_cols], x_ref[rows, g_cols]
        k, v = x_ref[:, k_cols], x_ref[:, v_cols]
        scores = lax.dot_general(q, k, last, preferred_element_type=f32) * scale + bias
        weights = jnp.exp(scores - jnp.max(scores, axis=1, keepdims=True))
        probs = weights * (1.0 / jnp.sum(weights, axis=1, keepdims=True))
        probs_low = probs.astype(bf16)
        out = jnp.dot(probs_low, v, preferred_element_type=f32)
        out_ref[rows, q_cols] = out.astype(bf16)
        prob_grad = lax.dot_general(g, v, last, preferred_element_type=f32)
        delta = jnp.sum(g.astype(f32) * out, axis=1, keepdims=True)
        score_grad = (probs * (prob_grad - delta)).astype(bf16)
        dq_ref[:, q_cols] = jnp.dot(score_grad, k, preferred_element_type=f32) * scale
        dk_ref[:, q_cols] += lax.dot_general(score_grad, q, first, preferred_element_type=f32) * scale
        dv_ref[:, q_cols] += lax.dot_general(probs_low, g, first, preferred_element_type=f32)
    out_ref[rows, width : 2 * width] = turn_back(dq_ref[...], rows)

    @pl.when(pl.program_id(0) == pl.num_programs(0) - 1)
    def _():
        for number in range(length // block):
            at = slice(number * block, (number + 1) * block)
            out_ref[at, 2 * width : 3 * width] = turn_back(dk_ref[at, :], at)
            out_ref[at, 3 * width :] = dv_ref[at, :].astype(bf16)


def attention(values, positions, segments, tables):
    length, width = values.shape[0], values.shape[1] // 4
    block = 256
    whole = lambda columns: pl.BlockSpec((length, columns), lambda i: (0, 0))
    column = pl.BlockSpec((block, 1), lambda i: (i, 0))
    line = pl.BlockSpec((1, length), lambda i: (0, 0))
    return pl.pallas_call(
        attention_kernel,
        grid=(length // block,),
        in_specs=[whole(4 * width), column, line, column, line] + [whole(tables[0].shape[1])] * 3,
        out_specs=whole(4 * width),
        out_shape=jax.ShapeDtypeStruct((length, 4 * width), bf16),
        scratch_shapes=[
            pltpu.VMEM((block, width), f32),
            pltpu.VMEM((length, width), f32),
            pltpu.VMEM((length, width), f32),
        ],
        cost_estimate=pl.CostEstimate(
            flops=14 * length * length * width,
            transcendentals=length * length * width // HEAD_DIM,
            bytes_accessed=20 * length * width,
        ),
    )(values, positions[:, None], positions[None], segments[:, None], segments[None], *tables)


MESH = pl.DeviceIdType.MESH


VMEM_BLOCK = pl.BlockSpec(memory_space=pltpu.VMEM)
ANY_BLOCK = pl.BlockSpec(memory_space=pl.ANY)


def busy(microseconds):
    return pl.CostEstimate(flops=int(microseconds * 900e6), transcendentals=0, bytes_accessed=0)


def place_in_mesh():
    c, f = lax.axis_index("ctx"), lax.axis_index("fsdp")
    z, k = lax.div(c, 2), lax.rem(c, 2)
    return c, f, z, k, 2 * f + k


def bounce(source, buffer, target, sem):
    one = pltpu.make_async_copy(source, buffer, sem)
    one.start()
    one.wait()
    two = pltpu.make_async_copy(buffer, target, sem)
    two.start()
    two.wait()


def gather_kernel(
    plan, tok, cot, doc, front, back, tok_out, cot_out, doc_out, w_out, b_out,
    w_buf, b_buf, tsend, trecv, csend, crecv, wsend, wrecv, rsend, rrecv, bsend, brecv, dsend, drecv, lsem,
):
    shards, unit, ranks = plan.fsdp, plan.unit, plan.ranks
    c, f, z, k, p = place_in_mesh()
    other = c + 1 - 2 * k
    width = D // shards
    both = ((tok, tok_out), (cot, cot_out))

    def cols(block):
        return pl.ds(pl.multiple_of(block * width, 128), width)

    def remote(src, dst, send, recv, device):
        return pltpu.make_async_remote_copy(
            src_ref=src, dst_ref=dst, send_sem=send, recv_sem=recv, device_id=device, device_id_type=MESH
        )

    def peer(step):
        return lax.rem(f + step, shards)

    def giver(step):
        return lax.rem(f + shards - step, shards)

    def send_tokens(n, step):
        src, out = both[n]
        return remote(src, out.at[f, k], tsend.at[n, step], trecv.at[n, step], (c, peer(step)))

    def get_tokens(n, step):
        here = both[n][1].at[giver(step), k]
        return remote(here, here, tsend.at[n, step], trecv.at[n, step], (c, peer(step)))

    def share(n, step):
        src, out = both[n]
        here = out.at[giver(step), k]
        return remote(src if step == 0 else here, here, csend.at[n, step], crecv.at[n, step], (other, f))

    def get_share(n, step):
        here = both[n][1].at[giver(step), 1 - k]
        return remote(here, here, csend.at[n, step], crecv.at[n, step], (other, f))

    def rows_of(dst):
        return pl.ds(pl.multiple_of((2 * dst + k) * unit, unit), unit)

    def send_back(step):
        return remote(
            back.at[rows_of(peer(step)), :], b_out.at[:, cols(f)], bsend.at[step], brecv.at[step], (c, peer(step))
        )

    def get_back(step):
        here = b_out.at[:, cols(giver(step))]
        return remote(here, here, bsend.at[step], brecv.at[step], (c, peer(step)))

    def send_doc(step):
        return remote(doc, doc_out, dsend.at[step], drecv, (c, peer(step)))

    start_weights, relay_weights, finish_weights = weight_moves(
        plan, front, w_out, w_buf, wsend, wrecv, rsend, rrecv, lsem.at[2]
    )
    own = [pltpu.make_async_copy(src, out.at[f, k], lsem.at[4 * n]) for n, (src, out) in enumerate(both)]
    own_doc = pltpu.make_async_copy(doc, doc_out, lsem.at[1])
    start_weights()
    for n in range(2):
        for step in range(1, shards):
            send_tokens(n, step).start()
        share(n, 0).start()
        own[n].start()
    for step in range(1, shards):
        send_back(step).start()

    @pl.when(f == z)
    def _():
        own_doc.start()
        for step in range(1, shards):
            send_doc(step).start()

    relay_weights()
    for n in range(2):
        for step in range(1, shards):
            get_tokens(n, step).wait_recv()
            share(n, step).start()
    bounce(back.at[rows_of(f), :], b_buf, b_out.at[:, cols(f)], lsem.at[3])
    for n in range(2):
        own[n].wait()

    @pl.when(f == z)
    def _():
        own_doc.wait()
        for step in range(1, shards):
            send_doc(step).wait_send()

    @pl.when(f != z)
    def _():
        send_doc(1).wait_recv()

    for n in range(2):
        for step in range(shards):
            get_share(n, step).wait_recv()
            share(n, step).wait_send()
        for step in range(1, shards):
            send_tokens(n, step).wait_send()
    for step in range(1, shards):
        send_back(step).wait_send()
        get_back(step).wait_recv()
    finish_weights()


def moves_between(moves, device_of):
    c, f, z, k, p = place_in_mesh()

    def remote(move):
        src, dst, source, target, send, recv, _, _ = move
        return pltpu.make_async_remote_copy(
            src_ref=source, dst_ref=target, send_sem=send, recv_sem=recv, device_id=device_of(c, dst), device_id_type=MESH
        )

    def start():
        for move in moves:
            if move[0] != move[1]:

                @pl.when(p == move[0])
                def _(move=move):
                    remote(move).start()

        for move in moves:
            if move[0] == move[1]:

                @pl.when(p == move[0])
                def _(move=move):
                    bounce(move[2], move[6], move[3], move[7])

    def finish():
        for move in moves:
            if move[0] != move[1]:

                @pl.when(p == move[0])
                def _(move=move):
                    remote(move).wait_send()

                @pl.when(p == move[1])
                def _(move=move):
                    remote(move).wait_recv()

    return start, finish


def weight_moves(plan, front, out, buffer, send, recv, relay_send, relay_recv, local):
    unit, moves, begin = plan.unit, [], 0
    c, f, z, k, p = place_in_mesh()
    half, parity = D // 2, lax.rem(z, 2)

    def rows(part):
        return pl.ds(pl.multiple_of(part * half, half), half)

    for slot, (units, wide) in enumerate(plan.slots):
        for dst in range(plan.ranks):
            src, at = units[dst] // plan.per_shard, units[dst] % plan.per_shard
            moves.append(
                (slot, 2 * src + dst % 2, dst, pl.ds(at * unit, wide * unit), pl.ds(begin * unit, wide * unit), wide * unit)
            )
        begin += wide

    def copy(move):
        slot, _, dst, source, target, _ = move
        return pltpu.make_async_remote_copy(
            src_ref=front.at[rows(parity), source],
            dst_ref=out.at[rows(parity), target],
            send_sem=send.at[slot, dst // 2],
            recv_sem=recv.at[slot],
            device_id=(c, dst // 2),
            device_id_type=MESH,
        )

    def pass_on(move, part):
        slot, _, _, _, target, _ = move
        here = out.at[rows(part), target]
        return pltpu.make_async_remote_copy(
            src_ref=here,
            dst_ref=here,
            send_sem=relay_send.at[slot],
            recv_sem=relay_recv.at[slot],
            device_id=(c + 2 - 4 * parity, f),
            device_id_type=MESH,
        )

    def start():
        for move in moves:
            if move[1] != move[2]:

                @pl.when(p == move[1])
                def _(move=move):
                    copy(move).start()

    def relay():
        for move in moves:
            if move[1] != move[2]:

                @pl.when(p == move[2])
                def _(move=move):
                    copy(move).wait_recv()
                    pass_on(move, parity).start()

    def finish():
        for move in moves:
            if move[1] == move[2]:

                @pl.when(p == move[2])
                def _(move=move):
                    bounce(front.at[:, move[3]], buffer.at[:, pl.ds(0, move[5])], out.at[:, move[4]], local)

        for move in moves:
            if move[1] != move[2]:

                @pl.when(p == move[1])
                def _(move=move):
                    copy(move).wait_send()

                @pl.when(p == move[2])
                def _(move=move):
                    pass_on(move, parity).wait_send()
                    pass_on(move, 1 - parity).wait_recv()

    return start, relay, finish


def back_moves(plan, back, out, buffer, send, recv, local):
    unit, width, moves = plan.unit, D // plan.fsdp, []
    for dst in range(plan.ranks):
        for src in range(plan.fsdp):
            for number in range(2):
                row = plan.back_units[dst][1 + 2 * number]
                moves.append(
                    (
                        2 * src + dst % 2,
                        dst,
                        back.at[pl.ds(row * unit, 2 * unit), :],
                        out.at[pl.ds(2 * number * unit, 2 * unit), pl.ds(src * width, width)],
                        send.at[number, dst // 2],
                        recv.at[number, src],
                        buffer,
                        local,
                    )
                )
    return moves_between(moves, lambda c, dst: (c, dst // 2))


def line_exchange(plan, src, out, send, recv, local):
    planes = plan.planes
    c, f, z, k, p = place_in_mesh()

    def copy(step):
        to = lax.rem(z + step, planes)
        return pltpu.make_async_remote_copy(
            src_ref=src.at[to],
            dst_ref=out.at[z],
            send_sem=send.at[step],
            recv_sem=recv.at[step],
            device_id=(2 * to + k, f),
            device_id_type=MESH,
        )

    def arrival(step):
        here = out.at[lax.rem(z + planes - step, planes)]
        return pltpu.make_async_remote_copy(
            src_ref=here,
            dst_ref=here,
            send_sem=send.at[step],
            recv_sem=recv.at[step],
            device_id=(2 * lax.rem(z + step, planes) + k, f),
            device_id_type=MESH,
        )

    keep = pltpu.make_async_copy(src.at[z], out.at[z], local)

    def start():
        for step in range(planes - 1, 0, -1):
            copy(step).start()
        keep.start()

    def finish():
        keep.wait()
        for step in range(1, planes):
            copy(step).wait_send()
            arrival(step).wait_recv()

    return start, finish


def gather_first(plan, tokens, cotangent, documents, front_weight, back_weight):
    shards, unit = plan.fsdp, plan.unit
    rows, length = tokens.shape[0], documents.shape[1]
    dma = pltpu.SemaphoreType.DMA
    return pl.pallas_call(
        functools.partial(gather_kernel, plan),
        in_specs=[VMEM_BLOCK] * 3 + [ANY_BLOCK] * 2,
        out_specs=[ANY_BLOCK] * 5,
        out_shape=[
            jax.ShapeDtypeStruct((shards, 2, rows, D), bf16),
            jax.ShapeDtypeStruct((shards, 2, rows, D), bf16),
            jax.ShapeDtypeStruct((1, length), f32),
            jax.ShapeDtypeStruct((D, 7 * unit), bf16),
            jax.ShapeDtypeStruct((unit, D), bf16),
        ],
        scratch_shapes=[
            pltpu.VMEM((D, 2 * unit), bf16),
            pltpu.VMEM((unit, D // shards), bf16),
            dma((2, shards)),
            dma((2, shards)),
            dma((2, shards)),
            dma((2, shards)),
            dma((5, shards)),
            dma((5,)),
            dma((5,)),
            dma((5,)),
            dma((shards,)),
            dma((shards,)),
            dma((shards,)),
            dma(()),
            dma((5,)),
        ],
        compiler_params=pltpu.CompilerParams(has_side_effects=True),
        cost_estimate=busy(130),
    )(tokens, cotangent, documents, front_weight, back_weight)


def tiles(rows, columns, tall, wide, first, last, body):
    across = columns // wide

    def one(i, carry):
        row = pl.multiple_of(lax.div(i, across) * tall, tall)
        column = pl.multiple_of(lax.rem(i, across) * wide, wide)
        body(row, column)
        return carry

    lax.fori_loop(first, last, one, 0)


def exchange_kernel(
    plan, src, normed, weight, bias, back, out, b_out, act, slope, buffer, send, recv, local, bsend, brecv
):
    unit = plan.unit
    start, finish = line_exchange(plan, src, out, send, recv, local.at[0])
    start_rows, finish_rows = back_moves(plan, back, b_out, buffer, bsend, brecv, local.at[1])
    start()
    start_rows()
    tall = 512

    def units(row, column):
        at, here = pl.ds(row, tall), pl.ds(column, unit)
        u = jnp.dot(
            normed[at, :],
            weight[:, pl.ds(pl.multiple_of(column + 3 * unit, unit), unit)],
            preferred_element_type=f32,
        )
        value, steep = gelu_parts(u + bias[:, here])
        act[at, here] = value.astype(bf16)
        slope[at, here] = steep

    tiles(act.shape[0], 4 * unit, tall, unit, 0, act.shape[0] // tall * 4, units)
    finish()
    finish_rows()


def exchange_first(plan, values, normed, weight, bias, back_weight):
    dma = pltpu.SemaphoreType.DMA
    unit, shards = plan.unit, plan.fsdp
    length = normed.shape[0]
    return pl.pallas_call(
        functools.partial(exchange_kernel, plan),
        in_specs=[VMEM_BLOCK] * 4 + [ANY_BLOCK],
        out_specs=[ANY_BLOCK, ANY_BLOCK, VMEM_BLOCK, VMEM_BLOCK],
        out_shape=[
            jax.ShapeDtypeStruct(values.shape, bf16),
            jax.ShapeDtypeStruct((4 * unit, D), bf16),
            jax.ShapeDtypeStruct((length, 4 * unit), bf16),
            jax.ShapeDtypeStruct((length, 4 * unit), f32),
        ],
        scratch_shapes=[
            pltpu.VMEM((2 * unit, D // shards), bf16),
            dma((plan.planes,)),
            dma((plan.planes,)),
            dma((2,)),
            dma((2, shards)),
            dma((2, shards)),
        ],
        compiler_params=pltpu.CompilerParams(has_side_effects=True),
        cost_estimate=busy(50),
    )(values, normed, weight, bias, back_weight)


def exchange_back_kernel(plan, src, grad, rows, slope, out, up_grad, send, recv, local):
    unit, tall = plan.unit, 512
    start, finish = line_exchange(plan, src, out, send, recv, local)
    start()

    def units(row, column):
        at, here = pl.ds(row, tall), pl.ds(column, unit)
        mixed_grad = lax.dot_general(
            grad[at, :], rows[here, :], (((1,), (1,)), ((), ())), preferred_element_type=f32
        )
        up_grad[at, here] = (mixed_grad * slope[at, here]).astype(bf16)

    tiles(grad.shape[0], 4 * unit, tall, unit, 0, grad.shape[0] // tall * 4, units)
    finish()


def exchange_back(plan, values, grad, rows, slope):
    dma = pltpu.SemaphoreType.DMA
    return pl.pallas_call(
        functools.partial(exchange_back_kernel, plan),
        in_specs=[VMEM_BLOCK] * 4,
        out_specs=[ANY_BLOCK, VMEM_BLOCK],
        out_shape=[
            jax.ShapeDtypeStruct(values.shape, bf16),
            jax.ShapeDtypeStruct(slope.shape, bf16),
        ],
        scratch_shapes=[dma((plan.planes,)), dma((plan.planes,)), dma(())],
        compiler_params=pltpu.CompilerParams(has_side_effects=True),
        cost_estimate=busy(50),
    )(values, grad, rows, slope)


def line_sum(plan, block, rising, falling, sends, gets, rows):
    planes, chunk = plan.planes, 64
    c, f, z, k, p = place_in_mesh()

    def copy(side, s, src):
        slots = (rising, falling)[side]
        return pltpu.make_async_remote_copy(
            src_ref=src,
            dst_ref=slots.at[s - 1],
            send_sem=sends.at[side, s - 1],
            recv_sem=gets.at[side, s - 1],
            device_id=(c + 2 - 4 * side, f),
            device_id_type=MESH,
        )

    def add(side, s, number):
        slots = (rising, falling)[side]
        term = block(number)

        def body(i, carry):
            at = pl.ds(pl.multiple_of(i * chunk, chunk), chunk)
            slots[s - 1, at, :] = (slots[s - 1, at, :].astype(f32) + term[at, :].astype(f32)).astype(bf16)
            return carry

        lax.fori_loop(0, rows // chunk, body, 0)

    def step(s):
        for side in range(2):
            place = z if side == 0 else planes - 1 - z
            number = planes - s + place
            number = number if side == 0 else planes - 1 - number

            @pl.when(place == 0)
            def _(side=side, number=number):
                copy(side, s, block(number)).start()

            if s > 1:

                @pl.when((place > 0) & (place < s) & (place < planes - 1))
                def _(side=side, number=number):
                    slots = (rising, falling)[side]
                    copy(side, s - 1, slots.at[s - 2]).wait_recv()
                    add(side, s - 1, number)
                    copy(side, s, slots.at[s - 2]).start()

    def finish(out):
        last = planes - 1
        for side in range(2):
            place = z if side == 0 else planes - 1 - z
            slots = (rising, falling)[side]

            @pl.when(place > 0)
            def _(side=side, slots=slots):
                copy(side, last, slots.at[last - 1]).wait_recv()

        mine = block(z)

        def total(ups, downs):
            def body(i, carry):
                at = pl.ds(pl.multiple_of(i * chunk, chunk), chunk)
                value = mine[at, :].astype(f32)
                if ups:
                    value = value + rising[last - 1, at, :].astype(f32)
                if downs:
                    value = value + falling[last - 1, at, :].astype(f32)
                out[at, :] = value.astype(out.dtype)
                return carry

            lax.fori_loop(0, rows // chunk, body, 0)

        @pl.when(z == 0)
        def _():
            total(False, True)

        @pl.when(z == planes - 1)
        def _():
            total(True, False)

        @pl.when((z > 0) & (z < planes - 1))
        def _():
            total(True, True)

        for side in range(2):
            place = z if side == 0 else planes - 1 - z
            slots = (rising, falling)[side]
            for s in range(1, planes):

                @pl.when((place < s) & (place < planes - 1))
                def _(side=side, slots=slots, s=s):
                    copy(side, s, slots.at[s - 1]).wait_send()

    return step, finish


def line_gather(plan, own, out, sends, gets, share_sends, share_gets, local, height):
    planes = plan.planes
    c, f, z, k, p = place_in_mesh()
    other = c + 1 - 2 * k

    def rows_of(plane, core):
        return out.at[pl.ds(pl.multiple_of((2 * plane + core) * height, height), height), :]

    def origin(side, s):
        return z - s if side == 0 else z + s

    def copy(side, s):
        plane = origin(side, s - 1)
        src = own if s == 1 else rows_of(plane, k)
        return pltpu.make_async_remote_copy(
            src_ref=src,
            dst_ref=rows_of(plane, k),
            send_sem=sends.at[side, s - 1],
            recv_sem=gets.at[side, s - 1],
            device_id=(c + 2 - 4 * side, f),
            device_id_type=MESH,
        )

    def arrival(side, s):
        here = rows_of(origin(side, s), k)
        return pltpu.make_async_remote_copy(
            src_ref=here,
            dst_ref=here,
            send_sem=sends.at[side, s - 1],
            recv_sem=gets.at[side, s - 1],
            device_id=(c + 2 - 4 * side, f),
            device_id_type=MESH,
        )

    def share(side, s, core):
        plane = origin(side, s)
        here = rows_of(plane, core)
        src = own if s == 0 else here
        return pltpu.make_async_remote_copy(
            src_ref=src,
            dst_ref=here,
            send_sem=share_sends.at[side, s],
            recv_sem=share_gets.at[side, s],
            device_id=(other, f),
            device_id_type=MESH,
        )

    keep = pltpu.make_async_copy(own, rows_of(z, k), local)

    def sends_at(side, s):
        place = z if side == 0 else planes - 1 - z
        return (place >= s - 1) & (place < planes - 1)

    def gets_at(side, s):
        place = z if side == 0 else planes - 1 - z
        return place >= s

    def take(s):
        for side in range(2):

            @pl.when(gets_at(side, s))
            def _(side=side):
                arrival(side, s).wait_recv()
                if s < planes - 1:

                    @pl.when(sends_at(side, s + 1))
                    def _():
                        copy(side, s + 1).start()

                share(side, s, k).start()

    def step(s):
        if s > 1:
            take(s - 1)
            return
        for side in range(2):

            @pl.when(sends_at(side, 1))
            def _(side=side):
                copy(side, 1).start()

        share(0, 0, k).start()
        keep.start()

    def finish():
        take(planes - 1)
        keep.wait()
        share(0, 0, k).wait_send()
        share(0, 0, 1 - k).wait_recv()
        for side in range(2):
            for s in range(1, planes):

                @pl.when(sends_at(side, s))
                def _(side=side, s=s):
                    copy(side, s).wait_send()

                @pl.when(gets_at(side, s))
                def _(side=side, s=s):
                    share(side, s, k).wait_send()
                    share(side, s, 1 - k).wait_recv()

    return step, finish


def back_owners(plan, src, out, send, recv, lsem):
    unit, ranks = plan.unit, plan.ranks
    c, f, z, k, p = place_in_mesh()

    def copy(j, owner, place):
        return pltpu.make_async_remote_copy(
            src_ref=src.at[pl.ds(j * unit, unit), :],
            dst_ref=out.at[pl.ds(place * unit, unit), :],
            send_sem=send.at[j],
            recv_sem=recv.at[place],
            device_id=(owner, z),
            device_id_type=MESH,
        )

    def local(j, place):
        return pltpu.make_async_copy(
            src.at[pl.ds(j * unit, unit), :], out.at[pl.ds(place * unit, unit), :], lsem.at[place]
        )

    blocks = [
        (rank, j, plan.back_units[rank][j] // 5, plan.back_units[rank][j] % 5)
        for rank in range(ranks)
        for j in range(5)
    ]

    def start():
        for rank, j, owner, place in blocks:

            @pl.when((p == rank) & ~((c == owner) & (f == z)))
            def _(j=j, owner=owner, place=place):
                copy(j, owner, place).start()

            @pl.when((p == rank) & (c == owner) & (f == z))
            def _(j=j, place=place):
                local(j, place).start()

    def finish():
        for rank, j, owner, place in blocks:

            @pl.when((p == rank) & ~((c == owner) & (f == z)))
            def _(j=j, owner=owner, place=place):
                copy(j, owner, place).wait_send()

            @pl.when((c == owner) & ~((p == rank) & (f == z)))
            def _(j=j, owner=owner, place=place):
                copy(j, owner, place).wait_recv()

            @pl.when((p == rank) & (c == owner) & (f == z))
            def _(j=j, place=place):
                local(j, place).wait()

    return start, finish


def front_owners(plan, src, out, send, recv, lsem):
    unit, ranks = plan.unit, plan.ranks
    c, f, z, k, p = place_in_mesh()
    height = src.shape[0] // 2
    moves, start_at = [], 0
    for slot, (units, wide) in enumerate(plan.slots):
        for rank in range(ranks):
            owner, place = units[rank] // plan.per_shard, units[rank] % plan.per_shard
            moves.append((slot, rank, owner, place, start_at, wide))
        start_at += wide

    def copy(slot, owner, place, begin, wide, half):
        return pltpu.make_async_remote_copy(
            src_ref=src.at[pl.ds(half * height, height), pl.ds(begin * unit, wide * unit)],
            dst_ref=out.at[:, pl.ds(place * unit, wide * unit)],
            send_sem=send.at[slot, half],
            recv_sem=recv.at[place],
            device_id=(2 * z + half, owner),
            device_id_type=MESH,
        )

    def local(place, begin, wide, half):
        return pltpu.make_async_copy(
            src.at[pl.ds(half * height, height), pl.ds(begin * unit, wide * unit)],
            out.at[:, pl.ds(place * unit, wide * unit)],
            lsem.at[place],
        )

    def start():
        for slot, rank, owner, place, begin, wide in moves:
            for half in range(2):
                if 2 * owner + half == rank:

                    @pl.when(p == rank)
                    def _(place=place, begin=begin, wide=wide, half=half):
                        local(place, begin, wide, half).start()

                else:

                    @pl.when(p == rank)
                    def _(slot=slot, owner=owner, place=place, begin=begin, wide=wide, half=half):
                        copy(slot, owner, place, begin, wide, half).start()

    def finish():
        for slot, rank, owner, place, begin, wide in moves:
            for half in range(2):
                if 2 * owner + half == rank:

                    @pl.when(p == rank)
                    def _(place=place, begin=begin, wide=wide, half=half):
                        local(place, begin, wide, half).wait()

                else:

                    @pl.when(p == rank)
                    def _(slot=slot, owner=owner, place=place, begin=begin, wide=wide, half=half):
                        copy(slot, owner, place, begin, wide, half).wait_send()

                    @pl.when(p == 2 * owner + half)
                    def _(slot=slot, owner=owner, place=place, begin=begin, wide=wide, half=half):
                        copy(slot, owner, place, begin, wide, half).wait_recv()

    return start, finish


def sum_scratch(plan, rows, columns):
    dma = pltpu.SemaphoreType.DMA
    steps = plan.planes - 1
    slots = pltpu.VMEM((steps, rows, columns), bf16)
    return [slots, slots, dma((2, steps)), dma((2, steps))]


def gather_scratch(plan):
    dma = pltpu.SemaphoreType.DMA
    return [dma((2, plan.planes - 1))] * 2 + [dma((2, plan.planes))] * 2 + [dma(())]


def back_sum_kernel(plan, width, src, normed, grad, out, partial, *scratch):
    unit, tall = plan.unit, 512

    def block(i):
        return src.at[:, pl.ds(pl.multiple_of(i * width, 128), width)]

    def term(row, column):
        here = pl.ds(column, unit)
        partial[pl.ds(row, tall), here] = lax.dot_general(
            normed[:, pl.ds(row, tall)], grad[:, here], (((0,), (0,)), ((), ())), preferred_element_type=f32
        ).astype(bf16)

    count = D // tall * 7
    step, finish = line_sum(plan, block, *scratch, src.shape[0])
    for s in range(1, plan.planes):
        step(s)
        tiles(
            D,
            7 * unit,
            tall,
            unit,
            count * (s - 1) // (plan.planes - 1),
            count * s // (plan.planes - 1),
            term,
        )
    finish(out)


def back_sums(plan, partial, normed, hidden_grad):
    rows, width = partial.shape[0], D // plan.planes
    return pl.pallas_call(
        functools.partial(back_sum_kernel, plan, width),
        in_specs=[VMEM_BLOCK] * 3,
        out_specs=[VMEM_BLOCK] * 2,
        out_shape=[
            jax.ShapeDtypeStruct((rows, width), bf16),
            jax.ShapeDtypeStruct((D, hidden_grad.shape[1]), bf16),
        ],
        scratch_shapes=sum_scratch(plan, rows, width),
        compiler_params=pltpu.CompilerParams(has_side_effects=True),
        cost_estimate=busy(90),
    )(partial, normed, hidden_grad)


def front_sum_kernel(plan, rows, src, back, out, owned, *scratch):
    start, done = back_owners(plan, back, owned, *scratch[:3])
    step, finish = line_sum(
        plan, lambda i: src.at[pl.ds(pl.multiple_of(i * rows, rows), rows), :], *scratch[3:], rows
    )
    step(1)
    start()
    for s in range(2, plan.planes):
        step(s)
    finish(out)
    done()


def front_sums(plan, partial, back_sum):
    dma = pltpu.SemaphoreType.DMA
    rows, width = partial.shape[0] // plan.planes, partial.shape[1]
    return pl.pallas_call(
        functools.partial(front_sum_kernel, plan, rows),
        in_specs=[VMEM_BLOCK, VMEM_BLOCK],
        out_specs=[VMEM_BLOCK, ANY_BLOCK],
        out_shape=[
            jax.ShapeDtypeStruct((rows, width), bf16),
            jax.ShapeDtypeStruct(back_sum.shape, bf16),
        ],
        scratch_shapes=[dma((5,))] * 3 + sum_scratch(plan, rows, width),
        compiler_params=pltpu.CompilerParams(has_side_effects=True),
        cost_estimate=busy(120),
    )(partial, back_sum)


def back_next_kernel(plan, own, src, out, owned, *scratch):
    start, done = front_owners(plan, src, owned, *scratch[:3])
    step, finish = line_gather(plan, own, out, *scratch[3:], own.shape[0])
    step(1)
    start()
    for s in range(2, plan.planes):
        step(s)
    finish()
    done()


def back_nexts(plan, own, front_sum):
    dma = pltpu.SemaphoreType.DMA
    return pl.pallas_call(
        functools.partial(back_next_kernel, plan),
        in_specs=[VMEM_BLOCK, VMEM_BLOCK],
        out_specs=[ANY_BLOCK, ANY_BLOCK],
        out_shape=[
            jax.ShapeDtypeStruct((2 * plan.planes * own.shape[0], own.shape[1]), bf16),
            jax.ShapeDtypeStruct((front_sum.shape[0] // 2, plan.per_shard * plan.unit), bf16),
        ],
        scratch_shapes=[dma((5, 2)), dma((plan.per_shard,)), dma((plan.per_shard,))] + gather_scratch(plan),
        compiler_params=pltpu.CompilerParams(has_side_effects=True),
        cost_estimate=busy(90),
    )(own, front_sum)


def vector_sum(plan, own, out, terms, sums, send, recv):
    planes, ranks = plan.planes, plan.ranks
    c, f, z, k, p = place_in_mesh()

    def in_plane(step, target):
        to = lax.rem(p + step, ranks)
        return pltpu.make_async_remote_copy(
            src_ref=own,
            dst_ref=terms.at[target],
            send_sem=send.at[step],
            recv_sem=recv.at[step],
            device_id=(2 * z + lax.rem(to, 2), lax.div(to, 2)),
            device_id_type=MESH,
        )

    def over_planes(step, target):
        to = lax.rem(z + step, planes)
        return pltpu.make_async_remote_copy(
            src_ref=out,
            dst_ref=sums.at[target],
            send_sem=send.at[ranks + step],
            recv_sem=recv.at[ranks + step],
            device_id=(2 * to + k, f),
            device_id_type=MESH,
        )

    def start():
        for step in range(1, ranks):
            in_plane(step, p).start()
        terms[p] = own[...]

    def middle():
        for step in range(1, ranks):
            in_plane(step, lax.rem(p + ranks - step, ranks)).wait_recv()
        total = terms[0]
        for rank in range(1, ranks):
            total = total + terms[rank]
        out[...] = total
        sums[z] = total
        for step in range(1, planes):
            over_planes(step, z).start()

    def finish():
        for step in range(1, ranks):
            in_plane(step, p).wait_send()
        for step in range(1, planes):
            over_planes(step, z).wait_send()
            over_planes(step, lax.rem(z + planes - step, planes)).wait_recv()
        total = sums[0]
        for plane in range(1, planes):
            total = total + sums[plane]
        out[...] = total

    return start, middle, finish


def front_next_kernel(plan, own, vector, out, vector_out, terms, sums, vsend, vrecv, *scratch):
    begin, middle, end = vector_sum(plan, vector, vector_out, terms, sums, vsend, vrecv)
    step, finish = line_gather(plan, own, out, *scratch, own.shape[0])
    begin()
    step(1)
    middle()
    for s in range(2, plan.planes):
        step(s)
    finish()
    end()


def front_nexts(plan, own, vector):
    dma = pltpu.SemaphoreType.DMA
    return pl.pallas_call(
        functools.partial(front_next_kernel, plan),
        in_specs=[VMEM_BLOCK, VMEM_BLOCK],
        out_specs=[ANY_BLOCK, VMEM_BLOCK],
        out_shape=[
            jax.ShapeDtypeStruct((2 * plan.planes * own.shape[0], own.shape[1]), bf16),
            jax.ShapeDtypeStruct(vector.shape, f32),
        ],
        scratch_shapes=[
            pltpu.VMEM((plan.ranks,) + vector.shape, f32),
            pltpu.VMEM((plan.planes,) + vector.shape, f32),
            dma((plan.ranks + plan.planes,)),
            dma((plan.ranks + plan.planes,)),
        ]
        + gather_scratch(plan),
        compiler_params=pltpu.CompilerParams(has_side_effects=True),
        cost_estimate=busy(120),
    )(own, vector)


def gelu_parts(u):
    scale = np.float32(np.sqrt(2.0 / np.pi))
    square = u * u
    inner = scale * u * (1.0 + 0.044715 * square)
    t = jnp.tanh(inner)
    value = 0.5 * u * (1.0 + t)
    slope = 0.5 * (1.0 + t) + 0.5 * u * (1.0 - t * t) * scale * (1.0 + 3 * 0.044715 * square)
    return value, slope


def adam_update(weight, first, second, grad, rate, count_now, decay):
    first_new = beta_first * first + (1.0 - beta_first) * grad
    second_new = beta_second * second + (1.0 - beta_second) * grad * grad
    steps_float = count_now.astype(f32)
    first_fix = 1.0 - jnp.power(beta_first, steps_float)
    second_fix = 1.0 - jnp.power(beta_second, steps_float)
    change = first_new / first_fix / (jnp.sqrt(second_new / second_fix) + adam_eps) + decay * weight
    return (weight - rate * change, first_new, second_new)


def after(value, *others):
    return lax.optimization_barrier((value,) + others)[0]


def per_device(
    tokens,
    cotangent,
    doc_ids,
    block_order,
    front_weight,
    back_weight,
    front_master,
    back_master,
    front_first,
    back_first,
    front_second,
    back_second,
    vectors,
    vector_first,
    vector_second,
    learn_rates,
    adam_step,
    *,
    plan,
):
    planes, shards, ranks, unit = plan.planes, plan.fsdp, plan.ranks, plan.unit
    both = ("ctx", "fsdp")
    contract_last = (((1,), (1,)), ((), ()))
    contract_first = (((0,), (0,)), ((), ()))
    c_index, f = lax.axis_index("ctx"), lax.axis_index("fsdp")
    z, k = c_index // 2, c_index % 2
    p = 2 * f + k
    rows = tokens.shape[1]
    plane_rows = 2 * shards * rows
    share = 2 * rows

    bias_front = vectors[:IN_COLS].reshape(-1, unit)
    bias_back = vectors[IN_COLS : IN_COLS + D]
    norm_gain = vectors[IN_COLS + D : IN_COLS + 2 * D]
    norm_shift = vectors[IN_COLS + 2 * D :]

    swap_pairs = [(2 * i + j, 2 * i + 1 - j) for i in range(planes) for j in range(2)]

    def swap_core(value):
        return lax.ppermute(value, "ctx", swap_pairs)

    def to_shard(value, step):
        return lax.ppermute(value, "fsdp", [(i, i ^ step) for i in range(shards)])

    def at(array, index):
        return lax.dynamic_index_in_dim(array, index, 0, keepdims=False)

    blocks = block_order.shape[0]
    block_tokens = doc_ids.shape[1] // blocks
    offsets = jnp.arange(block_tokens, dtype=jnp.int32)
    positions_all = (block_order[:, None] * block_tokens + offsets[None, :]).reshape(planes, share)

    plane_tokens, plane_grad, documents, weight_local, back_attention = gather_first(
        plan, tokens[0], cotangent[0], doc_ids.astype(f32), front_weight, back_weight
    )
    plane_tokens = plane_tokens.reshape(plane_rows, D)
    plane_grad = plane_grad.reshape(plane_rows, D)

    unit_table = pick(plan.rank_units, p)
    bias_local = jnp.take(bias_front, unit_table, axis=0).reshape(-1)

    seq_positions = positions_all.reshape(-1)
    tables = rotation_tables(seq_positions, 2 * HEAD_DIM)
    normed, qkvg = prepare(
        plane_tokens,
        plane_grad,
        weight_local,
        back_attention,
        bias_local[None, : 3 * unit],
        norm_gain[None],
        norm_shift[None],
        [lax.dynamic_slice(table, (z * share, 0), (share, 2 * HEAD_DIM)) for table in tables],
    )
    qkvg, back_up, activation, slope = exchange_first(
        plan, qkvg.reshape(planes, share, -1), normed, weight_local, bias_local[None, 3 * unit :], back_weight
    )
    qkvg = qkvg.reshape(planes * share, -1)

    doc_row = documents[0].astype(jnp.int32)
    seq_documents = jnp.take(doc_row.reshape(blocks, block_tokens), block_order, axis=0).reshape(-1)
    returned = attention(qkvg, seq_positions, seq_documents, tables)
    returned, up_grad = exchange_back(
        plan, returned.reshape(planes, share, -1), plane_grad, back_up, slope
    )
    returned = returned.reshape(plane_rows, -1)
    back_local = jnp.concatenate([back_attention, back_up], axis=0)

    mixed = jnp.concatenate([returned[:, :unit], activation], axis=1)
    hidden_grad = jnp.concatenate([returned[:, unit:], up_grad], axis=1)

    def sum_over_cores(value):
        shaped = value.reshape(shards, 2, rows, D)
        kept = lax.dynamic_index_in_dim(shaped, k, 1, keepdims=False)
        sent = lax.dynamic_index_in_dim(shaped, 1 - k, 1, keepdims=False).astype(bf16)
        return kept + swap_core(sent).astype(f32)

    def sum_over_shards(*values):
        totals = [at(value, f) for value in values]
        for step in range(1, shards):
            pieces = jnp.stack([at(value, f ^ step).astype(bf16) for value in values])
            pieces = to_shard(pieces, step).astype(f32)
            totals = [total + piece for total, piece in zip(totals, pieces)]
        return totals

    projected_cores = sum_over_cores(jnp.dot(mixed, back_local, preferred_element_type=f32))
    normed_grad_cores = sum_over_cores(
        lax.dot_general(hidden_grad, weight_local, contract_last, preferred_element_type=f32)
    )

    back_partial = lax.dot_general(
        mixed, plane_grad, contract_first, preferred_element_type=f32
    ).astype(bf16)
    back_sum, front_partial = back_sums(plan, back_partial, normed, hidden_grad)
    back_sum, projected_cores, normed_grad_cores = lax.optimization_barrier(
        (back_sum, projected_cores, normed_grad_cores)
    )
    projected, normed_grad = sum_over_shards(projected_cores, normed_grad_cores)
    front_sum, back_owned = front_sums(plan, front_partial, back_sum)
    front_sum, projected, normed_grad = lax.optimization_barrier((front_sum, projected, normed_grad))

    inputs = tokens[0].astype(f32)
    layer_out = (inputs + projected + bias_back).astype(bf16)[None]
    unscaled, factor = normalize(inputs)
    scaled = normed_grad * norm_gain
    input_grad = factor * (
        scaled
        - jnp.mean(scaled, axis=-1, keepdims=True)
        - unscaled * jnp.mean(scaled * unscaled, axis=-1, keepdims=True)
    )
    tokens_grad = (cotangent[0].astype(f32) + input_grad).astype(bf16)[None]

    back_grad = back_owned.astype(f32)
    back_new, back_first_new, back_second_new = adam_update(
        back_master, back_first, back_second, back_grad, learn_rates[1], adam_step[0], weight_decay
    )
    back_next, front_owned = back_nexts(plan, back_new.astype(bf16), front_sum)
    front_grad = front_owned.astype(f32)
    front_new, front_first_new, front_second_new = adam_update(
        front_master, front_first, front_second, front_grad, learn_rates[0], adam_step[0], weight_decay
    )
    def column_sums(value):
        ones = jnp.ones((8, value.shape[0]), bf16)
        return jnp.dot(ones, value, preferred_element_type=f32)[0]

    spread = (jnp.arange(7 * ranks)[:, None] == unit_table[None, :]).astype(f32)
    hidden_sum = column_sums(hidden_grad).reshape(7, unit)
    front_vector = jnp.sum(spread[:, :, None] * hidden_sum[None], axis=1).reshape(-1)
    vector_term = jnp.concatenate(
        [
            front_vector,
            column_sums(cotangent[0]),
            jnp.sum(normed_grad * unscaled, axis=0),
            jnp.sum(normed_grad, axis=0),
        ]
    )
    front_next, vector_grad = front_nexts(plan, front_new.astype(bf16), vector_term.reshape(-1, 128))
    vector_grad = vector_grad.reshape(-1)

    count_now = adam_step[0]
    vectors_new, vector_first_new, vector_second_new = adam_update(
        vectors, vector_first, vector_second, vector_grad, learn_rates[2], count_now, 0.0
    )

    return (
        layer_out,
        tokens_grad,
        front_grad,
        back_grad,
        vector_grad,
        front_new,
        back_new,
        vectors_new,
        front_first_new,
        back_first_new,
        vector_first_new,
        front_second_new,
        back_second_new,
        vector_second_new,
        front_next,
        back_next,
    )


def solution(mesh):
    plan = Layout(mesh.shape["ctx"], mesh.shape["fsdp"])
    tokens_spec = P("fsdp", "ctx", None)
    cols, owned, same = P(None, "fsdp"), P("ctx", "fsdp"), P()
    in_specs = (
        (tokens_spec, tokens_spec, P("fsdp", None), same, cols, cols)
        + (owned,) * 6
        + (same,) * 5
    )
    out_specs = (
        (tokens_spec, tokens_spec, owned, owned, same)
        + (owned, owned, same) * 3
        + (cols, cols)
    )
    return jax.shard_map(
        functools.partial(per_device, plan=plan),
        mesh=mesh,
        in_specs=in_specs,
        out_specs=out_specs,
        check_vma=False,
    )
```

```python
import functools

import jax
import jax.numpy as jnp
import numpy as np
from jax import lax
from jax.experimental import pallas as pl
from jax.experimental.pallas import tpu as pltpu
from jax.sharding import PartitionSpec as P

D = 2048
HEADS = 32
FF = 8192
ROT = 32
HEAD_DIM = 64
IN_COLS = 14336
BACK_ROWS = 10240

norm_eps = 1e-05
beta_first = 0.9
beta_second = 0.95
adam_eps = 1e-08
weight_decay = 0.1
masked_score = -1e30
bf16 = jnp.bfloat16
f32 = jnp.float32


class Layout:
    def __init__(self, ctx, fsdp):
        self.ctx, self.fsdp, self.planes, self.ranks = ctx, fsdp, ctx // 2, 2 * fsdp
        assert ctx % 2 == 0 and self.planes == fsdp
        self.unit = D // self.ranks
        self.per_shard = IN_COLS // self.unit // fsdp
        r = self.ranks
        first_up = 3 * r
        home = {f: [] for f in range(fsdp)}
        for g in range(first_up, 7 * r, 2):
            assert g // self.per_shard == (g + 1) // self.per_shard
            home[g // self.per_shard].append(g)
        pairs = {p: [None, None] for p in range(r)}
        for f in range(fsdp):
            if len(home[f]) >= 4:
                keep, home[f] = home[f][:4], home[f][4:]
                pairs[2 * f], pairs[2 * f + 1] = keep[:2], keep[2:]
            elif home[f]:
                some = (len(home[f]) + 1) // 2
                keep, home[f] = home[f][:some], home[f][some:]
                for i, g in enumerate(keep):
                    pairs[2 * f + i % 2][(i + i // 2) % 2] = g
        for s in range(2):
            for k in range(2):
                used = set()
                for f in range(fsdp):
                    p = 2 * f + k
                    if pairs[p][s] is not None:
                        continue
                    options = sorted(
                        (h for h in range(fsdp) if home[h]),
                        key=lambda h: (h in used, h == f, bin(h ^ f).count("1"), -len(home[h])),
                    )
                    used.add(options[0])
                    pairs[p][s] = home[options[0]].pop(0)
        self.pairs = pairs
        self.slots = [
            ([p for p in range(r)], 1),
            ([r + p for p in range(r)], 1),
            ([2 * r + p for p in range(r)], 1),
            ([pairs[p][0] for p in range(r)], 2),
            ([pairs[p][1] for p in range(r)], 2),
        ]
        self.rounds = []
        for units, _ in self.slots:
            rounds = []
            for k in range(2):
                for f in range(fsdp):
                    src = units[2 * f + k] // self.per_shard
                    if src == f:
                        continue
                    for one in rounds:
                        if all((src, k) != (a, c) for a, _, c in one):
                            one.append((src, f, k))
                            break
                    else:
                        rounds.append([(src, f, k)])
            self.rounds.append(rounds)
        self.rank_units = [
            [p, r + p, 2 * r + p, pairs[p][0], pairs[p][0] + 1, pairs[p][1], pairs[p][1] + 1]
            for p in range(r)
        ]
        self.back_units = [[p] + [g - 2 * r for g in self.rank_units[p][3:]] for p in range(r)]

    def device(self, z, k, f):
        return (2 * z + k) * self.fsdp + f


def pick(table, index):
    return jnp.asarray(np.asarray(table, np.int32))[index]


def normalize(values):
    values = values.astype(f32)
    centered = values - jnp.mean(values, axis=-1, keepdims=True)
    factor = lax.rsqrt(jnp.mean(centered * centered, axis=-1, keepdims=True) + norm_eps)
    return centered * factor, factor


def rotation_tables(positions, width):
    half = ROT // 2
    lane = np.arange(width) % HEAD_DIM
    frequency = jnp.power(
        10000.0, -2.0 * jnp.asarray(lane % half, f32) / ROT
    )
    angles = positions.astype(f32)[:, None] * frequency[None, :]
    rotated = jnp.asarray(lane < ROT)
    lower = jnp.asarray(lane < half)
    cosine = jnp.where(rotated, jnp.cos(angles), 1.0)
    sine = jnp.where(rotated, jnp.sin(angles), 0.0)
    return cosine, jnp.where(lower, -sine, 0.0), jnp.where(lower, 0.0, sine)


def across(table, width):
    return jnp.concatenate([table] * (width // table.shape[1]), axis=1)


def prepare_kernel(
    tok, grad, weight, back, bias, gain, shift, cosine, from_above, from_below, normed_ref, out_ref
):
    half, width = ROT // 2, back.shape[0]
    contract_last = (((1,), (1,)), ((), ()))
    normed = (normalize(tok[...])[0] * gain[...] + shift[...]).astype(bf16)
    normed_ref[...] = normed
    hidden = jnp.dot(normed, weight[...], preferred_element_type=f32) + bias[...]
    tables = [across(ref[...], width) for ref in (cosine, from_above, from_below)]
    for number in range(2):
        values = hidden[:, number * width : (number + 1) * width]
        out_ref[:, number * width : (number + 1) * width] = (
            values * tables[0]
            + pltpu.roll(values, width - half, 1) * tables[1]
            + pltpu.roll(values, half, 1) * tables[2]
        ).astype(bf16)
    out_ref[:, 2 * width : 3 * width] = hidden[:, 2 * width :].astype(bf16)
    out_ref[:, 3 * width :] = lax.dot_general(
        grad[...], back[...], contract_last, preferred_element_type=f32
    ).astype(bf16)


def prepare(tokens, grad, weight, back, bias, gain, shift, tables):
    length, width, block = tokens.shape[0], back.shape[0], tables[0].shape[0]
    rows = lambda columns: pl.BlockSpec((block, columns), lambda i: (i, 0))
    fixed = lambda height, columns: pl.BlockSpec((height, columns), lambda i: (0, 0))
    return pl.pallas_call(
        prepare_kernel,
        grid=(length // block,),
        in_specs=[
            rows(D),
            rows(D),
            fixed(D, 3 * width),
            fixed(width, D),
            fixed(1, 3 * width),
            fixed(1, D),
            fixed(1, D),
        ]
        + [fixed(block, tables[0].shape[1])] * 3,
        out_specs=[rows(D), rows(4 * width)],
        out_shape=[
            jax.ShapeDtypeStruct((length, D), bf16),
            jax.ShapeDtypeStruct((length, 4 * width), bf16),
        ],
        cost_estimate=pl.CostEstimate(
            flops=8 * length * width * D, transcendentals=0, bytes_accessed=16 * length * D
        ),
    )(tokens, grad, weight, back, bias, gain, shift, *tables)


def attention_kernel(
    x_ref, pos_q, pos_k, seg_q, seg_k, cosine, from_above, from_below, out_ref, dq_ref, dk_ref, dv_ref
):
    scale = HEAD_DIM ** (-0.5)
    half = ROT // 2
    block, width = dq_ref.shape
    length = dk_ref.shape[0]
    rows = pl.ds(pl.multiple_of(pl.program_id(0) * block, block), block)

    @pl.when(pl.program_id(0) == 0)
    def _():
        dk_ref[...] = jnp.zeros_like(dk_ref)
        dv_ref[...] = jnp.zeros_like(dv_ref)

    def turn_back(values, at):
        return (
            values * across(cosine[at, :], width)
            + pltpu.roll(values * across(from_above[at, :], width), half, 1)
            + pltpu.roll(values * across(from_below[at, :], width), width - half, 1)
        ).astype(bf16)

    allowed = (pos_k[...] <= pos_q[...]) & (seg_k[...] == seg_q[...])
    bias = jnp.where(allowed, 0.0, masked_score)
    last = (((1,), (1,)), ((), ()))
    first = (((0,), (0,)), ((), ()))
    for head in range(width // HEAD_DIM):
        q_cols, k_cols, v_cols, g_cols = (
            slice(n * width + head * HEAD_DIM, n * width + (head + 1) * HEAD_DIM) for n in range(4)
        )
        q, g = x_ref[rows, q_cols], x_ref[rows, g_cols]
        k, v = x_ref[:, k_cols], x_ref[:, v_cols]
        scores = lax.dot_general(q, k, last, preferred_element_type=f32) * scale + bias
        weights = jnp.exp(scores - jnp.max(scores, axis=1, keepdims=True))
        probs = weights * (1.0 / jnp.sum(weights, axis=1, keepdims=True))
        probs_low = probs.astype(bf16)
        out = jnp.dot(probs_low, v, preferred_element_type=f32)
        out_ref[rows, q_cols] = out.astype(bf16)
        prob_grad = lax.dot_general(g, v, last, preferred_element_type=f32)
        delta = jnp.sum(g.astype(f32) * out, axis=1, keepdims=True)
        score_grad = (probs * (prob_grad - delta)).astype(bf16)
        dq_ref[:, q_cols] = jnp.dot(score_grad, k, preferred_element_type=f32) * scale
        dk_ref[:, q_cols] += lax.dot_general(score_grad, q, first, preferred_element_type=f32) * scale
        dv_ref[:, q_cols] += lax.dot_general(probs_low, g, first, preferred_element_type=f32)
    out_ref[rows, width : 2 * width] = turn_back(dq_ref[...], rows)

    @pl.when(pl.program_id(0) == pl.num_programs(0) - 1)
    def _():
        for number in range(length // block):
            at = slice(number * block, (number + 1) * block)
            out_ref[at, 2 * width : 3 * width] = turn_back(dk_ref[at, :], at)
            out_ref[at, 3 * width :] = dv_ref[at, :].astype(bf16)


def attention(values, positions, segments, tables):
    length, width = values.shape[0], values.shape[1] // 4
    block = 256
    whole = lambda columns: pl.BlockSpec((length, columns), lambda i: (0, 0))
    column = pl.BlockSpec((block, 1), lambda i: (i, 0))
    line = pl.BlockSpec((1, length), lambda i: (0, 0))
    return pl.pallas_call(
        attention_kernel,
        grid=(length // block,),
        in_specs=[whole(4 * width), column, line, column, line] + [whole(tables[0].shape[1])] * 3,
        out_specs=whole(4 * width),
        out_shape=jax.ShapeDtypeStruct((length, 4 * width), bf16),
        scratch_shapes=[
            pltpu.VMEM((block, width), f32),
            pltpu.VMEM((length, width), f32),
            pltpu.VMEM((length, width), f32),
        ],
        cost_estimate=pl.CostEstimate(
            flops=14 * length * length * width,
            transcendentals=length * length * width // HEAD_DIM,
            bytes_accessed=20 * length * width,
        ),
    )(values, positions[:, None], positions[None], segments[:, None], segments[None], *tables)


MESH = pl.DeviceIdType.MESH


VMEM_BLOCK = pl.BlockSpec(memory_space=pltpu.VMEM)
ANY_BLOCK = pl.BlockSpec(memory_space=pl.ANY)


def busy(microseconds):
    return pl.CostEstimate(flops=int(microseconds * 900e6), transcendentals=0, bytes_accessed=0)


def place_in_mesh():
    c, f = lax.axis_index("ctx"), lax.axis_index("fsdp")
    z, k = lax.div(c, 2), lax.rem(c, 2)
    return c, f, z, k, 2 * f + k


def bounce(source, buffer, target, sem):
    one = pltpu.make_async_copy(source, buffer, sem)
    one.start()
    one.wait()
    two = pltpu.make_async_copy(buffer, target, sem)
    two.start()
    two.wait()


def gather_kernel(
    plan, tok, cot, doc, front, back, tok_out, cot_out, doc_out, w_out, b_out,
    w_buf, b_buf, tsend, trecv, csend, crecv, wsend, wrecv, rsend, rrecv, bsend, brecv, dsend, drecv, lsem,
):
    shards, unit, ranks = plan.fsdp, plan.unit, plan.ranks
    c, f, z, k, p = place_in_mesh()
    other = c + 1 - 2 * k
    width = D // shards
    both = ((tok, tok_out), (cot, cot_out))

    def cols(block):
        return pl.ds(pl.multiple_of(block * width, 128), width)

    def remote(src, dst, send, recv, device):
        return pltpu.make_async_remote_copy(
            src_ref=src, dst_ref=dst, send_sem=send, recv_sem=recv, device_id=device, device_id_type=MESH
        )

    def peer(step):
        return lax.rem(f + step, shards)

    def giver(step):
        return lax.rem(f + shards - step, shards)

    def send_tokens(n, step):
        src, out = both[n]
        return remote(src, out.at[f, k], tsend.at[n, step], trecv.at[n, step], (c, peer(step)))

    def get_tokens(n, step):
        here = both[n][1].at[giver(step), k]
        return remote(here, here, tsend.at[n, step], trecv.at[n, step], (c, peer(step)))

    def share(n, step):
        src, out = both[n]
        here = out.at[giver(step), k]
        return remote(src if step == 0 else here, here, csend.at[n, step], crecv.at[n, step], (other, f))

    def get_share(n, step):
        here = both[n][1].at[giver(step), 1 - k]
        return remote(here, here, csend.at[n, step], crecv.at[n, step], (other, f))

    def rows_of(dst):
        return pl.ds(pl.multiple_of((2 * dst + k) * unit, unit), unit)

    def send_back(step):
        return remote(
            back.at[rows_of(peer(step)), :], b_out.at[:, cols(f)], bsend.at[step], brecv.at[step], (c, peer(step))
        )

    def get_back(step):
        here = b_out.at[:, cols(giver(step))]
        return remote(here, here, bsend.at[step], brecv.at[step], (c, peer(step)))

    def send_doc(step):
        return remote(doc, doc_out, dsend.at[step], drecv, (c, peer(step)))

    start_weights, relay_weights, finish_weights = weight_moves(
        plan, front, w_out, w_buf, wsend, wrecv, rsend, rrecv, lsem.at[2]
    )
    own = [pltpu.make_async_copy(src, out.at[f, k], lsem.at[4 * n]) for n, (src, out) in enumerate(both)]
    own_doc = pltpu.make_async_copy(doc, doc_out, lsem.at[1])
    start_weights()
    for n in range(2):
        for step in range(1, shards):
            send_tokens(n, step).start()
        share(n, 0).start()
        own[n].start()
    for step in range(1, shards):
        send_back(step).start()

    @pl.when(f == z)
    def _():
        own_doc.start()
        for step in range(1, shards):
            send_doc(step).start()

    relay_weights()
    for n in range(2):
        for step in range(1, shards):
            get_tokens(n, step).wait_recv()
            share(n, step).start()
    bounce(back.at[rows_of(f), :], b_buf, b_out.at[:, cols(f)], lsem.at[3])
    for n in range(2):
        own[n].wait()

    @pl.when(f == z)
    def _():
        own_doc.wait()
        for step in range(1, shards):
            send_doc(step).wait_send()

    @pl.when(f != z)
    def _():
        send_doc(1).wait_recv()

    for n in range(2):
        for step in range(shards):
            get_share(n, step).wait_recv()
            share(n, step).wait_send()
        for step in range(1, shards):
            send_tokens(n, step).wait_send()
    for step in range(1, shards):
        send_back(step).wait_send()
        get_back(step).wait_recv()
    finish_weights()


def moves_between(moves, device_of):
    c, f, z, k, p = place_in_mesh()

    def remote(move):
        src, dst, source, target, send, recv, _, _ = move
        return pltpu.make_async_remote_copy(
            src_ref=source, dst_ref=target, send_sem=send, recv_sem=recv, device_id=device_of(c, dst), device_id_type=MESH
        )

    def start():
        for move in moves:
            if move[0] != move[1]:

                @pl.when(p == move[0])
                def _(move=move):
                    remote(move).start()

        for move in moves:
            if move[0] == move[1]:

                @pl.when(p == move[0])
                def _(move=move):
                    bounce(move[2], move[6], move[3], move[7])

    def finish():
        for move in moves:
            if move[0] != move[1]:

                @pl.when(p == move[0])
                def _(move=move):
                    remote(move).wait_send()

                @pl.when(p == move[1])
                def _(move=move):
                    remote(move).wait_recv()

    return start, finish


def weight_moves(plan, front, out, buffer, send, recv, relay_send, relay_recv, local):
    unit, moves, begin = plan.unit, [], 0
    c, f, z, k, p = place_in_mesh()
    half, parity = D // 2, lax.rem(z, 2)

    def rows(part):
        return pl.ds(pl.multiple_of(part * half, half), half)

    for slot, (units, wide) in enumerate(plan.slots):
        for dst in range(plan.ranks):
            src, at = units[dst] // plan.per_shard, units[dst] % plan.per_shard
            moves.append(
                (slot, 2 * src + dst % 2, dst, pl.ds(at * unit, wide * unit), pl.ds(begin * unit, wide * unit), wide * unit)
            )
        begin += wide

    def copy(move):
        slot, _, dst, source, target, _ = move
        return pltpu.make_async_remote_copy(
            src_ref=front.at[rows(parity), source],
            dst_ref=out.at[rows(parity), target],
            send_sem=send.at[slot, dst // 2],
            recv_sem=recv.at[slot],
            device_id=(c, dst // 2),
            device_id_type=MESH,
        )

    def pass_on(move, part):
        slot, _, _, _, target, _ = move
        here = out.at[rows(part), target]
        return pltpu.make_async_remote_copy(
            src_ref=here,
            dst_ref=here,
            send_sem=relay_send.at[slot],
            recv_sem=relay_recv.at[slot],
            device_id=(c + 2 - 4 * parity, f),
            device_id_type=MESH,
        )

    def start():
        for move in moves:
            if move[1] != move[2]:

                @pl.when(p == move[1])
                def _(move=move):
                    copy(move).start()

    def relay():
        for move in moves:
            if move[1] != move[2]:

                @pl.when(p == move[2])
                def _(move=move):
                    copy(move).wait_recv()
                    pass_on(move, parity).start()

    def finish():
        for move in moves:
            if move[1] == move[2]:

                @pl.when(p == move[2])
                def _(move=move):
                    bounce(front.at[:, move[3]], buffer.at[:, pl.ds(0, move[5])], out.at[:, move[4]], local)

        for move in moves:
            if move[1] != move[2]:

                @pl.when(p == move[1])
                def _(move=move):
                    copy(move).wait_send()

                @pl.when(p == move[2])
                def _(move=move):
                    pass_on(move, parity).wait_send()
                    pass_on(move, 1 - parity).wait_recv()

    return start, relay, finish


def back_moves(plan, back, out, buffer, send, recv, local):
    unit, width, moves = plan.unit, D // plan.fsdp, []
    for dst in range(plan.ranks):
        for src in range(plan.fsdp):
            for number in range(2):
                row = plan.back_units[dst][1 + 2 * number]
                moves.append(
                    (
                        2 * src + dst % 2,
                        dst,
                        back.at[pl.ds(row * unit, 2 * unit), :],
                        out.at[pl.ds(2 * number * unit, 2 * unit), pl.ds(src * width, width)],
                        send.at[number, dst // 2],
                        recv.at[number, src],
                        buffer,
                        local,
                    )
                )
    return moves_between(moves, lambda c, dst: (c, dst // 2))


def line_exchange(plan, src, out, send, recv, local):
    planes = plan.planes
    c, f, z, k, p = place_in_mesh()

    def copy(step):
        to = lax.rem(z + step, planes)
        return pltpu.make_async_remote_copy(
            src_ref=src.at[to],
            dst_ref=out.at[z],
            send_sem=send.at[step],
            recv_sem=recv.at[step],
            device_id=(2 * to + k, f),
            device_id_type=MESH,
        )

    def arrival(step):
        here = out.at[lax.rem(z + planes - step, planes)]
        return pltpu.make_async_remote_copy(
            src_ref=here,
            dst_ref=here,
            send_sem=send.at[step],
            recv_sem=recv.at[step],
            device_id=(2 * lax.rem(z + step, planes) + k, f),
            device_id_type=MESH,
        )

    keep = pltpu.make_async_copy(src.at[z], out.at[z], local)

    def start():
        for step in range(planes - 1, 0, -1):
            copy(step).start()
        keep.start()

    def finish():
        keep.wait()
        for step in range(1, planes):
            copy(step).wait_send()
            arrival(step).wait_recv()

    return start, finish


def gather_first(plan, tokens, cotangent, documents, front_weight, back_weight):
    shards, unit = plan.fsdp, plan.unit
    rows, length = tokens.shape[0], documents.shape[1]
    dma = pltpu.SemaphoreType.DMA
    return pl.pallas_call(
        functools.partial(gather_kernel, plan),
        in_specs=[VMEM_BLOCK] * 3 + [ANY_BLOCK] * 2,
        out_specs=[ANY_BLOCK] * 5,
        out_shape=[
            jax.ShapeDtypeStruct((shards, 2, rows, D), bf16),
            jax.ShapeDtypeStruct((shards, 2, rows, D), bf16),
            jax.ShapeDtypeStruct((1, length), f32),
            jax.ShapeDtypeStruct((D, 7 * unit), bf16),
            jax.ShapeDtypeStruct((unit, D), bf16),
        ],
        scratch_shapes=[
            pltpu.VMEM((D, 2 * unit), bf16),
            pltpu.VMEM((unit, D // shards), bf16),
            dma((2, shards)),
            dma((2, shards)),
            dma((2, shards)),
            dma((2, shards)),
            dma((5, shards)),
            dma((5,)),
            dma((5,)),
            dma((5,)),
            dma((shards,)),
            dma((shards,)),
            dma((shards,)),
            dma(()),
            dma((5,)),
        ],
        compiler_params=pltpu.CompilerParams(has_side_effects=True),
        cost_estimate=busy(130),
    )(tokens, cotangent, documents, front_weight, back_weight)


def tiles(rows, columns, tall, wide, first, last, body):
    across = columns // wide

    def one(i, carry):
        row = pl.multiple_of(lax.div(i, across) * tall, tall)
        column = pl.multiple_of(lax.rem(i, across) * wide, wide)
        body(row, column)
        return carry

    lax.fori_loop(first, last, one, 0)


def exchange_kernel(
    plan, src, normed, weight, bias, back, out, b_out, act, slope, buffer, send, recv, local, bsend, brecv
):
    unit = plan.unit
    start, finish = line_exchange(plan, src, out, send, recv, local.at[0])
    start_rows, finish_rows = back_moves(plan, back, b_out, buffer, bsend, brecv, local.at[1])
    start()
    start_rows()
    tall = 512

    def units(row, column):
        at, here = pl.ds(row, tall), pl.ds(column, unit)
        u = jnp.dot(
            normed[at, :],
            weight[:, pl.ds(pl.multiple_of(column + 3 * unit, unit), unit)],
            preferred_element_type=f32,
        )
        value, steep = gelu_parts(u + bias[:, here])
        act[at, here] = value.astype(bf16)
        slope[at, here] = steep

    tiles(act.shape[0], 4 * unit, tall, unit, 0, act.shape[0] // tall * 4, units)
    finish()
    finish_rows()


def exchange_first(plan, values, normed, weight, bias, back_weight):
    dma = pltpu.SemaphoreType.DMA
    unit, shards = plan.unit, plan.fsdp
    length = normed.shape[0]
    return pl.pallas_call(
        functools.partial(exchange_kernel, plan),
        in_specs=[VMEM_BLOCK] * 4 + [ANY_BLOCK],
        out_specs=[ANY_BLOCK, ANY_BLOCK, VMEM_BLOCK, VMEM_BLOCK],
        out_shape=[
            jax.ShapeDtypeStruct(values.shape, bf16),
            jax.ShapeDtypeStruct((4 * unit, D), bf16),
            jax.ShapeDtypeStruct((length, 4 * unit), bf16),
            jax.ShapeDtypeStruct((length, 4 * unit), f32),
        ],
        scratch_shapes=[
            pltpu.VMEM((2 * unit, D // shards), bf16),
            dma((plan.planes,)),
            dma((plan.planes,)),
            dma((2,)),
            dma((2, shards)),
            dma((2, shards)),
        ],
        compiler_params=pltpu.CompilerParams(has_side_effects=True),
        cost_estimate=busy(50),
    )(values, normed, weight, bias, back_weight)


def exchange_back_kernel(plan, src, grad, rows, slope, out, up_grad, send, recv, local):
    unit, tall = plan.unit, 512
    start, finish = line_exchange(plan, src, out, send, recv, local)
    start()

    def units(row, column):
        at, here = pl.ds(row, tall), pl.ds(column, unit)
        mixed_grad = lax.dot_general(
            grad[at, :], rows[here, :], (((1,), (1,)), ((), ())), preferred_element_type=f32
        )
        up_grad[at, here] = (mixed_grad * slope[at, here]).astype(bf16)

    tiles(grad.shape[0], 4 * unit, tall, unit, 0, grad.shape[0] // tall * 4, units)
    finish()


def exchange_back(plan, values, grad, rows, slope):
    dma = pltpu.SemaphoreType.DMA
    return pl.pallas_call(
        functools.partial(exchange_back_kernel, plan),
        in_specs=[VMEM_BLOCK] * 4,
        out_specs=[ANY_BLOCK, VMEM_BLOCK],
        out_shape=[
            jax.ShapeDtypeStruct(values.shape, bf16),
            jax.ShapeDtypeStruct(slope.shape, bf16),
        ],
        scratch_shapes=[dma((plan.planes,)), dma((plan.planes,)), dma(())],
        compiler_params=pltpu.CompilerParams(has_side_effects=True),
        cost_estimate=busy(50),
    )(values, grad, rows, slope)


def line_sum(plan, block, rising, falling, sends, gets, rows):
    planes, chunk = plan.planes, 64
    c, f, z, k, p = place_in_mesh()

    def copy(side, s, src):
        slots = (rising, falling)[side]
        return pltpu.make_async_remote_copy(
            src_ref=src,
            dst_ref=slots.at[s - 1],
            send_sem=sends.at[side, s - 1],
            recv_sem=gets.at[side, s - 1],
            device_id=(c + 2 - 4 * side, f),
            device_id_type=MESH,
        )

    def add(side, s, number):
        slots = (rising, falling)[side]
        term = block(number)

        def body(i, carry):
            at = pl.ds(pl.multiple_of(i * chunk, chunk), chunk)
            slots[s - 1, at, :] = (slots[s - 1, at, :].astype(f32) + term[at, :].astype(f32)).astype(bf16)
            return carry

        lax.fori_loop(0, rows // chunk, body, 0)

    def step(s):
        for side in range(2):
            place = z if side == 0 else planes - 1 - z
            number = planes - s + place
            number = number if side == 0 else planes - 1 - number

            @pl.when(place == 0)
            def _(side=side, number=number):
                copy(side, s, block(number)).start()

            if s > 1:

                @pl.when((place > 0) & (place < s) & (place < planes - 1))
                def _(side=side, number=number):
                    slots = (rising, falling)[side]
                    copy(side, s - 1, slots.at[s - 2]).wait_recv()
                    add(side, s - 1, number)
                    copy(side, s, slots.at[s - 2]).start()

    def finish(out):
        last = planes - 1
        for side in range(2):
            place = z if side == 0 else planes - 1 - z
            slots = (rising, falling)[side]

            @pl.when(place > 0)
            def _(side=side, slots=slots):
                copy(side, last, slots.at[last - 1]).wait_recv()

        mine = block(z)

        def total(ups, downs):
            def body(i, carry):
                at = pl.ds(pl.multiple_of(i * chunk, chunk), chunk)
                value = mine[at, :].astype(f32)
                if ups:
                    value = value + rising[last - 1, at, :].astype(f32)
                if downs:
                    value = value + falling[last - 1, at, :].astype(f32)
                out[at, :] = value.astype(out.dtype)
                return carry

            lax.fori_loop(0, rows // chunk, body, 0)

        @pl.when(z == 0)
        def _():
            total(False, True)

        @pl.when(z == planes - 1)
        def _():
            total(True, False)

        @pl.when((z > 0) & (z < planes - 1))
        def _():
            total(True, True)

        for side in range(2):
            place = z if side == 0 else planes - 1 - z
            slots = (rising, falling)[side]
            for s in range(1, planes):

                @pl.when((place < s) & (place < planes - 1))
                def _(side=side, slots=slots, s=s):
                    copy(side, s, slots.at[s - 1]).wait_send()

    return step, finish


def line_gather(plan, own, out, sends, gets, share_sends, share_gets, local, height):
    planes = plan.planes
    c, f, z, k, p = place_in_mesh()
    other = c + 1 - 2 * k

    def rows_of(plane, core):
        return out.at[pl.ds(pl.multiple_of((2 * plane + core) * height, height), height), :]

    def origin(side, s):
        return z - s if side == 0 else z + s

    def copy(side, s):
        plane = origin(side, s - 1)
        src = own if s == 1 else rows_of(plane, k)
        return pltpu.make_async_remote_copy(
            src_ref=src,
            dst_ref=rows_of(plane, k),
            send_sem=sends.at[side, s - 1],
            recv_sem=gets.at[side, s - 1],
            device_id=(c + 2 - 4 * side, f),
            device_id_type=MESH,
        )

    def arrival(side, s):
        here = rows_of(origin(side, s), k)
        return pltpu.make_async_remote_copy(
            src_ref=here,
            dst_ref=here,
            send_sem=sends.at[side, s - 1],
            recv_sem=gets.at[side, s - 1],
            device_id=(c + 2 - 4 * side, f),
            device_id_type=MESH,
        )

    def share(side, s, core):
        plane = origin(side, s)
        here = rows_of(plane, core)
        src = own if s == 0 else here
        return pltpu.make_async_remote_copy(
            src_ref=src,
            dst_ref=here,
            send_sem=share_sends.at[side, s],
            recv_sem=share_gets.at[side, s],
            device_id=(other, f),
            device_id_type=MESH,
        )

    keep = pltpu.make_async_copy(own, rows_of(z, k), local)

    def sends_at(side, s):
        place = z if side == 0 else planes - 1 - z
        return (place >= s - 1) & (place < planes - 1)

    def gets_at(side, s):
        place = z if side == 0 else planes - 1 - z
        return place >= s

    def take(s):
        for side in range(2):

            @pl.when(gets_at(side, s))
            def _(side=side):
                arrival(side, s).wait_recv()
                if s < planes - 1:

                    @pl.when(sends_at(side, s + 1))
                    def _():
                        copy(side, s + 1).start()

                share(side, s, k).start()

    def step(s):
        if s > 1:
            take(s - 1)
            return
        for side in range(2):

            @pl.when(sends_at(side, 1))
            def _(side=side):
                copy(side, 1).start()

        share(0, 0, k).start()
        keep.start()

    def finish():
        take(planes - 1)
        keep.wait()
        share(0, 0, k).wait_send()
        share(0, 0, 1 - k).wait_recv()
        for side in range(2):
            for s in range(1, planes):

                @pl.when(sends_at(side, s))
                def _(side=side, s=s):
                    copy(side, s).wait_send()

                @pl.when(gets_at(side, s))
                def _(side=side, s=s):
                    share(side, s, k).wait_send()
                    share(side, s, 1 - k).wait_recv()

    return step, finish


def back_owners(plan, src, out, send, recv, lsem):
    unit, ranks = plan.unit, plan.ranks
    c, f, z, k, p = place_in_mesh()

    def copy(j, owner, place):
        return pltpu.make_async_remote_copy(
            src_ref=src.at[pl.ds(j * unit, unit), :],
            dst_ref=out.at[pl.ds(place * unit, unit), :],
            send_sem=send.at[j],
            recv_sem=recv.at[place],
            device_id=(owner, z),
            device_id_type=MESH,
        )

    def local(j, place):
        return pltpu.make_async_copy(
            src.at[pl.ds(j * unit, unit), :], out.at[pl.ds(place * unit, unit), :], lsem.at[place]
        )

    blocks = [
        (rank, j, plan.back_units[rank][j] // 5, plan.back_units[rank][j] % 5)
        for rank in range(ranks)
        for j in range(5)
    ]

    def start():
        for rank, j, owner, place in blocks:

            @pl.when((p == rank) & ~((c == owner) & (f == z)))
            def _(j=j, owner=owner, place=place):
                copy(j, owner, place).start()

            @pl.when((p == rank) & (c == owner) & (f == z))
            def _(j=j, place=place):
                local(j, place).start()

    def finish():
        for rank, j, owner, place in blocks:

            @pl.when((p == rank) & ~((c == owner) & (f == z)))
            def _(j=j, owner=owner, place=place):
                copy(j, owner, place).wait_send()

            @pl.when((c == owner) & ~((p == rank) & (f == z)))
            def _(j=j, owner=owner, place=place):
                copy(j, owner, place).wait_recv()

            @pl.when((p == rank) & (c == owner) & (f == z))
            def _(j=j, place=place):
                local(j, place).wait()

    return start, finish


def front_owners(plan, src, out, send, recv, lsem):
    unit, ranks = plan.unit, plan.ranks
    c, f, z, k, p = place_in_mesh()
    height = src.shape[0] // 2
    moves, start_at = [], 0
    for slot, (units, wide) in enumerate(plan.slots):
        for rank in range(ranks):
            owner, place = units[rank] // plan.per_shard, units[rank] % plan.per_shard
            moves.append((slot, rank, owner, place, start_at, wide))
        start_at += wide

    def copy(slot, owner, place, begin, wide, half):
        return pltpu.make_async_remote_copy(
            src_ref=src.at[pl.ds(half * height, height), pl.ds(begin * unit, wide * unit)],
            dst_ref=out.at[:, pl.ds(place * unit, wide * unit)],
            send_sem=send.at[slot, half],
            recv_sem=recv.at[place],
            device_id=(2 * z + half, owner),
            device_id_type=MESH,
        )

    def local(place, begin, wide, half):
        return pltpu.make_async_copy(
            src.at[pl.ds(half * height, height), pl.ds(begin * unit, wide * unit)],
            out.at[:, pl.ds(place * unit, wide * unit)],
            lsem.at[place],
        )

    def start():
        for slot, rank, owner, place, begin, wide in moves:
            for half in range(2):
                if 2 * owner + half == rank:

                    @pl.when(p == rank)
                    def _(place=place, begin=begin, wide=wide, half=half):
                        local(place, begin, wide, half).start()

                else:

                    @pl.when(p == rank)
                    def _(slot=slot, owner=owner, place=place, begin=begin, wide=wide, half=half):
                        copy(slot, owner, place, begin, wide, half).start()

    def finish():
        for slot, rank, owner, place, begin, wide in moves:
            for half in range(2):
                if 2 * owner + half == rank:

                    @pl.when(p == rank)
                    def _(place=place, begin=begin, wide=wide, half=half):
                        local(place, begin, wide, half).wait()

                else:

                    @pl.when(p == rank)
                    def _(slot=slot, owner=owner, place=place, begin=begin, wide=wide, half=half):
                        copy(slot, owner, place, begin, wide, half).wait_send()

                    @pl.when(p == 2 * owner + half)
                    def _(slot=slot, owner=owner, place=place, begin=begin, wide=wide, half=half):
                        copy(slot, owner, place, begin, wide, half).wait_recv()

    return start, finish


def sum_scratch(plan, rows, columns):
    dma = pltpu.SemaphoreType.DMA
    steps = plan.planes - 1
    slots = pltpu.VMEM((steps, rows, columns), bf16)
    return [slots, slots, dma((2, steps)), dma((2, steps))]


def gather_scratch(plan):
    dma = pltpu.SemaphoreType.DMA
    return [dma((2, plan.planes - 1))] * 2 + [dma((2, plan.planes))] * 2 + [dma(())]


def back_sum_kernel(plan, width, src, normed, grad, out, partial, *scratch):
    unit, tall = plan.unit, 512

    def block(i):
        return src.at[:, pl.ds(pl.multiple_of(i * width, 128), width)]

    def term(row, column):
        here = pl.ds(column, unit)
        partial[pl.ds(row, tall), here] = lax.dot_general(
            normed[:, pl.ds(row, tall)], grad[:, here], (((0,), (0,)), ((), ())), preferred_element_type=f32
        ).astype(bf16)

    count = D // tall * 7
    step, finish = line_sum(plan, block, *scratch, src.shape[0])
    for s in range(1, plan.planes):
        step(s)
        tiles(
            D,
            7 * unit,
            tall,
            unit,
            count * (s - 1) // (plan.planes - 1),
            count * s // (plan.planes - 1),
            term,
        )
    finish(out)


def back_sums(plan, partial, normed, hidden_grad):
    rows, width = partial.shape[0], D // plan.planes
    return pl.pallas_call(
        functools.partial(back_sum_kernel, plan, width),
        in_specs=[VMEM_BLOCK] * 3,
        out_specs=[VMEM_BLOCK] * 2,
        out_shape=[
            jax.ShapeDtypeStruct((rows, width), bf16),
            jax.ShapeDtypeStruct((D, hidden_grad.shape[1]), bf16),
        ],
        scratch_shapes=sum_scratch(plan, rows, width),
        compiler_params=pltpu.CompilerParams(has_side_effects=True),
        cost_estimate=busy(90),
    )(partial, normed, hidden_grad)


def front_sum_kernel(plan, rows, src, back, out, owned, *scratch):
    start, done = back_owners(plan, back, owned, *scratch[:3])
    step, finish = line_sum(
        plan, lambda i: src.at[pl.ds(pl.multiple_of(i * rows, rows), rows), :], *scratch[3:], rows
    )
    step(1)
    start()
    for s in range(2, plan.planes):
        step(s)
    finish(out)
    done()


def front_sums(plan, partial, back_sum):
    dma = pltpu.SemaphoreType.DMA
    rows, width = partial.shape[0] // plan.planes, partial.shape[1]
    return pl.pallas_call(
        functools.partial(front_sum_kernel, plan, rows),
        in_specs=[VMEM_BLOCK, VMEM_BLOCK],
        out_specs=[VMEM_BLOCK, ANY_BLOCK],
        out_shape=[
            jax.ShapeDtypeStruct((rows, width), bf16),
            jax.ShapeDtypeStruct(back_sum.shape, bf16),
        ],
        scratch_shapes=[dma((5,))] * 3 + sum_scratch(plan, rows, width),
        compiler_params=pltpu.CompilerParams(has_side_effects=True),
        cost_estimate=busy(120),
    )(partial, back_sum)


def back_next_kernel(plan, own, src, out, owned, *scratch):
    start, done = front_owners(plan, src, owned, *scratch[:3])
    step, finish = line_gather(plan, own, out, *scratch[3:], own.shape[0])
    step(1)
    start()
    for s in range(2, plan.planes):
        step(s)
    finish()
    done()


def back_nexts(plan, own, front_sum):
    dma = pltpu.SemaphoreType.DMA
    return pl.pallas_call(
        functools.partial(back_next_kernel, plan),
        in_specs=[VMEM_BLOCK, VMEM_BLOCK],
        out_specs=[ANY_BLOCK, ANY_BLOCK],
        out_shape=[
            jax.ShapeDtypeStruct((2 * plan.planes * own.shape[0], own.shape[1]), bf16),
            jax.ShapeDtypeStruct((front_sum.shape[0] // 2, plan.per_shard * plan.unit), bf16),
        ],
        scratch_shapes=[dma((5, 2)), dma((plan.per_shard,)), dma((plan.per_shard,))] + gather_scratch(plan),
        compiler_params=pltpu.CompilerParams(has_side_effects=True),
        cost_estimate=busy(90),
    )(own, front_sum)


def vector_sum(plan, own, out, terms, sums, send, recv):
    planes, ranks = plan.planes, plan.ranks
    c, f, z, k, p = place_in_mesh()

    def in_plane(step, target):
        to = lax.rem(p + step, ranks)
        return pltpu.make_async_remote_copy(
            src_ref=own,
            dst_ref=terms.at[target],
            send_sem=send.at[step],
            recv_sem=recv.at[step],
            device_id=(2 * z + lax.rem(to, 2), lax.div(to, 2)),
            device_id_type=MESH,
        )

    def over_planes(step, target):
        to = lax.rem(z + step, planes)
        return pltpu.make_async_remote_copy(
            src_ref=out,
            dst_ref=sums.at[target],
            send_sem=send.at[ranks + step],
            recv_sem=recv.at[ranks + step],
            device_id=(2 * to + k, f),
            device_id_type=MESH,
        )

    def start():
        for step in range(1, ranks):
            in_plane(step, p).start()
        terms[p] = own[...]

    def middle():
        for step in range(1, ranks):
            in_plane(step, lax.rem(p + ranks - step, ranks)).wait_recv()
        total = terms[0]
        for rank in range(1, ranks):
            total = total + terms[rank]
        out[...] = total
        sums[z] = total
        for step in range(1, planes):
            over_planes(step, z).start()

    def finish():
        for step in range(1, ranks):
            in_plane(step, p).wait_send()
        for step in range(1, planes):
            over_planes(step, z).wait_send()
            over_planes(step, lax.rem(z + planes - step, planes)).wait_recv()
        total = sums[0]
        for plane in range(1, planes):
            total = total + sums[plane]
        out[...] = total

    return start, middle, finish


def front_next_kernel(plan, own, vector, out, vector_out, terms, sums, vsend, vrecv, *scratch):
    begin, middle, end = vector_sum(plan, vector, vector_out, terms, sums, vsend, vrecv)
    step, finish = line_gather(plan, own, out, *scratch, own.shape[0])
    begin()
    step(1)
    middle()
    for s in range(2, plan.planes):
        step(s)
    finish()
    end()


def front_nexts(plan, own, vector):
    dma = pltpu.SemaphoreType.DMA
    return pl.pallas_call(
        functools.partial(front_next_kernel, plan),
        in_specs=[VMEM_BLOCK, VMEM_BLOCK],
        out_specs=[ANY_BLOCK, VMEM_BLOCK],
        out_shape=[
            jax.ShapeDtypeStruct((2 * plan.planes * own.shape[0], own.shape[1]), bf16),
            jax.ShapeDtypeStruct(vector.shape, f32),
        ],
        scratch_shapes=[
            pltpu.VMEM((plan.ranks,) + vector.shape, f32),
            pltpu.VMEM((plan.planes,) + vector.shape, f32),
            dma((plan.ranks + plan.planes,)),
            dma((plan.ranks + plan.planes,)),
        ]
        + gather_scratch(plan),
        compiler_params=pltpu.CompilerParams(has_side_effects=True),
        cost_estimate=busy(120),
    )(own, vector)


def gelu_parts(u):
    scale = np.float32(np.sqrt(2.0 / np.pi))
    square = u * u
    inner = scale * u * (1.0 + 0.044715 * square)
    t = jnp.tanh(inner)
    value = 0.5 * u * (1.0 + t)
    slope = 0.5 * (1.0 + t) + 0.5 * u * (1.0 - t * t) * scale * (1.0 + 3 * 0.044715 * square)
    return value, slope


def adam_update(weight, first, second, grad, rate, count_now, decay):
    first_new = beta_first * first + (1.0 - beta_first) * grad
    second_new = beta_second * second + (1.0 - beta_second) * grad * grad
    steps_float = count_now.astype(f32)
    first_fix = 1.0 - jnp.power(beta_first, steps_float)
    second_fix = 1.0 - jnp.power(beta_second, steps_float)
    change = first_new / first_fix / (jnp.sqrt(second_new / second_fix) + adam_eps) + decay * weight
    return (weight - rate * change, first_new, second_new)


def after(value, *others):
    return lax.optimization_barrier((value,) + others)[0]


def per_device(
    tokens,
    cotangent,
    doc_ids,
    block_order,
    front_weight,
    back_weight,
    front_master,
    back_master,
    front_first,
    back_first,
    front_second,
    back_second,
    vectors,
    vector_first,
    vector_second,
    learn_rates,
    adam_step,
    *,
    plan,
):
    planes, shards, ranks, unit = plan.planes, plan.fsdp, plan.ranks, plan.unit
    both = ("ctx", "fsdp")
    contract_last = (((1,), (1,)), ((), ()))
    contract_first = (((0,), (0,)), ((), ()))
    c_index, f = lax.axis_index("ctx"), lax.axis_index("fsdp")
    z, k = c_index // 2, c_index % 2
    p = 2 * f + k
    rows = tokens.shape[1]
    plane_rows = 2 * shards * rows
    share = 2 * rows

    bias_front = vectors[:IN_COLS].reshape(-1, unit)
    bias_back = vectors[IN_COLS : IN_COLS + D]
    norm_gain = vectors[IN_COLS + D : IN_COLS + 2 * D]
    norm_shift = vectors[IN_COLS + 2 * D :]

    swap_pairs = [(2 * i + j, 2 * i + 1 - j) for i in range(planes) for j in range(2)]

    def swap_core(value):
        return lax.ppermute(value, "ctx", swap_pairs)

    def to_shard(value, step):
        return lax.ppermute(value, "fsdp", [(i, i ^ step) for i in range(shards)])

    def at(array, index):
        return lax.dynamic_index_in_dim(array, index, 0, keepdims=False)

    blocks = block_order.shape[0]
    block_tokens = doc_ids.shape[1] // blocks
    offsets = jnp.arange(block_tokens, dtype=jnp.int32)
    positions_all = (block_order[:, None] * block_tokens + offsets[None, :]).reshape(planes, share)

    plane_tokens, plane_grad, documents, weight_local, back_attention = gather_first(
        plan, tokens[0], cotangent[0], doc_ids.astype(f32), front_weight, back_weight
    )
    plane_tokens = plane_tokens.reshape(plane_rows, D)
    plane_grad = plane_grad.reshape(plane_rows, D)

    unit_table = pick(plan.rank_units, p)
    bias_local = jnp.take(bias_front, unit_table, axis=0).reshape(-1)

    seq_positions = positions_all.reshape(-1)
    tables = rotation_tables(seq_positions, 2 * HEAD_DIM)
    normed, qkvg = prepare(
        plane_tokens,
        plane_grad,
        weight_local,
        back_attention,
        bias_local[None, : 3 * unit],
        norm_gain[None],
        norm_shift[None],
        [lax.dynamic_slice(table, (z * share, 0), (share, 2 * HEAD_DIM)) for table in tables],
    )
    qkvg, back_up, activation, slope = exchange_first(
        plan, qkvg.reshape(planes, share, -1), normed, weight_local, bias_local[None, 3 * unit :], back_weight
    )
    qkvg = qkvg.reshape(planes * share, -1)

    doc_row = documents[0].astype(jnp.int32)
    seq_documents = jnp.take(doc_row.reshape(blocks, block_tokens), block_order, axis=0).reshape(-1)
    returned = attention(qkvg, seq_positions, seq_documents, tables)
    returned, up_grad = exchange_back(
        plan, returned.reshape(planes, share, -1), plane_grad, back_up, slope
    )
    returned = returned.reshape(plane_rows, -1)
    back_local = jnp.concatenate([back_attention, back_up], axis=0)

    mixed = jnp.concatenate([returned[:, :unit], activation], axis=1)
    hidden_grad = jnp.concatenate([returned[:, unit:], up_grad], axis=1)

    def sum_over_cores(value):
        shaped = value.reshape(shards, 2, rows, D)
        kept = lax.dynamic_index_in_dim(shaped, k, 1, keepdims=False)
        sent = lax.dynamic_index_in_dim(shaped, 1 - k, 1, keepdims=False).astype(bf16)
        return kept + swap_core(sent).astype(f32)

    def sum_over_shards(*values):
        totals = [at(value, f) for value in values]
        for step in range(1, shards):
            pieces = jnp.stack([at(value, f ^ step).astype(bf16) for value in values])
            pieces = to_shard(pieces, step).astype(f32)
            totals = [total + piece for total, piece in zip(totals, pieces)]
        return totals

    projected_cores = sum_over_cores(jnp.dot(mixed, back_local, preferred_element_type=f32))
    normed_grad_cores = sum_over_cores(
        lax.dot_general(hidden_grad, weight_local, contract_last, preferred_element_type=f32)
    )

    back_partial = lax.dot_general(
        mixed, plane_grad, contract_first, preferred_element_type=f32
    ).astype(bf16)
    back_sum, front_partial = back_sums(plan, back_partial, normed, hidden_grad)
    back_sum, projected_cores, normed_grad_cores = lax.optimization_barrier(
        (back_sum, projected_cores, normed_grad_cores)
    )
    projected, normed_grad = sum_over_shards(projected_cores, normed_grad_cores)
    front_sum, back_owned = front_sums(plan, front_partial, back_sum)
    front_sum, projected, normed_grad = lax.optimization_barrier((front_sum, projected, normed_grad))

    inputs = tokens[0].astype(f32)
    layer_out = (inputs + projected + bias_back).astype(bf16)[None]
    unscaled, factor = normalize(inputs)
    scaled = normed_grad * norm_gain
    input_grad = factor * (
        scaled
        - jnp.mean(scaled, axis=-1, keepdims=True)
        - unscaled * jnp.mean(scaled * unscaled, axis=-1, keepdims=True)
    )
    tokens_grad = (cotangent[0].astype(f32) + input_grad).astype(bf16)[None]

    back_grad = back_owned.astype(f32)
    back_new, back_first_new, back_second_new = adam_update(
        back_master, back_first, back_second, back_grad, learn_rates[1], adam_step[0], weight_decay
    )
    back_next, front_owned = back_nexts(plan, back_new.astype(bf16), front_sum)
    front_grad = front_owned.astype(f32)
    front_new, front_first_new, front_second_new = adam_update(
        front_master, front_first, front_second, front_grad, learn_rates[0], adam_step[0], weight_decay
    )
    def column_sums(value):
        ones = jnp.ones((8, value.shape[0]), bf16)
        return jnp.dot(ones, value, preferred_element_type=f32)[0]

    spread = (jnp.arange(7 * ranks)[:, None] == unit_table[None, :]).astype(f32)
    hidden_sum = column_sums(hidden_grad).reshape(7, unit)
    front_vector = jnp.sum(spread[:, :, None] * hidden_sum[None], axis=1).reshape(-1)
    vector_term = jnp.concatenate(
        [
            front_vector,
            column_sums(cotangent[0]),
            jnp.sum(normed_grad * unscaled, axis=0),
            jnp.sum(normed_grad, axis=0),
        ]
    )
    front_next, vector_grad = front_nexts(plan, front_new.astype(bf16), vector_term.reshape(-1, 128))
    vector_grad = vector_grad.reshape(-1)

    count_now = adam_step[0]
    vectors_new, vector_first_new, vector_second_new = adam_update(
        vectors, vector_first, vector_second, vector_grad, learn_rates[2], count_now, 0.0
    )

    return (
        layer_out,
        tokens_grad,
        front_grad,
        back_grad,
        vector_grad,
        front_new,
        back_new,
        vectors_new,
        front_first_new,
        back_first_new,
        vector_first_new,
        front_second_new,
        back_second_new,
        vector_second_new,
        front_next,
        back_next,
    )


def solution(mesh):
    plan = Layout(mesh.shape["ctx"], mesh.shape["fsdp"])
    tokens_spec = P("fsdp", "ctx", None)
    cols, owned, same = P(None, "fsdp"), P("ctx", "fsdp"), P()
    in_specs = (
        (tokens_spec, tokens_spec, P("fsdp", None), same, cols, cols)
        + (owned,) * 6
        + (same,) * 5
    )
    out_specs = (
        (tokens_spec, tokens_spec, owned, owned, same)
        + (owned, owned, same) * 3
        + (cols, cols)
    )
    return jax.shard_map(
        functools.partial(per_device, plan=plan),
        mesh=mesh,
        in_specs=in_specs,
        out_specs=out_specs,
        check_vma=False,
    )
```
